32 devices in a mesh: seq: 4 (over x, core), exp: 8 (over z, y).
Axes of the slice: x: 2, y: 2, z: 4, core: 2. Of those that a mesh axis runs over, the one named last changes fastest.
Arguments:
- tokens: bfloat16 [16, 1024, 1536], P('exp', 'seq'), may hold values from -6 to 6
- segment_ids: int32 [16, 1024], P('exp'), may hold values from -1 to 8, as said below
- routes: int32 [16, 1024, 6], P('exp', 'seq'), may hold values from 0 to 15, all different within a row; in each aligned block of 256 rows (0 to 255, 256 to 511, ..., all dimensions but the last counted through in order) at most 128 rows name the same one
- route_gates: float32 [16, 1024, 6], P('exp', 'seq'), may hold values from 0.1 to 0.35
- attn_gain: bfloat16 [1536], P(('seq', 'exp')), may hold values from 0.099609375 to 1.8984375
- query_proj: bfloat16 [1536, 1536], P(('seq', 'exp')), may hold values from -0.15625 to 0.15625
- key_proj: bfloat16 [1536, 512], P(('seq', 'exp')), may hold values from -0.15625 to 0.15625
- value_proj: bfloat16 [1536, 512], P(('seq', 'exp')), may hold values from -0.15625 to 0.15625
- output_proj: bfloat16 [1536, 1536], P(('seq', 'exp')), may hold values from -2 to 2
- ffn_gain: bfloat16 [1536], P(('seq', 'exp')), may hold values from 0.099609375 to 1.8984375
- shared_gate: bfloat16 [1536, 1024], P(('seq', 'exp')), may hold values from -0.15625 to 0.15625
- shared_up: bfloat16 [1536, 1024], P(('seq', 'exp')), may hold values from -0.15625 to 0.15625
- shared_down: bfloat16 [1024, 1536], P(('seq', 'exp')), may hold values from -0.1875 to 0.1875
- expert_gate: bfloat16 [16, 1536, 512], P('exp', 'seq'), may hold values from -0.15625 to 0.15625
- expert_up: bfloat16 [16, 1536, 512], P('exp', 'seq'), may hold values from -0.15625 to 0.15625
- expert_down: bfloat16 [16, 512, 1536], P('exp', 'seq'), may hold values from -0.5 to 0.5
- output_cot: bfloat16 [16, 1024, 1536], P('exp', 'seq'), may hold values from -6 to 6
Outputs:
- block_out: bfloat16 [16, 1024, 1536], P('exp', 'seq')
- tokens_grad: bfloat16 [16, 1024, 1536], P('exp', 'seq')
- gates_grad: float32 [16, 1024, 6], P('exp', 'seq')
- attn_gain_grad: float32 [1536], P(('seq', 'exp'))
- query_grad: float32 [1536, 1536], P(('seq', 'exp'))
- key_grad: float32 [1536, 512], P(('seq', 'exp'))
- value_grad: float32 [1536, 512], P(('seq', 'exp'))
- output_proj_grad: float32 [1536, 1536], P(('seq', 'exp'))
- ffn_gain_grad: float32 [1536], P(('seq', 'exp'))
- shared_gate_grad: float32 [1536, 1024], P(('seq', 'exp'))
- shared_up_grad: float32 [1536, 1024], P(('seq', 'exp'))
- shared_down_grad: float32 [1024, 1536], P(('seq', 'exp'))
- expert_gate_grad: float32 [16, 1536, 512], P('exp', 'seq')
- expert_up_grad: float32 [16, 1536, 512], P('exp', 'seq')
- expert_down_grad: float32 [16, 512, 1536], P('exp', 'seq')
The draws below stay inside these ranges and needn't reach their ends.
Inputs may be any that keep to these rules, and one draw needn't show every extreme that they name: `segment_ids`: within a sequence the ids never fall; the last 1 to 64 positions are padding, marked -1; the last document before the padding has the id 1024 // 200 + 3. `routes`: A row names 6 different experts. In the rows of one device and micro-batch (aligned blocks of 256 rows) no expert is named by more than 128 rows, a bound that some block reaches.
All inputs are finite; a program needn't handle non-finite values.
Results may differ from the reference program's by a relative error of at most 0.015.
Values may be sent and summed in bfloat16 or wider, within the bound.
A program may use at most 384 MiB of HBM per device.

```python
import math
import jax
import jax.numpy as jnp
import numpy as np
from jax import lax

D = 1536
HEADS = 12
KV_HEADS = 4
HEAD_DIM = 128
FFS = 1024
FFE = 512
TOPK = 6
TOK_MB = 256
MB = 2
DOC_MIN = 200
EXPERTS = 16
LEN = 1024
SEQS = 16
CAP = 128
QW = 1536
KVW = 512


def draw_segment_ids(key, part):
    key_pick, key_first, key_start, key_span, key_lengths, key_pad = jax.random.split(jax.random.fold_in(key, 7), 6)
    doc_slots = LEN // DOC_MIN + 2
    chosen_seq = jax.random.randint(key_pick, (SEQS // MB,), 0, MB)
    spanning = jnp.arange(SEQS) % MB == jnp.repeat(chosen_seq, MB)
    first_end = jax.random.randint(key_first, (SEQS,), 1, LEN + 1)
    span_begin = jax.random.randint(key_start, (SEQS,), 1, TOK_MB // 2)
    span_size = jax.random.randint(key_span, (SEQS,), LEN - TOK_MB, LEN - TOK_MB // 2 + 1)
    lengths = jax.random.randint(key_lengths, (SEQS, doc_slots), DOC_MIN, LEN + 1)
    head_part = jnp.where(spanning, span_begin, first_end)
    second_part = jnp.where(spanning, span_size, lengths[:, 0])
    increments = jnp.concatenate([head_part[:, None], second_part[:, None], lengths[:, 1:]], axis=1)
    bounds = jnp.cumsum(increments, axis=1)
    positions = jnp.arange(LEN)
    segment = jnp.sum((bounds[:, None, :] <= positions[None, :, None]).astype(jnp.int32), axis=2)
    padding = jax.random.randint(key_pad, (SEQS,), 1, TOK_MB // 4 + 1)
    last_real = jnp.take_along_axis(segment, (LEN - padding - 1)[:, None].astype(jnp.int32), axis=1)
    shifted = segment + (LEN // DOC_MIN + 3) - last_real
    return jnp.where(positions[None, :] >= LEN - padding[:, None], -1, shifted).astype(jnp.int32)


def block_scale(rng, dims, cuts, smallest, high):
    level, own = 1.0, jax.random.fold_in(rng, 6)
    for dim, parts in cuts:
        steps = jnp.exp(jax.random.uniform(jax.random.fold_in(own, dim), (parts,), jnp.float32, smallest / len(cuts), high / len(cuts)))
        level = level * jnp.repeat(steps, dims[dim] // parts).reshape([-1 if axis == dim else 1 for axis in range(len(dims))])
    return level


def routed_block(stream_key, own, number, rows, amount, top, bound, lean):
    sequence = jax.random.permutation(stream_key, amount)
    crowded, common = shares(amount, rows * top, bound, lean, True), shares(amount, rows * top, bound, lean, False)
    places = jnp.arange(amount)

    def named(sizes, rotation):
        used = int((sizes > 0).sum())
        fixed = max(1, used // 4)
        passed = fixed + (places - fixed + rotation * (used - fixed)) % max(1, amount - fixed)
        return jnp.zeros((amount,), jnp.int32).at[sequence[jnp.where(places < fixed, places, passed)]].set(jnp.asarray(sizes, jnp.int32))

    sizes = jnp.where(number % 4 == 0, named(crowded, number // 4), named(common, number - number // 4 - 1))
    mixed = jax.random.permutation(jax.random.fold_in(own, 3), amount)
    donor, taker = mixed[0:amount // 2 * 2:2], mixed[1:amount // 2 * 2:2]
    room = jnp.minimum(sizes[donor] - 1, bound - sizes[taker]) // 2
    room = jnp.where((donor == sequence[0]) | (taker == sequence[0]) | (sizes[taker] == 0), 0, jnp.maximum(room, 0))
    passed = jax.random.randint(jax.random.fold_in(own, 4), (amount // 2,), 0, 1 << 20) % (room + 1)
    sizes = sizes.at[donor].add(-passed).at[taker].add(passed)
    members = jnp.searchsorted(jnp.cumsum(sizes), jnp.arange(rows * top), side="right").astype(jnp.int32)
    listing = members.reshape(top, rows).T
    listing = listing[jax.random.permutation(jax.random.fold_in(own, 1), rows)]
    rotation = jax.random.randint(jax.random.fold_in(own, 2), (rows, 1), 0, top)
    return jnp.take_along_axis(listing, (jnp.arange(top)[None, :] + rotation) % top, axis=1)


def shares(amount, total, most, skew, full):
    loads = [(1 << 20) // math.isqrt(rank ** skew) + 1 for rank in range(1, amount + 1)]
    largest = most if full else min(most, max(-(-total // amount), total * loads[0] // sum(loads)))
    least = 1 if total - largest >= amount - 1 else 0
    holding, spare = [largest] + [least] * (amount - 1), total - largest - least * (amount - 1)
    while spare > 0:
        free = [i for i in range(1, amount) if holding[i] < largest] or [i for i in range(1, amount) if holding[i] < most]
        pool, budget = sum([loads[i] for i in free]), spare
        for i in free:
            extra = min(most - holding[i], max(1, budget * loads[i] // pool), spare)
            holding[i] = holding[i] + extra
            spare = spare - extra
    return np.array(holding)


def noise(stream_key, dims, width, most, cuts=(), held_as=jnp.bfloat16):
    array = jax.random.normal(stream_key, dims, jnp.float32) * width
    if len(cuts) > 0:
        array = block_scale(stream_key, dims, cuts, -0.22, 0.18) * array
    return jnp.clip(array, min=-most, max=most).astype(held_as)


def setup_inputs(seed: int = 0) -> dict:
    arg_keys = jax.random.split(jax.random.key(seed), 18)
    tokens = noise(arg_keys[0], (SEQS, LEN, D), 1.0, 6.0, ((0, 8), (1, 4)))
    segment_ids = draw_segment_ids(jax.random.fold_in(arg_keys[17], 71), 0)
    routes_keys = jax.random.split(jax.random.fold_in(arg_keys[2], 1), SEQS * LEN // TOK_MB)
    routes_turns = jax.random.permutation(jax.random.fold_in(arg_keys[2], 3), SEQS * LEN // TOK_MB)
    routes = jax.vmap(lambda own, number: routed_block(jax.random.fold_in(arg_keys[2], 2), own, number, TOK_MB, EXPERTS, TOPK, CAP, 2))(routes_keys, routes_turns).reshape((SEQS, LEN, TOPK))
    route_gates = jnp.clip(jnp.exp(math.log(0.35) - 1.2527629 * jax.random.uniform(arg_keys[3], (SEQS, LEN, TOPK), jnp.float32) ** block_scale(arg_keys[3], (SEQS, LEN, TOPK), ((0, 8), (1, 4)), -0.2, 0.2)), 0.1, 0.35)
    attn_gain = jnp.clip(1.0 + 0.18 * jax.random.normal(arg_keys[4], (D,), jnp.float32), 0.099609375, 1.8984375).astype(jnp.bfloat16)
    query_proj = noise(arg_keys[5], (D, QW), D ** -0.5, 0.15625, ((0, 32),))
    key_proj = noise(arg_keys[6], (D, KVW), D ** -0.5, 0.15625, ((0, 32),))
    value_proj = noise(arg_keys[7], (D, KVW), D ** -0.5, 0.15625, ((0, 32),))
    output_proj = noise(arg_keys[8], (QW, D), 8 ** -0.5, 2.0, ((0, 32),))
    ffn_gain = jnp.clip(1.0 + 0.18 * jax.random.normal(arg_keys[9], (D,), jnp.float32), 0.099609375, 1.8984375).astype(jnp.bfloat16)
    shared_gate = noise(arg_keys[10], (D, FFS), D ** -0.5, 0.15625, ((0, 32),))
    shared_up = noise(arg_keys[11], (D, FFS), D ** -0.5, 0.15625, ((0, 32),))
    shared_down = noise(arg_keys[12], (FFS, D), FFS ** -0.5, 0.1875, ((0, 32),))
    expert_gate = noise(arg_keys[13], (EXPERTS, D, FFE), D ** -0.5, 0.15625, ((0, 8), (1, 4)))
    expert_up = noise(arg_keys[14], (EXPERTS, D, FFE), D ** -0.5, 0.15625, ((0, 8), (1, 4)))
    expert_down = noise(arg_keys[15], (EXPERTS, FFE, D), (FFE // 4) ** -0.5, 0.5, ((0, 8), (1, 4)))
    output_cot = noise(arg_keys[16], (SEQS, LEN, D), 1.0, 6.0, ((0, 8), (1, 4)))
    return {"tokens": tokens, "segment_ids": segment_ids, "routes": routes, "route_gates": route_gates, "attn_gain": attn_gain, "query_proj": query_proj, "key_proj": key_proj, "value_proj": value_proj, "output_proj": output_proj, "ffn_gain": ffn_gain, "shared_gate": shared_gate, "shared_up": shared_up, "shared_down": shared_down, "expert_gate": expert_gate, "expert_up": expert_up, "expert_down": expert_down, "output_cot": output_cot}


EPSILON = 1e-05
NEGATIVE = -1e+30
HIGHEST = lax.Precision.HIGHEST

@jax.custom_vjp
def low(v):
    return lax.optimization_barrier(v.astype(jnp.bfloat16)).astype(jnp.float32)

@jax.custom_vjp
def low_back(v):
    return v

def low_keep(v):
    return (low(v), None)

def low_pass(kept, grad):
    return (grad,)

def back_keep(v):
    return (v, None)

def back_low(kept, grad):
    return (low(grad),)
low.defvjp(low_keep, low_pass)
low_back.defvjp(back_keep, back_low)

def matmul(left, right):
    return jnp.dot(left, right, precision=HIGHEST, preferred_element_type=jnp.float32)

def rms_normed(values, gain):
    inverse = lax.rsqrt(lax.optimization_barrier(jnp.mean(values * values, axis=-1, keepdims=True)) + EPSILON)
    return values * inverse * gain

def group_forward(weights, inputs, segments, route_ids, gate_part):
    attn_gain, query_proj, key_proj, value_proj, output_proj, ffn_gain, shared_gate, shared_up, shared_down, expert_gate, expert_up, expert_down = weights
    group_size, length, model_width = inputs.shape
    row_count = group_size * length
    flat_rows = inputs.reshape(row_count, model_width)
    normed = low(rms_normed(flat_rows, attn_gain))
    queries = low(low_back(matmul(normed, query_proj))).reshape(group_size, length, KV_HEADS, HEADS // KV_HEADS, HEAD_DIM)
    keys_all = low(low_back(matmul(normed, key_proj))).reshape(group_size, length, KV_HEADS, HEAD_DIM)
    values_all = low(low_back(matmul(normed, value_proj))).reshape(group_size, length, KV_HEADS, HEAD_DIM)
    score_scale = HEAD_DIM ** (-0.5)
    scores = low_back(score_scale * jnp.einsum('bikgd,bjkd->bkgij', queries, keys_all, precision=HIGHEST))
    positions = jnp.arange(length, dtype=jnp.int32)
    boundary = jnp.concatenate([jnp.ones((group_size, 1), jnp.bool_), segments[:, 1:] != segments[:, :-1]], axis=1)
    starts = lax.cummax(jnp.where(boundary, positions[None, :], 0), axis=1)
    allowed = (positions[None, None, :] >= starts[:, :, None]) & (positions[None, None, :] <= positions[None, :, None]) & (segments[:, :, None] >= 0)
    allowed = allowed[:, None, None, :, :]
    masked = jnp.where(allowed, scores, NEGATIVE)
    row_max = lax.optimization_barrier(jnp.max(masked, axis=-1, keepdims=True))
    exponent = jnp.where(allowed, jnp.exp(masked - row_max), 0.0)
    row_total = lax.optimization_barrier(jnp.sum(exponent, axis=-1, keepdims=True))
    weights_low = low(exponent / jnp.where(row_total > 0.5, row_total, 1.0))
    context = jnp.einsum('bkgij,bjkd->bikgd', weights_low, values_all, precision=HIGHEST).reshape(row_count, HEADS * HEAD_DIM)
    residual = flat_rows + low_back(matmul(low(low_back(context)), output_proj))
    normed_two = low(rms_normed(residual, ffn_gain))
    shared_pre_gate = low_back(matmul(normed_two, shared_gate))
    shared_pre_up = low_back(matmul(normed_two, shared_up))
    shared_out = low_back(matmul(low(jax.nn.silu(shared_pre_gate) * shared_pre_up), shared_down))
    flat_ids = route_ids.reshape(-1)
    flat_gates = gate_part.reshape(-1)
    pick_count = flat_ids.shape[0]
    expert_count = expert_gate.shape[0]
    sort_order = jnp.argsort(flat_ids, stable=True).astype(jnp.int32)
    counts = lax.optimization_barrier(jnp.sum((flat_ids[:, None] == jnp.arange(expert_count, dtype=jnp.int32)[None, :]).astype(jnp.int32), axis=0))
    offsets = jnp.cumsum(counts) - counts
    slot_room = row_count // TOK_MB * CAP
    slot_index = jnp.arange(slot_room, dtype=jnp.int32)
    slot_used = slot_index[None, :] < counts[:, None]
    chosen = sort_order[jnp.minimum(offsets[:, None] + slot_index[None, :], pick_count - 1)]
    token_rows = chosen // TOPK
    expert_inputs = jnp.where(slot_used[..., None], low_back(normed_two[token_rows]), 0.0)
    expert_pre_gate = low_back(jnp.einsum('emd,edf->emf', expert_inputs, expert_gate, precision=HIGHEST))
    expert_pre_up = low_back(jnp.einsum('emd,edf->emf', expert_inputs, expert_up, precision=HIGHEST))
    expert_hidden = low(jax.nn.silu(expert_pre_gate) * expert_pre_up)
    expert_value = low(low_back(jnp.einsum('emf,efd->emd', expert_hidden, expert_down, precision=HIGHEST)))
    weighted = jnp.where(slot_used[..., None], expert_value * flat_gates[chosen][..., None], 0.0)
    mixture = jax.ops.segment_sum(weighted.reshape(-1, model_width), token_rows.reshape(-1), num_segments=row_count)
    return (residual + shared_out + mixture).reshape(group_size, length, model_width)

def reference(tokens, segment_ids, routes, route_gates, attn_gain, query_proj, key_proj, value_proj, output_proj, ffn_gain, shared_gate, shared_up, shared_down, expert_gate, expert_up, expert_down, output_cot):
    group_size = math.gcd(SEQS, max(1, 4096 // LEN))
    block_count = SEQS // group_size

    def forward(tokens_f, gates_f, *weights):

        def step(state_carry, pieces):
            return (state_carry, group_forward(weights, pieces[0], pieces[1], pieces[2], pieces[3]))
        pieces = (tokens_f.reshape(block_count, group_size, LEN, D), segment_ids.reshape(block_count, group_size, LEN), routes.reshape(block_count, group_size, LEN, TOPK), gates_f.reshape(block_count, group_size, LEN, TOPK))
        state_carry, outputs = lax.scan(jax.checkpoint(step), jnp.zeros((), jnp.float32), pieces)
        return outputs.reshape(SEQS, LEN, D)
    floats = [attn_gain, query_proj, key_proj, value_proj, output_proj, ffn_gain, shared_gate, shared_up, shared_down, expert_gate, expert_up, expert_down]
    floats = [item.astype(jnp.float32) for item in floats]
    output, pullback = jax.vjp(forward, tokens.astype(jnp.float32), route_gates.astype(jnp.float32), *floats)
    grads = pullback(output_cot.astype(jnp.float32))
    return (output.astype(jnp.bfloat16), grads[0].astype(jnp.bfloat16), grads[1], grads[2], grads[3], grads[4], grads[5], grads[6], grads[7], grads[8], grads[9], grads[10], grads[11], grads[12], grads[13])
```

```python
import jax
import jax.numpy as jnp
from jax import lax
from jax.sharding import PartitionSpec as P

HEADS = 12
KV_HEADS = 4
HEAD_DIM = 128
GROUP_HEADS = HEADS // KV_HEADS
EPSILON = 1e-05
NEGATIVE = -1e30
F32 = jnp.float32
BF16 = jnp.bfloat16


def mm(spec, left, right):
    return jnp.einsum(spec, left, right, preferred_element_type=F32)


def exchange(value, axis, bit):
    size = lax.axis_size(axis)
    return lax.ppermute(value, axis, [(i, i ^ bit) for i in range(size)])


def rotate(value, axis, step):
    size = lax.axis_size(axis)
    return lax.ppermute(value, axis, [(i, (i + step) % size) for i in range(size)])


def in_order(flag, own, other, axis):
    return jnp.where(
        flag == 0,
        jnp.concatenate([own, other], axis),
        jnp.concatenate([other, own], axis),
    )


def silu_parts(pre_act):
    sigma_val = jax.nn.sigmoid(pre_act)
    return (pre_act * sigma_val, sigma_val * (1.0 + pre_act * (1.0 - sigma_val)))


def norm_back(grad_normed, values, inv_rms, gain):
    scaled = grad_normed * gain
    inner = jnp.mean(scaled * values, axis=1, keepdims=True)
    grad_values = inv_rms * scaled - values * (inv_rms * inv_rms * inv_rms) * inner
    return grad_values, jnp.sum(grad_normed * values * inv_rms, axis=0)


def group_gather(value):
    over_y = jnp.stack([value, exchange(value, "exp", 1)])
    over_z = jnp.concatenate([over_y, exchange(over_y, "exp", 2)])
    other = exchange(over_z, "seq", 1)
    return over_z, other


def group_scatter(own, other):
    part = own.astype(F32) + exchange(other, "seq", 1).astype(F32)
    part = part[:2] + exchange(part[2:].astype(BF16), "exp", 2).astype(F32)
    return part[0] + exchange(part[1].astype(BF16), "exp", 1).astype(F32)


def on_device(
    tokens,
    segment_ids,
    routes,
    route_gates,
    attn_gain,
    query_proj,
    key_proj,
    value_proj,
    output_proj,
    ffn_gain,
    shared_gate,
    shared_up,
    shared_down,
    expert_gate,
    expert_up,
    expert_down,
    output_cot,
):
    micro_count, row_count, model_width = tokens.shape
    exp_count = lax.axis_size("exp")
    local_experts, gate_rows, expert_width = expert_gate.shape
    down_rows = expert_down.shape[1]
    all_experts = local_experts * exp_count
    route_count = routes.shape[2]
    capacity = 4 * row_count * route_count // (3 * all_experts)
    score_scale = HEAD_DIM ** (-0.5)
    query_width = HEADS * HEAD_DIM
    kv_width = KV_HEADS * HEAD_DIM
    far_steps = exp_count // 4
    assert lax.axis_size("seq") == 4 and local_experts == 2

    seq_index = lax.axis_index("seq")
    exp_index = lax.axis_index("exp")
    core = seq_index % 2
    half = seq_index // 2
    everywhere = ("seq", "exp")

    pad = jnp.zeros((attn_gain.shape[0], 126), BF16)
    first = jnp.concatenate(
        [query_proj, key_proj, value_proj, attn_gain[:, None], ffn_gain[:, None], pad], axis=1
    )
    first = lax.all_gather(first, everywhere, axis=0, tiled=True)
    qkv_width = query_width + 2 * kv_width
    qkv_proj = first[:, :qkv_width]
    gain_one = first[:, qkv_width].astype(F32)
    gain_two = first[:, qkv_width + 1].astype(F32)
    out_proj = lax.all_gather(output_proj, everywhere, axis=0, tiled=True)
    up_proj = lax.all_gather(
        jnp.concatenate([shared_gate, shared_up], axis=1), everywhere, axis=0, tiled=True
    )
    down_proj = lax.all_gather(shared_down, everywhere, axis=0, tiled=True)

    wide = jnp.concatenate([expert_gate, expert_up], axis=2)

    def parity(value):
        kept = lax.dynamic_index_in_dim(value, core, 0, False)
        sent = lax.dynamic_index_in_dim(value, 1 - core, 0, False)
        return in_order(core, kept, exchange(sent, "seq", 1), 0)

    wide_part, down_part = parity(wide), parity(expert_down)
    wide_far, down_far = [wide_part], [down_part]
    for _ in range(far_steps - 1):
        wide_far.append(rotate(wide_far[-1], "exp", 4))
        down_far.append(rotate(down_far[-1], "exp", 4))
    wide_full = [in_order(half, w, exchange(w, "seq", 2), 0) for w in wide_far]
    down_full = [in_order(half, w, exchange(w, "seq", 2), 0) for w in down_far]
    expert_ids = [
        local_experts * ((exp_index - 4 * k + exp_count) % exp_count) + core
        for k in range(far_steps)
    ]

    expert_range = jnp.arange(all_experts, dtype=jnp.int32)
    gate_table = jnp.sum(
        jnp.where(
            jnp.swapaxes(routes, 1, 2)[:, :, None, :] == expert_range[None, None, :, None],
            jnp.swapaxes(route_gates, 1, 2)[:, :, None, :],
            0.0,
        ),
        axis=1,
    )
    gate_blocks = jnp.concatenate(group_gather(gate_table))
    cot_own, cot_other = group_gather(output_cot)

    order = jnp.arange(row_count, dtype=jnp.int32)
    before = (order[:, None] < order[None, :]).astype(BF16)
    slots = jnp.arange(capacity, dtype=jnp.int32)

    inputs = tokens.reshape(micro_count * row_count, model_width).astype(F32)
    inv_one = lax.rsqrt(jnp.mean(inputs * inputs, axis=1, keepdims=True) + EPSILON)
    normed_one = (inputs * inv_one * gain_one).astype(BF16)
    qkv = jnp.dot(normed_one, qkv_proj, preferred_element_type=F32).astype(BF16)
    qkv = qkv.reshape(micro_count, row_count, qkv_width)

    def attend(micro):
        queries = qkv[micro, :, :query_width]
        kv_own = qkv[micro, :, query_width:]
        kv_x = exchange(kv_own, "seq", 2)
        kv_core = exchange(jnp.stack([kv_own, kv_x]), "seq", 1)
        kv = jnp.concatenate([kv_own, kv_core[0], kv_x, kv_core[1]])
        query_heads = queries.reshape(row_count, KV_HEADS, GROUP_HEADS, HEAD_DIM)
        key_heads = kv[:, :kv_width].reshape(-1, KV_HEADS, HEAD_DIM)
        value_heads = kv[:, kv_width:].reshape(-1, KV_HEADS, HEAD_DIM)
        segments = segment_ids[micro].reshape(4, row_count)
        key_ids = jnp.concatenate(
            [lax.dynamic_index_in_dim(segments, seq_index ^ j, 0, False) for j in range(4)]
        )
        key_pos = jnp.concatenate([(seq_index ^ j) * row_count + order for j in range(4)])
        query_ids, query_pos = key_ids[:row_count], key_pos[:row_count]
        allowed = (
            (key_ids[None, :] == query_ids[:, None])
            & (key_pos[None, :] <= query_pos[:, None])
            & (query_ids[:, None] >= 0)
        )
        scores = mm("ikgd,jkd->kgij", query_heads, key_heads) * score_scale
        row_max = jnp.max(jnp.where(allowed, scores, NEGATIVE), axis=3, keepdims=True)
        exponent = jnp.where(allowed, jnp.exp(jnp.where(allowed, scores, NEGATIVE) - row_max), 0.0)
        row_total = jnp.sum(exponent, axis=3, keepdims=True)
        row_safe = jnp.where(row_total > 0.5, row_total, 1.0)
        weights_low = (exponent / row_safe).astype(BF16)
        context = mm("kgij,jkd->ikgd", weights_low, value_heads)
        context = context.reshape(row_count, query_width).astype(BF16)
        return context, (query_heads, key_heads, value_heads, allowed, row_max, row_safe)

    def attend_back(grad_context, kept):
        query_heads, key_heads, value_heads, allowed, row_max, row_safe = kept
        grad_context = grad_context.reshape(row_count, KV_HEADS, GROUP_HEADS, HEAD_DIM)
        scores = mm("ikgd,jkd->kgij", query_heads, key_heads) * score_scale
        weights = (
            jnp.where(allowed, jnp.exp(jnp.where(allowed, scores, NEGATIVE) - row_max), 0.0)
            / row_safe
        )
        grad_weights = mm("ikgd,jkd->kgij", grad_context, value_heads)
        row_delta = jnp.sum(weights * grad_weights, axis=3, keepdims=True)
        grad_scores = (weights * (grad_weights - row_delta)).astype(BF16)
        grad_queries = (mm("kgij,jkd->ikgd", grad_scores, key_heads) * score_scale).astype(BF16)
        grad_keys = mm("kgij,ikgd->jkd", grad_scores, query_heads) * score_scale
        grad_values = mm("kgij,ikgd->jkd", weights.astype(BF16), grad_context)
        grad_kv = jnp.concatenate(
            [grad_keys.reshape(-1, kv_width), grad_values.reshape(-1, kv_width)], axis=1
        ).reshape(4, row_count, 2 * kv_width)
        part = grad_kv[0::2] + exchange(grad_kv[1::2].astype(BF16), "seq", 1).astype(F32)
        grad_kv = part[0] + exchange(part[1].astype(BF16), "seq", 2).astype(F32)
        return jnp.concatenate([grad_queries.reshape(row_count, query_width), grad_kv.astype(BF16)], axis=1)

    def experts(micro, normed_blocks, cot_blocks):
        mixed, graded, kept = 0.0, 0.0, []
        for k in range(far_steps):
            gates = lax.dynamic_index_in_dim(gate_blocks[:, micro], expert_ids[k], 1, False)
            named = gates > 0.0
            rank = jnp.dot(named.astype(BF16), before, preferred_element_type=F32).astype(jnp.int32)
            picked = (rank[:, None, :] == slots[None, :, None]) & named[:, None, :]
            pick = picked.astype(BF16)
            slot_gates = jnp.sum(jnp.where(picked, gates[:, None, :], 0.0), axis=2).reshape(-1, 1)
            rows = mm("bst,btd->bsd", pick, normed_blocks).astype(BF16).reshape(-1, model_width)
            cots = mm("bst,btd->bsd", pick, cot_blocks).astype(BF16).reshape(-1, model_width)
            pre = jnp.dot(rows, wide_full[k], preferred_element_type=F32)
            pre_gate, pre_up = pre[:, :expert_width], pre[:, expert_width:]
            grad_hidden = mm("rd,fd->rf", cots, down_full[k])
            act, deriv = silu_parts(pre_gate)
            hidden = act * pre_up
            gate_grad = jnp.sum(hidden * grad_hidden, axis=1, keepdims=True)
            hidden = (hidden * slot_gates).astype(BF16)
            grad_hidden = grad_hidden * slot_gates
            grad_pre = jnp.concatenate(
                [(grad_hidden * pre_up * deriv).astype(BF16), (grad_hidden * act).astype(BF16)], axis=1
            )
            value = jnp.dot(hidden, down_full[k], preferred_element_type=F32).astype(BF16)
            column = (lax.broadcasted_iota(jnp.int32, (1, 128), 1) == expert_ids[k]).astype(F32)
            value = jnp.concatenate([value, (gate_grad * column).astype(BF16)], axis=1)
            grad_rows = mm("rf,df->rd", grad_pre, wide_full[k]).astype(BF16)
            blocks = pick.shape[0]
            mixed = mixed + mm("bst,bsd->btd", pick, value.reshape(blocks, capacity, -1))
            graded = graded + mm("bst,bsd->btd", pick, grad_rows.reshape(blocks, capacity, -1))
            kept.append((rows, cots, hidden, grad_pre))
        graded = graded.astype(BF16)
        mixed = mixed.astype(BF16)
        return group_scatter(graded[:4], graded[4:]), group_scatter(mixed[:4], mixed[4:]), kept

    contexts, residuals, inv_twos, normed_twos, attention_kept = [], [], [], [], []
    moe_grads, moe_outs, expert_kept = [], [], []
    for micro in range(micro_count):
        context, kept = attend(micro)
        residual = inputs[micro * row_count : (micro + 1) * row_count] + jnp.dot(
            context, out_proj, preferred_element_type=F32
        )
        inv_two = lax.rsqrt(jnp.mean(residual * residual, axis=1, keepdims=True) + EPSILON)
        normed_two = (residual * inv_two * gain_two).astype(BF16)
        contexts.append(context)
        residuals.append(residual)
        inv_twos.append(inv_two)
        normed_twos.append(normed_two)
        attention_kept.append(kept)
        normed_blocks = jnp.concatenate(group_gather(normed_two))
        cot_blocks = jnp.concatenate([cot_own[:, micro], cot_other[:, micro]])
        grads, outs, kept = experts(micro, normed_blocks, cot_blocks)
        moe_grads.append(grads)
        moe_outs.append(outs)
        expert_kept.append(kept)

    def expert_sum(left, right):
        own = None
        for k in reversed(range(far_steps)):
            lefts = jnp.concatenate([m[k][left] for m in expert_kept])
            rights = jnp.concatenate([m[k][right] for m in expert_kept])
            if far_steps > 2 and own is not None:
                lefts, rights, own = lax.optimization_barrier((lefts, rights, own))
            total = mm("rd,rf->df", lefts, rights)
            rows = total.shape[0] // 2
            total = total.reshape(2, rows, -1)
            mine = lax.dynamic_index_in_dim(total, half, 0, False)
            sent = lax.dynamic_index_in_dim(total, 1 - half, 0, False).astype(BF16)
            total = mine + exchange(sent, "seq", 2).astype(F32)
            own = total if own is None else total + rotate(own.astype(BF16), "exp", -4).astype(F32)
        rows = own.shape[0] // 2
        own = own.reshape(2, rows, -1)
        kept = lax.dynamic_index_in_dim(own, core, 0, False)
        sent = lax.dynamic_index_in_dim(own, 1 - core, 0, False).astype(BF16)
        other = exchange(sent, "seq", 1).astype(F32)
        return in_order(core, kept[None], other[None], 0)

    down_grad = expert_sum(2, 1)
    if far_steps > 2:
        down_grad, expert_kept = lax.optimization_barrier((down_grad, expert_kept))
    wide_grad = expert_sum(0, 3)

    normed_two = jnp.concatenate(normed_twos)
    upstream_low = output_cot.reshape(micro_count * row_count, model_width)
    shared_pre = jnp.dot(normed_two, up_proj, preferred_element_type=F32)
    shared_width = shared_gate.shape[1]
    shared_pre_gate, shared_pre_up = shared_pre[:, :shared_width], shared_pre[:, shared_width:]
    shared_act, shared_deriv = silu_parts(shared_pre_gate)
    shared_hidden = (shared_act * shared_pre_up).astype(BF16)
    shared_out = jnp.dot(shared_hidden, down_proj, preferred_element_type=F32)
    grad_shared_hidden = mm("rd,fd->rf", upstream_low, down_proj)
    grad_shared_pre = jnp.concatenate(
        [
            (grad_shared_hidden * shared_pre_up * shared_deriv).astype(BF16),
            (grad_shared_hidden * shared_act).astype(BF16),
        ],
        axis=1,
    )
    grad_from_shared = mm("rf,df->rd", grad_shared_pre, up_proj)

    def summed(value):
        return lax.psum_scatter(
            value.astype(BF16), everywhere, scatter_dimension=0, tiled=True
        ).astype(F32)

    shared_up_sum = summed(mm("rd,rf->df", normed_two, grad_shared_pre))
    shared_down_sum = summed(mm("rd,rf->df", shared_hidden, upstream_low))

    branches, grad_residuals, grad_qkv, outputs, gate_grads = [], [], [], [], []
    gain_two_sum = 0.0
    for micro in range(micro_count):
        rows = slice(micro * row_count, (micro + 1) * row_count)
        grad_normed = moe_grads[micro] + grad_from_shared[rows]
        grad_from_two, gain_part = norm_back(grad_normed, residuals[micro], inv_twos[micro], gain_two)
        gain_two_sum = gain_two_sum + gain_part
        grad_residual = upstream_low[rows].astype(F32) + grad_from_two
        grad_branch = grad_residual.astype(BF16)
        grad_residuals.append(grad_residual)
        branches.append(grad_branch)
        grad_context = mm("rd,id->ri", grad_branch, out_proj).astype(BF16)
        grad_qkv.append(attend_back(grad_context, attention_kept[micro]))
        out = moe_outs[micro]
        outputs.append(
            (residuals[micro] + shared_out[rows] + out[:, :model_width]).astype(BF16)
        )
        table = out[:, model_width : model_width + all_experts]
        gate_grads.append(
            jnp.sum(
                jnp.where(
                    routes[micro][:, :, None] == expert_range[None, None, :], table[:, None, :], 0.0
                ),
                axis=2,
            )
        )

    output_sum = summed(mm("rd,rf->df", jnp.concatenate(contexts), jnp.concatenate(branches)))
    grad_qkv = jnp.concatenate(grad_qkv)
    grad_normed_one = mm("ri,di->rd", grad_qkv, qkv_proj)
    grad_from_one, gain_one_sum = norm_back(grad_normed_one, inputs, inv_one, gain_one)
    token_grads = (jnp.concatenate(grad_residuals) + grad_from_one).astype(BF16)
    qkv_sum = mm("rd,rf->df", normed_one, grad_qkv).astype(BF16)
    gains = jnp.stack([gain_one_sum, gain_two_sum], axis=1).astype(BF16)
    gains = jnp.concatenate([gains, jnp.zeros((model_width, 126), BF16)], axis=1)
    last = summed(jnp.concatenate([qkv_sum, gains], axis=1))

    return (
        jnp.stack(outputs),
        token_grads.reshape(micro_count, row_count, model_width),
        jnp.stack(gate_grads),
        last[:, qkv_width],
        last[:, :query_width],
        last[:, query_width : query_width + kv_width],
        last[:, query_width + kv_width : qkv_width],
        output_sum,
        last[:, qkv_width + 1],
        shared_up_sum[:, :shared_width],
        shared_up_sum[:, shared_width:],
        shared_down_sum,
        wide_grad[:, :, :expert_width],
        wide_grad[:, :, expert_width:],
        down_grad,
    )


def solution(mesh):
    rows = P(("seq", "exp"), None)
    wide = P("exp", "seq", None)
    flat = P(("seq", "exp"))
    return jax.shard_map(
        on_device,
        mesh=mesh,
        in_specs=(wide, P("exp", None), wide, wide, flat, rows, rows, rows, rows, flat, rows, rows, rows)
        + (wide,) * 4,
        out_specs=(wide, wide, wide, flat, rows, rows, rows, rows, flat, rows, rows, rows)
        + (wide,) * 3,
        check_vma=False,
    )
```

```python
import functools

import jax
import jax.numpy as jnp
from jax import lax
from jax.experimental import pallas as pl
from jax.experimental.pallas import tpu as pltpu
from jax.sharding import PartitionSpec as P

HEADS = 12
KV_HEADS = 4
HEAD_DIM = 128
GROUP_HEADS = HEADS // KV_HEADS
EPSILON = 1e-05
NEGATIVE = -1e30
F32 = jnp.float32
BF16 = jnp.bfloat16


def mm(spec, left, right):
    return jnp.einsum(spec, left, right, preferred_element_type=F32)


def exchange(value, axis, bit):
    size = lax.axis_size(axis)
    return lax.ppermute(value, axis, [(i, i ^ bit) for i in range(size)])


def rotate(value, axis, step):
    size = lax.axis_size(axis)
    return lax.ppermute(value, axis, [(i, (i + step) % size) for i in range(size)])


def after(value, *others):
    return lax.optimization_barrier((value, others))[0]


def in_order(flag, own, other, axis):
    return jnp.where(
        flag == 0,
        jnp.concatenate([own, other], axis),
        jnp.concatenate([other, own], axis),
    )


def silu_parts(pre_act):
    sigma_val = jax.nn.sigmoid(pre_act)
    return (pre_act * sigma_val, sigma_val * (1.0 + pre_act * (1.0 - sigma_val)))


def norm_back(grad_normed, values, inv_rms, gain):
    scaled = grad_normed * gain
    inner = jnp.mean(scaled * values, axis=1, keepdims=True)
    grad_values = inv_rms * scaled - values * (inv_rms * inv_rms * inv_rms) * inner
    return grad_values, jnp.sum(grad_normed * values * inv_rms, axis=0)


def group_gather(value):
    over_y = jnp.stack([value, exchange(value, "exp", 1)])
    over_z = jnp.concatenate([over_y, exchange(over_y, "exp", 2)])
    other = exchange(over_z, "seq", 1)
    return over_z, other


def group_scatter(own, other):
    part = own.astype(F32) + exchange(other, "seq", 1).astype(F32)
    part = part[:2] + exchange(part[2:].astype(BF16), "exp", 2).astype(F32)
    return part[0] + exchange(part[1].astype(BF16), "exp", 1).astype(F32)


def dot(left, right, over):
    return lax.dot_general(left, right, ((over[:1], over[1:]), ((), ())), preferred_element_type=F32)


def masked_softmax(query, keys, allowed, scale):
    scores = jnp.where(allowed, dot(query, keys, (1, 1)) * scale, NEGATIVE)
    expo = jnp.where(allowed, jnp.exp(scores - jnp.max(scores, axis=1, keepdims=True)), 0.0)
    total = jnp.sum(expo, axis=1, keepdims=True)
    return expo * (1.0 / jnp.where(total > 0.5, total, 1.0))


def attention_kernel(scale, mask_ref, query_ref, *refs):
    keys = jnp.concatenate([r[...] for r in refs[:4]])
    values = jnp.concatenate([r[...] for r in refs[4:8]])
    context_ref = refs[8]
    allowed = mask_ref[...] > 0
    for g in range(GROUP_HEADS):
        lanes = slice(g * HEAD_DIM, (g + 1) * HEAD_DIM)
        weights = masked_softmax(query_ref[:, lanes], keys, allowed, scale)
        context_ref[:, lanes] = dot(weights.astype(BF16), values, (1, 0)).astype(BF16)


def attention_back_kernel(scale, mask_ref, query_ref, *refs):
    keys = jnp.concatenate([r[...] for r in refs[:4]])
    values = jnp.concatenate([r[...] for r in refs[4:8]])
    grad_ref, grad_query_ref, grad_key_ref, grad_value_ref = refs[8:]
    allowed = mask_ref[...] > 0
    grad_keys = grad_values = 0.0
    for g in range(GROUP_HEADS):
        lanes = slice(g * HEAD_DIM, (g + 1) * HEAD_DIM)
        query, grad = query_ref[:, lanes], grad_ref[:, lanes]
        weights = masked_softmax(query, keys, allowed, scale)
        grad_weights = dot(grad, values, (1, 1))
        delta = jnp.sum(weights * grad_weights, axis=1, keepdims=True)
        grad_scores = (weights * (grad_weights - delta)).astype(BF16)
        grad_query_ref[:, lanes] = (dot(grad_scores, keys, (1, 0)) * scale).astype(BF16)
        grad_keys = grad_keys + dot(query, grad_scores, (0, 0))
        grad_values = grad_values + dot(grad, weights.astype(BF16), (0, 0))
    grad_key_ref[...] = (grad_keys * scale).T.astype(BF16)
    grad_value_ref[...] = grad_values.T.astype(BF16)


def attention_specs(row_count):
    wide = GROUP_HEADS * HEAD_DIM
    whole = pl.BlockSpec((row_count, 4 * row_count), lambda h: (0, 0))
    query = pl.BlockSpec((row_count, wide), lambda h: (0, h))
    head = lambda at: pl.BlockSpec((row_count, HEAD_DIM), lambda h: (0, h + at))
    heads = [head(HEADS), *[head(0)] * 3, head(HEADS + KV_HEADS), *[head(KV_HEADS)] * 3]
    return whole, query, heads


def attention(mask, queries, kv):
    row_count = queries.shape[0]
    whole, query, heads = attention_specs(row_count)
    return pl.pallas_call(
        functools.partial(attention_kernel, HEAD_DIM ** (-0.5)),
        grid=(KV_HEADS,),
        in_specs=[whole, query, *heads],
        out_specs=query,
        out_shape=jax.ShapeDtypeStruct((row_count, HEADS * HEAD_DIM), BF16),
        compiler_params=pltpu.CompilerParams(vmem_limit_bytes=48 << 20),
        name="attention",
    )(mask, queries, *kv, *kv)


def attention_back(mask, queries, kv, grad):
    row_count = queries.shape[0]
    whole, query, heads = attention_specs(row_count)
    column = pl.BlockSpec((4 * row_count, HEAD_DIM), lambda h: (0, h))
    flat = jax.ShapeDtypeStruct((4 * row_count, KV_HEADS * HEAD_DIM), BF16)
    return pl.pallas_call(
        functools.partial(attention_back_kernel, HEAD_DIM ** (-0.5)),
        grid=(KV_HEADS,),
        in_specs=[whole, query, *heads, query],
        out_specs=[query, column, column],
        out_shape=[jax.ShapeDtypeStruct((row_count, HEADS * HEAD_DIM), BF16), flat, flat],
        compiler_params=pltpu.CompilerParams(vmem_limit_bytes=48 << 20),
        name="attention_back",
    )(mask, queries, *kv, *kv, grad)


def expert_kernel(
    slot_ref, gate_ref, column_ref, token_ref, cot_ref, wide_ref, down_ref, *refs
):
    rows_ref, cots_ref, hidden_ref, pre_ref, mixed_ref, graded_ref = refs[-10:-4]
    pick_ref, value_ref, extra_ref, back_ref = refs[-4:]
    count, width = down_ref.shape[0], down_ref.shape[1]
    blocks, row_count = token_ref.shape[0], token_ref.shape[1]
    room = rows_ref.shape[2] // blocks
    slot = lax.broadcasted_iota(jnp.int32, (room, row_count), 0)
    gates = []
    for b in range(blocks):
        for k in range(count):
            picked = slot == slot_ref[k, b]
            gates.append(jnp.sum(jnp.where(picked, gate_ref[k, b], 0.0), axis=1, keepdims=True))
            pick_ref[b, k * room : (k + 1) * room, :] = jnp.where(picked, 1.0, 0.0).astype(BF16)
        rows = dot(pick_ref[b], token_ref[b], (1, 0)).astype(BF16)
        cots = dot(pick_ref[b], cot_ref[b], (1, 0)).astype(BF16)
        for k in range(count):
            part = slice(b * room, (b + 1) * room)
            rows_ref[k, 0, part, :] = rows[k * room : (k + 1) * room]
            cots_ref[k, 0, part, :] = cots[k * room : (k + 1) * room]
    for k in range(count):
        gate = jnp.concatenate([gates[b * count + k] for b in range(blocks)])
        pre = dot(rows_ref[k, 0], wide_ref[k], (1, 0))
        grad_hidden = dot(cots_ref[k, 0], down_ref[k], (1, 1))
        pre_gate, pre_up = pre[:, :width], pre[:, width:]
        act, deriv = silu_parts(pre_gate)
        hidden = act * pre_up
        gate_grad = jnp.sum(hidden * grad_hidden, axis=1, keepdims=True)
        grad_hidden = grad_hidden * gate
        hidden_ref[k, 0] = (hidden * gate).astype(BF16)
        pre_ref[k, 0, :, :width] = (grad_hidden * pre_up * deriv).astype(BF16)
        pre_ref[k, 0, :, width:] = (grad_hidden * act).astype(BF16)
        value = dot(hidden_ref[k, 0], down_ref[k], (1, 0)).astype(BF16)
        back = dot(pre_ref[k, 0], wide_ref[k], (1, 1)).astype(BF16)
        extra = (gate_grad * column_ref[k]).astype(BF16)
        for b in range(blocks):
            to, part = slice(k * room, (k + 1) * room), slice(b * room, (b + 1) * room)
            value_ref[b, to, :] = value[part]
            back_ref[b, to, :] = back[part]
            extra_ref[b, to, :] = extra[part]
    model_width = token_ref.shape[2]
    for b in range(blocks):
        graded_ref[b] = dot(pick_ref[b], back_ref[b], (0, 0)).astype(BF16)
        mixed_ref[b, :, :model_width] = dot(pick_ref[b], value_ref[b], (0, 0)).astype(BF16)
        mixed_ref[b, :, model_width:] = dot(pick_ref[b], extra_ref[b], (0, 0)).astype(BF16)


def expert_pass(micro, micro_count, slots, gates, columns, tokens, cots, wide, down, room, kept):
    count, width, model_width = down.shape
    blocks, row_count = tokens.shape[0], tokens.shape[1]
    step = 2
    by_block = lambda *dims: pl.BlockSpec((step, *dims), lambda b: (b,) + (0,) * len(dims))
    by_slot = pl.BlockSpec((count, step, 1, row_count), lambda b: (0, b, 0, 0))
    whole = lambda *dims: pl.BlockSpec(dims, lambda b: (0,) * len(dims), pipeline_mode=pl.Buffered(1))
    saved = lambda cols: pl.BlockSpec((count, 1, step * room, cols), lambda b: (0, micro, b, 0))
    widths = (model_width, model_width, width, 2 * width)
    shapes = [jax.ShapeDtypeStruct((count, micro_count, blocks * room, w), BF16) for w in widths]
    args = [slots, gates, columns, tokens, cots, wide, down]
    in_specs = [
        by_slot,
        by_slot,
        whole(count, 1, 128),
        by_block(row_count, model_width),
        by_block(row_count, model_width),
        whole(count, model_width, 2 * width),
        whole(count, width, model_width),
    ]
    aliases = {}
    if kept:
        aliases = {len(args) + i: i for i in range(len(kept))}
        in_specs += [pl.BlockSpec(memory_space=pl.ANY)] * len(kept)
        args += list(kept)
    out = pl.pallas_call(
        expert_kernel,
        grid=(blocks // step,),
        in_specs=in_specs,
        out_specs=[saved(w) for w in widths]
        + [by_block(row_count, model_width + 128), by_block(row_count, model_width)],
        out_shape=shapes
        + [
            jax.ShapeDtypeStruct((blocks, row_count, model_width + 128), BF16),
            jax.ShapeDtypeStruct((blocks, row_count, model_width), BF16),
        ],
        scratch_shapes=[
            pltpu.VMEM((step, count * room, row_count), BF16),
            pltpu.VMEM((step, count * room, model_width), BF16),
            pltpu.VMEM((step, count * room, 128), BF16),
            pltpu.VMEM((step, count * room, model_width), BF16),
        ],
        input_output_aliases=aliases,
        compiler_params=pltpu.CompilerParams(vmem_limit_bytes=60 << 20),
        name="experts",
    )(*args)
    return out[:4], out[4], out[5]


def on_device(
    tokens,
    segment_ids,
    routes,
    route_gates,
    attn_gain,
    query_proj,
    key_proj,
    value_proj,
    output_proj,
    ffn_gain,
    shared_gate,
    shared_up,
    shared_down,
    expert_gate,
    expert_up,
    expert_down,
    output_cot,
):
    micro_count, row_count, model_width = tokens.shape
    exp_count = lax.axis_size("exp")
    local_experts, gate_rows, expert_width = expert_gate.shape
    down_rows = expert_down.shape[1]
    all_experts = local_experts * exp_count
    route_count = routes.shape[2]
    capacity = 4 * row_count * route_count // (3 * all_experts)
    query_width = HEADS * HEAD_DIM
    kv_width = KV_HEADS * HEAD_DIM
    far_steps = exp_count // 4
    assert lax.axis_size("seq") == 4 and local_experts == 2

    seq_index = lax.axis_index("seq")
    exp_index = lax.axis_index("exp")
    core = seq_index % 2
    half = seq_index // 2
    everywhere = ("seq", "exp")

    pad = jnp.zeros((attn_gain.shape[0], 126), BF16)
    first = jnp.concatenate(
        [query_proj, key_proj, value_proj, attn_gain[:, None], ffn_gain[:, None], pad], axis=1
    )
    first = lax.all_gather(first, everywhere, axis=0, tiled=True)
    qkv_width = query_width + 2 * kv_width
    qkv_proj = first[:, :qkv_width]
    gain_one = first[:, qkv_width].astype(F32)
    gain_two = first[:, qkv_width + 1].astype(F32)
    out_proj = lax.all_gather(output_proj, everywhere, axis=0, tiled=True)
    up_proj = lax.all_gather(
        jnp.concatenate([shared_gate, shared_up], axis=1), everywhere, axis=0, tiled=True
    )
    down_proj = lax.all_gather(shared_down, everywhere, axis=0, tiled=True)

    wide = jnp.concatenate([expert_gate, expert_up], axis=2)

    def parity(value):
        kept = lax.dynamic_index_in_dim(value, core, 0, False)
        sent = lax.dynamic_index_in_dim(value, 1 - core, 0, False)
        return in_order(core, kept, exchange(sent, "seq", 1), 0)

    wide_part, down_part = parity(wide), parity(expert_down)
    wide_far, down_far = [wide_part], [down_part]
    for _ in range(far_steps - 1):
        wide_far.append(rotate(wide_far[-1], "exp", 4))
        down_far.append(rotate(down_far[-1], "exp", 4))
    expert_ids = [
        local_experts * ((exp_index - 4 * k + exp_count) % exp_count) + core
        for k in range(far_steps)
    ]

    expert_range = jnp.arange(all_experts, dtype=jnp.int32)
    gate_table = jnp.sum(
        jnp.where(
            jnp.swapaxes(routes, 1, 2)[:, :, None, :] == expert_range[None, None, :, None],
            jnp.swapaxes(route_gates, 1, 2)[:, :, None, :],
            0.0,
        ),
        axis=1,
    )
    gate_blocks = jnp.concatenate(group_gather(gate_table))
    cot_own, cot_other = group_gather(output_cot)

    order = jnp.arange(row_count, dtype=jnp.int32)
    before = (order[:, None] < order[None, :]).astype(BF16)
    slots = jnp.arange(capacity, dtype=jnp.int32)

    inputs = tokens.reshape(micro_count * row_count, model_width).astype(F32)
    inv_one = lax.rsqrt(jnp.mean(inputs * inputs, axis=1, keepdims=True) + EPSILON)
    normed_one = (inputs * inv_one * gain_one).astype(BF16)
    qkv = jnp.dot(normed_one, qkv_proj, preferred_element_type=F32).astype(BF16)
    qkv = qkv.reshape(micro_count, row_count, qkv_width)

    def sequence_kv(micro):
        own = qkv[micro, :, query_width:]
        across = exchange(own, "seq", 2)
        return [qkv[micro], exchange(own, "seq", 1), across, exchange(across, "seq", 1)]

    def mask_of(micro):
        segments = segment_ids[micro].reshape(4, row_count)
        key_ids = jnp.concatenate(
            [lax.dynamic_index_in_dim(segments, seq_index ^ j, 0, False) for j in range(4)]
        )
        key_pos = jnp.concatenate([(seq_index ^ j) * row_count + order for j in range(4)])
        query_ids, query_pos = key_ids[:row_count], key_pos[:row_count]
        allowed = (
            (key_ids[None, :] == query_ids[:, None])
            & (key_pos[None, :] <= query_pos[:, None])
            & (query_ids[:, None] >= 0)
        )
        return allowed.astype(jnp.int32)

    def sequence_sum(grad_keys, grad_values):
        grad = jnp.concatenate([grad_keys, grad_values], axis=1).reshape(4, row_count, -1)
        part = grad[0::2].astype(F32) + exchange(grad[1::2], "seq", 1).astype(F32)
        return (part[0] + exchange(part[1].astype(BF16), "seq", 2).astype(F32)).astype(BF16)

    kept_rows = []

    def experts(micro, normed_blocks, cot_blocks):
        gates = jnp.stack(
            [lax.dynamic_index_in_dim(gate_blocks[:, micro], e, 1, False) for e in expert_ids]
        )
        named = gates > 0.0
        rank = mm("kbs,st->kbt", named.astype(BF16), before).astype(jnp.int32)
        slot = jnp.where(named, rank, -1)
        if far_steps > 2:
            return experts_plain(gates, slot, normed_blocks, cot_blocks)
        columns = (
            lax.broadcasted_iota(jnp.int32, (far_steps, 1, 128), 2)
            == jnp.stack(expert_ids)[:, None, None]
        ).astype(F32)
        kept, mixed, graded = expert_pass(
            micro, micro_count, slot[:, :, None], gates[:, :, None], columns,
            normed_blocks, cot_blocks, wide_all, down_all, capacity, kept_rows,
        )
        kept_rows[:] = kept
        return graded, mixed

    def experts_plain(gates, slot, normed_blocks, cot_blocks):
        mixed, graded, kept = 0.0, 0.0, []
        for k in range(far_steps):
            picked = slot[k][:, None, :] == slots[None, :, None]
            pick = picked.astype(BF16)
            slot_gates = jnp.sum(jnp.where(picked, gates[k][:, None, :], 0.0), axis=2).reshape(-1, 1)
            rows = mm("bst,btd->bsd", pick, normed_blocks).astype(BF16).reshape(-1, model_width)
            cots = mm("bst,btd->bsd", pick, cot_blocks).astype(BF16).reshape(-1, model_width)
            pre = jnp.dot(rows, wide_full[k], preferred_element_type=F32)
            pre_gate, pre_up = pre[:, :expert_width], pre[:, expert_width:]
            grad_hidden = mm("rd,fd->rf", cots, down_full[k])
            act, deriv = silu_parts(pre_gate)
            hidden = act * pre_up
            gate_grad = jnp.sum(hidden * grad_hidden, axis=1, keepdims=True)
            hidden = (hidden * slot_gates).astype(BF16)
            grad_hidden = grad_hidden * slot_gates
            grad_pre = jnp.concatenate(
                [(grad_hidden * pre_up * deriv).astype(BF16), (grad_hidden * act).astype(BF16)], axis=1
            )
            value = jnp.dot(hidden, down_full[k], preferred_element_type=F32).astype(BF16)
            column = (lax.broadcasted_iota(jnp.int32, (1, 128), 1) == expert_ids[k]).astype(F32)
            value = jnp.concatenate([value, (gate_grad * column).astype(BF16)], axis=1)
            grad_rows = mm("rf,df->rd", grad_pre, wide_full[k]).astype(BF16)
            blocks = pick.shape[0]
            mixed = mixed + mm("bst,bsd->btd", pick, value.reshape(blocks, capacity, -1))
            graded = graded + mm("bst,bsd->btd", pick, grad_rows.reshape(blocks, capacity, -1))
            kept.append((rows, cots, hidden, grad_pre))
        kept_rows.append(kept)
        return graded.astype(BF16), mixed.astype(BF16)

    kvs = [sequence_kv(micro) for micro in range(micro_count)]
    masks = [mask_of(micro) for micro in range(micro_count)]
    wide_far, down_far, kvs = lax.optimization_barrier((wide_far, down_far, kvs))
    wide_full = [in_order(half, w, exchange(w, "seq", 2), 0) for w in wide_far]
    down_full = [in_order(half, w, exchange(w, "seq", 2), 0) for w in down_far]
    if far_steps <= 2:
        wide_all, down_all = jnp.stack(wide_full), jnp.stack(down_full)

    contexts, residuals, inv_twos, normed_twos, token_blocks = [], [], [], [], []
    for micro in range(micro_count):
        context = attention(masks[micro], qkv[micro], kvs[micro])
        residual = inputs[micro * row_count : (micro + 1) * row_count] + jnp.dot(
            context, out_proj, preferred_element_type=F32
        )
        inv_two = lax.rsqrt(jnp.mean(residual * residual, axis=1, keepdims=True) + EPSILON)
        normed_two = (residual * inv_two * gain_two).astype(BF16)
        contexts.append(context)
        residuals.append(residual)
        inv_twos.append(inv_two)
        normed_twos.append(normed_two)
        token_blocks.append(jnp.concatenate(group_gather(normed_two)))

    normed_two = jnp.concatenate(normed_twos)
    upstream_low = output_cot.reshape(micro_count * row_count, model_width)
    shared_pre = jnp.dot(normed_two, up_proj, preferred_element_type=F32)
    shared_width = shared_gate.shape[1]
    shared_pre_gate, shared_pre_up = shared_pre[:, :shared_width], shared_pre[:, shared_width:]
    shared_act, shared_deriv = silu_parts(shared_pre_gate)
    shared_hidden = (shared_act * shared_pre_up).astype(BF16)
    shared_out = jnp.dot(shared_hidden, down_proj, preferred_element_type=F32)
    grad_shared_hidden = mm("rd,fd->rf", upstream_low, down_proj)
    grad_shared_pre = jnp.concatenate(
        [
            (grad_shared_hidden * shared_pre_up * shared_deriv).astype(BF16),
            (grad_shared_hidden * shared_act).astype(BF16),
        ],
        axis=1,
    )
    grad_from_shared = mm("rf,df->rd", grad_shared_pre, up_proj)
    if far_steps <= 2:
        token_blocks[0], shared_out, grad_from_shared = lax.optimization_barrier(
            (token_blocks[0], shared_out, grad_from_shared)
        )
    moe_grads, mixed_parts = [], []
    for micro in range(micro_count):
        cot_blocks = jnp.concatenate([cot_own[:, micro], cot_other[:, micro]])
        graded, mixed = experts(micro, token_blocks[micro], cot_blocks)
        moe_grads.append(group_scatter(graded[:4], graded[4:]))
        mixed_parts.append(mixed)

    products = []

    def expert_sum(left, right):
        own = None
        for k in reversed(range(far_steps)):
            if far_steps > 2:
                lefts = jnp.concatenate([m[k][left] for m in kept_rows])
                rights = jnp.concatenate([m[k][right] for m in kept_rows])
                if own is not None:
                    lefts, rights, own = lax.optimization_barrier((lefts, rights, own))
                total = mm("rd,rf->df", lefts, rights)
            else:
                total = mm("mrd,mrf->df", kept_rows[left][k], kept_rows[right][k])
            products.append(total)
            rows = total.shape[0] // 2
            total = total.reshape(2, rows, -1)
            mine = lax.dynamic_index_in_dim(total, half, 0, False)
            sent = lax.dynamic_index_in_dim(total, 1 - half, 0, False).astype(BF16)
            total = mine + exchange(sent, "seq", 2).astype(F32)
            own = total if own is None else total + rotate(own.astype(BF16), "exp", -4).astype(F32)
        rows = own.shape[0] // 2
        own = own.reshape(2, rows, -1)
        kept = lax.dynamic_index_in_dim(own, core, 0, False)
        sent = lax.dynamic_index_in_dim(own, 1 - core, 0, False).astype(BF16)
        other = exchange(sent, "seq", 1).astype(F32)
        return in_order(core, kept[None], other[None], 0)

    down_grad = expert_sum(2, 1)
    if far_steps > 2:
        down_grad, kept_rows = lax.optimization_barrier((down_grad, kept_rows))
    wide_grad = expert_sum(0, 3)
    if far_steps <= 2:
        moe_grads[0] = after(moe_grads[0], products)
    mixed = jnp.stack(mixed_parts, axis=1)
    moe_outs = group_scatter(mixed[:4], mixed[4:])

    def summed(value):
        return lax.psum_scatter(
            value.astype(BF16), everywhere, scatter_dimension=0, tiled=True
        ).astype(F32)

    shared_up_sum = summed(mm("rd,rf->df", normed_two, grad_shared_pre))
    shared_down_sum = summed(mm("rd,rf->df", shared_hidden, upstream_low))

    branches, grad_residuals, grad_qkv, outputs, gate_grads = [], [], [], [], []
    gain_two_sum = 0.0
    for micro in range(micro_count):
        rows = slice(micro * row_count, (micro + 1) * row_count)
        grad_normed = moe_grads[micro] + grad_from_shared[rows]
        grad_from_two, gain_part = norm_back(grad_normed, residuals[micro], inv_twos[micro], gain_two)
        gain_two_sum = gain_two_sum + gain_part
        grad_residual = upstream_low[rows].astype(F32) + grad_from_two
        grad_branch = grad_residual.astype(BF16)
        grad_residuals.append(grad_residual)
        branches.append(grad_branch)
        grad_context = mm("rd,id->ri", grad_branch, out_proj).astype(BF16)
        grad_query, grad_keys, grad_values = attention_back(
            masks[micro], qkv[micro], kvs[micro], grad_context
        )
        grad_kv = sequence_sum(grad_keys, grad_values)
        grad_qkv.append(jnp.concatenate([grad_query, grad_kv], axis=1))
        out = moe_outs[micro]
        outputs.append(
            (residuals[micro] + shared_out[rows] + out[:, :model_width]).astype(BF16)
        )
        table = out[:, model_width : model_width + all_experts]
        gate_grads.append(
            jnp.sum(
                jnp.where(
                    routes[micro][:, :, None] == expert_range[None, None, :], table[:, None, :], 0.0
                ),
                axis=2,
            )
        )

    output_sum = summed(mm("rd,rf->df", jnp.concatenate(contexts), jnp.concatenate(branches)))
    grad_qkv = jnp.concatenate(grad_qkv)
    grad_normed_one = mm("ri,di->rd", grad_qkv, qkv_proj)
    grad_from_one, gain_one_sum = norm_back(grad_normed_one, inputs, inv_one, gain_one)
    token_grads = (jnp.concatenate(grad_residuals) + grad_from_one).astype(BF16)
    qkv_sum = mm("rd,rf->df", normed_one, grad_qkv).astype(BF16)
    gains = jnp.stack([gain_one_sum, gain_two_sum], axis=1).astype(BF16)
    gains = jnp.concatenate([gains, jnp.zeros((model_width, 126), BF16)], axis=1)
    last = summed(jnp.concatenate([qkv_sum, gains], axis=1))

    return (
        jnp.stack(outputs),
        token_grads.reshape(micro_count, row_count, model_width),
        jnp.stack(gate_grads),
        last[:, qkv_width],
        last[:, :query_width],
        last[:, query_width : query_width + kv_width],
        last[:, query_width + kv_width : qkv_width],
        output_sum,
        last[:, qkv_width + 1],
        shared_up_sum[:, :shared_width],
        shared_up_sum[:, shared_width:],
        shared_down_sum,
        wide_grad[:, :, :expert_width],
        wide_grad[:, :, expert_width:],
        down_grad,
    )


def solution(mesh):
    rows = P(("seq", "exp"), None)
    wide = P("exp", "seq", None)
    flat = P(("seq", "exp"))
    return jax.shard_map(
        on_device,
        mesh=mesh,
        in_specs=(wide, P("exp", None), wide, wide, flat, rows, rows, rows, rows, flat, rows, rows, rows)
        + (wide,) * 4,
        out_specs=(wide, wide, wide, flat, rows, rows, rows, rows, flat, rows, rows, rows)
        + (wide,) * 3,
        check_vma=False,
    )
```

```python
import functools

import jax
import jax.numpy as jnp
from jax import lax
from jax.experimental import pallas as pl
from jax.experimental.pallas import tpu as pltpu
from jax.sharding import PartitionSpec as P

HEADS = 12
KV_HEADS = 4
HEAD_DIM = 128
GROUP_HEADS = HEADS // KV_HEADS
EPSILON = 1e-05
NEGATIVE = -1e30
F32 = jnp.float32
BF16 = jnp.bfloat16


def mm(spec, left, right):
    return jnp.einsum(spec, left, right, preferred_element_type=F32)


def exchange(value, axis, bit):
    size = lax.axis_size(axis)
    return lax.ppermute(value, axis, [(i, i ^ bit) for i in range(size)])


def rotate(value, axis, step):
    size = lax.axis_size(axis)
    return lax.ppermute(value, axis, [(i, (i + step) % size) for i in range(size)])


def after(value, *others):
    return lax.optimization_barrier((value, others))[0]


def in_order(flag, own, other, axis):
    return jnp.where(
        flag == 0,
        jnp.concatenate([own, other], axis),
        jnp.concatenate([other, own], axis),
    )


def silu_parts(pre_act):
    sigma_val = jax.nn.sigmoid(pre_act)
    return (pre_act * sigma_val, sigma_val * (1.0 + pre_act * (1.0 - sigma_val)))


def norm_back(grad_normed, values, inv_rms, gain):
    scaled = grad_normed * gain
    inner = jnp.mean(scaled * values, axis=1, keepdims=True)
    grad_values = inv_rms * scaled - values * (inv_rms * inv_rms * inv_rms) * inner
    return grad_values, jnp.sum(grad_normed * values * inv_rms, axis=0)


def group_gather(value):
    over_y = jnp.stack([value, exchange(value, "exp", 1)])
    over_z = jnp.concatenate([over_y, exchange(over_y, "exp", 2)])
    other = exchange(over_z, "seq", 1)
    return over_z, other


def group_scatter(own, other):
    part = own.astype(F32) + exchange(other, "seq", 1).astype(F32)
    part = part[:2] + exchange(part[2:].astype(BF16), "exp", 2).astype(F32)
    return part[0] + exchange(part[1].astype(BF16), "exp", 1).astype(F32)


def dot(left, right, over):
    return lax.dot_general(left, right, ((over[:1], over[1:]), ((), ())), preferred_element_type=F32)


def masked_softmax(query, keys, allowed, scale):
    scores = jnp.where(allowed, dot(query, keys, (1, 1)) * scale, NEGATIVE)
    expo = jnp.where(allowed, jnp.exp(scores - jnp.max(scores, axis=1, keepdims=True)), 0.0)
    total = jnp.sum(expo, axis=1, keepdims=True)
    return expo * (1.0 / jnp.where(total > 0.5, total, 1.0))


def attention_back_kernel(
    scale, mask_ref, query_ref, key_ref, value_ref, grad_ref, grad_query_ref, grad_key_ref, grad_value_ref
):
    keys = key_ref[...].reshape(-1, HEAD_DIM)
    values = value_ref[...].reshape(-1, HEAD_DIM)
    allowed = mask_ref[...] > 0
    grad_keys = grad_values = 0.0
    for g in range(GROUP_HEADS):
        lanes = slice(g * HEAD_DIM, (g + 1) * HEAD_DIM)
        query, grad = query_ref[:, lanes], grad_ref[:, lanes]
        weights = masked_softmax(query, keys, allowed, scale)
        grad_weights = dot(grad, values, (1, 1))
        delta = jnp.sum(weights * grad_weights, axis=1, keepdims=True)
        grad_scores = (weights * (grad_weights - delta)).astype(BF16)
        grad_query_ref[:, lanes] = (dot(grad_scores, keys, (1, 0)) * scale).astype(BF16)
        grad_keys = grad_keys + dot(query, grad_scores, (0, 0))
        grad_values = grad_values + dot(grad, weights.astype(BF16), (0, 0))
    grad_key_ref[...] = (grad_keys * scale).T.astype(BF16).reshape(grad_key_ref.shape)
    grad_value_ref[...] = grad_values.T.astype(BF16).reshape(grad_value_ref.shape)


MESH = pl.DeviceIdType.MESH
CORE, HALF = ("seq", 1), ("seq", 2)
SIDE, NEAR, FAR = ("exp", 1), ("exp", 2), ("exp", 4)


def bit_of(partner):
    axis, bit = partner
    return lax.axis_index(axis) // bit % 2


def device_of(partner):
    axis, bit = partner
    return {axis: lax.axis_index(axis) + bit - 2 * bit * bit_of(partner)}


def meet(partners):
    barrier = pltpu.get_barrier_semaphore()
    for partner in partners:
        pl.semaphore_signal(barrier, inc=1, device_id=device_of(partner), device_id_type=MESH)
    pl.semaphore_wait(barrier, len(partners))


class Sender:
    def __init__(self, send_sems, recv_sems):
        self.send_sems, self.recv_sems = send_sems, recv_sems
        self.copies, self.landed = [], set()

    def start(self, src, dst, partner):
        i = len(self.copies)
        copy = pltpu.make_async_remote_copy(
            src_ref=src,
            dst_ref=dst,
            send_sem=self.send_sems.at[i],
            recv_sem=self.recv_sems.at[i],
            device_id=device_of(partner),
            device_id_type=MESH,
        )
        copy.start()
        self.copies.append(copy)
        return i

    def arrived(self, *numbers):
        for i in numbers:
            if i not in self.landed:
                self.copies[i].wait_recv()
                self.landed.add(i)

    def finish(self):
        for i, copy in enumerate(self.copies):
            copy.wait_send()
            self.arrived(i)


def semaphores(count):
    return [pltpu.SemaphoreType.DMA((count,)), pltpu.SemaphoreType.DMA((count,))]


ANYWHERE = pl.BlockSpec(memory_space=pl.ANY)
VMEM = pl.BlockSpec(memory_space=pltpu.VMEM)
AXES = (HALF, CORE, FAR, NEAR, SIDE)


def doubling(sender, out, order, columns=None):
    held = []
    for partner in order:
        at = tuple(slice(None) if a in held else bit_of(a) for a in AXES)
        view = out.at[at] if columns is None else out.at[(*at, slice(None), columns)]
        number = sender.start(view, view, partner)
        yield
        sender.arrived(number)
        held.append(partner)


def in_turn(steps):
    steps = list(steps)
    while steps:
        steps = [s for s in steps if next(s, s) is not s]


def gather_kernel(query_ref, kv_ref, gain_ref, query_out, kv_out, gain_out, send, recv, local):
    own = tuple(bit_of(a) for a in AXES)
    pairs = ((query_ref, query_out), (kv_ref, kv_out), (gain_ref, gain_out))
    copies = [pltpu.make_async_copy(r, o.at[own], local.at[i]) for i, (r, o) in enumerate(pairs)]
    for copy in copies:
        copy.start()
    meet(AXES)
    for copy in copies:
        copy.wait()
    sender = Sender(send, recv)
    one, two = (NEAR, FAR, HALF, SIDE, CORE), (SIDE, NEAR, FAR, HALF, CORE)
    cut = query_ref.shape[1] // 2
    kv_cut = kv_ref.shape[1] // 2
    in_turn(
        [
            doubling(sender, gain_out, two),
            doubling(sender, query_out, one, pl.ds(0, cut)),
            doubling(sender, kv_out, two, pl.ds(0, kv_cut)),
            doubling(sender, query_out, one, pl.ds(cut, cut)),
            doubling(sender, kv_out, two, pl.ds(kv_cut, kv_cut)),
        ]
    )
    sender.finish()


def gather_first(query_proj, kv_proj, gains):
    shards = (query_proj, kv_proj, gains)
    return pl.pallas_call(
        gather_kernel,
        in_specs=[ANYWHERE] * 3,
        out_specs=[ANYWHERE] * 3,
        out_shape=[jax.ShapeDtypeStruct((2,) * 5 + w.shape, w.dtype) for w in shards],
        scratch_shapes=[*semaphores(25), pltpu.SemaphoreType.DMA((3,))],
        compiler_params=pltpu.CompilerParams(collective_id=0, has_side_effects=True),
        name="gather_first",
    )(*shards)


def attention_heads(scale, rows, mask_ref, query_ref, kv_ref, context_ref):
    allowed = mask_ref[rows, :] > 0
    blocks = [kv_ref.at[j, rows, :] for j in range(4)]

    def head(h, _):
        at = pl.ds(pl.multiple_of(h * HEAD_DIM, HEAD_DIM), HEAD_DIM)
        value_at = pl.ds(pl.multiple_of((h + KV_HEADS) * HEAD_DIM, HEAD_DIM), HEAD_DIM)
        keys = jnp.concatenate([b[:, at] for b in blocks])
        values = jnp.concatenate([b[:, value_at] for b in blocks])
        for g in range(GROUP_HEADS):
            lanes = pl.ds(pl.multiple_of((h * GROUP_HEADS + g) * HEAD_DIM, HEAD_DIM), HEAD_DIM)
            weights = masked_softmax(query_ref[rows, lanes], keys, allowed, scale)
            context_ref[rows, lanes] = dot(weights.astype(BF16), values, (1, 0)).astype(BF16)
        return 0

    lax.fori_loop(0, KV_HEADS, head, 0)


def attend_kernel(
    normed_ref, query_proj_ref, kv_proj_ref, mask_ref, gate_ref, up_ref, down_ref, cot_ref, table_ref,
    query_ref, kv_ref, context_ref, gate_out, up_out, down_out, cot_out, table_out, send, recv, local,
):
    core, half = bit_of(CORE), bit_of(HALF)
    other = 1 - core
    experts = ((gate_ref, gate_out), (up_ref, up_out), (down_ref, down_out))
    copies = [pltpu.make_async_copy(r.at[core], o.at[0, half, core], local.at[i]) for i, (r, o) in enumerate(experts)]
    copies.append(pltpu.make_async_copy(cot_ref, cot_out.at[0, 0, 0], local.at[3]))
    copies.append(pltpu.make_async_copy(table_ref, table_out.at[0, 0, 0], local.at[4]))
    for copy in copies:
        copy.start()
    meet(AXES)
    sender = Sender(send, recv)
    swaps = [sender.start(r.at[other], o.at[0, half, core], CORE) for r, o in experts]
    table_side = sender.start(table_ref, table_out.at[0, 0, 1], SIDE)
    cot_side = sender.start(cot_ref.at[0], cot_out.at[0, 0, 1, 0], SIDE)
    cot_near = sender.start(cot_ref.at[1], cot_out.at[0, 1, 0, 1], NEAR)

    kv_ref[0] = dot(normed_ref[...], kv_proj_ref[...], (1, 0)).astype(BF16)
    kv_half = sender.start(kv_ref.at[0], kv_ref.at[2], HALF)
    kv_core = sender.start(kv_ref.at[0], kv_ref.at[1], CORE)
    for copy in copies:
        copy.wait()
    sender.arrived(*swaps)
    fars = [sender.start(o.at[0, half], o.at[1, half], FAR) for _, o in experts]
    for _, o in experts:
        sender.start(o.at[0, half], o.at[0, half], HALF)
    query_ref[...] = dot(normed_ref[...], query_proj_ref[...], (1, 0)).astype(BF16)
    sender.arrived(table_side)
    table_near = sender.start(table_out.at[0, 0], table_out.at[0, 1], NEAR)
    sender.arrived(kv_half)
    kv_both = sender.start(kv_ref.at[2], kv_ref.at[3], CORE)
    sender.arrived(cot_side, cot_near)
    cots = [
        sender.start(cot_out.at[0, 0, :, 0], cot_out.at[0, 1, :, 0], NEAR),
        sender.start(cot_out.at[0, :, 0, 1], cot_out.at[0, :, 1, 1], SIDE),
    ]
    sender.arrived(table_near)
    sender.start(table_out.at[0], table_out.at[1], CORE)
    sender.arrived(kv_core, kv_both)
    scale = HEAD_DIM ** (-0.5)
    row_count = mask_ref.shape[1] // 4
    far_outs = [o for _, o in experts]
    for micro in range(normed_ref.shape[0] // row_count):
        rows = pl.ds(micro * row_count, row_count)
        attention_heads(scale, rows, mask_ref, query_ref, kv_ref, context_ref)
        if fars:
            sender.arrived(fars[0])
            sender.start(far_outs[0].at[1, half], far_outs[0].at[1, half], HALF)
            fars, far_outs = fars[1:], far_outs[1:]
    for number, out in zip(fars, far_outs):
        sender.arrived(number)
        sender.start(out.at[1, half], out.at[1, half], HALF)
    sender.arrived(*cots)
    sender.start(cot_out.at[0], cot_out.at[1], CORE)
    sender.finish()


def attend(normed, query_proj, kv_proj, masks, expert_gate, expert_up, expert_down, cot, table):
    rows, width = normed.shape
    shape = jax.ShapeDtypeStruct
    return pl.pallas_call(
        attend_kernel,
        in_specs=[VMEM] * 4 + [ANYWHERE] * 5,
        out_specs=[VMEM] * 3 + [ANYWHERE] * 5,
        out_shape=[
            shape((rows, query_proj.shape[1]), BF16),
            shape((4, rows, kv_proj.shape[1]), BF16),
            shape((rows, query_proj.shape[1]), BF16),
            *[shape((2, 2, 2) + w.shape[1:], BF16) for w in (expert_gate, expert_up, expert_down)],
            shape((2, 2, 2) + cot.shape, cot.dtype),
            shape((2, 2, 2) + table.shape, table.dtype),
        ],
        scratch_shapes=[*semaphores(28), pltpu.SemaphoreType.DMA((5,))],
        compiler_params=pltpu.CompilerParams(
            collective_id=1, has_side_effects=True, vmem_limit_bytes=60 << 20
        ),
        name="attend",
    )(normed, query_proj, kv_proj, masks, expert_gate, expert_up, expert_down, cot, table)


def attention_back(micro, masks, queries, kv, grad):
    row_count = grad.shape[0]
    wide = GROUP_HEADS * HEAD_DIM
    heads = lambda at: pl.BlockSpec((4, row_count, HEAD_DIM), lambda h: (0, micro, h + at))
    column = pl.BlockSpec((4, row_count, HEAD_DIM), lambda h: (0, 0, h))
    flat = jax.ShapeDtypeStruct((4, row_count, KV_HEADS * HEAD_DIM), BF16)
    return pl.pallas_call(
        functools.partial(attention_back_kernel, HEAD_DIM ** (-0.5)),
        grid=(KV_HEADS,),
        in_specs=[
            pl.BlockSpec((row_count, 4 * row_count), lambda h: (micro, 0)),
            pl.BlockSpec((row_count, wide), lambda h: (micro, h)),
            heads(0),
            heads(KV_HEADS),
            pl.BlockSpec((row_count, wide), lambda h: (0, h)),
        ],
        out_specs=[pl.BlockSpec((row_count, wide), lambda h: (0, h)), column, column],
        out_shape=[jax.ShapeDtypeStruct((row_count, HEADS * HEAD_DIM), BF16), flat, flat],
        compiler_params=pltpu.CompilerParams(vmem_limit_bytes=48 << 20),
        name="attention_back",
    )(masks, queries, kv, kv, grad)


def expert_kernel(
    slot_ref, scale_ref, column_ref, token_ref, cot_ref, gate_ref, up_ref, down_ref, *refs
):
    rows_ref, cots_ref, hidden_ref, pre_ref, mixed_ref, graded_ref = refs[-10:-4]
    pick_ref, value_ref, extra_ref, back_ref = refs[-4:]
    count, width = down_ref.shape[0], down_ref.shape[1]
    blocks, row_count = token_ref.shape[0], token_ref.shape[1]
    room = rows_ref.shape[2] // blocks
    slot = lax.broadcasted_iota(jnp.int32, (room, row_count), 0)
    gates = []
    for b in range(blocks):
        for k in range(count):
            picked = slot == slot_ref[k, b]
            gates.append(jnp.sum(jnp.where(picked, scale_ref[k, b], 0.0), axis=1, keepdims=True))
            pick_ref[b, k * room : (k + 1) * room, :] = jnp.where(picked, 1.0, 0.0).astype(BF16)
        rows = dot(pick_ref[b], token_ref[b], (1, 0)).astype(BF16)
        cots = dot(pick_ref[b], cot_ref[b, 0], (1, 0)).astype(BF16)
        for k in range(count):
            part = slice(b * room, (b + 1) * room)
            rows_ref[k, 0, part, :] = rows[k * room : (k + 1) * room]
            cots_ref[k, 0, part, :] = cots[k * room : (k + 1) * room]
    for k in range(count):
        gate = jnp.concatenate([gates[b * count + k] for b in range(blocks)])
        pre_gate = dot(rows_ref[k, 0], gate_ref[k], (1, 0))
        pre_up = dot(rows_ref[k, 0], up_ref[k], (1, 0))
        grad_hidden = dot(cots_ref[k, 0], down_ref[k], (1, 1))
        act, deriv = silu_parts(pre_gate)
        hidden = act * pre_up
        gate_grad = jnp.sum(hidden * grad_hidden, axis=1, keepdims=True)
        grad_hidden = grad_hidden * gate
        hidden_ref[k, 0] = (hidden * gate).astype(BF16)
        pre_ref[k, 0, :, :width] = (grad_hidden * pre_up * deriv).astype(BF16)
        pre_ref[k, 0, :, width:] = (grad_hidden * act).astype(BF16)
        value = dot(hidden_ref[k, 0], down_ref[k], (1, 0)).astype(BF16)
        back = dot(pre_ref[k, 0, :, :width], gate_ref[k], (1, 1))
        back = (back + dot(pre_ref[k, 0, :, width:], up_ref[k], (1, 1))).astype(BF16)
        extra = (gate_grad * column_ref[k]).astype(BF16)
        for b in range(blocks):
            to, part = slice(k * room, (k + 1) * room), slice(b * room, (b + 1) * room)
            value_ref[b, to, :] = value[part]
            back_ref[b, to, :] = back[part]
            extra_ref[b, to, :] = extra[part]
    model_width = token_ref.shape[2]
    for b in range(blocks):
        graded_ref[b] = dot(pick_ref[b], back_ref[b], (0, 0)).astype(BF16)
        mixed_ref[b, :, :model_width] = dot(pick_ref[b], value_ref[b], (0, 0)).astype(BF16)
        mixed_ref[b, :, model_width:] = dot(pick_ref[b], extra_ref[b], (0, 0)).astype(BF16)


def expert_pass(micro, micro_count, slots, scales, columns, tokens, cots, gate, up, down, room, kept):
    count, width, model_width = down.shape
    blocks, row_count = tokens.shape[0], tokens.shape[1]
    step = 2
    by_block = lambda *dims: pl.BlockSpec((step, *dims), lambda b: (b,) + (0,) * len(dims))
    by_slot = pl.BlockSpec((count, step, 1, row_count), lambda b: (0, b, 0, 0))
    whole = lambda *dims: pl.BlockSpec(dims, lambda b: (0,) * len(dims), pipeline_mode=pl.Buffered(1))
    saved = lambda cols: pl.BlockSpec((count, 1, step * room, cols), lambda b: (0, micro, b, 0))
    widths = (model_width, model_width, width, 2 * width)
    shapes = [jax.ShapeDtypeStruct((count, micro_count, blocks * room, w), BF16) for w in widths]
    args = [slots, scales, columns, tokens, cots, gate, up, down]
    in_specs = [
        by_slot,
        by_slot,
        whole(count, 1, 128),
        by_block(row_count, model_width),
        pl.BlockSpec((step, 1, row_count, model_width), lambda b: (b, micro, 0, 0)),
        whole(count, model_width, width),
        whole(count, model_width, width),
        whole(count, width, model_width),
    ]
    aliases = {}
    if kept:
        aliases = {len(args) + i: i for i in range(len(kept))}
        in_specs += [pl.BlockSpec(memory_space=pl.ANY)] * len(kept)
        args += list(kept)
    out = pl.pallas_call(
        expert_kernel,
        grid=(blocks // step,),
        in_specs=in_specs,
        out_specs=[saved(w) for w in widths]
        + [by_block(row_count, model_width + 128), by_block(row_count, model_width)],
        out_shape=shapes
        + [
            jax.ShapeDtypeStruct((blocks, row_count, model_width + 128), BF16),
            jax.ShapeDtypeStruct((blocks, row_count, model_width), BF16),
        ],
        scratch_shapes=[
            pltpu.VMEM((step, count * room, row_count), BF16),
            pltpu.VMEM((step, count * room, model_width), BF16),
            pltpu.VMEM((step, count * room, 128), BF16),
            pltpu.VMEM((step, count * room, model_width), BF16),
        ],
        input_output_aliases=aliases,
        compiler_params=pltpu.CompilerParams(vmem_limit_bytes=60 << 20),
        name="experts",
    )(*args)
    return out[:4], out[4], out[5]


def attend_plain(queries, kv, masks, micro):
    row_count = masks.shape[1] // 4
    rows = slice(micro * row_count, (micro + 1) * row_count)
    allowed = masks[rows] > 0
    wide = KV_HEADS * HEAD_DIM
    heads = queries[rows].reshape(row_count, KV_HEADS, GROUP_HEADS, HEAD_DIM)
    keys = kv[:, rows, :wide].reshape(-1, KV_HEADS, HEAD_DIM)
    values = kv[:, rows, wide:].reshape(-1, KV_HEADS, HEAD_DIM)
    scores = mm("ikgd,jkd->kgij", heads, keys) * HEAD_DIM ** (-0.5)
    row_max = jnp.max(jnp.where(allowed, scores, NEGATIVE), axis=3, keepdims=True)
    expo = jnp.where(allowed, jnp.exp(jnp.where(allowed, scores, NEGATIVE) - row_max), 0.0)
    total = jnp.sum(expo, axis=3, keepdims=True)
    weights = (expo / jnp.where(total > 0.5, total, 1.0)).astype(BF16)
    return mm("kgij,jkd->ikgd", weights, values).reshape(row_count, HEADS * HEAD_DIM).astype(BF16)


def on_device(
    tokens,
    segment_ids,
    routes,
    route_gates,
    attn_gain,
    query_proj,
    key_proj,
    value_proj,
    output_proj,
    ffn_gain,
    shared_gate,
    shared_up,
    shared_down,
    expert_gate,
    expert_up,
    expert_down,
    output_cot,
):
    micro_count, row_count, model_width = tokens.shape
    exp_count = lax.axis_size("exp")
    local_experts, gate_rows, expert_width = expert_gate.shape
    down_rows = expert_down.shape[1]
    all_experts = local_experts * exp_count
    route_count = routes.shape[2]
    capacity = 4 * row_count * route_count // (3 * all_experts)
    query_width = HEADS * HEAD_DIM
    kv_width = KV_HEADS * HEAD_DIM
    far_steps = exp_count // 4
    assert lax.axis_size("seq") == 4 and local_experts == 2

    seq_index = lax.axis_index("seq")
    exp_index = lax.axis_index("exp")
    core = seq_index % 2
    half = seq_index // 2
    everywhere = ("seq", "exp")

    linked = exp_count == 8
    qkv_width = query_width + 2 * kv_width
    expert_range = jnp.arange(all_experts, dtype=jnp.int32)
    gate_table = jnp.sum(
        jnp.where(
            jnp.swapaxes(routes, 1, 2)[:, :, None, :] == expert_range[None, None, :, None],
            jnp.swapaxes(route_gates, 1, 2)[:, :, None, :],
            0.0,
        ),
        axis=1,
    )
    order = jnp.arange(row_count, dtype=jnp.int32)
    before = (order[:, None] < order[None, :]).astype(BF16)
    slots = jnp.arange(capacity, dtype=jnp.int32)
    expert_ids = [
        local_experts * ((exp_index - 4 * k + exp_count) % exp_count) + core
        for k in range(far_steps)
    ]
    kv_proj = jnp.concatenate([key_proj, value_proj], axis=1)
    shared_wide = jnp.concatenate([shared_gate, shared_up], axis=1)

    def gathered(value):
        return lax.all_gather(value, everywhere, axis=0, tiled=True)

    def mask_of(micro):
        segments = segment_ids[micro].reshape(4, row_count)
        key_ids = jnp.concatenate(
            [lax.dynamic_index_in_dim(segments, seq_index ^ j, 0, False) for j in range(4)]
        )
        key_pos = jnp.concatenate([(seq_index ^ j) * row_count + order for j in range(4)])
        query_ids, query_pos = key_ids[:row_count], key_pos[:row_count]
        allowed = (
            (key_ids[None, :] == query_ids[:, None])
            & (key_pos[None, :] <= query_pos[:, None])
            & (query_ids[:, None] >= 0)
        )
        return allowed.astype(jnp.int32)

    inputs = tokens.reshape(micro_count * row_count, model_width).astype(F32)
    inv_one = lax.rsqrt(jnp.mean(inputs * inputs, axis=1, keepdims=True) + EPSILON)
    masks = jnp.concatenate([mask_of(micro) for micro in range(micro_count)])
    if linked:
        gains = jnp.stack([attn_gain, ffn_gain]).astype(F32)
        share = gains.shape[1]
        gains = jnp.pad(gains, ((0, 6), (0, 128 - share)))
        query_full, kv_full, gains = gather_first(query_proj, kv_proj, gains)
        query_full = query_full.reshape(model_width, query_width)
        kv_full = kv_full.reshape(model_width, 2 * kv_width)
        gains = gains.reshape(-1, 8, 128)[:, :2, :share]
        gain_one, gain_two = jnp.swapaxes(gains, 0, 1).reshape(2, model_width)
        output_proj, shared_wide, shared_down = after(
            (output_proj, shared_wide, shared_down), query_full
        )
    else:
        query_full, kv_full = gathered(query_proj), gathered(kv_proj)
        gain_one, gain_two = gathered(attn_gain).astype(F32), gathered(ffn_gain).astype(F32)
    out_proj, up_proj, down_proj = gathered(output_proj), gathered(shared_wide), gathered(shared_down)
    normed_one = (inputs * inv_one * gain_one).astype(BF16)

    if linked:
        queries, kv, contexts, gate_all, up_all, down_all, cots, tables = attend(
            normed_one, query_full, kv_full, masks, expert_gate, expert_up, expert_down, output_cot, gate_table
        )
        gate_all = gate_all.reshape(far_steps, model_width, expert_width)
        up_all = up_all.reshape(far_steps, model_width, expert_width)
        down_all = down_all.reshape(far_steps, expert_width, model_width)
        cot_blocks = cots.reshape(8, micro_count, row_count, model_width)
        gate_blocks = tables.reshape(8, micro_count, all_experts, row_count)
    else:
        queries = jnp.dot(normed_one, query_full, preferred_element_type=F32).astype(BF16)
        own = jnp.dot(normed_one, kv_full, preferred_element_type=F32).astype(BF16)
        across = exchange(own, "seq", 2)
        kv = jnp.stack([own, exchange(own, "seq", 1), across, exchange(across, "seq", 1)])
        contexts = jnp.concatenate([attend_plain(queries, kv, masks, m) for m in range(micro_count)])
        gate_blocks = jnp.concatenate(group_gather(gate_table))
        cot_blocks = jnp.concatenate(group_gather(output_cot))

        def parity(value):
            kept = lax.dynamic_index_in_dim(value, core, 0, False)
            sent = lax.dynamic_index_in_dim(value, 1 - core, 0, False)
            return in_order(core, kept, exchange(sent, "seq", 1), 0)

        wide_far = [parity(jnp.concatenate([expert_gate, expert_up], axis=2))]
        down_far = [parity(expert_down)]
        for _ in range(far_steps - 1):
            wide_far.append(rotate(wide_far[-1], "exp", 4))
            down_far.append(rotate(down_far[-1], "exp", 4))
        wide_full = [in_order(half, w, exchange(w, "seq", 2), 0) for w in wide_far]
        down_full = [in_order(half, w, exchange(w, "seq", 2), 0) for w in down_far]

    def sequence_sum(grad_keys, grad_values):
        grad = jnp.concatenate([grad_keys, grad_values], axis=2)
        part = grad[0::2].astype(F32) + exchange(grad[1::2], "seq", 1).astype(F32)
        return (part[0] + exchange(part[1].astype(BF16), "seq", 2).astype(F32)).astype(BF16)

    kept_rows = []

    def experts(micro, normed_blocks):
        gates = jnp.stack(
            [lax.dynamic_index_in_dim(gate_blocks[:, micro], e, 1, False) for e in expert_ids]
        )
        named = gates > 0.0
        rank = mm("kbs,st->kbt", named.astype(BF16), before).astype(jnp.int32)
        slot = jnp.where(named, rank, -1)
        if not linked:
            return experts_plain(gates, slot, normed_blocks, cot_blocks[:, micro])
        columns = (
            lax.broadcasted_iota(jnp.int32, (far_steps, 1, 128), 2)
            == jnp.stack(expert_ids)[:, None, None]
        ).astype(F32)
        kept, mixed, graded = expert_pass(
            micro, micro_count, slot[:, :, None], gates[:, :, None], columns,
            normed_blocks, cot_blocks, gate_all, up_all, down_all, capacity, kept_rows,
        )
        kept_rows[:] = kept
        return graded, mixed

    def experts_plain(gates, slot, normed_blocks, micro_cots):
        mixed, graded, kept = 0.0, 0.0, []
        for k in range(far_steps):
            picked = slot[k][:, None, :] == slots[None, :, None]
            pick = picked.astype(BF16)
            slot_gates = jnp.sum(jnp.where(picked, gates[k][:, None, :], 0.0), axis=2).reshape(-1, 1)
            rows = mm("bst,btd->bsd", pick, normed_blocks).astype(BF16).reshape(-1, model_width)
            cots = mm("bst,btd->bsd", pick, micro_cots).astype(BF16).reshape(-1, model_width)
            pre = jnp.dot(rows, wide_full[k], preferred_element_type=F32)
            pre_gate, pre_up = pre[:, :expert_width], pre[:, expert_width:]
            grad_hidden = mm("rd,fd->rf", cots, down_full[k])
            act, deriv = silu_parts(pre_gate)
            hidden = act * pre_up
            gate_grad = jnp.sum(hidden * grad_hidden, axis=1, keepdims=True)
            hidden = (hidden * slot_gates).astype(BF16)
            grad_hidden = grad_hidden * slot_gates
            grad_pre = jnp.concatenate(
                [(grad_hidden * pre_up * deriv).astype(BF16), (grad_hidden * act).astype(BF16)], axis=1
            )
            value = jnp.dot(hidden, down_full[k], preferred_element_type=F32).astype(BF16)
            column = (lax.broadcasted_iota(jnp.int32, (1, 128), 1) == expert_ids[k]).astype(F32)
            value = jnp.concatenate([value, (gate_grad * column).astype(BF16)], axis=1)
            grad_rows = mm("rf,df->rd", grad_pre, wide_full[k]).astype(BF16)
            blocks = pick.shape[0]
            mixed = mixed + mm("bst,bsd->btd", pick, value.reshape(blocks, capacity, -1))
            graded = graded + mm("bst,bsd->btd", pick, grad_rows.reshape(blocks, capacity, -1))
            kept.append((rows, cots, hidden, grad_pre))
        kept_rows.append(kept)
        return graded.astype(BF16), mixed.astype(BF16)

    residuals, inv_twos, normed_twos, token_blocks = [], [], [], []
    for micro in range(micro_count):
        rows = slice(micro * row_count, (micro + 1) * row_count)
        residual = inputs[rows] + jnp.dot(contexts[rows], out_proj, preferred_element_type=F32)
        inv_two = lax.rsqrt(jnp.mean(residual * residual, axis=1, keepdims=True) + EPSILON)
        normed_two = (residual * inv_two * gain_two).astype(BF16)
        residuals.append(residual)
        inv_twos.append(inv_two)
        normed_twos.append(normed_two)
        token_blocks.append(jnp.concatenate(group_gather(normed_two)))

    normed_two = jnp.concatenate(normed_twos)
    upstream_low = output_cot.reshape(micro_count * row_count, model_width)
    shared_pre = jnp.dot(normed_two, up_proj, preferred_element_type=F32)
    shared_width = shared_gate.shape[1]
    shared_pre_gate, shared_pre_up = shared_pre[:, :shared_width], shared_pre[:, shared_width:]
    shared_act, shared_deriv = silu_parts(shared_pre_gate)
    shared_hidden = (shared_act * shared_pre_up).astype(BF16)
    shared_out = jnp.dot(shared_hidden, down_proj, preferred_element_type=F32)
    grad_shared_hidden = mm("rd,fd->rf", upstream_low, down_proj)
    grad_shared_pre = jnp.concatenate(
        [
            (grad_shared_hidden * shared_pre_up * shared_deriv).astype(BF16),
            (grad_shared_hidden * shared_act).astype(BF16),
        ],
        axis=1,
    )
    grad_from_shared = mm("rf,df->rd", grad_shared_pre, up_proj)
    if linked:
        token_blocks[0], shared_out, grad_from_shared = lax.optimization_barrier(
            (token_blocks[0], shared_out, grad_from_shared)
        )
    moe_grads, mixed_parts = [], []
    for micro in range(micro_count):
        graded, mixed = experts(micro, token_blocks[micro])
        moe_grads.append(group_scatter(graded[:4], graded[4:]))
        mixed_parts.append(mixed)

    products = []

    def expert_sum(left, right):
        own = None
        for k in reversed(range(far_steps)):
            if not linked:
                lefts = jnp.concatenate([m[k][left] for m in kept_rows])
                rights = jnp.concatenate([m[k][right] for m in kept_rows])
                if own is not None:
                    lefts, rights, own = lax.optimization_barrier((lefts, rights, own))
                total = mm("rd,rf->df", lefts, rights)
            else:
                total = mm("mrd,mrf->df", kept_rows[left][k], kept_rows[right][k])
            products.append(total)
            rows = total.shape[0] // 2
            total = total.reshape(2, rows, -1)
            mine = lax.dynamic_index_in_dim(total, half, 0, False)
            sent = lax.dynamic_index_in_dim(total, 1 - half, 0, False).astype(BF16)
            total = mine + exchange(sent, "seq", 2).astype(F32)
            own = total if own is None else total + rotate(own.astype(BF16), "exp", -4).astype(F32)
        rows = own.shape[0] // 2
        own = own.reshape(2, rows, -1)
        kept = lax.dynamic_index_in_dim(own, core, 0, False)
        sent = lax.dynamic_index_in_dim(own, 1 - core, 0, False).astype(BF16)
        other = exchange(sent, "seq", 1).astype(F32)
        return in_order(core, kept[None], other[None], 0)

    down_grad = expert_sum(2, 1)
    if not linked:
        down_grad, kept_rows = lax.optimization_barrier((down_grad, kept_rows))
    wide_grad = expert_sum(0, 3)
    if linked:
        moe_grads[0] = after(moe_grads[0], products)
    mixed = jnp.stack(mixed_parts, axis=1)
    moe_outs = group_scatter(mixed[:4], mixed[4:])

    def summed(value):
        return lax.psum_scatter(
            value.astype(BF16), everywhere, scatter_dimension=0, tiled=True
        ).astype(F32)

    shared_up_sum = summed(mm("rd,rf->df", normed_two, grad_shared_pre))
    shared_down_sum = summed(mm("rd,rf->df", shared_hidden, upstream_low))

    branches, grad_residuals, grad_qkv, outputs, gate_grads = [], [], [], [], []
    gain_two_sum = 0.0
    for micro in range(micro_count):
        rows = slice(micro * row_count, (micro + 1) * row_count)
        grad_normed = moe_grads[micro] + grad_from_shared[rows]
        grad_from_two, gain_part = norm_back(grad_normed, residuals[micro], inv_twos[micro], gain_two)
        gain_two_sum = gain_two_sum + gain_part
        grad_residual = upstream_low[rows].astype(F32) + grad_from_two
        grad_branch = grad_residual.astype(BF16)
        grad_residuals.append(grad_residual)
        branches.append(grad_branch)
        grad_context = mm("rd,id->ri", grad_branch, out_proj).astype(BF16)
        grad_query, grad_keys, grad_values = attention_back(micro, masks, queries, kv, grad_context)
        grad_kv = sequence_sum(grad_keys, grad_values)
        grad_qkv.append(jnp.concatenate([grad_query, grad_kv], axis=1))
        out = moe_outs[micro]
        outputs.append(
            (residuals[micro] + shared_out[rows] + out[:, :model_width]).astype(BF16)
        )
        table = out[:, model_width : model_width + all_experts]
        gate_grads.append(
            jnp.sum(
                jnp.where(
                    routes[micro][:, :, None] == expert_range[None, None, :], table[:, None, :], 0.0
                ),
                axis=2,
            )
        )

    output_sum = summed(mm("rd,rf->df", contexts, jnp.concatenate(branches)))
    grad_qkv = jnp.concatenate(grad_qkv)
    grad_normed_one = mm("ri,di->rd", grad_qkv[:, :query_width], query_full)
    grad_normed_one = grad_normed_one + mm("ri,di->rd", grad_qkv[:, query_width:], kv_full)
    grad_from_one, gain_one_sum = norm_back(grad_normed_one, inputs, inv_one, gain_one)
    token_grads = (jnp.concatenate(grad_residuals) + grad_from_one).astype(BF16)
    column = lax.broadcasted_iota(jnp.int32, (1, qkv_width + 128), 1)
    last = mm("rd,rf->df", normed_one, jnp.pad(grad_qkv, ((0, 0), (0, 128))))
    last = jnp.where(column == qkv_width, gain_one_sum[:, None], last)
    last = summed(jnp.where(column == qkv_width + 1, gain_two_sum[:, None], last))

    return (
        jnp.stack(outputs),
        token_grads.reshape(micro_count, row_count, model_width),
        jnp.stack(gate_grads),
        last[:, qkv_width],
        last[:, :query_width],
        last[:, query_width : query_width + kv_width],
        last[:, query_width + kv_width : qkv_width],
        output_sum,
        last[:, qkv_width + 1],
        shared_up_sum[:, :shared_width],
        shared_up_sum[:, shared_width:],
        shared_down_sum,
        wide_grad[:, :, :expert_width],
        wide_grad[:, :, expert_width:],
        down_grad,
    )


def solution(mesh):
    rows = P(("seq", "exp"), None)
    wide = P("exp", "seq", None)
    flat = P(("seq", "exp"))
    return jax.shard_map(
        on_device,
        mesh=mesh,
        in_specs=(wide, P("exp", None), wide, wide, flat, rows, rows, rows, rows, flat, rows, rows, rows)
        + (wide,) * 4,
        out_specs=(wide, wide, wide, flat, rows, rows, rows, rows, flat, rows, rows, rows)
        + (wide,) * 3,
        check_vma=False,
    )
```

```python
import functools

import jax
import jax.numpy as jnp
from jax import lax
from jax.experimental import pallas as pl
from jax.experimental.pallas import tpu as pltpu
from jax.sharding import PartitionSpec as P

HEADS = 12
KV_HEADS = 4
HEAD_DIM = 128
GROUP_HEADS = HEADS // KV_HEADS
EPSILON = 1e-05
NEGATIVE = -1e30
F32 = jnp.float32
BF16 = jnp.bfloat16


def mm(spec, left, right):
    return jnp.einsum(spec, left, right, preferred_element_type=F32)


def exchange(value, axis, bit):
    size = lax.axis_size(axis)
    return lax.ppermute(value, axis, [(i, i ^ bit) for i in range(size)])


def rotate(value, axis, step):
    size = lax.axis_size(axis)
    return lax.ppermute(value, axis, [(i, (i + step) % size) for i in range(size)])


def after(value, *others):
    return lax.optimization_barrier((value, others))[0]


def in_order(flag, own, other, axis):
    return jnp.where(
        flag == 0,
        jnp.concatenate([own, other], axis),
        jnp.concatenate([other, own], axis),
    )


def silu_parts(pre_act):
    sigma_val = jax.nn.sigmoid(pre_act)
    return (pre_act * sigma_val, sigma_val * (1.0 + pre_act * (1.0 - sigma_val)))


def norm_back(grad_normed, values, inv_rms, gain):
    scaled = grad_normed * gain
    inner = jnp.mean(scaled * values, axis=1, keepdims=True)
    grad_values = inv_rms * scaled - values * (inv_rms * inv_rms * inv_rms) * inner
    return grad_values, jnp.sum(grad_normed * values * inv_rms, axis=0)


def group_gather(value):
    over_y = jnp.stack([value, exchange(value, "exp", 1)])
    over_z = jnp.concatenate([over_y, exchange(over_y, "exp", 2)])
    other = exchange(over_z, "seq", 1)
    return over_z, other


def group_scatter(own, other):
    part = own.astype(F32) + exchange(other, "seq", 1).astype(F32)
    part = part[:2] + exchange(part[2:].astype(BF16), "exp", 2).astype(F32)
    return part[0] + exchange(part[1].astype(BF16), "exp", 1).astype(F32)


def dot(left, right, over):
    return lax.dot_general(left, right, ((over[:1], over[1:]), ((), ())), preferred_element_type=F32)


def masked_softmax(query, keys, allowed, scale):
    scores = jnp.where(allowed, dot(query, keys, (1, 1)) * scale, NEGATIVE)
    expo = jnp.where(allowed, jnp.exp(scores - jnp.max(scores, axis=1, keepdims=True)), 0.0)
    total = jnp.sum(expo, axis=1, keepdims=True)
    return expo * (1.0 / jnp.where(total > 0.5, total, 1.0))


def attention_back_kernel(
    scale, mask_ref, query_ref, key_ref, value_ref, grad_ref, grad_query_ref, grad_key_ref, grad_value_ref
):
    keys = key_ref[...].reshape(-1, HEAD_DIM)
    values = value_ref[...].reshape(-1, HEAD_DIM)
    allowed = mask_ref[...] > 0
    grad_keys = grad_values = 0.0
    for g in range(GROUP_HEADS):
        lanes = slice(g * HEAD_DIM, (g + 1) * HEAD_DIM)
        query, grad = query_ref[:, lanes], grad_ref[:, lanes]
        weights = masked_softmax(query, keys, allowed, scale)
        grad_weights = dot(grad, values, (1, 1))
        delta = jnp.sum(weights * grad_weights, axis=1, keepdims=True)
        grad_scores = (weights * (grad_weights - delta)).astype(BF16)
        grad_query_ref[:, lanes] = (dot(grad_scores, keys, (1, 0)) * scale).astype(BF16)
        grad_keys = grad_keys + dot(query, grad_scores, (0, 0))
        grad_values = grad_values + dot(grad, weights.astype(BF16), (0, 0))
    grad_key_ref[...] = (grad_keys * scale).T.astype(BF16).reshape(grad_key_ref.shape)
    grad_value_ref[...] = grad_values.T.astype(BF16).reshape(grad_value_ref.shape)


MESH = pl.DeviceIdType.MESH
CORE, HALF = ("seq", 1), ("seq", 2)
SIDE, NEAR, FAR = ("exp", 1), ("exp", 2), ("exp", 4)


def bit_of(partner):
    axis, bit = partner
    return lax.axis_index(axis) // bit % 2


def device_of(partner):
    axis, bit = partner
    return {axis: lax.axis_index(axis) + bit - 2 * bit * bit_of(partner)}


def meet(partners):
    barrier = pltpu.get_barrier_semaphore()
    for partner in partners:
        pl.semaphore_signal(barrier, inc=1, device_id=device_of(partner), device_id_type=MESH)
    pl.semaphore_wait(barrier, len(partners))


class Sender:
    def __init__(self, send_sems, recv_sems):
        self.send_sems, self.recv_sems = send_sems, recv_sems
        self.copies, self.landed = [], set()

    def start(self, src, dst, partner):
        i = len(self.copies)
        copy = pltpu.make_async_remote_copy(
            src_ref=src,
            dst_ref=dst,
            send_sem=self.send_sems.at[i],
            recv_sem=self.recv_sems.at[i],
            device_id=device_of(partner),
            device_id_type=MESH,
        )
        copy.start()
        self.copies.append(copy)
        return i

    def arrived(self, *numbers):
        for i in numbers:
            if i not in self.landed:
                self.copies[i].wait_recv()
                self.landed.add(i)

    def finish(self):
        for i, copy in enumerate(self.copies):
            copy.wait_send()
            self.arrived(i)


def semaphores(count):
    return [pltpu.SemaphoreType.DMA((count,)), pltpu.SemaphoreType.DMA((count,))]


ANYWHERE = pl.BlockSpec(memory_space=pl.ANY)
VMEM = pl.BlockSpec(memory_space=pltpu.VMEM)
AXES = (HALF, CORE, FAR, NEAR, SIDE)


def doubling(sender, out, order, columns=None):
    held = []
    for partner in order:
        at = tuple(slice(None) if a in held else bit_of(a) for a in AXES)
        view = out.at[at] if columns is None else out.at[(*at, slice(None), columns)]
        number = sender.start(view, view, partner)
        yield
        sender.arrived(number)
        held.append(partner)


def in_turn(steps):
    steps = list(steps)
    while steps:
        steps = [s for s in steps if next(s, s) is not s]


def gather_kernel(
    query_ref, kv_ref, gain_ref, gate_ref, up_ref, down_ref, cot_ref,
    query_out, kv_out, gain_out, gate_out, up_out, down_out, far_out, side_out, near_out,
    send, recv, local,
):
    core, half = bit_of(CORE), bit_of(HALF)
    own = tuple(bit_of(a) for a in AXES)
    pairs = ((query_ref, query_out), (kv_ref, kv_out), (gain_ref, gain_out))
    experts = ((gate_ref, gate_out.at[half]), (up_ref, up_out.at[half]), (down_ref, down_out))
    moves = [(r, o.at[own]) for r, o in pairs] + [(r.at[core], o.at[core]) for r, o in experts]
    copies = [pltpu.make_async_copy(r, o, local.at[i]) for i, (r, o) in enumerate(moves)]
    for copy in copies:
        copy.start()
    meet(AXES)
    sender = Sender(send, recv)
    swaps = [sender.start(r.at[1 - core], o.at[core], CORE) for r, o in experts]
    for copy in copies:
        copy.wait()
    one, two = (NEAR, FAR, HALF, SIDE, CORE), (SIDE, NEAR, FAR, HALF, CORE)
    cut = query_ref.shape[1] // 2
    kv_cut = kv_ref.shape[1] // 2

    def near_experts():
        sender.arrived(*swaps)
        sender.start(gate_out.at[half], gate_out.at[half], HALF)
        for _ in range(3):
            yield
        sender.start(up_out.at[half], up_out.at[half], HALF)

    def far_expert():
        yield
        sender.start(gate_out.at[half], far_out, FAR)
        sender.start(cot_ref.at[0], side_out, SIDE)
        sender.start(cot_ref.at[1], near_out, NEAR)

    in_turn(
        [
            doubling(sender, gain_out, two),
            doubling(sender, query_out, one, pl.ds(0, cut)),
            doubling(sender, kv_out, two, pl.ds(0, kv_cut)),
            doubling(sender, query_out, one, pl.ds(cut, cut)),
            doubling(sender, kv_out, two, pl.ds(kv_cut, kv_cut)),
            near_experts(),
            far_expert(),
        ]
    )
    sender.finish()


def gather_first(query_proj, kv_proj, gains, expert_gate, expert_up, expert_down, cot):
    shape = jax.ShapeDtypeStruct
    shards = (query_proj, kv_proj, gains)
    experts = (expert_gate, expert_up, expert_down)
    return pl.pallas_call(
        gather_kernel,
        in_specs=[ANYWHERE] * 7,
        out_specs=[ANYWHERE] * 9,
        out_shape=[
            *[shape((2,) * 5 + w.shape, w.dtype) for w in shards],
            *[shape((2, 2) + w.shape[1:], BF16) for w in experts[:2]],
            shape((2,) + expert_down.shape[1:], BF16),
            shape((2,) + expert_gate.shape[1:], BF16),
            shape(cot.shape[1:], BF16),
            shape(cot.shape[1:], BF16),
        ],
        scratch_shapes=[*semaphores(34), pltpu.SemaphoreType.DMA((6,))],
        compiler_params=pltpu.CompilerParams(collective_id=0, has_side_effects=True),
        name="gather_first",
    )(*shards, *experts, cot)


def attention_heads(scale, rows, mask_ref, query_ref, kv_ref, context_ref):
    allowed = mask_ref[rows, :] > 0
    blocks = [kv_ref.at[j, rows, :] for j in range(4)]

    def head(h, _):
        at = pl.ds(pl.multiple_of(h * HEAD_DIM, HEAD_DIM), HEAD_DIM)
        value_at = pl.ds(pl.multiple_of((h + KV_HEADS) * HEAD_DIM, HEAD_DIM), HEAD_DIM)
        keys = jnp.concatenate([b[:, at] for b in blocks])
        values = jnp.concatenate([b[:, value_at] for b in blocks])
        for g in range(GROUP_HEADS):
            lanes = pl.ds(pl.multiple_of((h * GROUP_HEADS + g) * HEAD_DIM, HEAD_DIM), HEAD_DIM)
            weights = masked_softmax(query_ref[rows, lanes], keys, allowed, scale)
            context_ref[rows, lanes] = dot(weights.astype(BF16), values, (1, 0)).astype(BF16)
        return 0

    lax.fori_loop(0, KV_HEADS, head, 0)


def attend_kernel(
    normed_ref, query_proj_ref, kv_proj_ref, mask_ref, up_ref, down_ref, far_ref, cot_ref, side_ref, near_ref, table_ref,
    query_ref, kv_ref, context_ref, gate_out, up_out, down_out, near_out, cot_out, table_out,
    up_half, down_half, send, recv, local,
):
    half = bit_of(HALF)
    moves = (
        (far_ref, gate_out.at[half]),
        (down_ref, near_out.at[half]),
        (cot_ref, cot_out.at[0, 0, 0]),
        (side_ref, cot_out.at[0, 0, 1, 0]),
        (near_ref, cot_out.at[0, 1, 0, 1]),
        (table_ref, table_out.at[0, 0, 0]),
    )
    copies = [pltpu.make_async_copy(r, o, local.at[i]) for i, (r, o) in enumerate(moves)]
    for copy in copies:
        copy.start()
    meet(AXES)
    sender = Sender(send, recv)
    far_up = sender.start(up_ref.at[half], up_half, FAR)
    table_side = sender.start(table_ref, table_out.at[0, 0, 1], SIDE)
    cots = [
        sender.start(cot_ref.at[0], cot_out.at[0, 1, 0, 0], NEAR),
        sender.start(side_ref, cot_out.at[0, 1, 1, 0], NEAR),
        sender.start(cot_ref.at[1], cot_out.at[0, 0, 1, 1], SIDE),
        sender.start(near_ref, cot_out.at[0, 1, 1, 1], SIDE),
    ]
    kv_ref[0] = dot(normed_ref[...], kv_proj_ref[...], (1, 0)).astype(BF16)
    kv_half = sender.start(kv_ref.at[0], kv_ref.at[2], HALF)
    kv_core = sender.start(kv_ref.at[0], kv_ref.at[1], CORE)
    query_ref[...] = dot(normed_ref[...], query_proj_ref[...], (1, 0)).astype(BF16)
    for copy in copies:
        copy.wait()
    sender.arrived(table_side)
    table_near = sender.start(table_out.at[0, 0], table_out.at[0, 1], NEAR)
    sender.arrived(kv_half)
    kv_both = sender.start(kv_ref.at[2], kv_ref.at[3], CORE)
    sender.start(far_ref, gate_out.at[half], HALF)
    sender.arrived(far_up)
    far_down = sender.start(down_ref, down_half, FAR)
    sender.start(down_ref, near_out.at[half], HALF)
    sender.start(up_half, up_out.at[half], HALF)
    up_copy = pltpu.make_async_copy(up_half, up_out.at[half], local.at[6])
    up_copy.start()
    sender.arrived(table_near)
    sender.start(table_out.at[0], table_out.at[1], CORE)
    sender.arrived(kv_core, kv_both)
    scale = HEAD_DIM ** (-0.5)
    row_count = mask_ref.shape[1] // 4
    for micro in range(normed_ref.shape[0] // row_count):
        rows = pl.ds(micro * row_count, row_count)
        attention_heads(scale, rows, mask_ref, query_ref, kv_ref, context_ref)
        if micro == 0:
            sender.arrived(*cots)
            sender.start(cot_out.at[0], cot_out.at[1], CORE)
    sender.arrived(far_down)
    sender.start(down_half, down_out.at[half], HALF)
    down_copy = pltpu.make_async_copy(down_half, down_out.at[half], local.at[7])
    down_copy.start()
    up_copy.wait()
    down_copy.wait()
    sender.finish()


def attend(normed, query_proj, kv_proj, masks, up_near, down_half, gate_far, cot, side, near, table):
    rows, width = normed.shape
    shape = jax.ShapeDtypeStruct
    gate_shape = (2,) + gate_far.shape
    return pl.pallas_call(
        attend_kernel,
        in_specs=[VMEM] * 4 + [ANYWHERE] * 7,
        out_specs=[VMEM] * 3 + [ANYWHERE] * 8,
        out_shape=[
            shape((rows, query_proj.shape[1]), BF16),
            shape((4, rows, kv_proj.shape[1]), BF16),
            shape((rows, query_proj.shape[1]), BF16),
            shape(gate_shape, BF16),
            shape(up_near.shape, BF16),
            *[shape((2,) + down_half.shape, BF16)] * 2,
            shape((2, 2, 2) + cot.shape, cot.dtype),
            shape((2, 2, 2) + table.shape, table.dtype),
            shape(up_near.shape[1:], BF16),
            shape(down_half.shape, BF16),
        ],
        scratch_shapes=[*semaphores(18), pltpu.SemaphoreType.DMA((8,))],
        compiler_params=pltpu.CompilerParams(
            collective_id=1, has_side_effects=True, vmem_limit_bytes=60 << 20
        ),
        name="attend",
    )(normed, query_proj, kv_proj, masks, up_near, down_half, gate_far, cot, side, near, table)[:9]


def spread_kernel(value_ref, out, send, recv, local):
    copy = pltpu.make_async_copy(value_ref, out.at[0, 0, 0], local.at[0])
    copy.start()
    meet((CORE, SIDE, NEAR))
    sender = Sender(send, recv)
    firsts = (
        (sender.start(value_ref.at[0], out.at[0, 0, 1, 0], SIDE), (0, 0, 1, 0), NEAR, (0, 1, 1, 0)),
        (sender.start(value_ref.at[1], out.at[0, 1, 0, 1], NEAR), (0, 1, 0, 1), SIDE, (0, 1, 1, 1)),
    )
    seconds = [
        (sender.start(value_ref.at[0], out.at[0, 1, 0, 0], NEAR), (0, 1, 0, 0)),
        (sender.start(value_ref.at[1], out.at[0, 0, 1, 1], SIDE), (0, 0, 1, 1)),
    ]
    sender.start(value_ref, out.at[1, 0, 0], CORE)
    for number, at, partner, to in firsts:
        sender.arrived(number)
        seconds.append((sender.start(out.at[at], out.at[to], partner), to))
        sender.start(out.at[at], out.at[(1, *at[1:])], CORE)
    for number, at in seconds:
        sender.arrived(number)
        sender.start(out.at[at], out.at[(1, *at[1:])], CORE)
    copy.wait()
    sender.finish()


def spread(value):
    out = pl.pallas_call(
        spread_kernel,
        in_specs=[ANYWHERE],
        out_specs=ANYWHERE,
        out_shape=jax.ShapeDtypeStruct((2, 2, 2) + value.shape, value.dtype),
        scratch_shapes=[*semaphores(13), pltpu.SemaphoreType.DMA((1,))],
        compiler_params=pltpu.CompilerParams(collective_id=2, has_side_effects=True),
        name="spread",
    )(value)
    return out.reshape((8,) + value.shape)


def collect_kernel(first_ref, second_ref, out_ref, core_recv, total_ref, axis_recv, send, recv):
    meet((CORE, SIDE, NEAR))
    sender = Sender(send, recv)
    orders = ((first_ref, (NEAR, SIDE), (2, 3, 1, 0)), (second_ref, (SIDE, NEAR), (1, 3, 2, 0)))
    numbers = {}
    for place in range(4):
        for m, (ref, _, order) in enumerate(orders):
            b = order[place]
            numbers[m, b] = sender.start(ref.at[4 + b], core_recv.at[m, b], CORE)
    landing = {}
    for place in range(2):
        for m, (ref, axes, order) in enumerate(orders):
            b = order[place]
            sender.arrived(numbers[m, b])
            total_ref[m, b] = (ref[b].astype(F32) + core_recv[m, b].astype(F32)).astype(BF16)
            landing[m, place] = sender.start(total_ref.at[m, b], axis_recv.at[m, place], axes[0])
    for m, (ref, axes, order) in enumerate(orders):
        b = order[2]
        sender.arrived(numbers[m, b], landing[m, 1])
        total = ref[b].astype(F32) + core_recv[m, b].astype(F32) + axis_recv[m, 1].astype(F32)
        total_ref[m, b] = total.astype(BF16)
        landing[m, 2] = sender.start(total_ref.at[m, b], axis_recv.at[m, 2], axes[1])
    for m, (ref, _, order) in enumerate(orders):
        sender.arrived(numbers[m, 0], landing[m, 0])
        out_ref[m] = ref[0].astype(F32) + core_recv[m, 0].astype(F32) + axis_recv[m, 0].astype(F32)
    for m in range(2):
        sender.arrived(landing[m, 2])
        out_ref[m] = out_ref[m] + axis_recv[m, 2].astype(F32)
    sender.finish()


def collect(first, second, number):
    block = first.shape[1:]
    return pl.pallas_call(
        collect_kernel,
        in_specs=[VMEM] * 2,
        out_specs=VMEM,
        out_shape=jax.ShapeDtypeStruct((2, *block), F32),
        scratch_shapes=[
            pltpu.VMEM((2, 4, *block), BF16),
            pltpu.VMEM((2, 4, *block), BF16),
            pltpu.VMEM((2, 3, *block), BF16),
            *semaphores(14),
        ],
        compiler_params=pltpu.CompilerParams(
            collective_id=number, has_side_effects=True, vmem_limit_bytes=60 << 20
        ),
        name="collect",
    )(first, second)


def attention_back(micro, masks, queries, kv, grad):
    row_count = grad.shape[0]
    wide = GROUP_HEADS * HEAD_DIM
    heads = lambda at: pl.BlockSpec((4, row_count, HEAD_DIM), lambda h: (0, micro, h + at))
    column = pl.BlockSpec((4, row_count, HEAD_DIM), lambda h: (0, 0, h))
    flat = jax.ShapeDtypeStruct((4, row_count, KV_HEADS * HEAD_DIM), BF16)
    return pl.pallas_call(
        functools.partial(attention_back_kernel, HEAD_DIM ** (-0.5)),
        grid=(KV_HEADS,),
        in_specs=[
            pl.BlockSpec((row_count, 4 * row_count), lambda h: (micro, 0)),
            pl.BlockSpec((row_count, wide), lambda h: (micro, h)),
            heads(0),
            heads(KV_HEADS),
            pl.BlockSpec((row_count, wide), lambda h: (0, h)),
        ],
        out_specs=[pl.BlockSpec((row_count, wide), lambda h: (0, h)), column, column],
        out_shape=[jax.ShapeDtypeStruct((row_count, HEADS * HEAD_DIM), BF16), flat, flat],
        compiler_params=pltpu.CompilerParams(vmem_limit_bytes=48 << 20),
        name="attention_back",
    )(masks, queries, kv, kv, grad)


def expert_kernel(
    slot_ref, scale_ref, column_ref, token_ref, cot_ref, *refs
):
    count = column_ref.shape[0]
    gate_refs, up_refs, down_refs = refs[:count], refs[count : 2 * count], refs[2 * count : 3 * count]
    rows_ref, cots_ref, hidden_ref, pre_ref, mixed_ref, graded_ref = refs[-10:-4]
    pick_ref, value_ref, extra_ref, back_ref = refs[-4:]
    width = down_refs[0].shape[0]
    blocks, row_count = token_ref.shape[0], token_ref.shape[2]
    room = rows_ref.shape[2] // blocks
    slot = lax.broadcasted_iota(jnp.int32, (room, row_count), 0)
    gates = []
    for b in range(blocks):
        for k in range(count):
            picked = slot == slot_ref[k, b]
            gates.append(jnp.sum(jnp.where(picked, scale_ref[k, b], 0.0), axis=1, keepdims=True))
            pick_ref[b, k * room : (k + 1) * room, :] = jnp.where(picked, 1.0, 0.0).astype(BF16)
        rows = dot(pick_ref[b], token_ref[b, 0], (1, 0)).astype(BF16)
        cots = dot(pick_ref[b], cot_ref[b, 0], (1, 0)).astype(BF16)
        for k in range(count):
            part = slice(b * room, (b + 1) * room)
            rows_ref[k, 0, part, :] = rows[k * room : (k + 1) * room]
            cots_ref[k, 0, part, :] = cots[k * room : (k + 1) * room]
    for k in range(count):
        gate = jnp.concatenate([gates[b * count + k] for b in range(blocks)])
        pre_gate = dot(rows_ref[k, 0], gate_refs[k][...], (1, 0))
        pre_up = dot(rows_ref[k, 0], up_refs[k][...], (1, 0))
        grad_hidden = dot(cots_ref[k, 0], down_refs[k][...], (1, 1))
        act, deriv = silu_parts(pre_gate)
        hidden = act * pre_up
        gate_grad = jnp.sum(hidden * grad_hidden, axis=1, keepdims=True)
        grad_hidden = grad_hidden * gate
        hidden_ref[k, 0] = (hidden * gate).astype(BF16)
        pre_ref[k, 0, :, :width] = (grad_hidden * pre_up * deriv).astype(BF16)
        pre_ref[k, 0, :, width:] = (grad_hidden * act).astype(BF16)
        value = dot(hidden_ref[k, 0], down_refs[k][...], (1, 0)).astype(BF16)
        back = dot(pre_ref[k, 0, :, :width], gate_refs[k][...], (1, 1))
        back = (back + dot(pre_ref[k, 0, :, width:], up_refs[k][...], (1, 1))).astype(BF16)
        extra = (gate_grad * column_ref[k]).astype(BF16)
        for b in range(blocks):
            to, part = slice(k * room, (k + 1) * room), slice(b * room, (b + 1) * room)
            value_ref[b, to, :] = value[part]
            back_ref[b, to, :] = back[part]
            extra_ref[b, to, :] = extra[part]
    model_width = token_ref.shape[3]
    for b in range(blocks):
        graded_ref[b] = dot(pick_ref[b], back_ref[b], (0, 0)).astype(BF16)
        mixed_ref[b, :, :model_width] = dot(pick_ref[b], value_ref[b], (0, 0)).astype(BF16)
        mixed_ref[b, :, model_width:] = dot(pick_ref[b], extra_ref[b], (0, 0)).astype(BF16)


def expert_pass(micro, slots, scales, columns, tokens, cots, gates, ups, downs, room, kept):
    count, (width, model_width) = len(downs), downs[0].shape
    blocks, micro_count, row_count = tokens.shape[:3]
    step = 2
    by_block = lambda *dims: pl.BlockSpec((step, *dims), lambda b: (b,) + (0,) * len(dims))
    by_slot = pl.BlockSpec((count, step, 1, row_count), lambda b: (0, b, 0, 0))
    whole = lambda *dims: pl.BlockSpec(dims, lambda b: (0,) * len(dims), pipeline_mode=pl.Buffered(1))
    saved = lambda cols: pl.BlockSpec((count, 1, step * room, cols), lambda b: (0, micro, b, 0))
    widths = (model_width, model_width, width, 2 * width)
    shapes = [jax.ShapeDtypeStruct((count, micro_count, blocks * room, w), BF16) for w in widths]
    args = [slots, scales, columns, tokens, cots, *gates, *ups, *downs]
    in_specs = [
        by_slot,
        by_slot,
        whole(count, 1, 128),
        pl.BlockSpec((step, 1, row_count, model_width), lambda b: (b, micro, 0, 0)),
        pl.BlockSpec((step, 1, row_count, model_width), lambda b: (b, micro, 0, 0)),
        *[whole(model_width, width)] * (2 * count),
        *[whole(width, model_width)] * count,
    ]
    aliases = {}
    if kept:
        aliases = {len(args) + i: i for i in range(len(kept))}
        in_specs += [pl.BlockSpec(memory_space=pl.ANY)] * len(kept)
        args += list(kept)
    out = pl.pallas_call(
        expert_kernel,
        grid=(blocks // step,),
        in_specs=in_specs,
        out_specs=[saved(w) for w in widths]
        + [by_block(row_count, model_width + 128), by_block(row_count, model_width)],
        out_shape=shapes
        + [
            jax.ShapeDtypeStruct((blocks, row_count, model_width + 128), BF16),
            jax.ShapeDtypeStruct((blocks, row_count, model_width), BF16),
        ],
        scratch_shapes=[
            pltpu.VMEM((step, count * room, row_count), BF16),
            pltpu.VMEM((step, count * room, model_width), BF16),
            pltpu.VMEM((step, count * room, 128), BF16),
            pltpu.VMEM((step, count * room, model_width), BF16),
        ],
        input_output_aliases=aliases,
        compiler_params=pltpu.CompilerParams(vmem_limit_bytes=60 << 20),
        name="experts",
    )(*args)
    return out[:4], out[4], out[5]


def attend_plain(queries, kv, masks, micro):
    row_count = masks.shape[1] // 4
    rows = slice(micro * row_count, (micro + 1) * row_count)
    allowed = masks[rows] > 0
    wide = KV_HEADS * HEAD_DIM
    heads = queries[rows].reshape(row_count, KV_HEADS, GROUP_HEADS, HEAD_DIM)
    keys = kv[:, rows, :wide].reshape(-1, KV_HEADS, HEAD_DIM)
    values = kv[:, rows, wide:].reshape(-1, KV_HEADS, HEAD_DIM)
    scores = mm("ikgd,jkd->kgij", heads, keys) * HEAD_DIM ** (-0.5)
    row_max = jnp.max(jnp.where(allowed, scores, NEGATIVE), axis=3, keepdims=True)
    expo = jnp.where(allowed, jnp.exp(jnp.where(allowed, scores, NEGATIVE) - row_max), 0.0)
    total = jnp.sum(expo, axis=3, keepdims=True)
    weights = (expo / jnp.where(total > 0.5, total, 1.0)).astype(BF16)
    return mm("kgij,jkd->ikgd", weights, values).reshape(row_count, HEADS * HEAD_DIM).astype(BF16)


def on_device(
    tokens,
    segment_ids,
    routes,
    route_gates,
    attn_gain,
    query_proj,
    key_proj,
    value_proj,
    output_proj,
    ffn_gain,
    shared_gate,
    shared_up,
    shared_down,
    expert_gate,
    expert_up,
    expert_down,
    output_cot,
):
    micro_count, row_count, model_width = tokens.shape
    exp_count = lax.axis_size("exp")
    local_experts, gate_rows, expert_width = expert_gate.shape
    down_rows = expert_down.shape[1]
    all_experts = local_experts * exp_count
    route_count = routes.shape[2]
    capacity = 4 * row_count * route_count // (3 * all_experts)
    query_width = HEADS * HEAD_DIM
    kv_width = KV_HEADS * HEAD_DIM
    far_steps = exp_count // 4
    assert lax.axis_size("seq") == 4 and local_experts == 2

    seq_index = lax.axis_index("seq")
    exp_index = lax.axis_index("exp")
    core = seq_index % 2
    half = seq_index // 2
    everywhere = ("seq", "exp")

    linked = exp_count == 8
    qkv_width = query_width + 2 * kv_width
    expert_range = jnp.arange(all_experts, dtype=jnp.int32)
    gate_table = jnp.sum(
        jnp.where(
            jnp.swapaxes(routes, 1, 2)[:, :, None, :] == expert_range[None, None, :, None],
            jnp.swapaxes(route_gates, 1, 2)[:, :, None, :],
            0.0,
        ),
        axis=1,
    )
    order = jnp.arange(row_count, dtype=jnp.int32)
    before = (order[:, None] < order[None, :]).astype(BF16)
    slots = jnp.arange(capacity, dtype=jnp.int32)
    expert_ids = [
        local_experts * ((exp_index - 4 * k + exp_count) % exp_count) + core
        for k in range(far_steps)
    ]
    kv_proj = jnp.concatenate([key_proj, value_proj], axis=1)
    shared_wide = jnp.concatenate([shared_gate, shared_up], axis=1)

    def gathered(value):
        return lax.all_gather(value, everywhere, axis=0, tiled=True)

    def mask_of(micro):
        segments = segment_ids[micro].reshape(4, row_count)
        key_ids = jnp.concatenate(
            [lax.dynamic_index_in_dim(segments, seq_index ^ j, 0, False) for j in range(4)]
        )
        key_pos = jnp.concatenate([(seq_index ^ j) * row_count + order for j in range(4)])
        query_ids, query_pos = key_ids[:row_count], key_pos[:row_count]
        allowed = (
            (key_ids[None, :] == query_ids[:, None])
            & (key_pos[None, :] <= query_pos[:, None])
            & (query_ids[:, None] >= 0)
        )
        return allowed.astype(jnp.int32)

    inputs = tokens.reshape(micro_count * row_count, model_width).astype(F32)
    inv_one = lax.rsqrt(jnp.mean(inputs * inputs, axis=1, keepdims=True) + EPSILON)
    masks = jnp.concatenate([mask_of(micro) for micro in range(micro_count)])
    if linked:
        gains = jnp.stack([attn_gain, ffn_gain]).astype(F32)
        share = gains.shape[1]
        gains = jnp.pad(gains, ((0, 6), (0, 128 - share)))
        query_full, kv_full, gains, gate_near, up_near, down_half, gate_far, side, near = gather_first(
            query_proj, kv_proj, gains, expert_gate, expert_up, expert_down, output_cot
        )
        query_full = query_full.reshape(model_width, query_width)
        kv_full = kv_full.reshape(model_width, 2 * kv_width)
        gains = gains.reshape(-1, 8, 128)[:, :2, :share]
        gain_one, gain_two = jnp.swapaxes(gains, 0, 1).reshape(2, model_width)
        output_proj = after(output_proj, query_full)
    else:
        query_full, kv_full = gathered(query_proj), gathered(kv_proj)
        gain_one, gain_two = gathered(attn_gain).astype(F32), gathered(ffn_gain).astype(F32)
    out_proj = gathered(output_proj)
    normed_one = (inputs * inv_one * gain_one).astype(BF16)

    if linked:
        queries, kv, contexts, gate_far, up_far, down_far, down_near, cots, tables = attend(
            normed_one, query_full, kv_full, masks, up_near, down_half, gate_far, output_cot, side, near, gate_table
        )
        gate_all = [w.reshape(model_width, expert_width) for w in (gate_near, gate_far)]
        up_all = [w.reshape(model_width, expert_width) for w in (up_near, up_far)]
        down_all = [w.reshape(expert_width, model_width) for w in (down_near, down_far)]
        shared_wide, shared_down = after((shared_wide, shared_down), contexts)
        cot_blocks = cots.reshape(8, micro_count, row_count, model_width)
        gate_blocks = tables.reshape(8, micro_count, all_experts, row_count)
    else:
        queries = jnp.dot(normed_one, query_full, preferred_element_type=F32).astype(BF16)
        own = jnp.dot(normed_one, kv_full, preferred_element_type=F32).astype(BF16)
        across = exchange(own, "seq", 2)
        kv = jnp.stack([own, exchange(own, "seq", 1), across, exchange(across, "seq", 1)])
        contexts = jnp.concatenate([attend_plain(queries, kv, masks, m) for m in range(micro_count)])
        gate_blocks = jnp.concatenate(group_gather(gate_table))
        cot_blocks = jnp.concatenate(group_gather(output_cot))

        def parity(value):
            kept = lax.dynamic_index_in_dim(value, core, 0, False)
            sent = lax.dynamic_index_in_dim(value, 1 - core, 0, False)
            return in_order(core, kept, exchange(sent, "seq", 1), 0)

        wide_far = [parity(jnp.concatenate([expert_gate, expert_up], axis=2))]
        down_far = [parity(expert_down)]
        for _ in range(far_steps - 1):
            wide_far.append(rotate(wide_far[-1], "exp", 4))
            down_far.append(rotate(down_far[-1], "exp", 4))
        wide_full = [in_order(half, w, exchange(w, "seq", 2), 0) for w in wide_far]
        down_full = [in_order(half, w, exchange(w, "seq", 2), 0) for w in down_far]

    def sequence_sum(grad_keys, grad_values):
        grad = jnp.concatenate([grad_keys, grad_values], axis=2)
        part = grad[0::2].astype(F32) + exchange(grad[1::2], "seq", 1).astype(F32)
        return (part[0] + exchange(part[1].astype(BF16), "seq", 2).astype(F32)).astype(BF16)

    kept_rows = []

    def experts(micro, normed_blocks):
        gates = jnp.stack(
            [lax.dynamic_index_in_dim(gate_blocks[:, micro], e, 1, False) for e in expert_ids]
        )
        named = gates > 0.0
        rank = mm("kbs,st->kbt", named.astype(BF16), before).astype(jnp.int32)
        slot = jnp.where(named, rank, -1)
        if not linked:
            return experts_plain(gates, slot, normed_blocks[:, micro], cot_blocks[:, micro])
        columns = (
            lax.broadcasted_iota(jnp.int32, (far_steps, 1, 128), 2)
            == jnp.stack(expert_ids)[:, None, None]
        ).astype(F32)
        kept, mixed, graded = expert_pass(
            micro, slot[:, :, None], gates[:, :, None], columns,
            normed_blocks, cot_blocks, gate_all, up_all, down_all, capacity, kept_rows,
        )
        kept_rows[:] = kept
        return graded, mixed

    def experts_plain(gates, slot, normed_blocks, micro_cots):
        mixed, graded, kept = 0.0, 0.0, []
        for k in range(far_steps):
            picked = slot[k][:, None, :] == slots[None, :, None]
            pick = picked.astype(BF16)
            slot_gates = jnp.sum(jnp.where(picked, gates[k][:, None, :], 0.0), axis=2).reshape(-1, 1)
            rows = mm("bst,btd->bsd", pick, normed_blocks).astype(BF16).reshape(-1, model_width)
            cots = mm("bst,btd->bsd", pick, micro_cots).astype(BF16).reshape(-1, model_width)
            pre = jnp.dot(rows, wide_full[k], preferred_element_type=F32)
            pre_gate, pre_up = pre[:, :expert_width], pre[:, expert_width:]
            grad_hidden = mm("rd,fd->rf", cots, down_full[k])
            act, deriv = silu_parts(pre_gate)
            hidden = act * pre_up
            gate_grad = jnp.sum(hidden * grad_hidden, axis=1, keepdims=True)
            hidden = (hidden * slot_gates).astype(BF16)
            grad_hidden = grad_hidden * slot_gates
            grad_pre = jnp.concatenate(
                [(grad_hidden * pre_up * deriv).astype(BF16), (grad_hidden * act).astype(BF16)], axis=1
            )
            value = jnp.dot(hidden, down_full[k], preferred_element_type=F32).astype(BF16)
            column = (lax.broadcasted_iota(jnp.int32, (1, 128), 1) == expert_ids[k]).astype(F32)
            value = jnp.concatenate([value, (gate_grad * column).astype(BF16)], axis=1)
            grad_rows = mm("rf,df->rd", grad_pre, wide_full[k]).astype(BF16)
            blocks = pick.shape[0]
            mixed = mixed + mm("bst,bsd->btd", pick, value.reshape(blocks, capacity, -1))
            graded = graded + mm("bst,bsd->btd", pick, grad_rows.reshape(blocks, capacity, -1))
            kept.append((rows, cots, hidden, grad_pre))
        kept_rows.append(kept)
        return graded.astype(BF16), mixed.astype(BF16)

    up_proj, down_proj = gathered(shared_wide), gathered(shared_down)
    residual = inputs + jnp.dot(contexts, out_proj, preferred_element_type=F32)
    inv_two = lax.rsqrt(jnp.mean(residual * residual, axis=1, keepdims=True) + EPSILON)
    normed_two = (residual * inv_two * gain_two).astype(BF16)
    per_micro = normed_two.reshape(micro_count, row_count, model_width)
    token_blocks = spread(per_micro) if linked else jnp.concatenate(group_gather(per_micro))

    graded_parts, mixed_parts = [], []
    for micro in range(micro_count):
        graded, mixed = experts(micro, token_blocks)
        if not linked:
            graded = group_scatter(graded[:4], graded[4:])
            mixed = group_scatter(mixed[:4], mixed[4:])
            graded, mixed, token_blocks = lax.optimization_barrier((graded, mixed, token_blocks))
        graded_parts.append(graded)
        mixed_parts.append(mixed)
    moe_grads = collect(*graded_parts, 3) if linked else graded_parts

    upstream_low = output_cot.reshape(micro_count * row_count, model_width)
    shared_pre = jnp.dot(normed_two, up_proj, preferred_element_type=F32)
    shared_width = shared_gate.shape[1]
    shared_pre_gate, shared_pre_up = shared_pre[:, :shared_width], shared_pre[:, shared_width:]
    shared_act, shared_deriv = silu_parts(shared_pre_gate)
    shared_hidden = (shared_act * shared_pre_up).astype(BF16)
    shared_out = jnp.dot(shared_hidden, down_proj, preferred_element_type=F32)
    grad_shared_hidden = mm("rd,fd->rf", upstream_low, down_proj)
    grad_shared_pre = jnp.concatenate(
        [
            (grad_shared_hidden * shared_pre_up * shared_deriv).astype(BF16),
            (grad_shared_hidden * shared_act).astype(BF16),
        ],
        axis=1,
    )
    grad_from_shared = mm("rf,df->rd", grad_shared_pre, up_proj)
    def expert_sum(left, right):
        own = None
        for k in reversed(range(far_steps)):
            if not linked:
                lefts = jnp.concatenate([m[k][left] for m in kept_rows])
                rights = jnp.concatenate([m[k][right] for m in kept_rows])
                if own is not None:
                    lefts, rights, own = lax.optimization_barrier((lefts, rights, own))
                total = mm("rd,rf->df", lefts, rights)
            else:
                total = mm("mrd,mrf->df", kept_rows[left][k], kept_rows[right][k])
            rows = total.shape[0] // 2
            total = total.reshape(2, rows, -1)
            mine = lax.dynamic_index_in_dim(total, half, 0, False)
            sent = lax.dynamic_index_in_dim(total, 1 - half, 0, False).astype(BF16)
            total = mine + exchange(sent, "seq", 2).astype(F32)
            own = total if own is None else total + rotate(own.astype(BF16), "exp", -4).astype(F32)
        rows = own.shape[0] // 2
        own = own.reshape(2, rows, -1)
        kept = lax.dynamic_index_in_dim(own, core, 0, False)
        sent = lax.dynamic_index_in_dim(own, 1 - core, 0, False).astype(BF16)
        other = exchange(sent, "seq", 1).astype(F32)
        return in_order(core, kept[None], other[None], 0)

    down_grad = expert_sum(2, 1)
    if not linked:
        down_grad, kept_rows = lax.optimization_barrier((down_grad, kept_rows))
    wide_grad = expert_sum(0, 3)
    moe_outs = collect(*mixed_parts, 4) if linked else mixed_parts

    def summed(value):
        return lax.psum_scatter(
            value.astype(BF16), everywhere, scatter_dimension=0, tiled=True
        ).astype(F32)

    shared_up_sum = summed(mm("rd,rf->df", normed_two, grad_shared_pre))
    shared_down_sum = summed(mm("rd,rf->df", shared_hidden, upstream_low))

    branches, grad_residuals, grad_qkv, outputs, gate_grads = [], [], [], [], []
    gain_two_sum = 0.0
    for micro in range(micro_count):
        rows = slice(micro * row_count, (micro + 1) * row_count)
        grad_normed = moe_grads[micro] + grad_from_shared[rows]
        grad_from_two, gain_part = norm_back(grad_normed, residual[rows], inv_two[rows], gain_two)
        gain_two_sum = gain_two_sum + gain_part
        grad_residual = upstream_low[rows].astype(F32) + grad_from_two
        grad_branch = grad_residual.astype(BF16)
        grad_residuals.append(grad_residual)
        branches.append(grad_branch)
        grad_context = mm("rd,id->ri", grad_branch, out_proj).astype(BF16)
        grad_query, grad_keys, grad_values = attention_back(micro, masks, queries, kv, grad_context)
        grad_kv = sequence_sum(grad_keys, grad_values)
        grad_qkv.append(jnp.concatenate([grad_query, grad_kv], axis=1))
        out = moe_outs[micro]
        outputs.append(
            (residual[rows] + shared_out[rows] + out[:, :model_width]).astype(BF16)
        )
        table = out[:, model_width : model_width + all_experts]
        gate_grads.append(
            jnp.sum(
                jnp.where(
                    routes[micro][:, :, None] == expert_range[None, None, :], table[:, None, :], 0.0
                ),
                axis=2,
            )
        )

    output_sum = summed(mm("rd,rf->df", contexts, jnp.concatenate(branches)))
    grad_qkv = jnp.concatenate(grad_qkv)
    grad_normed_one = mm("ri,di->rd", grad_qkv[:, :query_width], query_full)
    grad_normed_one = grad_normed_one + mm("ri,di->rd", grad_qkv[:, query_width:], kv_full)
    grad_from_one, gain_one_sum = norm_back(grad_normed_one, inputs, inv_one, gain_one)
    token_grads = (jnp.concatenate(grad_residuals) + grad_from_one).astype(BF16)
    column = lax.broadcasted_iota(jnp.int32, (1, qkv_width + 128), 1)
    last = mm("rd,rf->df", normed_one, jnp.pad(grad_qkv, ((0, 0), (0, 128))))
    last = jnp.where(column == qkv_width, gain_one_sum[:, None], last)
    last = summed(jnp.where(column == qkv_width + 1, gain_two_sum[:, None], last))

    return (
        jnp.stack(outputs),
        token_grads.reshape(micro_count, row_count, model_width),
        jnp.stack(gate_grads),
        last[:, qkv_width],
        last[:, :query_width],
        last[:, query_width : query_width + kv_width],
        last[:, query_width + kv_width : qkv_width],
        output_sum,
        last[:, qkv_width + 1],
        shared_up_sum[:, :shared_width],
        shared_up_sum[:, shared_width:],
        shared_down_sum,
        wide_grad[:, :, :expert_width],
        wide_grad[:, :, expert_width:],
        down_grad,
    )


def solution(mesh):
    rows = P(("seq", "exp"), None)
    wide = P("exp", "seq", None)
    flat = P(("seq", "exp"))
    return jax.shard_map(
        on_device,
        mesh=mesh,
        in_specs=(wide, P("exp", None), wide, wide, flat, rows, rows, rows, rows, flat, rows, rows, rows)
        + (wide,) * 4,
        out_specs=(wide, wide, wide, flat, rows, rows, rows, rows, flat, rows, rows, rows)
        + (wide,) * 3,
        check_vma=False,
    )
```

```python
import functools

import jax
import jax.numpy as jnp
from jax import lax
from jax.experimental import pallas as pl
from jax.experimental.pallas import tpu as pltpu
from jax.sharding import PartitionSpec as P

HEADS = 12
KV_HEADS = 4
HEAD_DIM = 128
GROUP_HEADS = HEADS // KV_HEADS
EPSILON = 1e-05
NEGATIVE = -1e30
F32 = jnp.float32
BF16 = jnp.bfloat16


def mm(spec, left, right):
    return jnp.einsum(spec, left, right, preferred_element_type=F32)


def exchange(value, axis, bit):
    size = lax.axis_size(axis)
    return lax.ppermute(value, axis, [(i, i ^ bit) for i in range(size)])


def rotate(value, axis, step):
    size = lax.axis_size(axis)
    return lax.ppermute(value, axis, [(i, (i + step) % size) for i in range(size)])


def after(value, *others):
    return lax.optimization_barrier((value, others))[0]


def in_order(flag, own, other, axis):
    return jnp.where(
        flag == 0,
        jnp.concatenate([own, other], axis),
        jnp.concatenate([other, own], axis),
    )


def silu_parts(pre_act):
    sigma_val = jax.nn.sigmoid(pre_act)
    return (pre_act * sigma_val, sigma_val * (1.0 + pre_act * (1.0 - sigma_val)))


def norm_back(grad_normed, values, inv_rms, gain):
    scaled = grad_normed * gain
    inner = jnp.mean(scaled * values, axis=1, keepdims=True)
    grad_values = inv_rms * scaled - values * (inv_rms * inv_rms * inv_rms) * inner
    return grad_values, jnp.sum(grad_normed * values * inv_rms, axis=0)


def group_gather(value):
    over_y = jnp.stack([value, exchange(value, "exp", 1)])
    over_z = jnp.concatenate([over_y, exchange(over_y, "exp", 2)])
    other = exchange(over_z, "seq", 1)
    return over_z, other


def group_scatter(own, other):
    part = own.astype(F32) + exchange(other, "seq", 1).astype(F32)
    part = part[:2] + exchange(part[2:].astype(BF16), "exp", 2).astype(F32)
    return part[0] + exchange(part[1].astype(BF16), "exp", 1).astype(F32)


def dot(left, right, over):
    return lax.dot_general(left, right, ((over[:1], over[1:]), ((), ())), preferred_element_type=F32)


def masked_softmax(query, keys, allowed, scale):
    scores = jnp.where(allowed, dot(query, keys, (1, 1)) * scale, NEGATIVE)
    expo = jnp.where(allowed, jnp.exp(scores - jnp.max(scores, axis=1, keepdims=True)), 0.0)
    total = jnp.sum(expo, axis=1, keepdims=True)
    return expo * (1.0 / jnp.where(total > 0.5, total, 1.0))


def attention_back_kernel(
    scale, mask_ref, query_ref, key_ref, value_ref, grad_ref, grad_query_ref, grad_key_ref, grad_value_ref
):
    keys = key_ref[...].reshape(-1, HEAD_DIM)
    values = value_ref[...].reshape(-1, HEAD_DIM)
    allowed = mask_ref[...] > 0
    grad_keys = grad_values = 0.0
    for g in range(GROUP_HEADS):
        lanes = slice(g * HEAD_DIM, (g + 1) * HEAD_DIM)
        query, grad = query_ref[:, lanes], grad_ref[:, lanes]
        weights = masked_softmax(query, keys, allowed, scale)
        grad_weights = dot(grad, values, (1, 1))
        delta = jnp.sum(weights * grad_weights, axis=1, keepdims=True)
        grad_scores = (weights * (grad_weights - delta)).astype(BF16)
        grad_query_ref[:, lanes] = (dot(grad_scores, keys, (1, 0)) * scale).astype(BF16)
        grad_keys = grad_keys + dot(query, grad_scores, (0, 0))
        grad_values = grad_values + dot(grad, weights.astype(BF16), (0, 0))
    grad_key_ref[...] = (grad_keys * scale).T.astype(BF16).reshape(grad_key_ref.shape)
    grad_value_ref[...] = grad_values.T.astype(BF16).reshape(grad_value_ref.shape)


MESH = pl.DeviceIdType.MESH
CORE, HALF = ("seq", 1), ("seq", 2)
SIDE, NEAR, FAR = ("exp", 1), ("exp", 2), ("exp", 4)


def bit_of(partner):
    axis, bit = partner
    return lax.axis_index(axis) // bit % 2


def device_of(partner):
    axis, bit = partner
    return {axis: lax.axis_index(axis) + bit - 2 * bit * bit_of(partner)}


def meet(partners):
    barrier = pltpu.get_barrier_semaphore()
    for partner in partners:
        pl.semaphore_signal(barrier, inc=1, device_id=device_of(partner), device_id_type=MESH)
    pl.semaphore_wait(barrier, len(partners))


class Sender:
    def __init__(self, send_sems, recv_sems):
        self.send_sems, self.recv_sems = send_sems, recv_sems
        self.copies, self.landed = [], set()

    def start(self, src, dst, partner):
        i = len(self.copies)
        copy = pltpu.make_async_remote_copy(
            src_ref=src,
            dst_ref=dst,
            send_sem=self.send_sems.at[i],
            recv_sem=self.recv_sems.at[i],
            device_id=device_of(partner),
            device_id_type=MESH,
        )
        copy.start()
        self.copies.append(copy)
        return i

    def arrived(self, *numbers):
        for i in numbers:
            if i not in self.landed:
                self.copies[i].wait_recv()
                self.landed.add(i)

    def finish(self):
        for i, copy in enumerate(self.copies):
            copy.wait_send()
            self.arrived(i)


def semaphores(count):
    return [pltpu.SemaphoreType.DMA((count,)), pltpu.SemaphoreType.DMA((count,))]


ANYWHERE = pl.BlockSpec(memory_space=pl.ANY)
VMEM = pl.BlockSpec(memory_space=pltpu.VMEM)
AXES = (HALF, CORE, FAR, NEAR, SIDE)


def doubling(sender, out, order, columns=None):
    held = []
    for partner in order:
        at = tuple(slice(None) if a in held else bit_of(a) for a in AXES)
        view = out.at[at] if columns is None else out.at[(*at, slice(None), columns)]
        number = sender.start(view, view, partner)
        yield
        sender.arrived(number)
        held.append(partner)


def in_turn(steps):
    steps = list(steps)
    while steps:
        steps = [s for s in steps if next(s, s) is not s]


def gather_kernel(
    query_ref, kv_ref, gain_ref, gate_ref, up_ref, down_ref, cot_ref,
    query_out, kv_out, gain_out, gate_out, up_out, down_out, far_out, side_out, near_out,
    send, recv, local,
):
    core, half = bit_of(CORE), bit_of(HALF)
    own = tuple(bit_of(a) for a in AXES)
    pairs = ((query_ref, query_out), (kv_ref, kv_out), (gain_ref, gain_out))
    experts = ((gate_ref, gate_out.at[half]), (up_ref, up_out.at[half]), (down_ref, down_out))
    moves = [(r, o.at[own]) for r, o in pairs] + [(r.at[core], o.at[core]) for r, o in experts]
    copies = [pltpu.make_async_copy(r, o, local.at[i]) for i, (r, o) in enumerate(moves)]
    for copy in copies:
        copy.start()
    meet(AXES)
    sender = Sender(send, recv)
    swaps = [sender.start(r.at[1 - core], o.at[core], CORE) for r, o in experts]
    for copy in copies:
        copy.wait()
    one, two = (NEAR, FAR, HALF, SIDE, CORE), (SIDE, NEAR, FAR, HALF, CORE)
    cut = query_ref.shape[1] // 2
    kv_cut = kv_ref.shape[1] // 2

    def near_experts():
        sender.arrived(*swaps)
        sender.start(gate_out.at[half], gate_out.at[half], HALF)
        for _ in range(3):
            yield
        sender.start(up_out.at[half], up_out.at[half], HALF)

    def far_expert():
        yield
        sender.start(gate_out.at[half], far_out, FAR)
        sender.start(cot_ref.at[0], side_out, SIDE)
        sender.start(cot_ref.at[1], near_out, NEAR)

    in_turn(
        [
            doubling(sender, gain_out, two),
            doubling(sender, query_out, one, pl.ds(0, cut)),
            doubling(sender, kv_out, two, pl.ds(0, kv_cut)),
            doubling(sender, query_out, one, pl.ds(cut, cut)),
            doubling(sender, kv_out, two, pl.ds(kv_cut, kv_cut)),
            near_experts(),
            far_expert(),
        ]
    )
    sender.finish()


def gather_first(query_proj, kv_proj, gains, expert_gate, expert_up, expert_down, cot):
    shape = jax.ShapeDtypeStruct
    shards = (query_proj, kv_proj, gains)
    experts = (expert_gate, expert_up, expert_down)
    return pl.pallas_call(
        gather_kernel,
        in_specs=[VMEM] * 7,
        out_specs=[ANYWHERE] * 9,
        out_shape=[
            *[shape((2,) * 5 + w.shape, w.dtype) for w in shards],
            *[shape((2, 2) + w.shape[1:], BF16) for w in experts[:2]],
            shape((2,) + expert_down.shape[1:], BF16),
            shape((2,) + expert_gate.shape[1:], BF16),
            shape(cot.shape[1:], BF16),
            shape(cot.shape[1:], BF16),
        ],
        scratch_shapes=[*semaphores(34), pltpu.SemaphoreType.DMA((6,))],
        compiler_params=pltpu.CompilerParams(
            collective_id=0, has_side_effects=True, vmem_limit_bytes=32 << 20
        ),
        name="gather_first",
    )(*shards, *experts, cot)


def attention_heads(scale, rows, mask_ref, query_ref, kv_ref, context_ref):
    allowed = mask_ref[rows, :] > 0
    blocks = [kv_ref.at[j, rows, :] for j in range(4)]

    def head(h, _):
        at = pl.ds(pl.multiple_of(h * HEAD_DIM, HEAD_DIM), HEAD_DIM)
        value_at = pl.ds(pl.multiple_of((h + KV_HEADS) * HEAD_DIM, HEAD_DIM), HEAD_DIM)
        keys = jnp.concatenate([b[:, at] for b in blocks])
        values = jnp.concatenate([b[:, value_at] for b in blocks])
        for g in range(GROUP_HEADS):
            lanes = pl.ds(pl.multiple_of((h * GROUP_HEADS + g) * HEAD_DIM, HEAD_DIM), HEAD_DIM)
            weights = masked_softmax(query_ref[rows, lanes], keys, allowed, scale)
            context_ref[rows, lanes] = dot(weights.astype(BF16), values, (1, 0)).astype(BF16)
        return 0

    lax.fori_loop(0, KV_HEADS, head, 0)


def attend_kernel(
    normed_ref, query_proj_ref, kv_proj_ref, mask_ref, up_ref, down_ref, far_ref, cot_ref, side_ref, near_ref, table_ref,
    query_ref, kv_ref, context_ref, gate_out, up_out, down_out, near_out, cot_out, table_out,
    up_half, down_half, send, recv, local,
):
    half = bit_of(HALF)
    moves = (
        (far_ref, gate_out.at[half]),
        (down_ref, near_out.at[half]),
        (cot_ref, cot_out.at[0, 0, 0]),
        (side_ref, cot_out.at[0, 0, 1, 0]),
        (near_ref, cot_out.at[0, 1, 0, 1]),
        (table_ref, table_out.at[0, 0, 0]),
    )
    copies = [pltpu.make_async_copy(r, o, local.at[i]) for i, (r, o) in enumerate(moves)]
    for copy in copies:
        copy.start()
    meet(AXES)
    sender = Sender(send, recv)
    far_up = sender.start(up_ref.at[half], up_half, FAR)
    table_side = sender.start(table_ref, table_out.at[0, 0, 1], SIDE)
    cots = [
        sender.start(cot_ref.at[0], cot_out.at[0, 1, 0, 0], NEAR),
        sender.start(side_ref, cot_out.at[0, 1, 1, 0], NEAR),
        sender.start(cot_ref.at[1], cot_out.at[0, 0, 1, 1], SIDE),
        sender.start(near_ref, cot_out.at[0, 1, 1, 1], SIDE),
    ]
    kv_ref[0] = dot(normed_ref[...], kv_proj_ref[...], (1, 0)).astype(BF16)
    kv_half = sender.start(kv_ref.at[0], kv_ref.at[2], HALF)
    kv_core = sender.start(kv_ref.at[0], kv_ref.at[1], CORE)
    query_ref[...] = dot(normed_ref[...], query_proj_ref[...], (1, 0)).astype(BF16)
    for copy in copies:
        copy.wait()
    sender.arrived(table_side)
    table_near = sender.start(table_out.at[0, 0], table_out.at[0, 1], NEAR)
    sender.arrived(kv_half)
    kv_both = sender.start(kv_ref.at[2], kv_ref.at[3], CORE)
    sender.start(far_ref, gate_out.at[half], HALF)
    sender.arrived(far_up)
    far_down = sender.start(down_ref, down_half, FAR)
    sender.start(down_ref, near_out.at[half], HALF)
    sender.start(up_half, up_out.at[half], HALF)
    up_copy = pltpu.make_async_copy(up_half, up_out.at[half], local.at[6])
    up_copy.start()
    sender.arrived(table_near)
    sender.start(table_out.at[0], table_out.at[1], CORE)
    sender.arrived(kv_core, kv_both)
    scale = HEAD_DIM ** (-0.5)
    row_count = mask_ref.shape[1] // 4
    for micro in range(normed_ref.shape[0] // row_count):
        rows = pl.ds(micro * row_count, row_count)
        attention_heads(scale, rows, mask_ref, query_ref, kv_ref, context_ref)
        if micro == 0:
            sender.arrived(*cots)
            sender.start(cot_out.at[0], cot_out.at[1], CORE)
    sender.arrived(far_down)
    sender.start(down_half, down_out.at[half], HALF)
    down_copy = pltpu.make_async_copy(down_half, down_out.at[half], local.at[7])
    down_copy.start()
    up_copy.wait()
    down_copy.wait()
    sender.finish()


def attend(normed, query_proj, kv_proj, masks, up_near, down_half, gate_far, cot, side, near, table):
    rows, width = normed.shape
    shape = jax.ShapeDtypeStruct
    gate_shape = (2,) + gate_far.shape
    return pl.pallas_call(
        attend_kernel,
        in_specs=[VMEM] * 4 + [ANYWHERE] + [VMEM] * 6,
        out_specs=[VMEM] * 3 + [ANYWHERE] * 6,
        out_shape=[
            shape((rows, query_proj.shape[1]), BF16),
            shape((4, rows, kv_proj.shape[1]), BF16),
            shape((rows, query_proj.shape[1]), BF16),
            shape(gate_shape, BF16),
            shape(up_near.shape, BF16),
            *[shape((2,) + down_half.shape, BF16)] * 2,
            shape((2, 2, 2) + cot.shape, cot.dtype),
            shape((2, 2, 2) + table.shape, table.dtype),
        ],
        scratch_shapes=[
            pltpu.VMEM(up_near.shape[1:], BF16),
            pltpu.VMEM(down_half.shape, BF16),
            *semaphores(18),
            pltpu.SemaphoreType.DMA((8,)),
        ],
        compiler_params=pltpu.CompilerParams(
            collective_id=1, has_side_effects=True, vmem_limit_bytes=60 << 20
        ),
        name="attend",
    )(normed, query_proj, kv_proj, masks, up_near, down_half, gate_far, cot, side, near, table)


def spread_kernel(value_ref, out, send, recv, local):
    copy = pltpu.make_async_copy(value_ref, out.at[0, 0, 0], local.at[0])
    copy.start()
    meet((CORE, SIDE, NEAR))
    sender = Sender(send, recv)
    firsts = (
        (sender.start(value_ref.at[0], out.at[0, 0, 1, 0], SIDE), (0, 0, 1, 0), NEAR, (0, 1, 1, 0)),
        (sender.start(value_ref.at[1], out.at[0, 1, 0, 1], NEAR), (0, 1, 0, 1), SIDE, (0, 1, 1, 1)),
    )
    seconds = [
        (sender.start(value_ref.at[0], out.at[0, 1, 0, 0], NEAR), (0, 1, 0, 0)),
        (sender.start(value_ref.at[1], out.at[0, 0, 1, 1], SIDE), (0, 0, 1, 1)),
    ]
    sender.start(value_ref, out.at[1, 0, 0], CORE)
    for number, at, partner, to in firsts:
        sender.arrived(number)
        seconds.append((sender.start(out.at[at], out.at[to], partner), to))
        sender.start(out.at[at], out.at[(1, *at[1:])], CORE)
    for number, at in seconds:
        sender.arrived(number)
        sender.start(out.at[at], out.at[(1, *at[1:])], CORE)
    copy.wait()
    sender.finish()


def spread(value):
    out = pl.pallas_call(
        spread_kernel,
        in_specs=[VMEM],
        out_specs=ANYWHERE,
        out_shape=jax.ShapeDtypeStruct((2, 2, 2) + value.shape, value.dtype),
        scratch_shapes=[*semaphores(13), pltpu.SemaphoreType.DMA((1,))],
        compiler_params=pltpu.CompilerParams(collective_id=2, has_side_effects=True),
        name="spread",
    )(value)
    return out.reshape((8,) + value.shape)


def collect_kernel(first_ref, second_ref, out_ref, core_recv, total_ref, axis_recv, send, recv):
    meet((CORE, SIDE, NEAR))
    sender = Sender(send, recv)
    orders = ((first_ref, (NEAR, SIDE), (2, 3, 1, 0)), (second_ref, (SIDE, NEAR), (1, 3, 2, 0)))
    numbers = {}
    for place in range(4):
        for m, (ref, _, order) in enumerate(orders):
            b = order[place]
            numbers[m, b] = sender.start(ref.at[4 + b], core_recv.at[m, b], CORE)
    landing = {}
    for place in range(2):
        for m, (ref, axes, order) in enumerate(orders):
            b = order[place]
            sender.arrived(numbers[m, b])
            total_ref[m, b] = (ref[b].astype(F32) + core_recv[m, b].astype(F32)).astype(BF16)
            landing[m, place] = sender.start(total_ref.at[m, b], axis_recv.at[m, place], axes[0])
    for m, (ref, axes, order) in enumerate(orders):
        b = order[2]
        sender.arrived(numbers[m, b], landing[m, 1])
        total = ref[b].astype(F32) + core_recv[m, b].astype(F32) + axis_recv[m, 1].astype(F32)
        total_ref[m, b] = total.astype(BF16)
        landing[m, 2] = sender.start(total_ref.at[m, b], axis_recv.at[m, 2], axes[1])
    for m, (ref, _, order) in enumerate(orders):
        sender.arrived(numbers[m, 0], landing[m, 0])
        out_ref[m] = ref[0].astype(F32) + core_recv[m, 0].astype(F32) + axis_recv[m, 0].astype(F32)
    for m in range(2):
        sender.arrived(landing[m, 2])
        out_ref[m] = out_ref[m] + axis_recv[m, 2].astype(F32)
    sender.finish()


def collect(first, second, number):
    block = first.shape[1:]
    return pl.pallas_call(
        collect_kernel,
        in_specs=[VMEM] * 2,
        out_specs=VMEM,
        out_shape=jax.ShapeDtypeStruct((2, *block), F32),
        scratch_shapes=[
            pltpu.VMEM((2, 4, *block), BF16),
            pltpu.VMEM((2, 4, *block), BF16),
            pltpu.VMEM((2, 3, *block), BF16),
            *semaphores(14),
        ],
        compiler_params=pltpu.CompilerParams(
            collective_id=number, has_side_effects=True, vmem_limit_bytes=60 << 20
        ),
        name="collect",
    )(first, second)


def back_kernel(
    mask_ref, query_ref, kv_ref, grad_ref, near_wide, near_down, far_wide, far_down,
    grad_query_ref, grad_kv_ref, wide_out, down_out,
    part_ref, kv_core, kv_send, kv_half, far_wide_recv, far_down_recv, near_wide_recv, near_down_recv,
    wide_send, down_send, wide_recv, down_recv, wide_core, down_core, wide_own, down_own, send, recv,
):
    core, half = bit_of(CORE), bit_of(HALF)
    scale = HEAD_DIM ** (-0.5)
    row_count = mask_ref.shape[1] // 4

    def heads(micro):
        rows = pl.ds(micro * row_count, row_count)
        allowed = mask_ref[rows, :] > 0

        def head(h, _):
            at = pl.ds(pl.multiple_of(h * HEAD_DIM, HEAD_DIM), HEAD_DIM)
            value_at = pl.ds(pl.multiple_of((h + KV_HEADS) * HEAD_DIM, HEAD_DIM), HEAD_DIM)
            keys = jnp.concatenate([kv_ref[j, rows, at] for j in range(4)])
            values = jnp.concatenate([kv_ref[j, rows, value_at] for j in range(4)])
            grad_keys = grad_values = 0.0
            for g in range(GROUP_HEADS):
                lanes = pl.ds(pl.multiple_of((h * GROUP_HEADS + g) * HEAD_DIM, HEAD_DIM), HEAD_DIM)
                query, grad = query_ref[rows, lanes], grad_ref[rows, lanes]
                weights = masked_softmax(query, keys, allowed, scale)
                grad_weights = dot(grad, values, (1, 1))
                delta = jnp.sum(weights * grad_weights, axis=1, keepdims=True)
                grad_scores = (weights * (grad_weights - delta)).astype(BF16)
                grad_query_ref[rows, lanes] = (dot(grad_scores, keys, (1, 0)) * scale).astype(BF16)
                grad_keys = grad_keys + dot(query, grad_scores, (0, 0))
                grad_values = grad_values + dot(grad, weights.astype(BF16), (0, 0))
            grad_keys = (grad_keys * scale).T.astype(BF16)
            grad_values = grad_values.T.astype(BF16)
            for j in range(4):
                part_ref[j, rows, at] = grad_keys[j * row_count : (j + 1) * row_count]
                part_ref[j, rows, value_at] = grad_values[j * row_count : (j + 1) * row_count]
            return 0

        lax.fori_loop(0, KV_HEADS, head, 0)

    def add(*values):
        total = values[0][...].astype(F32)
        for value in values[1:]:
            total = total + value[...].astype(F32)
        return total

    meet((CORE, HALF, FAR))
    sender = Sender(send, recv)
    other = 1 - half
    across = [sender.start(far_wide.at[other, 0], far_wide_recv.at[0], HALF)]
    heads(0)
    across.append(sender.start(far_wide.at[other, 1], far_wide_recv.at[1], HALF))
    fars = []
    for q in range(2):
        if q:
            heads(1)
            kv_sums = [sender.start(part_ref.at[2 * j + 1], kv_core.at[j], CORE) for j in range(2)]
        sender.arrived(across[q])
        wide_send[q] = add(far_wide[half, q], far_wide_recv[q]).astype(BF16)
        fars.append(sender.start(wide_send.at[q], wide_recv.at[q], FAR))
    far_last = sender.start(far_down.at[other], far_down_recv, HALF)
    sender.arrived(*kv_sums)
    kv_send[...] = add(part_ref[2], kv_core[1]).astype(BF16)
    kv_last = sender.start(kv_send, kv_half, HALF)
    near = [sender.start(near_wide.at[other], near_wide_recv, HALF)]
    sender.arrived(far_last)
    down_send[...] = add(far_down[half], far_down_recv).astype(BF16)
    fars.append(sender.start(down_send, down_recv, FAR))
    near.append(sender.start(near_down.at[other], near_down_recv, HALF))
    sender.arrived(kv_last)
    grad_kv_ref[...] = add(part_ref[0], kv_core[0], kv_half[...]).astype(BF16)
    sender.arrived(*near, *fars[:2])

    def finish(near_ref, near_recv, far_recv, own_ref, core_ref, out_ref):
        own_ref[...] = add(near_ref[half, 1 - core], near_recv[1 - core], far_recv[1 - core]).astype(BF16)
        number = sender.start(own_ref, core_ref, CORE)
        out_ref[core] = add(near_ref[half, core], near_recv[core], far_recv[core])
        return number

    wide_last = finish(near_wide, near_wide_recv, wide_recv, wide_own, wide_core, wide_out)
    sender.arrived(wide_last)
    wide_out[1 - core] = wide_core[...].astype(F32)
    sender.arrived(*fars)
    down_last = finish(near_down, near_down_recv, down_recv, down_own, down_core, down_out)
    sender.arrived(down_last)
    down_out[1 - core] = down_core[...].astype(F32)
    sender.finish()


def back(masks, queries, kv, grad, near_wide, near_down, far_wide, far_down):
    shape = jax.ShapeDtypeStruct
    rows, width = kv.shape[1:]
    wide, down = near_wide.shape[1:], near_down.shape[1:]
    space = lambda *dims: pltpu.VMEM(dims, BF16)
    return pl.pallas_call(
        back_kernel,
        in_specs=[VMEM] * 8,
        out_specs=[VMEM] * 4,
        out_shape=[
            shape(queries.shape, BF16),
            shape((rows, width), BF16),
            shape((2,) + wide[1:], F32),
            shape((2,) + down[1:], F32),
        ],
        scratch_shapes=[
            space(4, rows, width),
            space(2, rows, width),
            space(rows, width),
            space(rows, width),
            *[space(*wide), space(*down)] * 4,
            *[space(*wide[1:]), space(*down[1:])] * 2,
            *semaphores(14),
        ],
        compiler_params=pltpu.CompilerParams(
            collective_id=5, has_side_effects=True, vmem_limit_bytes=62 << 20
        ),
        name="back",
    )(masks, queries, kv, grad, near_wide, near_down, far_wide, far_down)


def halving(sender, value, spaces, order, out, columns):
    left = list(AXES)
    for partner, (landing, total_ref) in zip(order, spaces):
        place = left.index(partner)
        left.pop(place)
        rest = (slice(None),) * (len(left) - place + 1)
        at = lambda bit: (*(slice(None),) * place, bit, *rest, columns)
        into = (*(slice(None),) * (len(left) + 1), columns)
        own = bit_of(partner)
        number = sender.start(value.at[at(1 - own)], landing.at[into], partner)
        yield
        sender.arrived(number)
        total = value[at(own)].astype(F32) + landing[into].astype(F32)
        if left:
            total_ref[into] = total.astype(BF16)
            value = total_ref
        else:
            out[into] = total


def reduce_kernel(first_ref, second_ref, first_out, second_out, *refs):
    send, recv = refs[-2:]
    spaces = list(zip(refs[:-2:2], refs[1:-2:2]))
    first, second = spaces[:5], spaces[5:]
    meet(AXES)
    sender = Sender(send, recv)
    one, two = (CORE, SIDE, HALF, FAR, NEAR), (CORE, HALF, FAR, NEAR, SIDE)
    cut = first_ref.shape[-1] // 2
    other_cut = second_ref.shape[-1] // 256 * 128
    in_turn(
        [
            halving(sender, first_ref, first, one, first_out, pl.ds(0, cut)),
            halving(sender, second_ref, second, two, second_out, pl.ds(0, other_cut)),
            halving(sender, first_ref, first, one, first_out, pl.ds(cut, cut)),
            halving(
                sender, second_ref, second, two, second_out,
                pl.ds(other_cut, second_ref.shape[-1] - other_cut),
            ),
        ]
    )
    sender.finish()


def reduce_dense(first, second):
    values, scratch = [], []
    for value in (first, second):
        rows = value.shape[0] // 32
        values.append(value.reshape((2,) * 5 + (rows, -1)).astype(BF16))
        for left in range(4, -1, -1):
            dims = (2,) * left + values[-1].shape[5:]
            scratch += [pltpu.VMEM(dims, BF16), pltpu.VMEM(dims if left else (8, 128), BF16)]
    return pl.pallas_call(
        reduce_kernel,
        in_specs=[VMEM] * 2,
        out_specs=[VMEM] * 2,
        out_shape=[jax.ShapeDtypeStruct(v.shape[5:], F32) for v in values],
        scratch_shapes=[*scratch, *semaphores(20)],
        compiler_params=pltpu.CompilerParams(
            collective_id=6, has_side_effects=True, vmem_limit_bytes=60 << 20
        ),
        name="reduce_dense",
    )(*values)


def attention_back(micro, masks, queries, kv, grad):
    row_count = grad.shape[0]
    wide = GROUP_HEADS * HEAD_DIM
    heads = lambda at: pl.BlockSpec((4, row_count, HEAD_DIM), lambda h: (0, micro, h + at))
    column = pl.BlockSpec((4, row_count, HEAD_DIM), lambda h: (0, 0, h))
    flat = jax.ShapeDtypeStruct((4, row_count, KV_HEADS * HEAD_DIM), BF16)
    return pl.pallas_call(
        functools.partial(attention_back_kernel, HEAD_DIM ** (-0.5)),
        grid=(KV_HEADS,),
        in_specs=[
            pl.BlockSpec((row_count, 4 * row_count), lambda h: (micro, 0)),
            pl.BlockSpec((row_count, wide), lambda h: (micro, h)),
            heads(0),
            heads(KV_HEADS),
            pl.BlockSpec((row_count, wide), lambda h: (0, h)),
        ],
        out_specs=[pl.BlockSpec((row_count, wide), lambda h: (0, h)), column, column],
        out_shape=[jax.ShapeDtypeStruct((row_count, HEADS * HEAD_DIM), BF16), flat, flat],
        compiler_params=pltpu.CompilerParams(vmem_limit_bytes=48 << 20),
        name="attention_back",
    )(masks, queries, kv, kv, grad)


def expert_kernel(
    slot_ref, scale_ref, column_ref, token_ref, cot_ref, *refs
):
    count = column_ref.shape[0]
    gate_refs, up_refs, down_refs = refs[:count], refs[count : 2 * count], refs[2 * count : 3 * count]
    rows_ref, cots_ref, hidden_ref, pre_ref, mixed_ref, graded_ref = refs[-10:-4]
    pick_ref, value_ref, extra_ref, back_ref = refs[-4:]
    width = down_refs[0].shape[0]
    blocks, row_count = token_ref.shape[0], token_ref.shape[2]
    room = rows_ref.shape[2] // blocks
    slot = lax.broadcasted_iota(jnp.int32, (room, row_count), 0)
    gates = []
    for b in range(blocks):
        for k in range(count):
            picked = slot == slot_ref[k, b]
            gates.append(jnp.sum(jnp.where(picked, scale_ref[k, b], 0.0), axis=1, keepdims=True))
            pick_ref[b, k * room : (k + 1) * room, :] = jnp.where(picked, 1.0, 0.0).astype(BF16)
        rows = dot(pick_ref[b], token_ref[b, 0], (1, 0)).astype(BF16)
        cots = dot(pick_ref[b], cot_ref[b, 0], (1, 0)).astype(BF16)
        for k in range(count):
            part = slice(b * room, (b + 1) * room)
            rows_ref[k, 0, part, :] = rows[k * room : (k + 1) * room]
            cots_ref[k, 0, part, :] = cots[k * room : (k + 1) * room]
    for k in range(count):
        gate = jnp.concatenate([gates[b * count + k] for b in range(blocks)])
        pre_gate = dot(rows_ref[k, 0], gate_refs[k][...], (1, 0))
        pre_up = dot(rows_ref[k, 0], up_refs[k][...], (1, 0))
        grad_hidden = dot(cots_ref[k, 0], down_refs[k][...], (1, 1))
        act, deriv = silu_parts(pre_gate)
        hidden = act * pre_up
        gate_grad = jnp.sum(hidden * grad_hidden, axis=1, keepdims=True)
        grad_hidden = grad_hidden * gate
        hidden_ref[k, 0] = (hidden * gate).astype(BF16)
        pre_ref[k, 0, :, :width] = (grad_hidden * pre_up * deriv).astype(BF16)
        pre_ref[k, 0, :, width:] = (grad_hidden * act).astype(BF16)
        value = dot(hidden_ref[k, 0], down_refs[k][...], (1, 0)).astype(BF16)
        back = dot(pre_ref[k, 0, :, :width], gate_refs[k][...], (1, 1))
        back = (back + dot(pre_ref[k, 0, :, width:], up_refs[k][...], (1, 1))).astype(BF16)
        extra = (gate_grad * column_ref[k]).astype(BF16)
        for b in range(blocks):
            to, part = slice(k * room, (k + 1) * room), slice(b * room, (b + 1) * room)
            value_ref[b, to, :] = value[part]
            back_ref[b, to, :] = back[part]
            extra_ref[b, to, :] = extra[part]
    model_width = token_ref.shape[3]
    for b in range(blocks):
        graded_ref[b] = dot(pick_ref[b], back_ref[b], (0, 0)).astype(BF16)
        mixed_ref[b, :, :model_width] = dot(pick_ref[b], value_ref[b], (0, 0)).astype(BF16)
        mixed_ref[b, :, model_width:] = dot(pick_ref[b], extra_ref[b], (0, 0)).astype(BF16)


def expert_pass(micro, slots, scales, columns, tokens, cots, gates, ups, downs, room, kept):
    count, (width, model_width) = len(downs), downs[0].shape
    blocks, micro_count, row_count = tokens.shape[:3]
    step = 2
    by_block = lambda *dims: pl.BlockSpec((step, *dims), lambda b: (b,) + (0,) * len(dims))
    by_slot = pl.BlockSpec((count, step, 1, row_count), lambda b: (0, b, 0, 0))
    whole = lambda *dims: pl.BlockSpec(dims, lambda b: (0,) * len(dims), pipeline_mode=pl.Buffered(1))
    saved = lambda cols: pl.BlockSpec((count, 1, step * room, cols), lambda b: (0, micro, b, 0))
    widths = (model_width, model_width, width, 2 * width)
    shapes = [jax.ShapeDtypeStruct((count, micro_count, blocks * room, w), BF16) for w in widths]
    args = [slots, scales, columns, tokens, cots, *gates, *ups, *downs]
    in_specs = [
        by_slot,
        by_slot,
        whole(count, 1, 128),
        pl.BlockSpec((step, 1, row_count, model_width), lambda b: (b, micro, 0, 0)),
        pl.BlockSpec((step, 1, row_count, model_width), lambda b: (b, micro, 0, 0)),
        *[whole(model_width, width)] * (2 * count),
        *[whole(width, model_width)] * count,
    ]
    aliases = {}
    if kept:
        aliases = {len(args) + i: i for i in range(len(kept))}
        in_specs += [pl.BlockSpec(memory_space=pl.ANY)] * len(kept)
        args += list(kept)
    out = pl.pallas_call(
        expert_kernel,
        grid=(blocks // step,),
        in_specs=in_specs,
        out_specs=[saved(w) for w in widths]
        + [by_block(row_count, model_width + 128), by_block(row_count, model_width)],
        out_shape=shapes
        + [
            jax.ShapeDtypeStruct((blocks, row_count, model_width + 128), BF16),
            jax.ShapeDtypeStruct((blocks, row_count, model_width), BF16),
        ],
        scratch_shapes=[
            pltpu.VMEM((step, count * room, row_count), BF16),
            pltpu.VMEM((step, count * room, model_width), BF16),
            pltpu.VMEM((step, count * room, 128), BF16),
            pltpu.VMEM((step, count * room, model_width), BF16),
        ],
        input_output_aliases=aliases,
        compiler_params=pltpu.CompilerParams(vmem_limit_bytes=60 << 20),
        name="experts",
    )(*args)
    return out[:4], out[4], out[5]


def attend_plain(queries, kv, masks, micro):
    row_count = masks.shape[1] // 4
    rows = slice(micro * row_count, (micro + 1) * row_count)
    allowed = masks[rows] > 0
    wide = KV_HEADS * HEAD_DIM
    heads = queries[rows].reshape(row_count, KV_HEADS, GROUP_HEADS, HEAD_DIM)
    keys = kv[:, rows, :wide].reshape(-1, KV_HEADS, HEAD_DIM)
    values = kv[:, rows, wide:].reshape(-1, KV_HEADS, HEAD_DIM)
    scores = mm("ikgd,jkd->kgij", heads, keys) * HEAD_DIM ** (-0.5)
    row_max = jnp.max(jnp.where(allowed, scores, NEGATIVE), axis=3, keepdims=True)
    expo = jnp.where(allowed, jnp.exp(jnp.where(allowed, scores, NEGATIVE) - row_max), 0.0)
    total = jnp.sum(expo, axis=3, keepdims=True)
    weights = (expo / jnp.where(total > 0.5, total, 1.0)).astype(BF16)
    return mm("kgij,jkd->ikgd", weights, values).reshape(row_count, HEADS * HEAD_DIM).astype(BF16)


def on_device(
    tokens,
    segment_ids,
    routes,
    route_gates,
    attn_gain,
    query_proj,
    key_proj,
    value_proj,
    output_proj,
    ffn_gain,
    shared_gate,
    shared_up,
    shared_down,
    expert_gate,
    expert_up,
    expert_down,
    output_cot,
):
    micro_count, row_count, model_width = tokens.shape
    exp_count = lax.axis_size("exp")
    local_experts, gate_rows, expert_width = expert_gate.shape
    down_rows = expert_down.shape[1]
    all_experts = local_experts * exp_count
    route_count = routes.shape[2]
    capacity = 4 * row_count * route_count // (3 * all_experts)
    query_width = HEADS * HEAD_DIM
    kv_width = KV_HEADS * HEAD_DIM
    far_steps = exp_count // 4
    assert lax.axis_size("seq") == 4 and local_experts == 2

    seq_index = lax.axis_index("seq")
    exp_index = lax.axis_index("exp")
    core = seq_index % 2
    half = seq_index // 2
    everywhere = ("seq", "exp")

    linked = exp_count == 8
    expert_range = jnp.arange(all_experts, dtype=jnp.int32)
    gate_table = jnp.sum(
        jnp.where(
            jnp.swapaxes(routes, 1, 2)[:, :, None, :] == expert_range[None, None, :, None],
            jnp.swapaxes(route_gates, 1, 2)[:, :, None, :],
            0.0,
        ),
        axis=1,
    )
    order = jnp.arange(row_count, dtype=jnp.int32)
    before = (order[:, None] < order[None, :]).astype(BF16)
    slots = jnp.arange(capacity, dtype=jnp.int32)
    expert_ids = [
        local_experts * ((exp_index - 4 * k + exp_count) % exp_count) + core
        for k in range(far_steps)
    ]
    kv_proj = jnp.concatenate([key_proj, value_proj], axis=1)
    shared_wide = jnp.concatenate([shared_gate, shared_up], axis=1)

    def gathered(value):
        return lax.all_gather(value, everywhere, axis=0, tiled=True)

    def mask_of(micro):
        segments = segment_ids[micro].reshape(4, row_count)
        key_ids = jnp.concatenate(
            [lax.dynamic_index_in_dim(segments, seq_index ^ j, 0, False) for j in range(4)]
        )
        key_pos = jnp.concatenate([(seq_index ^ j) * row_count + order for j in range(4)])
        query_ids, query_pos = key_ids[:row_count], key_pos[:row_count]
        allowed = (
            (key_ids[None, :] == query_ids[:, None])
            & (key_pos[None, :] <= query_pos[:, None])
            & (query_ids[:, None] >= 0)
        )
        return allowed.astype(jnp.int32)

    inputs = tokens.reshape(micro_count * row_count, model_width).astype(F32)
    inv_one = lax.rsqrt(jnp.mean(inputs * inputs, axis=1, keepdims=True) + EPSILON)
    masks = jnp.concatenate([mask_of(micro) for micro in range(micro_count)])
    if linked:
        gains = jnp.stack([attn_gain, ffn_gain]).astype(F32)
        share = gains.shape[1]
        gains = jnp.pad(gains, ((0, 6), (0, 128 - share)))
        query_full, kv_full, gains, gate_near, up_near, down_half, gate_far, side, near = gather_first(
            query_proj, kv_proj, gains, expert_gate, expert_up, expert_down, output_cot
        )
        query_full = query_full.reshape(model_width, query_width)
        kv_full = kv_full.reshape(model_width, 2 * kv_width)
        gains = gains.reshape(-1, 8, 128)[:, :2, :share]
        gain_one, gain_two = jnp.swapaxes(gains, 0, 1).reshape(2, model_width)
        output_proj = after(output_proj, query_full)
    else:
        query_full, kv_full = gathered(query_proj), gathered(kv_proj)
        gain_one, gain_two = gathered(attn_gain).astype(F32), gathered(ffn_gain).astype(F32)
    out_proj = gathered(output_proj)
    normed_one = (inputs * inv_one * gain_one).astype(BF16)

    if linked:
        queries, kv, contexts, gate_far, up_far, down_far, down_near, cots, tables = attend(
            normed_one, query_full, kv_full, masks, up_near, down_half, gate_far, output_cot, side, near, gate_table
        )
        gate_all = [w.reshape(model_width, expert_width) for w in (gate_near, gate_far)]
        up_all = [w.reshape(model_width, expert_width) for w in (up_near, up_far)]
        down_all = [w.reshape(expert_width, model_width) for w in (down_near, down_far)]
        shared_wide, shared_down = after((shared_wide, shared_down), contexts)
        cot_blocks = cots.reshape(8, micro_count, row_count, model_width)
        gate_blocks = tables.reshape(8, micro_count, all_experts, row_count)
    else:
        queries = jnp.dot(normed_one, query_full, preferred_element_type=F32).astype(BF16)
        own = jnp.dot(normed_one, kv_full, preferred_element_type=F32).astype(BF16)
        across = exchange(own, "seq", 2)
        kv = jnp.stack([own, exchange(own, "seq", 1), across, exchange(across, "seq", 1)])
        contexts = jnp.concatenate([attend_plain(queries, kv, masks, m) for m in range(micro_count)])
        gate_blocks = jnp.concatenate(group_gather(gate_table))
        cot_blocks = jnp.concatenate(group_gather(output_cot))

        def parity(value):
            kept = lax.dynamic_index_in_dim(value, core, 0, False)
            sent = lax.dynamic_index_in_dim(value, 1 - core, 0, False)
            return in_order(core, kept, exchange(sent, "seq", 1), 0)

        wide_far = [parity(jnp.concatenate([expert_gate, expert_up], axis=2))]
        down_far = [parity(expert_down)]
        for _ in range(far_steps - 1):
            wide_far.append(rotate(wide_far[-1], "exp", 4))
            down_far.append(rotate(down_far[-1], "exp", 4))
        wide_full = [in_order(half, w, exchange(w, "seq", 2), 0) for w in wide_far]
        down_full = [in_order(half, w, exchange(w, "seq", 2), 0) for w in down_far]

    def sequence_sum(grad_keys, grad_values):
        grad = jnp.concatenate([grad_keys, grad_values], axis=2)
        part = grad[0::2].astype(F32) + exchange(grad[1::2], "seq", 1).astype(F32)
        return (part[0] + exchange(part[1].astype(BF16), "seq", 2).astype(F32)).astype(BF16)

    kept_rows = []

    def experts(micro, normed_blocks):
        gates = jnp.stack(
            [lax.dynamic_index_in_dim(gate_blocks[:, micro], e, 1, False) for e in expert_ids]
        )
        named = gates > 0.0
        rank = mm("kbs,st->kbt", named.astype(BF16), before).astype(jnp.int32)
        slot = jnp.where(named, rank, -1)
        if not linked:
            return experts_plain(gates, slot, normed_blocks[:, micro], cot_blocks[:, micro])
        columns = (
            lax.broadcasted_iota(jnp.int32, (far_steps, 1, 128), 2)
            == jnp.stack(expert_ids)[:, None, None]
        ).astype(F32)
        kept, mixed, graded = expert_pass(
            micro, slot[:, :, None], gates[:, :, None], columns,
            normed_blocks, cot_blocks, gate_all, up_all, down_all, capacity, kept_rows,
        )
        kept_rows[:] = kept
        return graded, mixed

    def experts_plain(gates, slot, normed_blocks, micro_cots):
        mixed, graded, kept = 0.0, 0.0, []
        for k in range(far_steps):
            picked = slot[k][:, None, :] == slots[None, :, None]
            pick = picked.astype(BF16)
            slot_gates = jnp.sum(jnp.where(picked, gates[k][:, None, :], 0.0), axis=2).reshape(-1, 1)
            rows = mm("bst,btd->bsd", pick, normed_blocks).astype(BF16).reshape(-1, model_width)
            cots = mm("bst,btd->bsd", pick, micro_cots).astype(BF16).reshape(-1, model_width)
            pre = jnp.dot(rows, wide_full[k], preferred_element_type=F32)
            pre_gate, pre_up = pre[:, :expert_width], pre[:, expert_width:]
            grad_hidden = mm("rd,fd->rf", cots, down_full[k])
            act, deriv = silu_parts(pre_gate)
            hidden = act * pre_up
            gate_grad = jnp.sum(hidden * grad_hidden, axis=1, keepdims=True)
            hidden = (hidden * slot_gates).astype(BF16)
            grad_hidden = grad_hidden * slot_gates
            grad_pre = jnp.concatenate(
                [(grad_hidden * pre_up * deriv).astype(BF16), (grad_hidden * act).astype(BF16)], axis=1
            )
            value = jnp.dot(hidden, down_full[k], preferred_element_type=F32).astype(BF16)
            column = (lax.broadcasted_iota(jnp.int32, (1, 128), 1) == expert_ids[k]).astype(F32)
            value = jnp.concatenate([value, (gate_grad * column).astype(BF16)], axis=1)
            grad_rows = mm("rf,df->rd", grad_pre, wide_full[k]).astype(BF16)
            blocks = pick.shape[0]
            mixed = mixed + mm("bst,bsd->btd", pick, value.reshape(blocks, capacity, -1))
            graded = graded + mm("bst,bsd->btd", pick, grad_rows.reshape(blocks, capacity, -1))
            kept.append((rows, cots, hidden, grad_pre))
        kept_rows.append(kept)
        return graded.astype(BF16), mixed.astype(BF16)

    up_proj, down_proj = gathered(shared_wide), gathered(shared_down)
    residual = inputs + jnp.dot(contexts, out_proj, preferred_element_type=F32)
    inv_two = lax.rsqrt(jnp.mean(residual * residual, axis=1, keepdims=True) + EPSILON)
    normed_two = (residual * inv_two * gain_two).astype(BF16)
    per_micro = normed_two.reshape(micro_count, row_count, model_width)
    token_blocks = spread(per_micro) if linked else jnp.concatenate(group_gather(per_micro))

    graded_parts, mixed_parts = [], []
    for micro in range(micro_count):
        graded, mixed = experts(micro, token_blocks)
        if not linked:
            graded = group_scatter(graded[:4], graded[4:])
            mixed = group_scatter(mixed[:4], mixed[4:])
            graded, mixed, token_blocks = lax.optimization_barrier((graded, mixed, token_blocks))
        graded_parts.append(graded)
        mixed_parts.append(mixed)
    moe_grads = collect(*graded_parts, 3) if linked else graded_parts

    upstream_low = output_cot.reshape(micro_count * row_count, model_width)
    shared_pre = jnp.dot(normed_two, up_proj, preferred_element_type=F32)
    shared_width = shared_gate.shape[1]
    shared_pre_gate, shared_pre_up = shared_pre[:, :shared_width], shared_pre[:, shared_width:]
    shared_act, shared_deriv = silu_parts(shared_pre_gate)
    shared_hidden = (shared_act * shared_pre_up).astype(BF16)
    shared_out = jnp.dot(shared_hidden, down_proj, preferred_element_type=F32)
    grad_shared_hidden = mm("rd,fd->rf", upstream_low, down_proj)
    grad_shared_pre = jnp.concatenate(
        [
            (grad_shared_hidden * shared_pre_up * shared_deriv).astype(BF16),
            (grad_shared_hidden * shared_act).astype(BF16),
        ],
        axis=1,
    )
    grad_from_shared = mm("rf,df->rd", grad_shared_pre, up_proj)
    moe_outs = collect(*mixed_parts, 4) if linked else mixed_parts

    def summed(value):
        return lax.psum_scatter(
            value.astype(BF16), everywhere, scatter_dimension=0, tiled=True
        ).astype(F32)

    shared_up_sum = summed(mm("rd,rf->df", normed_two, grad_shared_pre))
    shared_down_sum = summed(mm("rd,rf->df", shared_hidden, upstream_low))

    def flat(value):
        return value.reshape(micro_count * row_count, -1)

    if linked:
        moe_grads, moe_outs = flat(moe_grads), flat(moe_outs)
    else:
        moe_grads, moe_outs = jnp.concatenate(moe_grads), jnp.concatenate(moe_outs)
    grad_normed = moe_grads + grad_from_shared
    grad_from_two, gain_two_sum = norm_back(grad_normed, residual, inv_two, gain_two)
    grad_residual = upstream_low.astype(F32) + grad_from_two
    grad_branch = grad_residual.astype(BF16)
    grad_context = mm("rd,id->ri", grad_branch, out_proj).astype(BF16)
    output_sum = summed(mm("rd,rf->df", contexts, grad_branch))

    def expert_sum(left, right):
        own = None
        for k in reversed(range(far_steps)):
            lefts = jnp.concatenate([m[k][left] for m in kept_rows])
            rights = jnp.concatenate([m[k][right] for m in kept_rows])
            if own is not None:
                lefts, rights, own = lax.optimization_barrier((lefts, rights, own))
            total = mm("rd,rf->df", lefts, rights)
            rows = total.shape[0] // 2
            total = total.reshape(2, rows, -1)
            mine = lax.dynamic_index_in_dim(total, half, 0, False)
            sent = lax.dynamic_index_in_dim(total, 1 - half, 0, False).astype(BF16)
            total = mine + exchange(sent, "seq", 2).astype(F32)
            own = total if own is None else total + rotate(own.astype(BF16), "exp", -4).astype(F32)
        rows = own.shape[0] // 2
        own = own.reshape(2, rows, -1)
        kept = lax.dynamic_index_in_dim(own, core, 0, False)
        sent = lax.dynamic_index_in_dim(own, 1 - core, 0, False).astype(BF16)
        other = exchange(sent, "seq", 1).astype(F32)
        return in_order(core, kept[None], other[None], 0)

    if linked:
        products = []
        for k in range(far_steps):
            for left, right in ((0, 3), (2, 1)):
                total = mm("mrd,mrf->df", kept_rows[left][k], kept_rows[right][k]).astype(BF16)
                products.append(total.reshape(2, 2, total.shape[0] // 4, -1))
        grad_query, grad_kv, wide_grad, down_grad = back(masks, queries, kv, grad_context, *products)
    else:
        down_grad = expert_sum(2, 1)
        down_grad, kept_rows = lax.optimization_barrier((down_grad, kept_rows))
        wide_grad = expert_sum(0, 3)
        grad_queries, grad_kvs = [], []
        for micro in range(micro_count):
            rows = slice(micro * row_count, (micro + 1) * row_count)
            grad_query, grad_keys, grad_values = attention_back(
                micro, masks, queries, kv, grad_context[rows]
            )
            grad_queries.append(grad_query)
            grad_kvs.append(sequence_sum(grad_keys, grad_values))
        grad_query, grad_kv = jnp.concatenate(grad_queries), jnp.concatenate(grad_kvs)

    outputs = (residual + shared_out + moe_outs[:, :model_width]).astype(BF16)
    table = moe_outs[:, model_width : model_width + all_experts]
    gate_grads = jnp.sum(
        jnp.where(flat(routes)[:, :, None] == expert_range[None, None, :], table[:, None, :], 0.0),
        axis=2,
    )
    grad_normed_one = mm("ri,di->rd", grad_query, query_full) + mm("ri,di->rd", grad_kv, kv_full)
    grad_from_one, gain_one_sum = norm_back(grad_normed_one, inputs, inv_one, gain_one)
    token_grads = (grad_residual + grad_from_one).astype(BF16)
    column = lax.broadcasted_iota(jnp.int32, (1, 2 * kv_width + 128), 1)
    query_sum = mm("rd,rf->df", normed_one, grad_query)
    kv_sum = mm("rd,rf->df", normed_one, jnp.pad(grad_kv, ((0, 0), (0, 128))))
    kv_sum = jnp.where(column == 2 * kv_width, gain_one_sum[:, None], kv_sum)
    kv_sum = jnp.where(column == 2 * kv_width + 1, gain_two_sum[:, None], kv_sum)
    if linked:
        query_sum, kv_sum = reduce_dense(query_sum, kv_sum)
    else:
        query_sum, kv_sum = summed(query_sum), summed(kv_sum)

    return (
        outputs.reshape(tokens.shape),
        token_grads.reshape(tokens.shape),
        gate_grads.reshape(routes.shape),
        kv_sum[:, 2 * kv_width],
        query_sum,
        kv_sum[:, :kv_width],
        kv_sum[:, kv_width : 2 * kv_width],
        output_sum,
        kv_sum[:, 2 * kv_width + 1],
        shared_up_sum[:, :shared_width],
        shared_up_sum[:, shared_width:],
        shared_down_sum,
        wide_grad[:, :, :expert_width],
        wide_grad[:, :, expert_width:],
        down_grad,
    )


def solution(mesh):
    rows = P(("seq", "exp"), None)
    wide = P("exp", "seq", None)
    flat = P(("seq", "exp"))
    return jax.shard_map(
        on_device,
        mesh=mesh,
        in_specs=(wide, P("exp", None), wide, wide, flat, rows, rows, rows, rows, flat, rows, rows, rows)
        + (wide,) * 4,
        out_specs=(wide, wide, wide, flat, rows, rows, rows, rows, flat, rows, rows, rows)
        + (wide,) * 3,
        check_vma=False,
    )
```

```python
import functools

import jax
import jax.numpy as jnp
from jax import lax
from jax.experimental import pallas as pl
from jax.experimental.pallas import tpu as pltpu
from jax.sharding import PartitionSpec as P

HEADS = 12
KV_HEADS = 4
HEAD_DIM = 128
GROUP_HEADS = HEADS // KV_HEADS
EPSILON = 1e-05
NEGATIVE = -1e30
F32 = jnp.float32
BF16 = jnp.bfloat16


def mm(spec, left, right):
    return jnp.einsum(spec, left, right, preferred_element_type=F32)


def exchange(value, axis, bit):
    size = lax.axis_size(axis)
    return lax.ppermute(value, axis, [(i, i ^ bit) for i in range(size)])


def rotate(value, axis, step):
    size = lax.axis_size(axis)
    return lax.ppermute(value, axis, [(i, (i + step) % size) for i in range(size)])


def after(value, *others):
    return lax.optimization_barrier((value, others))[0]


def in_order(flag, own, other, axis):
    return jnp.where(
        flag == 0,
        jnp.concatenate([own, other], axis),
        jnp.concatenate([other, own], axis),
    )


def silu_parts(pre_act):
    sigma_val = jax.nn.sigmoid(pre_act)
    return (pre_act * sigma_val, sigma_val * (1.0 + pre_act * (1.0 - sigma_val)))


def norm_back(grad_normed, values, inv_rms, gain):
    scaled = grad_normed * gain
    inner = jnp.mean(scaled * values, axis=1, keepdims=True)
    grad_values = inv_rms * scaled - values * (inv_rms * inv_rms * inv_rms) * inner
    return grad_values, jnp.sum(grad_normed * values * inv_rms, axis=0)


def group_gather(value):
    over_y = jnp.stack([value, exchange(value, "exp", 1)])
    over_z = jnp.concatenate([over_y, exchange(over_y, "exp", 2)])
    other = exchange(over_z, "seq", 1)
    return over_z, other


def group_scatter(own, other):
    part = own.astype(F32) + exchange(other, "seq", 1).astype(F32)
    part = part[:2] + exchange(part[2:].astype(BF16), "exp", 2).astype(F32)
    return part[0] + exchange(part[1].astype(BF16), "exp", 1).astype(F32)


def dot(left, right, over):
    return lax.dot_general(left, right, ((over[:1], over[1:]), ((), ())), preferred_element_type=F32)


def masked_softmax(query, keys, allowed, scale):
    scores = jnp.where(allowed, dot(query, keys, (1, 1)) * scale, NEGATIVE)
    expo = jnp.where(allowed, jnp.exp(scores - jnp.max(scores, axis=1, keepdims=True)), 0.0)
    total = jnp.sum(expo, axis=1, keepdims=True)
    return expo * (1.0 / jnp.where(total > 0.5, total, 1.0))


def attention_back_kernel(
    scale, mask_ref, query_ref, key_ref, value_ref, grad_ref, grad_query_ref, grad_key_ref, grad_value_ref
):
    keys = key_ref[...].reshape(-1, HEAD_DIM)
    values = value_ref[...].reshape(-1, HEAD_DIM)
    allowed = mask_ref[...] > 0
    grad_keys = grad_values = 0.0
    for g in range(GROUP_HEADS):
        lanes = slice(g * HEAD_DIM, (g + 1) * HEAD_DIM)
        query, grad = query_ref[:, lanes], grad_ref[:, lanes]
        weights = masked_softmax(query, keys, allowed, scale)
        grad_weights = dot(grad, values, (1, 1))
        delta = jnp.sum(weights * grad_weights, axis=1, keepdims=True)
        grad_scores = (weights * (grad_weights - delta)).astype(BF16)
        grad_query_ref[:, lanes] = (dot(grad_scores, keys, (1, 0)) * scale).astype(BF16)
        grad_keys = grad_keys + dot(query, grad_scores, (0, 0))
        grad_values = grad_values + dot(grad, weights.astype(BF16), (0, 0))
    grad_key_ref[...] = (grad_keys * scale).T.astype(BF16).reshape(grad_key_ref.shape)
    grad_value_ref[...] = grad_values.T.astype(BF16).reshape(grad_value_ref.shape)


MESH = pl.DeviceIdType.MESH
CORE, HALF = ("seq", 1), ("seq", 2)
SIDE, NEAR, FAR = ("exp", 1), ("exp", 2), ("exp", 4)


def bit_of(partner):
    axis, bit = partner
    return lax.axis_index(axis) // bit % 2


def device_of(partner):
    axis, bit = partner
    return {axis: lax.axis_index(axis) + bit - 2 * bit * bit_of(partner)}


def meet(partners):
    barrier = pltpu.get_barrier_semaphore()
    for partner in partners:
        pl.semaphore_signal(barrier, inc=1, device_id=device_of(partner), device_id_type=MESH)
    pl.semaphore_wait(barrier, len(partners))


class Sender:
    def __init__(self, send_sems, recv_sems):
        self.send_sems, self.recv_sems = send_sems, recv_sems
        self.copies, self.landed = [], set()

    def start(self, src, dst, partner):
        i = len(self.copies)
        copy = pltpu.make_async_remote_copy(
            src_ref=src,
            dst_ref=dst,
            send_sem=self.send_sems.at[i],
            recv_sem=self.recv_sems.at[i],
            device_id=device_of(partner),
            device_id_type=MESH,
        )
        copy.start()
        self.copies.append(copy)
        return i

    def arrived(self, *numbers):
        for i in numbers:
            if i not in self.landed:
                self.copies[i].wait_recv()
                self.landed.add(i)

    def finish(self):
        for i, copy in enumerate(self.copies):
            copy.wait_send()
            self.arrived(i)


def semaphores(count):
    return [pltpu.SemaphoreType.DMA((count,)), pltpu.SemaphoreType.DMA((count,))]


ANYWHERE = pl.BlockSpec(memory_space=pl.ANY)
VMEM = pl.BlockSpec(memory_space=pltpu.VMEM)
AXES = (HALF, CORE, FAR, NEAR, SIDE)


def doubling(sender, out, order, columns=None):
    held = []
    for partner in order:
        at = tuple(slice(None) if a in held else bit_of(a) for a in AXES)
        view = out.at[at] if columns is None else out.at[(*at, slice(None), columns)]
        number = sender.start(view, view, partner)
        yield
        sender.arrived(number)
        held.append(partner)


def in_turn(steps):
    steps = list(steps)
    while steps:
        steps = [s for s in steps if next(s, s) is not s]


def gather_kernel(
    query_ref, kv_ref, gain_ref, gate_ref, up_ref, down_ref, cot_ref,
    query_out, kv_out, gain_out, gate_out, up_out, down_out, far_out, side_out, near_out,
    send, recv, local,
):
    core, half = bit_of(CORE), bit_of(HALF)
    own = tuple(bit_of(a) for a in AXES)
    pairs = ((query_ref, query_out), (kv_ref, kv_out), (gain_ref, gain_out))
    experts = ((gate_ref, gate_out.at[half]), (up_ref, up_out.at[half]), (down_ref, down_out))
    moves = [(r, o.at[own]) for r, o in pairs] + [(r.at[core], o.at[core]) for r, o in experts]
    copies = [pltpu.make_async_copy(r, o, local.at[i]) for i, (r, o) in enumerate(moves)]
    for copy in copies:
        copy.start()
    meet(AXES)
    sender = Sender(send, recv)
    swaps = [sender.start(r.at[1 - core], o.at[core], CORE) for r, o in experts]
    for copy in copies:
        copy.wait()
    one, two = (NEAR, FAR, HALF, SIDE, CORE), (SIDE, NEAR, FAR, HALF, CORE)
    cut = query_ref.shape[1] // 2
    kv_cut = kv_ref.shape[1] // 2

    def near_experts():
        sender.arrived(*swaps)
        sender.start(gate_out.at[half], gate_out.at[half], HALF)
        for _ in range(3):
            yield
        sender.start(up_out.at[half], up_out.at[half], HALF)

    def far_expert():
        yield
        sender.start(gate_out.at[half], far_out, FAR)
        sender.start(cot_ref.at[0], side_out, SIDE)
        sender.start(cot_ref.at[1], near_out, NEAR)

    in_turn(
        [
            doubling(sender, gain_out, two),
            doubling(sender, query_out, one, pl.ds(0, cut)),
            doubling(sender, kv_out, two, pl.ds(0, kv_cut)),
            doubling(sender, query_out, one, pl.ds(cut, cut)),
            doubling(sender, kv_out, two, pl.ds(kv_cut, kv_cut)),
            near_experts(),
            far_expert(),
        ]
    )
    sender.finish()


def gather_first(query_proj, kv_proj, gains, expert_gate, expert_up, expert_down, cot):
    shape = jax.ShapeDtypeStruct
    shards = (query_proj, kv_proj, gains)
    experts = (expert_gate, expert_up, expert_down)
    return pl.pallas_call(
        gather_kernel,
        in_specs=[VMEM] * 7,
        out_specs=[ANYWHERE] * 9,
        out_shape=[
            *[shape((2,) * 5 + w.shape, w.dtype) for w in shards],
            *[shape((2, 2) + w.shape[1:], BF16) for w in experts[:2]],
            shape((2,) + expert_down.shape[1:], BF16),
            shape((2,) + expert_gate.shape[1:], BF16),
            shape(cot.shape[1:], BF16),
            shape(cot.shape[1:], BF16),
        ],
        scratch_shapes=[*semaphores(34), pltpu.SemaphoreType.DMA((6,))],
        compiler_params=pltpu.CompilerParams(
            collective_id=0, has_side_effects=True, vmem_limit_bytes=32 << 20
        ),
        name="gather_first",
    )(*shards, *experts, cot)


def attention_heads(scale, rows, mask_ref, query_ref, kv_ref, context_ref):
    allowed = mask_ref[rows, :] > 0
    blocks = [kv_ref.at[j, rows, :] for j in range(4)]

    def head(h, _):
        at = pl.ds(pl.multiple_of(h * HEAD_DIM, HEAD_DIM), HEAD_DIM)
        value_at = pl.ds(pl.multiple_of((h + KV_HEADS) * HEAD_DIM, HEAD_DIM), HEAD_DIM)
        keys = jnp.concatenate([b[:, at] for b in blocks])
        values = jnp.concatenate([b[:, value_at] for b in blocks])
        for g in range(GROUP_HEADS):
            lanes = pl.ds(pl.multiple_of((h * GROUP_HEADS + g) * HEAD_DIM, HEAD_DIM), HEAD_DIM)
            weights = masked_softmax(query_ref[rows, lanes], keys, allowed, scale)
            context_ref[rows, lanes] = dot(weights.astype(BF16), values, (1, 0)).astype(BF16)
        return 0

    lax.fori_loop(0, KV_HEADS, head, 0)


def attend_kernel(
    normed_ref, query_proj_ref, kv_proj_ref, mask_ref, up_ref, down_ref, far_ref, cot_ref, side_ref, near_ref, table_ref,
    query_ref, kv_ref, context_ref, gate_out, up_out, down_out, near_out, cot_out, table_out,
    up_half, down_half, send, recv, local,
):
    half = bit_of(HALF)
    moves = (
        (far_ref, gate_out.at[half]),
        (down_ref, near_out.at[half]),
        (cot_ref, cot_out.at[0, 0, 0]),
        (side_ref, cot_out.at[0, 0, 1, 0]),
        (near_ref, cot_out.at[0, 1, 0, 1]),
        (table_ref, table_out.at[0, 0, 0]),
    )
    copies = [pltpu.make_async_copy(r, o, local.at[i]) for i, (r, o) in enumerate(moves)]
    for copy in copies:
        copy.start()
    meet(AXES)
    sender = Sender(send, recv)
    far_up = sender.start(up_ref.at[half], up_half, FAR)
    table_side = sender.start(table_ref, table_out.at[0, 0, 1], SIDE)
    cots = [
        sender.start(cot_ref.at[0], cot_out.at[0, 1, 0, 0], NEAR),
        sender.start(side_ref, cot_out.at[0, 1, 1, 0], NEAR),
        sender.start(cot_ref.at[1], cot_out.at[0, 0, 1, 1], SIDE),
        sender.start(near_ref, cot_out.at[0, 1, 1, 1], SIDE),
    ]
    kv_ref[0] = dot(normed_ref[...], kv_proj_ref[...], (1, 0)).astype(BF16)
    kv_half = sender.start(kv_ref.at[0], kv_ref.at[2], HALF)
    kv_core = sender.start(kv_ref.at[0], kv_ref.at[1], CORE)
    query_ref[...] = dot(normed_ref[...], query_proj_ref[...], (1, 0)).astype(BF16)
    for copy in copies:
        copy.wait()
    sender.arrived(table_side)
    table_near = sender.start(table_out.at[0, 0], table_out.at[0, 1], NEAR)
    sender.arrived(kv_half)
    kv_both = sender.start(kv_ref.at[2], kv_ref.at[3], CORE)
    sender.start(far_ref, gate_out.at[half], HALF)
    sender.arrived(far_up)
    far_down = sender.start(down_ref, down_half, FAR)
    sender.start(down_ref, near_out.at[half], HALF)
    sender.start(up_half, up_out.at[half], HALF)
    up_copy = pltpu.make_async_copy(up_half, up_out.at[half], local.at[6])
    up_copy.start()
    sender.arrived(table_near)
    sender.start(table_out.at[0], table_out.at[1], CORE)
    sender.arrived(kv_core, kv_both)
    scale = HEAD_DIM ** (-0.5)
    row_count = mask_ref.shape[1] // 4
    for micro in range(normed_ref.shape[0] // row_count):
        rows = pl.ds(micro * row_count, row_count)
        attention_heads(scale, rows, mask_ref, query_ref, kv_ref, context_ref)
        if micro == 0:
            sender.arrived(*cots)
            sender.start(cot_out.at[0], cot_out.at[1], CORE)
    sender.arrived(far_down)
    sender.start(down_half, down_out.at[half], HALF)
    down_copy = pltpu.make_async_copy(down_half, down_out.at[half], local.at[7])
    down_copy.start()
    up_copy.wait()
    down_copy.wait()
    sender.finish()


def attend(normed, query_proj, kv_proj, masks, up_near, down_half, gate_far, cot, side, near, table):
    rows, width = normed.shape
    shape = jax.ShapeDtypeStruct
    gate_shape = (2,) + gate_far.shape
    return pl.pallas_call(
        attend_kernel,
        in_specs=[VMEM] * 4 + [ANYWHERE] + [VMEM] * 6,
        out_specs=[VMEM] * 3 + [ANYWHERE] * 6,
        out_shape=[
            shape((rows, query_proj.shape[1]), BF16),
            shape((4, rows, kv_proj.shape[1]), BF16),
            shape((rows, query_proj.shape[1]), BF16),
            shape(gate_shape, BF16),
            shape(up_near.shape, BF16),
            *[shape((2,) + down_half.shape, BF16)] * 2,
            shape((2, 2, 2) + cot.shape, cot.dtype),
            shape((2, 2, 2) + table.shape, table.dtype),
        ],
        scratch_shapes=[
            pltpu.VMEM(up_near.shape[1:], BF16),
            pltpu.VMEM(down_half.shape, BF16),
            *semaphores(18),
            pltpu.SemaphoreType.DMA((8,)),
        ],
        compiler_params=pltpu.CompilerParams(
            collective_id=1, has_side_effects=True, vmem_limit_bytes=60 << 20
        ),
        name="attend",
    )(normed, query_proj, kv_proj, masks, up_near, down_half, gate_far, cot, side, near, table)


def spread_kernel(value_ref, out, send, recv, local):
    copy = pltpu.make_async_copy(value_ref, out.at[0, 0, 0], local.at[0])
    copy.start()
    meet((CORE, SIDE, NEAR))
    sender = Sender(send, recv)
    firsts = (
        (sender.start(value_ref.at[0], out.at[0, 0, 1, 0], SIDE), (0, 0, 1, 0), NEAR, (0, 1, 1, 0)),
        (sender.start(value_ref.at[1], out.at[0, 1, 0, 1], NEAR), (0, 1, 0, 1), SIDE, (0, 1, 1, 1)),
    )
    seconds = [
        (sender.start(value_ref.at[0], out.at[0, 1, 0, 0], NEAR), (0, 1, 0, 0)),
        (sender.start(value_ref.at[1], out.at[0, 0, 1, 1], SIDE), (0, 0, 1, 1)),
    ]
    sender.start(value_ref, out.at[1, 0, 0], CORE)
    for number, at, partner, to in firsts:
        sender.arrived(number)
        seconds.append((sender.start(out.at[at], out.at[to], partner), to))
        sender.start(out.at[at], out.at[(1, *at[1:])], CORE)
    for number, at in seconds:
        sender.arrived(number)
        sender.start(out.at[at], out.at[(1, *at[1:])], CORE)
    copy.wait()
    sender.finish()


def spread(value):
    out = pl.pallas_call(
        spread_kernel,
        in_specs=[VMEM],
        out_specs=ANYWHERE,
        out_shape=jax.ShapeDtypeStruct((2, 2, 2) + value.shape, value.dtype),
        scratch_shapes=[*semaphores(13), pltpu.SemaphoreType.DMA((1,))],
        compiler_params=pltpu.CompilerParams(collective_id=2, has_side_effects=True),
        name="spread",
    )(value)
    return out.reshape((8,) + value.shape)


def collecting(sender, parts, core_recv, axis_recv, done):
    orders = ((parts[0], (NEAR, SIDE), (2, 3, 1, 0)), (parts[1], (SIDE, NEAR), (1, 3, 2, 0)))
    numbers, landing = {}, {}
    for place in range(4):
        for m, (ref, _, order) in enumerate(orders):
            b = order[place]
            numbers[m, b] = sender.start(ref.at[4 + b], core_recv.at[m, b], CORE)
    yield
    for place in range(2):
        for m, (ref, axes, order) in enumerate(orders):
            b = order[place]
            sender.arrived(numbers[m, b])
            core_recv[m, b] = (ref[b].astype(F32) + core_recv[m, b].astype(F32)).astype(BF16)
            landing[m, place] = sender.start(core_recv.at[m, b], axis_recv.at[m, place], axes[0])
    yield
    for m, (ref, axes, order) in enumerate(orders):
        b = order[2]
        sender.arrived(numbers[m, b], landing[m, 1])
        total = ref[b].astype(F32) + core_recv[m, b].astype(F32) + axis_recv[m, 1].astype(F32)
        core_recv[m, b] = total.astype(BF16)
        landing[m, 2] = sender.start(core_recv.at[m, b], axis_recv.at[m, 2], axes[1])
    yield
    for m, (ref, _, order) in enumerate(orders):
        sender.arrived(numbers[m, 0], landing[m, 0], landing[m, 2])
        total = ref[0].astype(F32) + core_recv[m, 0].astype(F32)
        done(m, total + axis_recv[m, 0].astype(F32) + axis_recv[m, 2].astype(F32))


def collecting_spaces(block):
    return [pltpu.VMEM((2, 4, *block), BF16), pltpu.VMEM((2, 3, *block), BF16)]


def collect_kernel(
    first_ref, second_ref, normed_ref, cot_ref, wide_ref, down_ref,
    grad_ref, hidden_ref, pre_ref, out_ref, core_recv, axis_recv, send, recv,
):
    meet((CORE, SIDE, NEAR))
    sender = Sender(send, recv)
    width = down_ref.shape[0]
    row_count = first_ref.shape[1]

    def done(m, total):
        rows = pl.ds(m * row_count, row_count)
        grad_ref[rows, :] = grad_ref[rows, :] + total

    parts = collecting(sender, (first_ref, second_ref), core_recv, axis_recv, done)
    next(parts)
    pre_gate = dot(normed_ref[...], wide_ref[:, :width], (1, 0))
    pre_up = dot(normed_ref[...], wide_ref[:, width:], (1, 0))
    next(parts)
    act, deriv = silu_parts(pre_gate)
    hidden_ref[...] = (act * pre_up).astype(BF16)
    grad_hidden = dot(cot_ref[...], down_ref[...], (1, 1))
    pre_ref[:, :width] = (grad_hidden * pre_up * deriv).astype(BF16)
    pre_ref[:, width:] = (grad_hidden * act).astype(BF16)
    out_ref[...] = dot(hidden_ref[...], down_ref[...], (1, 0)).astype(out_ref.dtype)
    grad_ref[...] = dot(pre_ref[...], wide_ref[...], (1, 1))
    for _ in parts:
        pass
    sender.finish()


def collect(first, second, normed, cot, wide, down):
    block = first.shape[1:]
    rows, model_width = normed.shape
    shape = jax.ShapeDtypeStruct
    return pl.pallas_call(
        collect_kernel,
        in_specs=[VMEM] * 6,
        out_specs=[VMEM] * 4,
        out_shape=[
            shape((rows, model_width), F32),
            shape((rows, down.shape[0]), BF16),
            shape((rows, wide.shape[1]), BF16),
            shape((rows, model_width), F32),
        ],
        scratch_shapes=[*collecting_spaces(block), *semaphores(14)],
        compiler_params=pltpu.CompilerParams(
            collective_id=3, has_side_effects=True, vmem_limit_bytes=63 << 20
        ),
        name="collect",
    )(first, second, normed, cot, wide, down)


def back_kernel(
    mask_ref, query_ref, kv_ref, grad_ref, near_wide, near_down, far_wide, far_down,
    grad_query_ref, grad_kv_ref, wide_out, down_out,
    part_ref, kv_core, kv_send, kv_half, far_wide_recv, far_down_recv, near_wide_recv, near_down_recv,
    wide_send, down_send, wide_recv, down_recv, wide_core, down_core, wide_own, down_own, send, recv,
):
    core, half = bit_of(CORE), bit_of(HALF)
    scale = HEAD_DIM ** (-0.5)
    row_count = mask_ref.shape[1] // 4

    def heads(micro):
        rows = pl.ds(micro * row_count, row_count)
        allowed = mask_ref[rows, :] > 0

        def head(h, _):
            at = pl.ds(pl.multiple_of(h * HEAD_DIM, HEAD_DIM), HEAD_DIM)
            value_at = pl.ds(pl.multiple_of((h + KV_HEADS) * HEAD_DIM, HEAD_DIM), HEAD_DIM)
            keys = jnp.concatenate([kv_ref[j, rows, at] for j in range(4)])
            values = jnp.concatenate([kv_ref[j, rows, value_at] for j in range(4)])
            grad_keys = grad_values = 0.0
            for g in range(GROUP_HEADS):
                lanes = pl.ds(pl.multiple_of((h * GROUP_HEADS + g) * HEAD_DIM, HEAD_DIM), HEAD_DIM)
                query, grad = query_ref[rows, lanes], grad_ref[rows, lanes]
                weights = masked_softmax(query, keys, allowed, scale)
                grad_weights = dot(grad, values, (1, 1))
                delta = jnp.sum(weights * grad_weights, axis=1, keepdims=True)
                grad_scores = (weights * (grad_weights - delta)).astype(BF16)
                grad_query_ref[rows, lanes] = (dot(grad_scores, keys, (1, 0)) * scale).astype(BF16)
                grad_keys = grad_keys + dot(query, grad_scores, (0, 0))
                grad_values = grad_values + dot(grad, weights.astype(BF16), (0, 0))
            grad_keys = (grad_keys * scale).T.astype(BF16)
            grad_values = grad_values.T.astype(BF16)
            for j in range(4):
                part_ref[j, rows, at] = grad_keys[j * row_count : (j + 1) * row_count]
                part_ref[j, rows, value_at] = grad_values[j * row_count : (j + 1) * row_count]
            return 0

        lax.fori_loop(0, KV_HEADS, head, 0)

    def add(*values):
        total = values[0][...].astype(F32)
        for value in values[1:]:
            total = total + value[...].astype(F32)
        return total

    meet((CORE, HALF, FAR))
    sender = Sender(send, recv)
    other = 1 - half
    across = [sender.start(far_wide.at[other, 0], far_wide_recv.at[0], HALF)]
    heads(0)
    across.append(sender.start(far_wide.at[other, 1], far_wide_recv.at[1], HALF))
    fars = []
    for q in range(2):
        if q:
            heads(1)
            kv_sums = [sender.start(part_ref.at[2 * j + 1], kv_core.at[j], CORE) for j in range(2)]
        sender.arrived(across[q])
        wide_send[q] = add(far_wide[half, q], far_wide_recv[q]).astype(BF16)
        fars.append(sender.start(wide_send.at[q], wide_recv.at[q], FAR))
    far_last = sender.start(far_down.at[other], far_down_recv, HALF)
    sender.arrived(*kv_sums)
    kv_send[...] = add(part_ref[2], kv_core[1]).astype(BF16)
    kv_last = sender.start(kv_send, kv_half, HALF)
    near = [sender.start(near_wide.at[other], near_wide_recv, HALF)]
    sender.arrived(far_last)
    down_send[...] = add(far_down[half], far_down_recv).astype(BF16)
    fars.append(sender.start(down_send, down_recv, FAR))
    near.append(sender.start(near_down.at[other], near_down_recv, HALF))
    sender.arrived(kv_last)
    grad_kv_ref[...] = add(part_ref[0], kv_core[0], kv_half[...]).astype(BF16)
    sender.arrived(*near, *fars[:2])

    def finish(near_ref, near_recv, far_recv, own_ref, core_ref, out_ref):
        own_ref[...] = add(near_ref[half, 1 - core], near_recv[1 - core], far_recv[1 - core]).astype(BF16)
        number = sender.start(own_ref, core_ref, CORE)
        out_ref[core] = add(near_ref[half, core], near_recv[core], far_recv[core])
        return number

    wide_last = finish(near_wide, near_wide_recv, wide_recv, wide_own, wide_core, wide_out)
    sender.arrived(wide_last)
    wide_out[1 - core] = wide_core[...].astype(F32)
    sender.arrived(*fars)
    down_last = finish(near_down, near_down_recv, down_recv, down_own, down_core, down_out)
    sender.arrived(down_last)
    down_out[1 - core] = down_core[...].astype(F32)
    sender.finish()


def back(masks, queries, kv, grad, near_wide, near_down, far_wide, far_down):
    shape = jax.ShapeDtypeStruct
    rows, width = kv.shape[1:]
    wide, down = near_wide.shape[1:], near_down.shape[1:]
    space = lambda *dims: pltpu.VMEM(dims, BF16)
    return pl.pallas_call(
        back_kernel,
        in_specs=[VMEM] * 8,
        out_specs=[VMEM] * 4,
        out_shape=[
            shape(queries.shape, BF16),
            shape((rows, width), BF16),
            shape((2,) + wide[1:], F32),
            shape((2,) + down[1:], F32),
        ],
        scratch_shapes=[
            space(4, rows, width),
            space(2, rows, width),
            space(rows, width),
            space(rows, width),
            *[space(*wide), space(*down)] * 4,
            *[space(*wide[1:]), space(*down[1:])] * 2,
            *semaphores(14),
        ],
        compiler_params=pltpu.CompilerParams(
            collective_id=5, has_side_effects=True, vmem_limit_bytes=62 << 20
        ),
        name="back",
    )(masks, queries, kv, grad, near_wide, near_down, far_wide, far_down)


def halving(sender, value, spaces, order, out, columns):
    left = list(AXES)
    for partner, (landing, total_ref) in zip(order, spaces):
        place = left.index(partner)
        left.pop(place)
        rest = (slice(None),) * (len(left) - place + 1)
        at = lambda bit: (*(slice(None),) * place, bit, *rest, columns)
        into = (*(slice(None),) * (len(left) + 1), columns)
        own = bit_of(partner)
        number = sender.start(value.at[at(1 - own)], landing.at[into], partner)
        yield
        sender.arrived(number)
        total = value[at(own)].astype(F32) + landing[into].astype(F32)
        if left:
            total_ref[into] = total.astype(BF16)
            value = total_ref
        else:
            out[into] = total


def reduce_kernel(first_ref, second_ref, part_ref, other_part, first_out, second_out, part_out, *refs):
    core_recv, axis_recv, send, recv = refs[-4:]
    spaces = list(zip(refs[:-4:2], refs[1:-4:2]))

    def done(m, total):
        part_out[m] = total

    first, second = spaces[:5], spaces[5:]
    meet(AXES)
    sender = Sender(send, recv)
    one, two = (CORE, SIDE, HALF, FAR, NEAR), (CORE, HALF, FAR, NEAR, SIDE)
    cut = first_ref.shape[-1] // 2
    other_cut = second_ref.shape[-1] // 256 * 128
    in_turn(
        [
            halving(sender, first_ref, first, one, first_out, pl.ds(0, cut)),
            halving(sender, second_ref, second, two, second_out, pl.ds(0, other_cut)),
            halving(sender, first_ref, first, one, first_out, pl.ds(cut, cut)),
            halving(
                sender, second_ref, second, two, second_out,
                pl.ds(other_cut, second_ref.shape[-1] - other_cut),
            ),
            collecting(sender, (part_ref, other_part), core_recv, axis_recv, done),
        ]
    )
    sender.finish()


def reduce_dense(first, second, parts):
    values, scratch = [], []
    for value in (first, second):
        rows = value.shape[0] // 32
        values.append(value.reshape((2,) * 5 + (rows, -1)).astype(BF16))
        for left in range(4, -1, -1):
            dims = (2,) * left + values[-1].shape[5:]
            scratch += [pltpu.VMEM(dims, BF16), pltpu.VMEM(dims if left else (8, 128), BF16)]
    return pl.pallas_call(
        reduce_kernel,
        in_specs=[VMEM] * 4,
        out_specs=[VMEM] * 3,
        out_shape=[
            *[jax.ShapeDtypeStruct(v.shape[5:], F32) for v in values],
            jax.ShapeDtypeStruct((2, *parts[0].shape[1:]), F32),
        ],
        scratch_shapes=[*scratch, *collecting_spaces(parts[0].shape[1:]), *semaphores(34)],
        compiler_params=pltpu.CompilerParams(
            collective_id=6, has_side_effects=True, vmem_limit_bytes=63 << 20
        ),
        name="reduce_dense",
    )(*values, *parts)


def attention_back(micro, masks, queries, kv, grad):
    row_count = grad.shape[0]
    wide = GROUP_HEADS * HEAD_DIM
    heads = lambda at: pl.BlockSpec((4, row_count, HEAD_DIM), lambda h: (0, micro, h + at))
    column = pl.BlockSpec((4, row_count, HEAD_DIM), lambda h: (0, 0, h))
    flat = jax.ShapeDtypeStruct((4, row_count, KV_HEADS * HEAD_DIM), BF16)
    return pl.pallas_call(
        functools.partial(attention_back_kernel, HEAD_DIM ** (-0.5)),
        grid=(KV_HEADS,),
        in_specs=[
            pl.BlockSpec((row_count, 4 * row_count), lambda h: (micro, 0)),
            pl.BlockSpec((row_count, wide), lambda h: (micro, h)),
            heads(0),
            heads(KV_HEADS),
            pl.BlockSpec((row_count, wide), lambda h: (0, h)),
        ],
        out_specs=[pl.BlockSpec((row_count, wide), lambda h: (0, h)), column, column],
        out_shape=[jax.ShapeDtypeStruct((row_count, HEADS * HEAD_DIM), BF16), flat, flat],
        compiler_params=pltpu.CompilerParams(vmem_limit_bytes=48 << 20),
        name="attention_back",
    )(masks, queries, kv, kv, grad)


def expert_kernel(
    slot_ref, scale_ref, column_ref, token_ref, cot_ref, *refs
):
    count = column_ref.shape[0]
    gate_refs, up_refs, down_refs = refs[:count], refs[count : 2 * count], refs[2 * count : 3 * count]
    rows_ref, cots_ref, hidden_ref, pre_ref, mixed_ref, graded_ref = refs[-10:-4]
    pick_ref, value_ref, extra_ref, back_ref = refs[-4:]
    width = down_refs[0].shape[0]
    blocks, row_count = token_ref.shape[0], token_ref.shape[2]
    room = rows_ref.shape[2] // blocks
    slot = lax.broadcasted_iota(jnp.int32, (room, row_count), 0)
    gates = []
    for b in range(blocks):
        for k in range(count):
            picked = slot == slot_ref[k, b]
            gates.append(jnp.sum(jnp.where(picked, scale_ref[k, b], 0.0), axis=1, keepdims=True))
            pick_ref[b, k * room : (k + 1) * room, :] = jnp.where(picked, 1.0, 0.0).astype(BF16)
        rows = dot(pick_ref[b], token_ref[b, 0], (1, 0)).astype(BF16)
        cots = dot(pick_ref[b], cot_ref[b, 0], (1, 0)).astype(BF16)
        for k in range(count):
            part = slice(b * room, (b + 1) * room)
            rows_ref[k, 0, part, :] = rows[k * room : (k + 1) * room]
            cots_ref[k, 0, part, :] = cots[k * room : (k + 1) * room]
    for k in range(count):
        gate = jnp.concatenate([gates[b * count + k] for b in range(blocks)])
        pre_gate = dot(rows_ref[k, 0], gate_refs[k][...], (1, 0))
        pre_up = dot(rows_ref[k, 0], up_refs[k][...], (1, 0))
        grad_hidden = dot(cots_ref[k, 0], down_refs[k][...], (1, 1))
        act, deriv = silu_parts(pre_gate)
        hidden = act * pre_up
        gate_grad = jnp.sum(hidden * grad_hidden, axis=1, keepdims=True)
        grad_hidden = grad_hidden * gate
        hidden_ref[k, 0] = (hidden * gate).astype(BF16)
        pre_ref[k, 0, :, :width] = (grad_hidden * pre_up * deriv).astype(BF16)
        pre_ref[k, 0, :, width:] = (grad_hidden * act).astype(BF16)
        value = dot(hidden_ref[k, 0], down_refs[k][...], (1, 0)).astype(BF16)
        back = dot(pre_ref[k, 0, :, :width], gate_refs[k][...], (1, 1))
        back = (back + dot(pre_ref[k, 0, :, width:], up_refs[k][...], (1, 1))).astype(BF16)
        extra = (gate_grad * column_ref[k]).astype(BF16)
        for b in range(blocks):
            to, part = slice(k * room, (k + 1) * room), slice(b * room, (b + 1) * room)
            value_ref[b, to, :] = value[part]
            back_ref[b, to, :] = back[part]
            extra_ref[b, to, :] = extra[part]
    model_width = token_ref.shape[3]
    for b in range(blocks):
        graded_ref[b] = dot(pick_ref[b], back_ref[b], (0, 0)).astype(BF16)
        mixed_ref[b, :, :model_width] = dot(pick_ref[b], value_ref[b], (0, 0)).astype(BF16)
        mixed_ref[b, :, model_width:] = dot(pick_ref[b], extra_ref[b], (0, 0)).astype(BF16)


def expert_pass(micro, slots, scales, columns, tokens, cots, gates, ups, downs, room, kept):
    count, (width, model_width) = len(downs), downs[0].shape
    blocks, micro_count, row_count = tokens.shape[:3]
    step = 2
    by_block = lambda *dims: pl.BlockSpec((step, *dims), lambda b: (b,) + (0,) * len(dims))
    by_slot = pl.BlockSpec((count, step, 1, row_count), lambda b: (0, b, 0, 0))
    whole = lambda *dims: pl.BlockSpec(dims, lambda b: (0,) * len(dims), pipeline_mode=pl.Buffered(1))
    saved = lambda cols: pl.BlockSpec((count, 1, step * room, cols), lambda b: (0, micro, b, 0))
    widths = (model_width, model_width, width, 2 * width)
    shapes = [jax.ShapeDtypeStruct((count, micro_count, blocks * room, w), BF16) for w in widths]
    args = [slots, scales, columns, tokens, cots, *gates, *ups, *downs]
    in_specs = [
        by_slot,
        by_slot,
        whole(count, 1, 128),
        pl.BlockSpec((step, 1, row_count, model_width), lambda b: (b, micro, 0, 0)),
        pl.BlockSpec((step, 1, row_count, model_width), lambda b: (b, micro, 0, 0)),
        *[whole(model_width, width)] * (2 * count),
        *[whole(width, model_width)] * count,
    ]
    aliases = {}
    if kept:
        aliases = {len(args) + i: i for i in range(len(kept))}
        in_specs += [pl.BlockSpec(memory_space=pl.ANY)] * len(kept)
        args += list(kept)
    out = pl.pallas_call(
        expert_kernel,
        grid=(blocks // step,),
        in_specs=in_specs,
        out_specs=[saved(w) for w in widths]
        + [by_block(row_count, model_width + 128), by_block(row_count, model_width)],
        out_shape=shapes
        + [
            jax.ShapeDtypeStruct((blocks, row_count, model_width + 128), BF16),
            jax.ShapeDtypeStruct((blocks, row_count, model_width), BF16),
        ],
        scratch_shapes=[
            pltpu.VMEM((step, count * room, row_count), BF16),
            pltpu.VMEM((step, count * room, model_width), BF16),
            pltpu.VMEM((step, count * room, 128), BF16),
            pltpu.VMEM((step, count * room, model_width), BF16),
        ],
        input_output_aliases=aliases,
        compiler_params=pltpu.CompilerParams(vmem_limit_bytes=60 << 20),
        name="experts",
    )(*args)
    return out[:4], out[4], out[5]


def attend_plain(queries, kv, masks, micro):
    row_count = masks.shape[1] // 4
    rows = slice(micro * row_count, (micro + 1) * row_count)
    allowed = masks[rows] > 0
    wide = KV_HEADS * HEAD_DIM
    heads = queries[rows].reshape(row_count, KV_HEADS, GROUP_HEADS, HEAD_DIM)
    keys = kv[:, rows, :wide].reshape(-1, KV_HEADS, HEAD_DIM)
    values = kv[:, rows, wide:].reshape(-1, KV_HEADS, HEAD_DIM)
    scores = mm("ikgd,jkd->kgij", heads, keys) * HEAD_DIM ** (-0.5)
    row_max = jnp.max(jnp.where(allowed, scores, NEGATIVE), axis=3, keepdims=True)
    expo = jnp.where(allowed, jnp.exp(jnp.where(allowed, scores, NEGATIVE) - row_max), 0.0)
    total = jnp.sum(expo, axis=3, keepdims=True)
    weights = (expo / jnp.where(total > 0.5, total, 1.0)).astype(BF16)
    return mm("kgij,jkd->ikgd", weights, values).reshape(row_count, HEADS * HEAD_DIM).astype(BF16)


def on_device(
    tokens,
    segment_ids,
    routes,
    route_gates,
    attn_gain,
    query_proj,
    key_proj,
    value_proj,
    output_proj,
    ffn_gain,
    shared_gate,
    shared_up,
    shared_down,
    expert_gate,
    expert_up,
    expert_down,
    output_cot,
):
    micro_count, row_count, model_width = tokens.shape
    exp_count = lax.axis_size("exp")
    local_experts, gate_rows, expert_width = expert_gate.shape
    down_rows = expert_down.shape[1]
    all_experts = local_experts * exp_count
    route_count = routes.shape[2]
    capacity = 4 * row_count * route_count // (3 * all_experts)
    query_width = HEADS * HEAD_DIM
    kv_width = KV_HEADS * HEAD_DIM
    far_steps = exp_count // 4
    assert lax.axis_size("seq") == 4 and local_experts == 2

    seq_index = lax.axis_index("seq")
    exp_index = lax.axis_index("exp")
    core = seq_index % 2
    half = seq_index // 2
    everywhere = ("seq", "exp")

    linked = exp_count == 8
    expert_range = jnp.arange(all_experts, dtype=jnp.int32)
    gate_table = jnp.sum(
        jnp.where(
            jnp.swapaxes(routes, 1, 2)[:, :, None, :] == expert_range[None, None, :, None],
            jnp.swapaxes(route_gates, 1, 2)[:, :, None, :],
            0.0,
        ),
        axis=1,
    )
    order = jnp.arange(row_count, dtype=jnp.int32)
    before = (order[:, None] < order[None, :]).astype(BF16)
    slots = jnp.arange(capacity, dtype=jnp.int32)
    expert_ids = [
        local_experts * ((exp_index - 4 * k + exp_count) % exp_count) + core
        for k in range(far_steps)
    ]
    kv_proj = jnp.concatenate([key_proj, value_proj], axis=1)
    shared_wide = jnp.concatenate([shared_gate, shared_up], axis=1)

    def gathered(value):
        return lax.all_gather(value, everywhere, axis=0, tiled=True)

    def mask_of(micro):
        segments = segment_ids[micro].reshape(4, row_count)
        key_ids = jnp.concatenate(
            [lax.dynamic_index_in_dim(segments, seq_index ^ j, 0, False) for j in range(4)]
        )
        key_pos = jnp.concatenate([(seq_index ^ j) * row_count + order for j in range(4)])
        query_ids, query_pos = key_ids[:row_count], key_pos[:row_count]
        allowed = (
            (key_ids[None, :] == query_ids[:, None])
            & (key_pos[None, :] <= query_pos[:, None])
            & (query_ids[:, None] >= 0)
        )
        return allowed.astype(jnp.int32)

    inputs = tokens.reshape(micro_count * row_count, model_width).astype(F32)
    inv_one = lax.rsqrt(jnp.mean(inputs * inputs, axis=1, keepdims=True) + EPSILON)
    masks = jnp.concatenate([mask_of(micro) for micro in range(micro_count)])
    if linked:
        gains = jnp.stack([attn_gain, ffn_gain]).astype(F32)
        share = gains.shape[1]
        gains = jnp.pad(gains, ((0, 6), (0, 128 - share)))
        query_full, kv_full, gains, gate_near, up_near, down_half, gate_far, side, near = gather_first(
            query_proj, kv_proj, gains, expert_gate, expert_up, expert_down, output_cot
        )
        query_full = query_full.reshape(model_width, query_width)
        kv_full = kv_full.reshape(model_width, 2 * kv_width)
        gains = gains.reshape(-1, 8, 128)[:, :2, :share]
        gain_one, gain_two = jnp.swapaxes(gains, 0, 1).reshape(2, model_width)
        output_proj = after(output_proj, query_full)
    else:
        query_full, kv_full = gathered(query_proj), gathered(kv_proj)
        gain_one, gain_two = gathered(attn_gain).astype(F32), gathered(ffn_gain).astype(F32)
    out_proj = gathered(output_proj)
    normed_one = (inputs * inv_one * gain_one).astype(BF16)

    if linked:
        queries, kv, contexts, gate_far, up_far, down_far, down_near, cots, tables = attend(
            normed_one, query_full, kv_full, masks, up_near, down_half, gate_far, output_cot, side, near, gate_table
        )
        gate_all = [w.reshape(model_width, expert_width) for w in (gate_near, gate_far)]
        up_all = [w.reshape(model_width, expert_width) for w in (up_near, up_far)]
        down_all = [w.reshape(expert_width, model_width) for w in (down_near, down_far)]
        shared_wide, shared_down = after((shared_wide, shared_down), contexts)
        cot_blocks = cots.reshape(8, micro_count, row_count, model_width)
        gate_blocks = tables.reshape(8, micro_count, all_experts, row_count)
    else:
        queries = jnp.dot(normed_one, query_full, preferred_element_type=F32).astype(BF16)
        own = jnp.dot(normed_one, kv_full, preferred_element_type=F32).astype(BF16)
        across = exchange(own, "seq", 2)
        kv = jnp.stack([own, exchange(own, "seq", 1), across, exchange(across, "seq", 1)])
        contexts = jnp.concatenate([attend_plain(queries, kv, masks, m) for m in range(micro_count)])
        gate_blocks = jnp.concatenate(group_gather(gate_table))
        cot_blocks = jnp.concatenate(group_gather(output_cot))

        def parity(value):
            kept = lax.dynamic_index_in_dim(value, core, 0, False)
            sent = lax.dynamic_index_in_dim(value, 1 - core, 0, False)
            return in_order(core, kept, exchange(sent, "seq", 1), 0)

        wide_far = [parity(jnp.concatenate([expert_gate, expert_up], axis=2))]
        down_far = [parity(expert_down)]
        for _ in range(far_steps - 1):
            wide_far.append(rotate(wide_far[-1], "exp", 4))
            down_far.append(rotate(down_far[-1], "exp", 4))
        wide_full = [in_order(half, w, exchange(w, "seq", 2), 0) for w in wide_far]
        down_full = [in_order(half, w, exchange(w, "seq", 2), 0) for w in down_far]

    def sequence_sum(grad_keys, grad_values):
        grad = jnp.concatenate([grad_keys, grad_values], axis=2)
        part = grad[0::2].astype(F32) + exchange(grad[1::2], "seq", 1).astype(F32)
        return (part[0] + exchange(part[1].astype(BF16), "seq", 2).astype(F32)).astype(BF16)

    kept_rows = []

    def experts(micro, normed_blocks):
        gates = jnp.stack(
            [lax.dynamic_index_in_dim(gate_blocks[:, micro], e, 1, False) for e in expert_ids]
        )
        named = gates > 0.0
        rank = mm("kbs,st->kbt", named.astype(BF16), before).astype(jnp.int32)
        slot = jnp.where(named, rank, -1)
        if not linked:
            return experts_plain(gates, slot, normed_blocks[:, micro], cot_blocks[:, micro])
        columns = (
            lax.broadcasted_iota(jnp.int32, (far_steps, 1, 128), 2)
            == jnp.stack(expert_ids)[:, None, None]
        ).astype(F32)
        kept, mixed, graded = expert_pass(
            micro, slot[:, :, None], gates[:, :, None], columns,
            normed_blocks, cot_blocks, gate_all, up_all, down_all, capacity, kept_rows,
        )
        kept_rows[:] = kept
        return graded, mixed

    def experts_plain(gates, slot, normed_blocks, micro_cots):
        mixed, graded, kept = 0.0, 0.0, []
        for k in range(far_steps):
            picked = slot[k][:, None, :] == slots[None, :, None]
            pick = picked.astype(BF16)
            slot_gates = jnp.sum(jnp.where(picked, gates[k][:, None, :], 0.0), axis=2).reshape(-1, 1)
            rows = mm("bst,btd->bsd", pick, normed_blocks).astype(BF16).reshape(-1, model_width)
            cots = mm("bst,btd->bsd", pick, micro_cots).astype(BF16).reshape(-1, model_width)
            pre = jnp.dot(rows, wide_full[k], preferred_element_type=F32)
            pre_gate, pre_up = pre[:, :expert_width], pre[:, expert_width:]
            grad_hidden = mm("rd,fd->rf", cots, down_full[k])
            act, deriv = silu_parts(pre_gate)
            hidden = act * pre_up
            gate_grad = jnp.sum(hidden * grad_hidden, axis=1, keepdims=True)
            hidden = (hidden * slot_gates).astype(BF16)
            grad_hidden = grad_hidden * slot_gates
            grad_pre = jnp.concatenate(
                [(grad_hidden * pre_up * deriv).astype(BF16), (grad_hidden * act).astype(BF16)], axis=1
            )
            value = jnp.dot(hidden, down_full[k], preferred_element_type=F32).astype(BF16)
            column = (lax.broadcasted_iota(jnp.int32, (1, 128), 1) == expert_ids[k]).astype(F32)
            value = jnp.concatenate([value, (gate_grad * column).astype(BF16)], axis=1)
            grad_rows = mm("rf,df->rd", grad_pre, wide_full[k]).astype(BF16)
            blocks = pick.shape[0]
            mixed = mixed + mm("bst,bsd->btd", pick, value.reshape(blocks, capacity, -1))
            graded = graded + mm("bst,bsd->btd", pick, grad_rows.reshape(blocks, capacity, -1))
            kept.append((rows, cots, hidden, grad_pre))
        kept_rows.append(kept)
        return graded.astype(BF16), mixed.astype(BF16)

    up_proj, down_proj = gathered(shared_wide), gathered(shared_down)
    residual = inputs + jnp.dot(contexts, out_proj, preferred_element_type=F32)
    inv_two = lax.rsqrt(jnp.mean(residual * residual, axis=1, keepdims=True) + EPSILON)
    normed_two = (residual * inv_two * gain_two).astype(BF16)
    per_micro = normed_two.reshape(micro_count, row_count, model_width)
    token_blocks = spread(per_micro) if linked else jnp.concatenate(group_gather(per_micro))

    graded_parts, mixed_parts = [], []
    for micro in range(micro_count):
        graded, mixed = experts(micro, token_blocks)
        if not linked:
            graded = group_scatter(graded[:4], graded[4:])
            mixed = group_scatter(mixed[:4], mixed[4:])
            graded, mixed, token_blocks = lax.optimization_barrier((graded, mixed, token_blocks))
        graded_parts.append(graded)
        mixed_parts.append(mixed)

    upstream_low = output_cot.reshape(micro_count * row_count, model_width)
    shared_width = shared_gate.shape[1]
    if linked:
        grad_normed, shared_hidden, grad_shared_pre, shared_out = collect(
            *graded_parts, normed_two, upstream_low, up_proj, down_proj
        )
    else:
        shared_pre = jnp.dot(normed_two, up_proj, preferred_element_type=F32)
        shared_pre_gate, shared_pre_up = shared_pre[:, :shared_width], shared_pre[:, shared_width:]
        shared_act, shared_deriv = silu_parts(shared_pre_gate)
        shared_hidden = (shared_act * shared_pre_up).astype(BF16)
        shared_out = jnp.dot(shared_hidden, down_proj, preferred_element_type=F32)
        grad_shared_hidden = mm("rd,fd->rf", upstream_low, down_proj)
        grad_shared_pre = jnp.concatenate(
            [
                (grad_shared_hidden * shared_pre_up * shared_deriv).astype(BF16),
                (grad_shared_hidden * shared_act).astype(BF16),
            ],
            axis=1,
        )
        grad_from_shared = mm("rf,df->rd", grad_shared_pre, up_proj)
        grad_normed = jnp.concatenate(graded_parts) + grad_from_shared

    def summed(value):
        return lax.psum_scatter(
            value.astype(BF16), everywhere, scatter_dimension=0, tiled=True
        ).astype(F32)

    shared_up_sum = summed(mm("rd,rf->df", normed_two, grad_shared_pre))
    shared_down_sum = summed(mm("rd,rf->df", shared_hidden, upstream_low))

    def flat(value):
        return value.reshape(micro_count * row_count, -1)

    grad_from_two, gain_two_sum = norm_back(grad_normed, residual, inv_two, gain_two)
    grad_residual = upstream_low.astype(F32) + grad_from_two
    grad_branch = grad_residual.astype(BF16)
    grad_context = mm("rd,id->ri", grad_branch, out_proj).astype(BF16)
    output_sum = summed(mm("rd,rf->df", contexts, grad_branch))

    def expert_sum(left, right):
        own = None
        for k in reversed(range(far_steps)):
            lefts = jnp.concatenate([m[k][left] for m in kept_rows])
            rights = jnp.concatenate([m[k][right] for m in kept_rows])
            if own is not None:
                lefts, rights, own = lax.optimization_barrier((lefts, rights, own))
            total = mm("rd,rf->df", lefts, rights)
            rows = total.shape[0] // 2
            total = total.reshape(2, rows, -1)
            mine = lax.dynamic_index_in_dim(total, half, 0, False)
            sent = lax.dynamic_index_in_dim(total, 1 - half, 0, False).astype(BF16)
            total = mine + exchange(sent, "seq", 2).astype(F32)
            own = total if own is None else total + rotate(own.astype(BF16), "exp", -4).astype(F32)
        rows = own.shape[0] // 2
        own = own.reshape(2, rows, -1)
        kept = lax.dynamic_index_in_dim(own, core, 0, False)
        sent = lax.dynamic_index_in_dim(own, 1 - core, 0, False).astype(BF16)
        other = exchange(sent, "seq", 1).astype(F32)
        return in_order(core, kept[None], other[None], 0)

    if linked:
        products = []
        for k in range(far_steps):
            for left, right in ((0, 3), (2, 1)):
                total = mm("mrd,mrf->df", kept_rows[left][k], kept_rows[right][k]).astype(BF16)
                products.append(total.reshape(2, 2, total.shape[0] // 4, -1))
        grad_query, grad_kv, wide_grad, down_grad = back(masks, queries, kv, grad_context, *products)
    else:
        down_grad = expert_sum(2, 1)
        down_grad, kept_rows = lax.optimization_barrier((down_grad, kept_rows))
        wide_grad = expert_sum(0, 3)
        grad_queries, grad_kvs = [], []
        for micro in range(micro_count):
            rows = slice(micro * row_count, (micro + 1) * row_count)
            grad_query, grad_keys, grad_values = attention_back(
                micro, masks, queries, kv, grad_context[rows]
            )
            grad_queries.append(grad_query)
            grad_kvs.append(sequence_sum(grad_keys, grad_values))
        grad_query, grad_kv = jnp.concatenate(grad_queries), jnp.concatenate(grad_kvs)

    grad_normed_one = mm("ri,di->rd", grad_query, query_full) + mm("ri,di->rd", grad_kv, kv_full)
    grad_from_one, gain_one_sum = norm_back(grad_normed_one, inputs, inv_one, gain_one)
    token_grads = (grad_residual + grad_from_one).astype(BF16)
    column = lax.broadcasted_iota(jnp.int32, (1, 2 * kv_width + 128), 1)
    query_sum = mm("rd,rf->df", normed_one, grad_query)
    kv_sum = mm("rd,rf->df", normed_one, jnp.pad(grad_kv, ((0, 0), (0, 128))))
    kv_sum = jnp.where(column == 2 * kv_width, gain_one_sum[:, None], kv_sum)
    kv_sum = jnp.where(column == 2 * kv_width + 1, gain_two_sum[:, None], kv_sum)
    if linked:
        query_sum, kv_sum, moe_outs = reduce_dense(query_sum, kv_sum, mixed_parts)
        moe_outs = flat(moe_outs)
    else:
        query_sum, kv_sum, moe_outs = summed(query_sum), summed(kv_sum), jnp.concatenate(mixed_parts)
    outputs = (residual + shared_out + moe_outs[:, :model_width]).astype(BF16)
    table = moe_outs[:, model_width : model_width + all_experts]
    gate_grads = jnp.sum(
        jnp.where(flat(routes)[:, :, None] == expert_range[None, None, :], table[:, None, :], 0.0),
        axis=2,
    )

    return (
        outputs.reshape(tokens.shape),
        token_grads.reshape(tokens.shape),
        gate_grads.reshape(routes.shape),
        kv_sum[:, 2 * kv_width],
        query_sum,
        kv_sum[:, :kv_width],
        kv_sum[:, kv_width : 2 * kv_width],
        output_sum,
        kv_sum[:, 2 * kv_width + 1],
        shared_up_sum[:, :shared_width],
        shared_up_sum[:, shared_width:],
        shared_down_sum,
        wide_grad[:, :, :expert_width],
        wide_grad[:, :, expert_width:],
        down_grad,
    )


def solution(mesh):
    rows = P(("seq", "exp"), None)
    wide = P("exp", "seq", None)
    flat = P(("seq", "exp"))
    return jax.shard_map(
        on_device,
        mesh=mesh,
        in_specs=(wide, P("exp", None), wide, wide, flat, rows, rows, rows, rows, flat, rows, rows, rows)
        + (wide,) * 4,
        out_specs=(wide, wide, wide, flat, rows, rows, rows, rows, flat, rows, rows, rows)
        + (wide,) * 3,
        check_vma=False,
    )
```

```python
import functools

import jax
import jax.numpy as jnp
from jax import lax
from jax.experimental import pallas as pl
from jax.experimental.pallas import tpu as pltpu
from jax.sharding import PartitionSpec as P

HEADS = 12
KV_HEADS = 4
HEAD_DIM = 128
GROUP_HEADS = HEADS // KV_HEADS
EPSILON = 1e-05
NEGATIVE = -1e30
F32 = jnp.float32
BF16 = jnp.bfloat16


def mm(spec, left, right):
    return jnp.einsum(spec, left, right, preferred_element_type=F32)


def exchange(value, axis, bit):
    size = lax.axis_size(axis)
    return lax.ppermute(value, axis, [(i, i ^ bit) for i in range(size)])


def rotate(value, axis, step):
    size = lax.axis_size(axis)
    return lax.ppermute(value, axis, [(i, (i + step) % size) for i in range(size)])


def after(value, *others):
    return lax.optimization_barrier((value, others))[0]


def in_order(flag, own, other, axis):
    return jnp.where(
        flag == 0,
        jnp.concatenate([own, other], axis),
        jnp.concatenate([other, own], axis),
    )


def silu_parts(pre_act):
    sigma_val = jax.nn.sigmoid(pre_act)
    return (pre_act * sigma_val, sigma_val * (1.0 + pre_act * (1.0 - sigma_val)))


def norm_back(grad_normed, values, inv_rms, gain):
    scaled = grad_normed * gain
    inner = jnp.mean(scaled * values, axis=1, keepdims=True)
    grad_values = inv_rms * scaled - values * (inv_rms * inv_rms * inv_rms) * inner
    return grad_values, jnp.sum(grad_normed * values * inv_rms, axis=0)


def group_gather(value):
    over_y = jnp.stack([value, exchange(value, "exp", 1)])
    over_z = jnp.concatenate([over_y, exchange(over_y, "exp", 2)])
    other = exchange(over_z, "seq", 1)
    return over_z, other


def group_scatter(own, other):
    part = own.astype(F32) + exchange(other, "seq", 1).astype(F32)
    part = part[:2] + exchange(part[2:].astype(BF16), "exp", 2).astype(F32)
    return part[0] + exchange(part[1].astype(BF16), "exp", 1).astype(F32)


def dot(left, right, over):
    return lax.dot_general(left, right, ((over[:1], over[1:]), ((), ())), preferred_element_type=F32)


def masked_softmax(query, keys, allowed, scale):
    scores = jnp.where(allowed, dot(query, keys, (1, 1)) * scale, NEGATIVE)
    expo = jnp.where(allowed, jnp.exp(scores - jnp.max(scores, axis=1, keepdims=True)), 0.0)
    total = jnp.sum(expo, axis=1, keepdims=True)
    return expo * (1.0 / jnp.where(total > 0.5, total, 1.0))


def attention_back_kernel(
    scale, mask_ref, query_ref, key_ref, value_ref, grad_ref, grad_query_ref, grad_key_ref, grad_value_ref
):
    keys = key_ref[...].reshape(-1, HEAD_DIM)
    values = value_ref[...].reshape(-1, HEAD_DIM)
    allowed = mask_ref[...] > 0
    grad_keys = grad_values = 0.0
    for g in range(GROUP_HEADS):
        lanes = slice(g * HEAD_DIM, (g + 1) * HEAD_DIM)
        query, grad = query_ref[:, lanes], grad_ref[:, lanes]
        weights = masked_softmax(query, keys, allowed, scale)
        grad_weights = dot(grad, values, (1, 1))
        delta = jnp.sum(weights * grad_weights, axis=1, keepdims=True)
        grad_scores = (weights * (grad_weights - delta)).astype(BF16)
        grad_query_ref[:, lanes] = (dot(grad_scores, keys, (1, 0)) * scale).astype(BF16)
        grad_keys = grad_keys + dot(query, grad_scores, (0, 0))
        grad_values = grad_values + dot(grad, weights.astype(BF16), (0, 0))
    grad_key_ref[...] = (grad_keys * scale).T.astype(BF16).reshape(grad_key_ref.shape)
    grad_value_ref[...] = grad_values.T.astype(BF16).reshape(grad_value_ref.shape)


MESH = pl.DeviceIdType.MESH
CORE, HALF = ("seq", 1), ("seq", 2)
SIDE, NEAR, FAR = ("exp", 1), ("exp", 2), ("exp", 4)


def bit_of(partner):
    axis, bit = partner
    return lax.axis_index(axis) // bit % 2


def device_of(partner):
    axis, bit = partner
    return {axis: lax.axis_index(axis) + bit - 2 * bit * bit_of(partner)}


def meet(partners):
    barrier = pltpu.get_barrier_semaphore()
    for partner in partners:
        pl.semaphore_signal(barrier, inc=1, device_id=device_of(partner), device_id_type=MESH)
    pl.semaphore_wait(barrier, len(partners))


class Sender:
    def __init__(self, send_sems, recv_sems):
        self.send_sems, self.recv_sems = send_sems, recv_sems
        self.copies, self.landed = [], set()

    def start(self, src, dst, partner):
        i = len(self.copies)
        copy = pltpu.make_async_remote_copy(
            src_ref=src,
            dst_ref=dst,
            send_sem=self.send_sems.at[i],
            recv_sem=self.recv_sems.at[i],
            device_id=device_of(partner),
            device_id_type=MESH,
        )
        copy.start()
        self.copies.append(copy)
        return i

    def arrived(self, *numbers):
        for i in numbers:
            if i not in self.landed:
                self.copies[i].wait_recv()
                self.landed.add(i)

    def finish(self):
        for i, copy in enumerate(self.copies):
            copy.wait_send()
            self.arrived(i)


def semaphores(count):
    return [pltpu.SemaphoreType.DMA((count,)), pltpu.SemaphoreType.DMA((count,))]


ANYWHERE = pl.BlockSpec(memory_space=pl.ANY)
VMEM = pl.BlockSpec(memory_space=pltpu.VMEM)
AXES = (HALF, CORE, FAR, NEAR, SIDE)


def doubling(sender, out, order, columns=None):
    held = []
    for partner in order:
        at = tuple(slice(None) if a in held else bit_of(a) for a in AXES)
        view = out.at[at] if columns is None else out.at[(*at, slice(None), columns)]
        number = sender.start(view, view, partner)
        yield
        sender.arrived(number)
        held.append(partner)


def in_turn(steps):
    steps = list(steps)
    while steps:
        steps = [s for s in steps if next(s, s) is not s]


def attention_heads(scale, rows, mask_ref, query_ref, kv_ref, context_ref):
    allowed = mask_ref[rows, :] > 0
    blocks = [kv_ref.at[j, rows, :] for j in range(4)]

    def head(h, _):
        at = pl.ds(pl.multiple_of(h * HEAD_DIM, HEAD_DIM), HEAD_DIM)
        value_at = pl.ds(pl.multiple_of((h + KV_HEADS) * HEAD_DIM, HEAD_DIM), HEAD_DIM)
        keys = jnp.concatenate([b[:, at] for b in blocks])
        values = jnp.concatenate([b[:, value_at] for b in blocks])
        for g in range(GROUP_HEADS):
            lanes = pl.ds(pl.multiple_of((h * GROUP_HEADS + g) * HEAD_DIM, HEAD_DIM), HEAD_DIM)
            weights = masked_softmax(query_ref[rows, lanes], keys, allowed, scale)
            context_ref[rows, lanes] = dot(weights.astype(BF16), values, (1, 0)).astype(BF16)
        return 0

    lax.fori_loop(0, KV_HEADS, head, 0)


def begin_kernel(
    token_ref, query_shard, kv_shard, gain_shard, place_ref, mask_ref, gate_ref, up_ref, down_ref, cot_ref, table_ref,
    query_full, kv_full, gain_ref, normed_ref, query_ref, kv_ref, context_ref,
    gate_near, up_near, down_near, gate_far, up_far, down_far, cot_out, table_out,
    gain_land, gate_own, up_own, down_own, gate_half, up_half, down_half, send, recv, local,
):
    core, half = bit_of(CORE), bit_of(HALF)
    own = tuple(bit_of(a) for a in AXES)
    shards = ((query_shard, query_full), (kv_shard, kv_full), (gain_shard, gain_land))
    experts = ((gate_ref, gate_own), (up_ref, up_own), (down_ref, down_own))
    nears, fars = (gate_near, up_near, down_near), (gate_far, up_far, down_far)
    owns, halves = (gate_own, up_own, down_own), (gate_half, up_half, down_half)
    for shard, full in shards:
        full[own] = shard[...]
    for ref, mine in experts:
        mine[core] = ref[core]
    copies = [
        pltpu.make_async_copy(cot_ref, cot_out.at[0, 0, 0], local.at[6]),
        pltpu.make_async_copy(table_ref, table_out.at[0, 0, 0], local.at[7]),
    ]
    for copy in copies:
        copy.start()

    def keep(ref, out, i):
        copy = pltpu.make_async_copy(ref, out.at[half], local.at[i])
        copy.start()
        copies.append(copy)
        return sender.start(ref, out.at[half], HALF)

    meet(AXES)
    sender = Sender(send, recv)
    one, two = (NEAR, FAR, HALF, SIDE, CORE), (SIDE, NEAR, FAR, HALF, CORE)
    cut, kv_cut = query_shard.shape[1] // 2, kv_shard.shape[1] // 2
    gathers = [
        doubling(sender, gain_land, two),
        doubling(sender, query_full, one, pl.ds(0, cut)),
        doubling(sender, kv_full, two, pl.ds(0, kv_cut)),
        doubling(sender, query_full, one, pl.ds(cut, cut)),
        doubling(sender, kv_full, two, pl.ds(kv_cut, kv_cut)),
    ]

    def turn():
        for g in gathers:
            next(g, None)

    turn()
    swaps = [sender.start(r.at[1 - core], o.at[core], CORE) for r, o in experts]
    table_side = sender.start(table_ref, table_out.at[0, 0, 1], SIDE)
    cot_side = sender.start(cot_ref.at[0], cot_out.at[0, 0, 1, 0], SIDE)
    cot_near = sender.start(cot_ref.at[1], cot_out.at[0, 1, 0, 1], NEAR)
    values = token_ref[...].astype(F32)
    inverse = lax.rsqrt(jnp.mean(values * values, axis=1, keepdims=True) + EPSILON)
    turn()
    sender.arrived(*swaps)
    keep(gate_own, gate_near, 0)
    turn()
    turn()
    gate_sent = sender.start(gate_own, gate_half, FAR)
    turn()
    keep(up_own, up_near, 1)
    sender.arrived(table_side, cot_side, cot_near)
    for copy in copies[:2]:
        copy.wait()
    table_near = sender.start(table_out.at[0, 0], table_out.at[0, 1], NEAR)
    cots = [
        sender.start(cot_out.at[0, 0, :, 0], cot_out.at[0, 1, :, 0], NEAR),
        sender.start(cot_out.at[0, :, 0, 1], cot_out.at[0, :, 1, 1], SIDE),
    ]
    turn()
    share = query_shard.shape[0]
    gains = gain_land[...].reshape(-1, 8, gain_land.shape[-1])
    owner = lax.broadcasted_iota(jnp.int32, (gains.shape[0], place_ref.shape[1]), 0)
    lane = lax.broadcasted_iota(jnp.int32, owner.shape, 1)
    mine = (lane >= owner * share) & (lane < (owner + 1) * share)
    for i in range(2):
        rows = dot(gains[:, i, :].astype(BF16), place_ref[...], (1, 0))
        gain_ref[i : i + 1, :] = jnp.sum(jnp.where(mine, rows, 0.0), axis=0, keepdims=True)
    normed_ref[...] = (values * inverse * gain_ref[0:1, :]).astype(BF16)
    width = normed_ref.shape[1]
    kv_ref[0] = dot(normed_ref[...], kv_full[...].reshape(width, -1), (1, 0)).astype(BF16)
    kv_half = sender.start(kv_ref.at[0], kv_ref.at[2], HALF)
    kv_core = sender.start(kv_ref.at[0], kv_ref.at[1], CORE)
    query_ref[...] = dot(normed_ref[...], query_full[...].reshape(width, -1), (1, 0)).astype(BF16)
    sender.arrived(gate_sent)
    up_sent = sender.start(up_own, up_half, FAR)
    sender.arrived(kv_half)
    kv_both = sender.start(kv_ref.at[2], kv_ref.at[3], CORE)
    keep(gate_half, gate_far, 3)
    sender.arrived(table_near)
    sender.start(table_out.at[0], table_out.at[1], CORE)
    sender.arrived(kv_core, kv_both)
    scale = HEAD_DIM ** (-0.5)
    row_count = mask_ref.shape[1] // 4
    attention_heads(scale, pl.ds(0, row_count), mask_ref, query_ref, kv_ref, context_ref)
    sender.arrived(up_sent)
    down_sent = sender.start(down_own, down_half, FAR)
    keep(up_half, up_far, 4)
    keep(down_own, down_near, 2)
    attention_heads(scale, pl.ds(row_count, row_count), mask_ref, query_ref, kv_ref, context_ref)
    sender.arrived(*cots)
    sender.start(cot_out.at[0], cot_out.at[1], CORE)
    sender.arrived(down_sent)
    keep(down_half, down_far, 5)
    for copy in copies[2:]:
        copy.wait()
    sender.finish()


def begin(tokens, query_proj, kv_proj, gains, place, masks, experts, cot, table):
    shape = jax.ShapeDtypeStruct
    rows, width = tokens.shape
    shards = (query_proj, kv_proj, gains)
    halves = [(2,) + w.shape[1:] for w in experts]
    full = lambda w: (2,) * 5 + w.shape
    return pl.pallas_call(
        begin_kernel,
        in_specs=[VMEM] * 11,
        out_specs=[VMEM] * 7 + [ANYWHERE] * 8,
        out_shape=[
            shape(full(query_proj), BF16),
            shape(full(kv_proj), BF16),
            shape((8, width), F32),
            shape((rows, width), BF16),
            shape((rows, query_proj.shape[1]), BF16),
            shape((4, rows, kv_proj.shape[1]), BF16),
            shape((rows, query_proj.shape[1]), BF16),
            *[shape((2, *h), BF16) for h in halves] * 2,
            shape((2, 2, 2) + cot.shape, cot.dtype),
            shape((2, 2, 2) + table.shape, table.dtype),
        ],
        scratch_shapes=[
            pltpu.VMEM(full(gains), F32),
            *[pltpu.VMEM(h, BF16) for h in halves] * 2,
            *semaphores(52),
            pltpu.SemaphoreType.DMA((8,)),
        ],
        compiler_params=pltpu.CompilerParams(
            collective_id=0, has_side_effects=True, vmem_limit_bytes=60 << 20
        ),
        name="begin",
    )(tokens, *shards, place, masks, *experts, cot, table)


def spread_kernel(value_ref, out, send, recv, local):
    copy = pltpu.make_async_copy(value_ref, out.at[0, 0, 0], local.at[0])
    copy.start()
    meet((CORE, SIDE, NEAR))
    sender = Sender(send, recv)
    firsts = (
        (sender.start(value_ref.at[0], out.at[0, 0, 1, 0], SIDE), (0, 0, 1, 0), NEAR, (0, 1, 1, 0)),
        (sender.start(value_ref.at[1], out.at[0, 1, 0, 1], NEAR), (0, 1, 0, 1), SIDE, (0, 1, 1, 1)),
    )
    seconds = [
        (sender.start(value_ref.at[0], out.at[0, 1, 0, 0], NEAR), (0, 1, 0, 0)),
        (sender.start(value_ref.at[1], out.at[0, 0, 1, 1], SIDE), (0, 0, 1, 1)),
    ]
    sender.start(value_ref, out.at[1, 0, 0], CORE)
    for number, at, partner, to in firsts:
        sender.arrived(number)
        seconds.append((sender.start(out.at[at], out.at[to], partner), to))
        sender.start(out.at[at], out.at[(1, *at[1:])], CORE)
    for number, at in seconds:
        sender.arrived(number)
        sender.start(out.at[at], out.at[(1, *at[1:])], CORE)
    copy.wait()
    sender.finish()


def spread(value):
    out = pl.pallas_call(
        spread_kernel,
        in_specs=[VMEM],
        out_specs=ANYWHERE,
        out_shape=jax.ShapeDtypeStruct((2, 2, 2) + value.shape, value.dtype),
        scratch_shapes=[*semaphores(13), pltpu.SemaphoreType.DMA((1,))],
        compiler_params=pltpu.CompilerParams(collective_id=2, has_side_effects=True),
        name="spread",
    )(value)
    return out.reshape((8,) + value.shape)


def collecting(sender, parts, core_recv, axis_recv, done):
    orders = ((parts[0], (NEAR, SIDE), (2, 3, 1, 0)), (parts[1], (SIDE, NEAR), (1, 3, 2, 0)))
    numbers, landing = {}, {}
    for place in range(4):
        for m, (ref, _, order) in enumerate(orders):
            b = order[place]
            numbers[m, b] = sender.start(ref.at[4 + b], core_recv.at[m, b], CORE)
    yield
    for place in range(2):
        for m, (ref, axes, order) in enumerate(orders):
            b = order[place]
            sender.arrived(numbers[m, b])
            core_recv[m, b] = ref[b] + core_recv[m, b]
            landing[m, place] = sender.start(core_recv.at[m, b], axis_recv.at[m, place], axes[0])
    yield
    for m, (ref, axes, order) in enumerate(orders):
        b = order[2]
        sender.arrived(numbers[m, b], landing[m, 1])
        total = ref[b].astype(F32) + core_recv[m, b].astype(F32) + axis_recv[m, 1].astype(F32)
        core_recv[m, b] = total.astype(BF16)
        landing[m, 2] = sender.start(core_recv.at[m, b], axis_recv.at[m, 2], axes[1])
    yield
    for m, (ref, _, order) in enumerate(orders):
        sender.arrived(numbers[m, 0], landing[m, 0], landing[m, 2])
        total = ref[0].astype(F32) + core_recv[m, 0].astype(F32)
        done(m, total + axis_recv[m, 0].astype(F32) + axis_recv[m, 2].astype(F32))


def collecting_spaces(block):
    return [pltpu.VMEM((2, 4, *block), BF16), pltpu.VMEM((2, 3, *block), BF16)]


def collect_kernel(
    first_ref, second_ref, normed_ref, cot_ref, wide_ref, down_ref,
    grad_ref, hidden_ref, pre_ref, out_ref, core_recv, axis_recv, send, recv,
):
    meet((CORE, SIDE, NEAR))
    sender = Sender(send, recv)
    width = down_ref.shape[0]
    row_count = first_ref.shape[1]

    def done(m, total):
        rows = pl.ds(m * row_count, row_count)
        grad_ref[rows, :] = grad_ref[rows, :] + total

    parts = collecting(sender, (first_ref, second_ref), core_recv, axis_recv, done)
    next(parts)
    pre_gate = dot(normed_ref[...], wide_ref[:, :width], (1, 0))
    pre_up = dot(normed_ref[...], wide_ref[:, width:], (1, 0))
    next(parts)
    act, deriv = silu_parts(pre_gate)
    hidden_ref[...] = (act * pre_up).astype(BF16)
    grad_hidden = dot(cot_ref[...], down_ref[...], (1, 1))
    pre_ref[:, :width] = (grad_hidden * pre_up * deriv).astype(BF16)
    pre_ref[:, width:] = (grad_hidden * act).astype(BF16)
    out_ref[...] = dot(hidden_ref[...], down_ref[...], (1, 0)).astype(out_ref.dtype)
    grad_ref[...] = dot(pre_ref[...], wide_ref[...], (1, 1))
    for _ in parts:
        pass
    sender.finish()


def collect(first, second, normed, cot, wide, down):
    block = first.shape[1:]
    rows, model_width = normed.shape
    shape = jax.ShapeDtypeStruct
    return pl.pallas_call(
        collect_kernel,
        in_specs=[VMEM] * 6,
        out_specs=[VMEM] * 4,
        out_shape=[
            shape((rows, model_width), F32),
            shape((rows, down.shape[0]), BF16),
            shape((rows, wide.shape[1]), BF16),
            shape((rows, model_width), F32),
        ],
        scratch_shapes=[*collecting_spaces(block), *semaphores(14)],
        compiler_params=pltpu.CompilerParams(
            collective_id=3, has_side_effects=True, vmem_limit_bytes=63 << 20
        ),
        name="collect",
    )(first, second, normed, cot, wide, down)


def back_kernel(
    mask_ref, query_ref, kv_ref, grad_ref, near_wide, near_down, far_wide, far_down,
    grad_query_ref, grad_kv_ref, wide_out, down_out,
    part_ref, kv_core, kv_send, kv_half, far_wide_recv, far_down_recv, near_wide_recv, near_down_recv,
    wide_send, down_send, wide_recv, down_recv, wide_core, down_core, wide_own, down_own, send, recv,
):
    core, half = bit_of(CORE), bit_of(HALF)
    scale = HEAD_DIM ** (-0.5)
    row_count = mask_ref.shape[1] // 4

    def heads(micro):
        rows = pl.ds(micro * row_count, row_count)
        allowed = mask_ref[rows, :] > 0

        def head(h, _):
            at = pl.ds(pl.multiple_of(h * HEAD_DIM, HEAD_DIM), HEAD_DIM)
            value_at = pl.ds(pl.multiple_of((h + KV_HEADS) * HEAD_DIM, HEAD_DIM), HEAD_DIM)
            keys = jnp.concatenate([kv_ref[j, rows, at] for j in range(4)])
            values = jnp.concatenate([kv_ref[j, rows, value_at] for j in range(4)])
            grad_keys = grad_values = 0.0
            for g in range(GROUP_HEADS):
                lanes = pl.ds(pl.multiple_of((h * GROUP_HEADS + g) * HEAD_DIM, HEAD_DIM), HEAD_DIM)
                query, grad = query_ref[rows, lanes], grad_ref[rows, lanes]
                weights = masked_softmax(query, keys, allowed, scale)
                grad_weights = dot(grad, values, (1, 1))
                delta = jnp.sum(weights * grad_weights, axis=1, keepdims=True)
                grad_scores = (weights * (grad_weights - delta)).astype(BF16)
                grad_query_ref[rows, lanes] = (dot(grad_scores, keys, (1, 0)) * scale).astype(BF16)
                grad_keys = grad_keys + dot(query, grad_scores, (0, 0))
                grad_values = grad_values + dot(grad, weights.astype(BF16), (0, 0))
            grad_keys = (grad_keys * scale).T.astype(BF16)
            grad_values = grad_values.T.astype(BF16)
            for j in range(4):
                part_ref[j, rows, at] = grad_keys[j * row_count : (j + 1) * row_count]
                part_ref[j, rows, value_at] = grad_values[j * row_count : (j + 1) * row_count]
            return 0

        lax.fori_loop(0, KV_HEADS, head, 0)

    def add(*values):
        total = values[0][...].astype(F32)
        for value in values[1:]:
            total = total + value[...].astype(F32)
        return total

    meet((CORE, HALF, FAR))
    sender = Sender(send, recv)
    other = 1 - half
    across = [sender.start(far_wide.at[other, 0], far_wide_recv.at[0], HALF)]
    heads(0)
    across.append(sender.start(far_wide.at[other, 1], far_wide_recv.at[1], HALF))
    fars = []
    for q in range(2):
        if q:
            heads(1)
            kv_sums = [sender.start(part_ref.at[2 * j + 1], kv_core.at[j], CORE) for j in range(2)]
        sender.arrived(across[q])
        wide_send[q] = add(far_wide[half, q], far_wide_recv[q]).astype(BF16)
        fars.append(sender.start(wide_send.at[q], wide_recv.at[q], FAR))
    far_last = sender.start(far_down.at[other], far_down_recv, HALF)
    sender.arrived(*kv_sums)
    kv_send[...] = add(part_ref[2], kv_core[1]).astype(BF16)
    kv_last = sender.start(kv_send, kv_half, HALF)
    near = [sender.start(near_wide.at[other], near_wide_recv, HALF)]
    sender.arrived(far_last)
    down_send[...] = add(far_down[half], far_down_recv).astype(BF16)
    fars.append(sender.start(down_send, down_recv, FAR))
    near.append(sender.start(near_down.at[other], near_down_recv, HALF))
    sender.arrived(kv_last)
    grad_kv_ref[...] = add(part_ref[0], kv_core[0], kv_half[...]).astype(BF16)
    sender.arrived(*near, *fars[:2])

    def finish(near_ref, near_recv, far_recv, own_ref, core_ref, out_ref):
        own_ref[...] = add(near_ref[half, 1 - core], near_recv[1 - core], far_recv[1 - core]).astype(BF16)
        number = sender.start(own_ref, core_ref, CORE)
        out_ref[core] = add(near_ref[half, core], near_recv[core], far_recv[core])
        return number

    wide_last = finish(near_wide, near_wide_recv, wide_recv, wide_own, wide_core, wide_out)
    sender.arrived(wide_last)
    wide_out[1 - core] = wide_core[...].astype(F32)
    sender.arrived(*fars)
    down_last = finish(near_down, near_down_recv, down_recv, down_own, down_core, down_out)
    sender.arrived(down_last)
    down_out[1 - core] = down_core[...].astype(F32)
    sender.finish()


def back(masks, queries, kv, grad, near_wide, near_down, far_wide, far_down):
    shape = jax.ShapeDtypeStruct
    rows, width = kv.shape[1:]
    wide, down = near_wide.shape[1:], near_down.shape[1:]
    space = lambda *dims: pltpu.VMEM(dims, BF16)
    return pl.pallas_call(
        back_kernel,
        in_specs=[VMEM] * 8,
        out_specs=[VMEM] * 4,
        out_shape=[
            shape(queries.shape, BF16),
            shape((rows, width), BF16),
            shape((2,) + wide[1:], F32),
            shape((2,) + down[1:], F32),
        ],
        scratch_shapes=[
            space(4, rows, width),
            space(2, rows, width),
            space(rows, width),
            space(rows, width),
            *[space(*wide), space(*down)] * 4,
            *[space(*wide[1:]), space(*down[1:])] * 2,
            *semaphores(14),
        ],
        compiler_params=pltpu.CompilerParams(
            collective_id=5, has_side_effects=True, vmem_limit_bytes=62 << 20
        ),
        name="back",
    )(masks, queries, kv, grad, near_wide, near_down, far_wide, far_down)


def halving(sender, value, spaces, order, out, columns):
    left = list(AXES)
    for partner, landing in zip(order, spaces):
        place = left.index(partner)
        left.pop(place)
        rest = (slice(None),) * (len(left) - place + 1)
        at = lambda bit: (*(slice(None),) * place, bit, *rest, columns)
        into = (*(slice(None),) * (len(left) + 1), columns)
        own = bit_of(partner)
        number = sender.start(value.at[at(1 - own)], landing.at[into], partner)
        yield
        sender.arrived(number)
        if left:
            landing[into] = value[at(own)] + landing[into]
            value = landing
        else:
            out[into] = value[at(own)].astype(F32) + landing[into].astype(F32)


def reduce_kernel(*refs):
    values, parts, outs, part_out = refs[:3], refs[3:5], refs[5:8], refs[8]
    spaces, (core_recv, axis_recv, send, recv) = refs[9:-4], refs[-4:]

    def done(m, total):
        part_out[m] = total

    meet(AXES)
    sender = Sender(send, recv)
    orders = (
        (CORE, HALF, FAR, NEAR, SIDE),
        (CORE, SIDE, HALF, FAR, NEAR),
        (CORE, HALF, SIDE, FAR, NEAR),
    )
    steps = {}
    for i, (value, order) in enumerate(zip(values, orders)):
        cut, width = value.shape[-1] // 256 * 128, value.shape[-1]
        space = spaces[5 * i : 5 * i + 5]
        steps[i, 0] = halving(sender, value, space, order, outs[i], pl.ds(0, cut))
        steps[i, 1] = halving(sender, value, space, order, outs[i], pl.ds(cut, width - cut))
    collected = collecting(sender, parts, core_recv, axis_recv, done)
    in_turn([steps[1, 0], steps[1, 1], steps[0, 0], steps[2, 0], steps[0, 1], steps[2, 1], collected])
    sender.finish()


def reduce_dense(values, parts):
    blocks, scratch = [], []
    for value in values:
        rows = value.shape[0] // 32
        blocks.append(value.reshape((2,) * 5 + (rows, -1)).astype(BF16))
        scratch += [pltpu.VMEM((2,) * left + blocks[-1].shape[5:], BF16) for left in range(4, -1, -1)]
    return pl.pallas_call(
        reduce_kernel,
        in_specs=[VMEM] * 5,
        out_specs=[VMEM] * 4,
        out_shape=[
            *[jax.ShapeDtypeStruct(v.shape[5:], F32) for v in blocks],
            jax.ShapeDtypeStruct((2, *parts[0].shape[1:]), F32),
        ],
        scratch_shapes=[*scratch, *collecting_spaces(parts[0].shape[1:]), *semaphores(44)],
        compiler_params=pltpu.CompilerParams(
            collective_id=6, has_side_effects=True, vmem_limit_bytes=63 << 20
        ),
        name="reduce_dense",
    )(*blocks, *parts)


def attention_back(micro, masks, queries, kv, grad):
    row_count = grad.shape[0]
    wide = GROUP_HEADS * HEAD_DIM
    heads = lambda at: pl.BlockSpec((4, row_count, HEAD_DIM), lambda h: (0, micro, h + at))
    column = pl.BlockSpec((4, row_count, HEAD_DIM), lambda h: (0, 0, h))
    flat = jax.ShapeDtypeStruct((4, row_count, KV_HEADS * HEAD_DIM), BF16)
    return pl.pallas_call(
        functools.partial(attention_back_kernel, HEAD_DIM ** (-0.5)),
        grid=(KV_HEADS,),
        in_specs=[
            pl.BlockSpec((row_count, 4 * row_count), lambda h: (micro, 0)),
            pl.BlockSpec((row_count, wide), lambda h: (micro, h)),
            heads(0),
            heads(KV_HEADS),
            pl.BlockSpec((row_count, wide), lambda h: (0, h)),
        ],
        out_specs=[pl.BlockSpec((row_count, wide), lambda h: (0, h)), column, column],
        out_shape=[jax.ShapeDtypeStruct((row_count, HEADS * HEAD_DIM), BF16), flat, flat],
        compiler_params=pltpu.CompilerParams(vmem_limit_bytes=48 << 20),
        name="attention_back",
    )(masks, queries, kv, kv, grad)


def expert_kernel(
    slot_ref, scale_ref, column_ref, token_ref, cot_ref, *refs
):
    count = column_ref.shape[0]
    gate_refs, up_refs, down_refs = refs[:count], refs[count : 2 * count], refs[2 * count : 3 * count]
    rows_ref, cots_ref, hidden_ref, pre_ref, mixed_ref, graded_ref = refs[-10:-4]
    pick_ref, value_ref, extra_ref, back_ref = refs[-4:]
    width = down_refs[0].shape[0]
    blocks, row_count = token_ref.shape[0], token_ref.shape[2]
    room = rows_ref.shape[2] // blocks
    slot = lax.broadcasted_iota(jnp.int32, (room, row_count), 0)
    gates = []
    for b in range(blocks):
        for k in range(count):
            picked = slot == slot_ref[k, b]
            gates.append(jnp.sum(jnp.where(picked, scale_ref[k, b], 0.0), axis=1, keepdims=True))
            pick_ref[b, k * room : (k + 1) * room, :] = jnp.where(picked, 1.0, 0.0).astype(BF16)
        rows = dot(pick_ref[b], token_ref[b, 0], (1, 0)).astype(BF16)
        cots = dot(pick_ref[b], cot_ref[b, 0], (1, 0)).astype(BF16)
        for k in range(count):
            part = slice(b * room, (b + 1) * room)
            rows_ref[k, 0, part, :] = rows[k * room : (k + 1) * room]
            cots_ref[k, 0, part, :] = cots[k * room : (k + 1) * room]
    for k in range(count):
        gate = jnp.concatenate([gates[b * count + k] for b in range(blocks)])
        pre_gate = dot(rows_ref[k, 0], gate_refs[k][...], (1, 0))
        pre_up = dot(rows_ref[k, 0], up_refs[k][...], (1, 0))
        grad_hidden = dot(cots_ref[k, 0], down_refs[k][...], (1, 1))
        act, deriv = silu_parts(pre_gate)
        hidden = act * pre_up
        gate_grad = jnp.sum(hidden * grad_hidden, axis=1, keepdims=True)
        grad_hidden = grad_hidden * gate
        hidden_ref[k, 0] = (hidden * gate).astype(BF16)
        pre_ref[k, 0, :, :width] = (grad_hidden * pre_up * deriv).astype(BF16)
        pre_ref[k, 0, :, width:] = (grad_hidden * act).astype(BF16)
        value = dot(hidden_ref[k, 0], down_refs[k][...], (1, 0)).astype(BF16)
        back = dot(pre_ref[k, 0, :, :width], gate_refs[k][...], (1, 1))
        back = (back + dot(pre_ref[k, 0, :, width:], up_refs[k][...], (1, 1))).astype(BF16)
        extra = (gate_grad * column_ref[k]).astype(BF16)
        for b in range(blocks):
            to, part = slice(k * room, (k + 1) * room), slice(b * room, (b + 1) * room)
            value_ref[b, to, :] = value[part]
            back_ref[b, to, :] = back[part]
            extra_ref[b, to, :] = extra[part]
    model_width = token_ref.shape[3]
    for b in range(blocks):
        graded_ref[b] = dot(pick_ref[b], back_ref[b], (0, 0)).astype(BF16)
        mixed_ref[b, :, :model_width] = dot(pick_ref[b], value_ref[b], (0, 0)).astype(BF16)
        mixed_ref[b, :, model_width:] = dot(pick_ref[b], extra_ref[b], (0, 0)).astype(BF16)


def expert_pass(micro, slots, scales, columns, tokens, cots, gates, ups, downs, room, kept):
    count, (width, model_width) = len(downs), downs[0].shape
    blocks, micro_count, row_count = tokens.shape[:3]
    step = 2
    by_block = lambda *dims: pl.BlockSpec((step, *dims), lambda b: (b,) + (0,) * len(dims))
    by_slot = pl.BlockSpec((count, step, 1, row_count), lambda b: (0, b, 0, 0))
    whole = lambda *dims: pl.BlockSpec(dims, lambda b: (0,) * len(dims), pipeline_mode=pl.Buffered(1))
    saved = lambda cols: pl.BlockSpec((count, 1, step * room, cols), lambda b: (0, micro, b, 0))
    widths = (model_width, model_width, width, 2 * width)
    shapes = [jax.ShapeDtypeStruct((count, micro_count, blocks * room, w), BF16) for w in widths]
    args = [slots, scales, columns, tokens, cots, *gates, *ups, *downs]
    in_specs = [
        by_slot,
        by_slot,
        whole(count, 1, 128),
        pl.BlockSpec((step, 1, row_count, model_width), lambda b: (b, micro, 0, 0)),
        pl.BlockSpec((step, 1, row_count, model_width), lambda b: (b, micro, 0, 0)),
        *[whole(model_width, width)] * (2 * count),
        *[whole(width, model_width)] * count,
    ]
    aliases = {}
    if kept:
        aliases = {len(args) + i: i for i in range(len(kept))}
        in_specs += [pl.BlockSpec(memory_space=pl.ANY)] * len(kept)
        args += list(kept)
    out = pl.pallas_call(
        expert_kernel,
        grid=(blocks // step,),
        in_specs=in_specs,
        out_specs=[saved(w) for w in widths]
        + [by_block(row_count, model_width + 128), by_block(row_count, model_width)],
        out_shape=shapes
        + [
            jax.ShapeDtypeStruct((blocks, row_count, model_width + 128), BF16),
            jax.ShapeDtypeStruct((blocks, row_count, model_width), BF16),
        ],
        scratch_shapes=[
            pltpu.VMEM((step, count * room, row_count), BF16),
            pltpu.VMEM((step, count * room, model_width), BF16),
            pltpu.VMEM((step, count * room, 128), BF16),
            pltpu.VMEM((step, count * room, model_width), BF16),
        ],
        input_output_aliases=aliases,
        compiler_params=pltpu.CompilerParams(vmem_limit_bytes=60 << 20),
        name="experts",
    )(*args)
    return out[:4], out[4], out[5]


def attend_plain(queries, kv, masks, micro):
    row_count = masks.shape[1] // 4
    rows = slice(micro * row_count, (micro + 1) * row_count)
    allowed = masks[rows] > 0
    wide = KV_HEADS * HEAD_DIM
    heads = queries[rows].reshape(row_count, KV_HEADS, GROUP_HEADS, HEAD_DIM)
    keys = kv[:, rows, :wide].reshape(-1, KV_HEADS, HEAD_DIM)
    values = kv[:, rows, wide:].reshape(-1, KV_HEADS, HEAD_DIM)
    scores = mm("ikgd,jkd->kgij", heads, keys) * HEAD_DIM ** (-0.5)
    row_max = jnp.max(jnp.where(allowed, scores, NEGATIVE), axis=3, keepdims=True)
    expo = jnp.where(allowed, jnp.exp(jnp.where(allowed, scores, NEGATIVE) - row_max), 0.0)
    total = jnp.sum(expo, axis=3, keepdims=True)
    weights = (expo / jnp.where(total > 0.5, total, 1.0)).astype(BF16)
    return mm("kgij,jkd->ikgd", weights, values).reshape(row_count, HEADS * HEAD_DIM).astype(BF16)


def on_device(
    tokens,
    segment_ids,
    routes,
    route_gates,
    attn_gain,
    query_proj,
    key_proj,
    value_proj,
    output_proj,
    ffn_gain,
    shared_gate,
    shared_up,
    shared_down,
    expert_gate,
    expert_up,
    expert_down,
    output_cot,
):
    micro_count, row_count, model_width = tokens.shape
    exp_count = lax.axis_size("exp")
    local_experts, gate_rows, expert_width = expert_gate.shape
    down_rows = expert_down.shape[1]
    all_experts = local_experts * exp_count
    route_count = routes.shape[2]
    capacity = 4 * row_count * route_count // (3 * all_experts)
    query_width = HEADS * HEAD_DIM
    kv_width = KV_HEADS * HEAD_DIM
    far_steps = exp_count // 4
    assert lax.axis_size("seq") == 4 and local_experts == 2

    seq_index = lax.axis_index("seq")
    exp_index = lax.axis_index("exp")
    core = seq_index % 2
    half = seq_index // 2
    everywhere = ("seq", "exp")

    linked = exp_count == 8
    expert_range = jnp.arange(all_experts, dtype=jnp.int32)
    gate_table = jnp.sum(
        jnp.where(
            jnp.swapaxes(routes, 1, 2)[:, :, None, :] == expert_range[None, None, :, None],
            jnp.swapaxes(route_gates, 1, 2)[:, :, None, :],
            0.0,
        ),
        axis=1,
    )
    order = jnp.arange(row_count, dtype=jnp.int32)
    before = (order[:, None] < order[None, :]).astype(BF16)
    slots = jnp.arange(capacity, dtype=jnp.int32)
    expert_ids = [
        local_experts * ((exp_index - 4 * k + exp_count) % exp_count) + core
        for k in range(far_steps)
    ]
    kv_proj = jnp.concatenate([key_proj, value_proj], axis=1)
    shared_wide = jnp.concatenate([shared_gate, shared_up], axis=1)

    def gathered(value):
        return lax.all_gather(value, everywhere, axis=0, tiled=True)

    def mask_of(micro):
        segments = segment_ids[micro].reshape(4, row_count)
        key_ids = jnp.concatenate(
            [lax.dynamic_index_in_dim(segments, seq_index ^ j, 0, False) for j in range(4)]
        )
        key_pos = jnp.concatenate([(seq_index ^ j) * row_count + order for j in range(4)])
        query_ids, query_pos = key_ids[:row_count], key_pos[:row_count]
        allowed = (
            (key_ids[None, :] == query_ids[:, None])
            & (key_pos[None, :] <= query_pos[:, None])
            & (query_ids[:, None] >= 0)
        )
        return allowed.astype(jnp.int32)

    inputs = tokens.reshape(micro_count * row_count, model_width).astype(F32)
    inv_one = lax.rsqrt(jnp.mean(inputs * inputs, axis=1, keepdims=True) + EPSILON)
    masks = jnp.concatenate([mask_of(micro) for micro in range(micro_count)])
    if linked:
        gains = jnp.stack([attn_gain, ffn_gain]).astype(F32)
        share = gains.shape[1]
        gains = jnp.pad(gains, ((0, 6), (0, 128 - share)))
        lane = jnp.arange(128)[:, None]
        place = (lane == jnp.arange(model_width)[None, :] % share).astype(BF16)
        out = begin(
            tokens.reshape(micro_count * row_count, model_width), query_proj, kv_proj, gains, place, masks,
            (expert_gate, expert_up, expert_down), output_cot, gate_table,
        )
        query_full = out[0].reshape(model_width, query_width)
        kv_full = out[1].reshape(model_width, 2 * kv_width)
        gain_one, gain_two = out[2][0], out[2][1]
        normed_one, queries, kv, contexts = out[3:7]
        gate_all = [w.reshape(model_width, expert_width) for w in (out[7], out[10])]
        up_all = [w.reshape(model_width, expert_width) for w in (out[8], out[11])]
        down_all = [w.reshape(expert_width, model_width) for w in (out[9], out[12])]
        cot_blocks = out[13].reshape(8, micro_count, row_count, model_width)
        gate_blocks = out[14].reshape(8, micro_count, all_experts, row_count)
        out_proj = gathered(output_proj)
        shared_wide, shared_down = after((shared_wide, shared_down), contexts)
    else:
        query_full, kv_full = gathered(query_proj), gathered(kv_proj)
        gain_one, gain_two = gathered(attn_gain).astype(F32), gathered(ffn_gain).astype(F32)
        out_proj = gathered(output_proj)
        normed_one = (inputs * inv_one * gain_one).astype(BF16)
        queries = jnp.dot(normed_one, query_full, preferred_element_type=F32).astype(BF16)
        own = jnp.dot(normed_one, kv_full, preferred_element_type=F32).astype(BF16)
        across = exchange(own, "seq", 2)
        kv = jnp.stack([own, exchange(own, "seq", 1), across, exchange(across, "seq", 1)])
        contexts = jnp.concatenate([attend_plain(queries, kv, masks, m) for m in range(micro_count)])
        gate_blocks = jnp.concatenate(group_gather(gate_table))
        cot_blocks = jnp.concatenate(group_gather(output_cot))

        def parity(value):
            kept = lax.dynamic_index_in_dim(value, core, 0, False)
            sent = lax.dynamic_index_in_dim(value, 1 - core, 0, False)
            return in_order(core, kept, exchange(sent, "seq", 1), 0)

        wide_far = [parity(jnp.concatenate([expert_gate, expert_up], axis=2))]
        down_far = [parity(expert_down)]
        for _ in range(far_steps - 1):
            wide_far.append(rotate(wide_far[-1], "exp", 4))
            down_far.append(rotate(down_far[-1], "exp", 4))
        wide_full = [in_order(half, w, exchange(w, "seq", 2), 0) for w in wide_far]
        down_full = [in_order(half, w, exchange(w, "seq", 2), 0) for w in down_far]

    def sequence_sum(grad_keys, grad_values):
        grad = jnp.concatenate([grad_keys, grad_values], axis=2)
        part = grad[0::2].astype(F32) + exchange(grad[1::2], "seq", 1).astype(F32)
        return (part[0] + exchange(part[1].astype(BF16), "seq", 2).astype(F32)).astype(BF16)

    kept_rows = []

    def experts(micro, normed_blocks):
        gates = jnp.stack(
            [lax.dynamic_index_in_dim(gate_blocks[:, micro], e, 1, False) for e in expert_ids]
        )
        named = gates > 0.0
        rank = mm("kbs,st->kbt", named.astype(BF16), before).astype(jnp.int32)
        slot = jnp.where(named, rank, -1)
        if not linked:
            return experts_plain(gates, slot, normed_blocks[:, micro], cot_blocks[:, micro])
        columns = (
            lax.broadcasted_iota(jnp.int32, (far_steps, 1, 128), 2)
            == jnp.stack(expert_ids)[:, None, None]
        ).astype(F32)
        kept, mixed, graded = expert_pass(
            micro, slot[:, :, None], gates[:, :, None], columns,
            normed_blocks, cot_blocks, gate_all, up_all, down_all, capacity, kept_rows,
        )
        kept_rows[:] = kept
        return graded, mixed

    def experts_plain(gates, slot, normed_blocks, micro_cots):
        mixed, graded, kept = 0.0, 0.0, []
        for k in range(far_steps):
            picked = slot[k][:, None, :] == slots[None, :, None]
            pick = picked.astype(BF16)
            slot_gates = jnp.sum(jnp.where(picked, gates[k][:, None, :], 0.0), axis=2).reshape(-1, 1)
            rows = mm("bst,btd->bsd", pick, normed_blocks).astype(BF16).reshape(-1, model_width)
            cots = mm("bst,btd->bsd", pick, micro_cots).astype(BF16).reshape(-1, model_width)
            pre = jnp.dot(rows, wide_full[k], preferred_element_type=F32)
            pre_gate, pre_up = pre[:, :expert_width], pre[:, expert_width:]
            grad_hidden = mm("rd,fd->rf", cots, down_full[k])
            act, deriv = silu_parts(pre_gate)
            hidden = act * pre_up
            gate_grad = jnp.sum(hidden * grad_hidden, axis=1, keepdims=True)
            hidden = (hidden * slot_gates).astype(BF16)
            grad_hidden = grad_hidden * slot_gates
            grad_pre = jnp.concatenate(
                [(grad_hidden * pre_up * deriv).astype(BF16), (grad_hidden * act).astype(BF16)], axis=1
            )
            value = jnp.dot(hidden, down_full[k], preferred_element_type=F32).astype(BF16)
            column = (lax.broadcasted_iota(jnp.int32, (1, 128), 1) == expert_ids[k]).astype(F32)
            value = jnp.concatenate([value, (gate_grad * column).astype(BF16)], axis=1)
            grad_rows = mm("rf,df->rd", grad_pre, wide_full[k]).astype(BF16)
            blocks = pick.shape[0]
            mixed = mixed + mm("bst,bsd->btd", pick, value.reshape(blocks, capacity, -1))
            graded = graded + mm("bst,bsd->btd", pick, grad_rows.reshape(blocks, capacity, -1))
            kept.append((rows, cots, hidden, grad_pre))
        kept_rows.append(kept)
        return graded.astype(BF16), mixed.astype(BF16)

    up_proj, down_proj = gathered(shared_wide), gathered(shared_down)
    residual = inputs + jnp.dot(contexts, out_proj, preferred_element_type=F32)
    inv_two = lax.rsqrt(jnp.mean(residual * residual, axis=1, keepdims=True) + EPSILON)
    normed_two = (residual * inv_two * gain_two).astype(BF16)
    per_micro = normed_two.reshape(micro_count, row_count, model_width)
    token_blocks = spread(per_micro) if linked else jnp.concatenate(group_gather(per_micro))

    graded_parts, mixed_parts = [], []
    for micro in range(micro_count):
        graded, mixed = experts(micro, token_blocks)
        if not linked:
            graded = group_scatter(graded[:4], graded[4:])
            mixed = group_scatter(mixed[:4], mixed[4:])
            graded, mixed, token_blocks = lax.optimization_barrier((graded, mixed, token_blocks))
        graded_parts.append(graded)
        mixed_parts.append(mixed)

    upstream_low = output_cot.reshape(micro_count * row_count, model_width)
    shared_width = shared_gate.shape[1]
    if linked:
        grad_normed, shared_hidden, grad_shared_pre, shared_out = collect(
            *graded_parts, normed_two, upstream_low, up_proj, down_proj
        )
    else:
        shared_pre = jnp.dot(normed_two, up_proj, preferred_element_type=F32)
        shared_pre_gate, shared_pre_up = shared_pre[:, :shared_width], shared_pre[:, shared_width:]
        shared_act, shared_deriv = silu_parts(shared_pre_gate)
        shared_hidden = (shared_act * shared_pre_up).astype(BF16)
        shared_out = jnp.dot(shared_hidden, down_proj, preferred_element_type=F32)
        grad_shared_hidden = mm("rd,fd->rf", upstream_low, down_proj)
        grad_shared_pre = jnp.concatenate(
            [
                (grad_shared_hidden * shared_pre_up * shared_deriv).astype(BF16),
                (grad_shared_hidden * shared_act).astype(BF16),
            ],
            axis=1,
        )
        grad_from_shared = mm("rf,df->rd", grad_shared_pre, up_proj)
        grad_normed = jnp.concatenate(graded_parts) + grad_from_shared

    def summed(value):
        return lax.psum_scatter(
            value.astype(BF16), everywhere, scatter_dimension=0, tiled=True
        ).astype(F32)

    shared_up_sum = summed(mm("rd,rf->df", normed_two, grad_shared_pre))
    shared_down_sum = summed(mm("rd,rf->df", shared_hidden, upstream_low))

    def flat(value):
        return value.reshape(micro_count * row_count, -1)

    grad_from_two, gain_two_sum = norm_back(grad_normed, residual, inv_two, gain_two)
    grad_residual = upstream_low.astype(F32) + grad_from_two
    grad_branch = grad_residual.astype(BF16)
    grad_context = mm("rd,id->ri", grad_branch, out_proj).astype(BF16)
    output_sum = mm("rd,rf->df", contexts, grad_branch)

    def expert_sum(left, right):
        own = None
        for k in reversed(range(far_steps)):
            lefts = jnp.concatenate([m[k][left] for m in kept_rows])
            rights = jnp.concatenate([m[k][right] for m in kept_rows])
            if own is not None:
                lefts, rights, own = lax.optimization_barrier((lefts, rights, own))
            total = mm("rd,rf->df", lefts, rights)
            rows = total.shape[0] // 2
            total = total.reshape(2, rows, -1)
            mine = lax.dynamic_index_in_dim(total, half, 0, False)
            sent = lax.dynamic_index_in_dim(total, 1 - half, 0, False).astype(BF16)
            total = mine + exchange(sent, "seq", 2).astype(F32)
            own = total if own is None else total + rotate(own.astype(BF16), "exp", -4).astype(F32)
        rows = own.shape[0] // 2
        own = own.reshape(2, rows, -1)
        kept = lax.dynamic_index_in_dim(own, core, 0, False)
        sent = lax.dynamic_index_in_dim(own, 1 - core, 0, False).astype(BF16)
        other = exchange(sent, "seq", 1).astype(F32)
        return in_order(core, kept[None], other[None], 0)

    if linked:
        products = []
        for k in range(far_steps):
            for left, right in ((0, 3), (2, 1)):
                total = mm("mrd,mrf->df", kept_rows[left][k], kept_rows[right][k]).astype(BF16)
                products.append(total.reshape(2, 2, total.shape[0] // 4, -1))
        grad_query, grad_kv, wide_grad, down_grad = back(masks, queries, kv, grad_context, *products)
    else:
        down_grad = expert_sum(2, 1)
        down_grad, kept_rows = lax.optimization_barrier((down_grad, kept_rows))
        wide_grad = expert_sum(0, 3)
        grad_queries, grad_kvs = [], []
        for micro in range(micro_count):
            rows = slice(micro * row_count, (micro + 1) * row_count)
            grad_query, grad_keys, grad_values = attention_back(
                micro, masks, queries, kv, grad_context[rows]
            )
            grad_queries.append(grad_query)
            grad_kvs.append(sequence_sum(grad_keys, grad_values))
        grad_query, grad_kv = jnp.concatenate(grad_queries), jnp.concatenate(grad_kvs)

    grad_normed_one = mm("ri,di->rd", grad_query, query_full) + mm("ri,di->rd", grad_kv, kv_full)
    grad_from_one, gain_one_sum = norm_back(grad_normed_one, inputs, inv_one, gain_one)
    token_grads = (grad_residual + grad_from_one).astype(BF16)
    column = lax.broadcasted_iota(jnp.int32, (1, 2 * kv_width + 128), 1)
    query_sum = mm("rd,rf->df", normed_one, grad_query)
    kv_sum = mm("rd,rf->df", normed_one, jnp.pad(grad_kv, ((0, 0), (0, 128))))
    kv_sum = jnp.where(column == 2 * kv_width, gain_one_sum[:, None], kv_sum)
    kv_sum = jnp.where(column == 2 * kv_width + 1, gain_two_sum[:, None], kv_sum)
    if linked:
        output_sum, query_sum, kv_sum, moe_outs = reduce_dense((output_sum, query_sum, kv_sum), mixed_parts)
        moe_outs = flat(moe_outs)
    else:
        output_sum, query_sum, kv_sum = summed(output_sum), summed(query_sum), summed(kv_sum)
        moe_outs = jnp.concatenate(mixed_parts)
    outputs = (residual + shared_out + moe_outs[:, :model_width]).astype(BF16)
    table = moe_outs[:, model_width : model_width + all_experts]
    gate_grads = jnp.sum(
        jnp.where(flat(routes)[:, :, None] == expert_range[None, None, :], table[:, None, :], 0.0),
        axis=2,
    )

    return (
        outputs.reshape(tokens.shape),
        token_grads.reshape(tokens.shape),
        gate_grads.reshape(routes.shape),
        kv_sum[:, 2 * kv_width],
        query_sum,
        kv_sum[:, :kv_width],
        kv_sum[:, kv_width : 2 * kv_width],
        output_sum,
        kv_sum[:, 2 * kv_width + 1],
        shared_up_sum[:, :shared_width],
        shared_up_sum[:, shared_width:],
        shared_down_sum,
        wide_grad[:, :, :expert_width],
        wide_grad[:, :, expert_width:],
        down_grad,
    )


def solution(mesh):
    rows = P(("seq", "exp"), None)
    wide = P("exp", "seq", None)
    flat = P(("seq", "exp"))
    return jax.shard_map(
        on_device,
        mesh=mesh,
        in_specs=(wide, P("exp", None), wide, wide, flat, rows, rows, rows, rows, flat, rows, rows, rows)
        + (wide,) * 4,
        out_specs=(wide, wide, wide, flat, rows, rows, rows, rows, flat, rows, rows, rows)
        + (wide,) * 3,
        check_vma=False,
    )
```

```python
import functools

import jax
import jax.numpy as jnp
from jax import lax
from jax.experimental import pallas as pl
from jax.experimental.pallas import tpu as pltpu
from jax.sharding import PartitionSpec as P

HEADS = 12
KV_HEADS = 4
HEAD_DIM = 128
GROUP_HEADS = HEADS // KV_HEADS
EPSILON = 1e-05
NEGATIVE = -1e30
F32 = jnp.float32
BF16 = jnp.bfloat16


def mm(spec, left, right):
    return jnp.einsum(spec, left, right, preferred_element_type=F32)


def exchange(value, axis, bit):
    size = lax.axis_size(axis)
    return lax.ppermute(value, axis, [(i, i ^ bit) for i in range(size)])


def rotate(value, axis, step):
    size = lax.axis_size(axis)
    return lax.ppermute(value, axis, [(i, (i + step) % size) for i in range(size)])


def after(value, *others):
    return lax.optimization_barrier((value, others))[0]


def in_order(flag, own, other, axis):
    return jnp.where(
        flag == 0,
        jnp.concatenate([own, other], axis),
        jnp.concatenate([other, own], axis),
    )


def silu_parts(pre_act):
    sigma_val = jax.nn.sigmoid(pre_act)
    return (pre_act * sigma_val, sigma_val * (1.0 + pre_act * (1.0 - sigma_val)))


def norm_back(grad_normed, values, inv_rms, gain):
    scaled = grad_normed * gain
    inner = jnp.mean(scaled * values, axis=1, keepdims=True)
    grad_values = inv_rms * scaled - values * (inv_rms * inv_rms * inv_rms) * inner
    return grad_values, jnp.sum(grad_normed * values * inv_rms, axis=0)


def group_gather(value):
    over_y = jnp.stack([value, exchange(value, "exp", 1)])
    over_z = jnp.concatenate([over_y, exchange(over_y, "exp", 2)])
    other = exchange(over_z, "seq", 1)
    return over_z, other


def group_scatter(own, other):
    part = own.astype(F32) + exchange(other, "seq", 1).astype(F32)
    part = part[:2] + exchange(part[2:].astype(BF16), "exp", 2).astype(F32)
    return part[0] + exchange(part[1].astype(BF16), "exp", 1).astype(F32)


def dot(left, right, over):
    return lax.dot_general(left, right, ((over[:1], over[1:]), ((), ())), preferred_element_type=F32)


def masked_softmax(query, keys, allowed, scale):
    scores = jnp.where(allowed, dot(query, keys, (1, 1)) * scale, NEGATIVE)
    expo = jnp.where(allowed, jnp.exp(scores - jnp.max(scores, axis=1, keepdims=True)), 0.0)
    total = jnp.sum(expo, axis=1, keepdims=True)
    return expo * (1.0 / jnp.where(total > 0.5, total, 1.0))


def attention_back_kernel(
    scale, mask_ref, query_ref, key_ref, value_ref, grad_ref, grad_query_ref, grad_key_ref, grad_value_ref
):
    keys = key_ref[...].reshape(-1, HEAD_DIM)
    values = value_ref[...].reshape(-1, HEAD_DIM)
    allowed = mask_ref[...] > 0
    grad_keys = grad_values = 0.0
    for g in range(GROUP_HEADS):
        lanes = slice(g * HEAD_DIM, (g + 1) * HEAD_DIM)
        query, grad = query_ref[:, lanes], grad_ref[:, lanes]
        weights = masked_softmax(query, keys, allowed, scale)
        grad_weights = dot(grad, values, (1, 1))
        delta = jnp.sum(weights * grad_weights, axis=1, keepdims=True)
        grad_scores = (weights * (grad_weights - delta)).astype(BF16)
        grad_query_ref[:, lanes] = (dot(grad_scores, keys, (1, 0)) * scale).astype(BF16)
        grad_keys = grad_keys + dot(query, grad_scores, (0, 0))
        grad_values = grad_values + dot(grad, weights.astype(BF16), (0, 0))
    grad_key_ref[...] = (grad_keys * scale).T.astype(BF16).reshape(grad_key_ref.shape)
    grad_value_ref[...] = grad_values.T.astype(BF16).reshape(grad_value_ref.shape)


MESH = pl.DeviceIdType.MESH
CORE, HALF = ("seq", 1), ("seq", 2)
SIDE, NEAR, FAR = ("exp", 1), ("exp", 2), ("exp", 4)


def bit_of(partner):
    axis, bit = partner
    return lax.axis_index(axis) // bit % 2


def device_of(partner):
    axis, bit = partner
    return {axis: lax.axis_index(axis) + bit - 2 * bit * bit_of(partner)}


def meet(partners):
    barrier = pltpu.get_barrier_semaphore()
    for partner in partners:
        pl.semaphore_signal(barrier, inc=1, device_id=device_of(partner), device_id_type=MESH)
    pl.semaphore_wait(barrier, len(partners))


class Sender:
    def __init__(self, send_sems, recv_sems):
        self.send_sems, self.recv_sems = send_sems, recv_sems
        self.copies, self.landed = [], set()

    def start(self, src, dst, partner):
        i = len(self.copies)
        copy = pltpu.make_async_remote_copy(
            src_ref=src,
            dst_ref=dst,
            send_sem=self.send_sems.at[i],
            recv_sem=self.recv_sems.at[i],
            device_id=device_of(partner),
            device_id_type=MESH,
        )
        copy.start()
        self.copies.append(copy)
        return i

    def arrived(self, *numbers):
        for i in numbers:
            if i not in self.landed:
                self.copies[i].wait_recv()
                self.landed.add(i)

    def finish(self):
        for i, copy in enumerate(self.copies):
            copy.wait_send()
            self.arrived(i)


def semaphores(count):
    return [pltpu.SemaphoreType.DMA((count,)), pltpu.SemaphoreType.DMA((count,))]


ANYWHERE = pl.BlockSpec(memory_space=pl.ANY)
VMEM = pl.BlockSpec(memory_space=pltpu.VMEM)
AXES = (HALF, CORE, FAR, NEAR, SIDE)


def doubling(sender, out, order, columns=None):
    held = []
    for partner in order:
        at = tuple(slice(None) if a in held else bit_of(a) for a in AXES)
        view = out.at[at] if columns is None else out.at[(*at, slice(None), columns)]
        number = sender.start(view, view, partner)
        yield
        sender.arrived(number)
        held.append(partner)


def in_turn(steps):
    steps = list(steps)
    while steps:
        steps = [s for s in steps if next(s, s) is not s]


def attention_heads(scale, rows, mask_ref, query_ref, kv_ref, context_ref):
    allowed = mask_ref[rows, :] > 0
    blocks = [kv_ref.at[j, rows, :] for j in range(4)]

    def head(h, _):
        at = pl.ds(pl.multiple_of(h * HEAD_DIM, HEAD_DIM), HEAD_DIM)
        value_at = pl.ds(pl.multiple_of((h + KV_HEADS) * HEAD_DIM, HEAD_DIM), HEAD_DIM)
        keys = jnp.concatenate([b[:, at] for b in blocks])
        values = jnp.concatenate([b[:, value_at] for b in blocks])
        for g in range(GROUP_HEADS):
            lanes = pl.ds(pl.multiple_of((h * GROUP_HEADS + g) * HEAD_DIM, HEAD_DIM), HEAD_DIM)
            weights = masked_softmax(query_ref[rows, lanes], keys, allowed, scale)
            context_ref[rows, lanes] = dot(weights.astype(BF16), values, (1, 0)).astype(BF16)
        return 0

    lax.fori_loop(0, KV_HEADS, head, 0)


def begin_kernel(
    token_ref, query_shard, kv_shard, gain_shard, place_ref, mask_ref, gate_ref, up_ref, down_ref, cot_ref, table_ref,
    query_full, kv_full, gain_ref, normed_ref, query_ref, kv_ref, context_ref,
    gate_near, up_near, down_near, gate_far, up_far, down_far, cot_out, table_out,
    gain_land, gate_own, up_own, down_own, gate_half, up_half, down_half, send, recv, local,
):
    core, half = bit_of(CORE), bit_of(HALF)
    own = tuple(bit_of(a) for a in AXES)
    shards = ((query_shard, query_full), (kv_shard, kv_full), (gain_shard, gain_land))
    experts = ((gate_ref, gate_own), (up_ref, up_own), (down_ref, down_own))
    nears, fars = (gate_near, up_near, down_near), (gate_far, up_far, down_far)
    owns, halves = (gate_own, up_own, down_own), (gate_half, up_half, down_half)
    for shard, full in shards:
        full[own] = shard[...]
    for ref, mine in experts:
        mine[core] = ref[core]
    copies = [
        pltpu.make_async_copy(cot_ref, cot_out.at[0, 0, 0], local.at[6]),
        pltpu.make_async_copy(table_ref, table_out.at[0, 0, 0], local.at[7]),
    ]
    for copy in copies:
        copy.start()

    def keep(ref, out, i):
        copy = pltpu.make_async_copy(ref, out.at[half], local.at[i])
        copy.start()
        copies.append(copy)
        return sender.start(ref, out.at[half], HALF)

    meet(AXES)
    sender = Sender(send, recv)
    one, two = (NEAR, FAR, HALF, SIDE, CORE), (SIDE, NEAR, FAR, HALF, CORE)
    cut, kv_cut = query_shard.shape[1] // 2, kv_shard.shape[1] // 2
    gathers = [
        doubling(sender, gain_land, two),
        doubling(sender, query_full, one, pl.ds(0, cut)),
        doubling(sender, kv_full, two, pl.ds(0, kv_cut)),
        doubling(sender, query_full, one, pl.ds(cut, cut)),
        doubling(sender, kv_full, two, pl.ds(kv_cut, kv_cut)),
    ]

    def turn():
        for g in gathers:
            next(g, None)

    turn()
    swaps = [sender.start(r.at[1 - core], o.at[core], CORE) for r, o in experts]
    table_side = sender.start(table_ref, table_out.at[0, 0, 1], SIDE)
    cot_side = sender.start(cot_ref.at[0], cot_out.at[0, 0, 1, 0], SIDE)
    cot_near = sender.start(cot_ref.at[1], cot_out.at[0, 1, 0, 1], NEAR)
    values = token_ref[...].astype(F32)
    inverse = lax.rsqrt(jnp.mean(values * values, axis=1, keepdims=True) + EPSILON)
    turn()
    sender.arrived(*swaps)
    keep(gate_own, gate_near, 0)
    turn()
    turn()
    gate_sent = sender.start(gate_own, gate_half, FAR)
    turn()
    keep(up_own, up_near, 1)
    sender.arrived(table_side, cot_side, cot_near)
    for copy in copies[:2]:
        copy.wait()
    table_near = sender.start(table_out.at[0, 0], table_out.at[0, 1], NEAR)
    cots = [
        sender.start(cot_out.at[0, 0, :, 0], cot_out.at[0, 1, :, 0], NEAR),
        sender.start(cot_out.at[0, :, 0, 1], cot_out.at[0, :, 1, 1], SIDE),
    ]
    turn()
    share = query_shard.shape[0]
    gains = gain_land[...].reshape(-1, 8, gain_land.shape[-1])
    owner = lax.broadcasted_iota(jnp.int32, (gains.shape[0], place_ref.shape[1]), 0)
    lane = lax.broadcasted_iota(jnp.int32, owner.shape, 1)
    mine = (lane >= owner * share) & (lane < (owner + 1) * share)
    for i in range(2):
        rows = dot(gains[:, i, :].astype(BF16), place_ref[...], (1, 0))
        gain_ref[i : i + 1, :] = jnp.sum(jnp.where(mine, rows, 0.0), axis=0, keepdims=True)
    normed_ref[...] = (values * inverse * gain_ref[0:1, :]).astype(BF16)
    width = normed_ref.shape[1]
    kv_ref[0] = dot(normed_ref[...], kv_full[...].reshape(width, -1), (1, 0)).astype(BF16)
    kv_half = sender.start(kv_ref.at[0], kv_ref.at[2], HALF)
    kv_core = sender.start(kv_ref.at[0], kv_ref.at[1], CORE)
    query_ref[...] = dot(normed_ref[...], query_full[...].reshape(width, -1), (1, 0)).astype(BF16)
    sender.arrived(gate_sent)
    up_sent = sender.start(up_own, up_half, FAR)
    sender.arrived(kv_half)
    kv_both = sender.start(kv_ref.at[2], kv_ref.at[3], CORE)
    keep(gate_half, gate_far, 3)
    sender.arrived(table_near)
    sender.start(table_out.at[0], table_out.at[1], CORE)
    sender.arrived(kv_core, kv_both)
    scale = HEAD_DIM ** (-0.5)
    row_count = mask_ref.shape[1] // 4
    attention_heads(scale, pl.ds(0, row_count), mask_ref, query_ref, kv_ref, context_ref)
    sender.arrived(up_sent)
    down_sent = sender.start(down_own, down_half, FAR)
    keep(up_half, up_far, 4)
    keep(down_own, down_near, 2)
    attention_heads(scale, pl.ds(row_count, row_count), mask_ref, query_ref, kv_ref, context_ref)
    sender.arrived(*cots)
    sender.start(cot_out.at[0], cot_out.at[1], CORE)
    sender.arrived(down_sent)
    keep(down_half, down_far, 5)
    for copy in copies[2:]:
        copy.wait()
    sender.finish()


def begin(tokens, query_proj, kv_proj, gains, place, masks, experts, cot, table):
    shape = jax.ShapeDtypeStruct
    rows, width = tokens.shape
    shards = (query_proj, kv_proj, gains)
    halves = [(2,) + w.shape[1:] for w in experts]
    full = lambda w: (2,) * 5 + w.shape
    return pl.pallas_call(
        begin_kernel,
        in_specs=[VMEM] * 11,
        out_specs=[VMEM] * 7 + [ANYWHERE] * 8,
        out_shape=[
            shape(full(query_proj), BF16),
            shape(full(kv_proj), BF16),
            shape((8, width), F32),
            shape((rows, width), BF16),
            shape((rows, query_proj.shape[1]), BF16),
            shape((4, rows, kv_proj.shape[1]), BF16),
            shape((rows, query_proj.shape[1]), BF16),
            *[shape((2, *h), BF16) for h in halves] * 2,
            shape((2, 2, 2) + cot.shape, cot.dtype),
            shape((2, 2, 2) + table.shape, table.dtype),
        ],
        scratch_shapes=[
            pltpu.VMEM(full(gains), F32),
            *[pltpu.VMEM(h, BF16) for h in halves] * 2,
            *semaphores(52),
            pltpu.SemaphoreType.DMA((8,)),
        ],
        compiler_params=pltpu.CompilerParams(
            collective_id=0, has_side_effects=True, vmem_limit_bytes=60 << 20
        ),
        name="begin",
    )(tokens, *shards, place, masks, *experts, cot, table)


def spread_kernel(value_ref, out, send, recv, local):
    copy = pltpu.make_async_copy(value_ref, out.at[0, 0, 0], local.at[0])
    copy.start()
    meet((CORE, SIDE, NEAR))
    sender = Sender(send, recv)
    firsts = (
        (sender.start(value_ref.at[0], out.at[0, 0, 1, 0], SIDE), (0, 0, 1, 0), NEAR, (0, 1, 1, 0)),
        (sender.start(value_ref.at[1], out.at[0, 1, 0, 1], NEAR), (0, 1, 0, 1), SIDE, (0, 1, 1, 1)),
    )
    seconds = [
        (sender.start(value_ref.at[0], out.at[0, 1, 0, 0], NEAR), (0, 1, 0, 0)),
        (sender.start(value_ref.at[1], out.at[0, 0, 1, 1], SIDE), (0, 0, 1, 1)),
    ]
    sender.start(value_ref, out.at[1, 0, 0], CORE)
    for number, at, partner, to in firsts:
        sender.arrived(number)
        seconds.append((sender.start(out.at[at], out.at[to], partner), to))
        sender.start(out.at[at], out.at[(1, *at[1:])], CORE)
    for number, at in seconds:
        sender.arrived(number)
        sender.start(out.at[at], out.at[(1, *at[1:])], CORE)
    copy.wait()
    sender.finish()


def spread(value):
    out = pl.pallas_call(
        spread_kernel,
        in_specs=[VMEM],
        out_specs=ANYWHERE,
        out_shape=jax.ShapeDtypeStruct((2, 2, 2) + value.shape, value.dtype),
        scratch_shapes=[*semaphores(13), pltpu.SemaphoreType.DMA((1,))],
        compiler_params=pltpu.CompilerParams(collective_id=2, has_side_effects=True),
        name="spread",
    )(value)
    return out.reshape((8,) + value.shape)


def collecting(sender, parts, core_recv, axis_recv, done):
    orders = ((parts[0], (NEAR, SIDE), (2, 3, 1, 0)), (parts[1], (SIDE, NEAR), (1, 3, 2, 0)))
    numbers, landing = {}, {}
    for place in range(4):
        for m, (ref, _, order) in enumerate(orders):
            b = order[place]
            numbers[m, b] = sender.start(ref.at[4 + b], core_recv.at[m, b], CORE)
    yield
    for place in range(2):
        for m, (ref, axes, order) in enumerate(orders):
            b = order[place]
            sender.arrived(numbers[m, b])
            core_recv[m, b] = ref[b] + core_recv[m, b]
            landing[m, place] = sender.start(core_recv.at[m, b], axis_recv.at[m, place], axes[0])
    yield
    for m, (ref, axes, order) in enumerate(orders):
        b = order[2]
        sender.arrived(numbers[m, b], landing[m, 1])
        total = ref[b].astype(F32) + core_recv[m, b].astype(F32) + axis_recv[m, 1].astype(F32)
        core_recv[m, b] = total.astype(BF16)
        landing[m, 2] = sender.start(core_recv.at[m, b], axis_recv.at[m, 2], axes[1])
    yield
    for m, (ref, _, order) in enumerate(orders):
        sender.arrived(numbers[m, 0], landing[m, 0], landing[m, 2])
        total = ref[0].astype(F32) + core_recv[m, 0].astype(F32)
        done(m, total + axis_recv[m, 0].astype(F32) + axis_recv[m, 2].astype(F32))


def collecting_spaces(block):
    return [pltpu.VMEM((2, 4, *block), BF16), pltpu.VMEM((2, 3, *block), BF16)]


def collect_kernel(
    first_ref, second_ref, normed_ref, cot_ref, wide_ref, down_ref,
    grad_ref, hidden_ref, pre_ref, out_ref, core_recv, axis_recv, send, recv,
):
    meet((CORE, SIDE, NEAR))
    sender = Sender(send, recv)
    width = down_ref.shape[0]
    row_count = first_ref.shape[1]

    def done(m, total):
        rows = pl.ds(m * row_count, row_count)
        grad_ref[rows, :] = grad_ref[rows, :] + total

    parts = collecting(sender, (first_ref, second_ref), core_recv, axis_recv, done)
    next(parts)
    pre_gate = dot(normed_ref[...], wide_ref[:, :width], (1, 0))
    pre_up = dot(normed_ref[...], wide_ref[:, width:], (1, 0))
    next(parts)
    act, deriv = silu_parts(pre_gate)
    hidden_ref[...] = (act * pre_up).astype(BF16)
    grad_hidden = dot(cot_ref[...], down_ref[...], (1, 1))
    pre_ref[:, :width] = (grad_hidden * pre_up * deriv).astype(BF16)
    pre_ref[:, width:] = (grad_hidden * act).astype(BF16)
    out_ref[...] = dot(hidden_ref[...], down_ref[...], (1, 0)).astype(out_ref.dtype)
    grad_ref[...] = dot(pre_ref[...], wide_ref[...], (1, 1))
    for _ in parts:
        pass
    sender.finish()


def collect(first, second, normed, cot, wide, down):
    block = first.shape[1:]
    rows, model_width = normed.shape
    shape = jax.ShapeDtypeStruct
    return pl.pallas_call(
        collect_kernel,
        in_specs=[VMEM] * 6,
        out_specs=[VMEM] * 4,
        out_shape=[
            shape((rows, model_width), F32),
            shape((rows, down.shape[0]), BF16),
            shape((rows, wide.shape[1]), BF16),
            shape((rows, model_width), F32),
        ],
        scratch_shapes=[*collecting_spaces(block), *semaphores(14)],
        compiler_params=pltpu.CompilerParams(
            collective_id=3, has_side_effects=True, vmem_limit_bytes=63 << 20
        ),
        name="collect",
    )(first, second, normed, cot, wide, down)


def back_kernel(
    mask_ref, query_ref, kv_ref, grad_ref, near_wide, near_down, far_wide, far_down, shared_ref,
    grad_query_ref, grad_kv_ref, wide_out, down_out, shared_out,
    part_ref, kv_core, kv_send, kv_half, far_wide_recv, far_down_recv, near_wide_recv, near_down_recv,
    wide_send, down_send, wide_recv, down_recv, wide_core, down_core, wide_own, down_own, *refs,
):
    spaces, (send, recv) = refs[:-2], refs[-2:]
    core, half = bit_of(CORE), bit_of(HALF)
    scale = HEAD_DIM ** (-0.5)
    row_count = mask_ref.shape[1] // 4

    def heads(micro):
        rows = pl.ds(micro * row_count, row_count)
        allowed = mask_ref[rows, :] > 0

        def head(h, _):
            at = pl.ds(pl.multiple_of(h * HEAD_DIM, HEAD_DIM), HEAD_DIM)
            value_at = pl.ds(pl.multiple_of((h + KV_HEADS) * HEAD_DIM, HEAD_DIM), HEAD_DIM)
            keys = jnp.concatenate([kv_ref[j, rows, at] for j in range(4)])
            values = jnp.concatenate([kv_ref[j, rows, value_at] for j in range(4)])
            grad_keys = grad_values = 0.0
            for g in range(GROUP_HEADS):
                lanes = pl.ds(pl.multiple_of((h * GROUP_HEADS + g) * HEAD_DIM, HEAD_DIM), HEAD_DIM)
                query, grad = query_ref[rows, lanes], grad_ref[rows, lanes]
                weights = masked_softmax(query, keys, allowed, scale)
                grad_weights = dot(grad, values, (1, 1))
                delta = jnp.sum(weights * grad_weights, axis=1, keepdims=True)
                grad_scores = (weights * (grad_weights - delta)).astype(BF16)
                grad_query_ref[rows, lanes] = (dot(grad_scores, keys, (1, 0)) * scale).astype(BF16)
                grad_keys = grad_keys + dot(query, grad_scores, (0, 0))
                grad_values = grad_values + dot(grad, weights.astype(BF16), (0, 0))
            grad_keys = (grad_keys * scale).T.astype(BF16)
            grad_values = grad_values.T.astype(BF16)
            for j in range(4):
                part_ref[j, rows, at] = grad_keys[j * row_count : (j + 1) * row_count]
                part_ref[j, rows, value_at] = grad_values[j * row_count : (j + 1) * row_count]
            return 0

        lax.fori_loop(0, KV_HEADS, head, 0)

    def add(*values):
        total = values[0][...].astype(F32)
        for value in values[1:]:
            total = total + value[...].astype(F32)
        return total

    meet(AXES)
    sender = Sender(send, recv)
    other = 1 - half
    across = [sender.start(far_wide.at[other, 0], far_wide_recv.at[0], HALF)]
    order = (CORE, SIDE, HALF, FAR, NEAR)
    shared = halving(sender, shared_ref, spaces, order, shared_out, slice(None))
    next(shared)
    heads(0)
    next(shared)
    across.append(sender.start(far_wide.at[other, 1], far_wide_recv.at[1], HALF))
    fars = []
    for q in range(2):
        if q:
            heads(1)
            next(shared)
            kv_sums = [sender.start(part_ref.at[2 * j + 1], kv_core.at[j], CORE) for j in range(2)]
        sender.arrived(across[q])
        wide_send[q] = add(far_wide[half, q], far_wide_recv[q]).astype(BF16)
        fars.append(sender.start(wide_send.at[q], wide_recv.at[q], FAR))
    far_last = sender.start(far_down.at[other], far_down_recv, HALF)
    sender.arrived(*kv_sums)
    kv_send[...] = add(part_ref[2], kv_core[1]).astype(BF16)
    kv_last = sender.start(kv_send, kv_half, HALF)
    near = [sender.start(near_wide.at[other], near_wide_recv, HALF)]
    sender.arrived(far_last)
    down_send[...] = add(far_down[half], far_down_recv).astype(BF16)
    fars.append(sender.start(down_send, down_recv, FAR))
    near.append(sender.start(near_down.at[other], near_down_recv, HALF))
    next(shared)
    sender.arrived(kv_last)
    grad_kv_ref[...] = add(part_ref[0], kv_core[0], kv_half[...]).astype(BF16)
    sender.arrived(*near, *fars[:2])
    next(shared)

    def finish(near_ref, near_recv, far_recv, own_ref, core_ref, out_ref):
        own_ref[...] = add(near_ref[half, 1 - core], near_recv[1 - core], far_recv[1 - core]).astype(BF16)
        number = sender.start(own_ref, core_ref, CORE)
        out_ref[core] = add(near_ref[half, core], near_recv[core], far_recv[core])
        return number

    wide_last = finish(near_wide, near_wide_recv, wide_recv, wide_own, wide_core, wide_out)
    sender.arrived(wide_last)
    wide_out[1 - core] = wide_core[...].astype(F32)
    sender.arrived(*fars)
    down_last = finish(near_down, near_down_recv, down_recv, down_own, down_core, down_out)
    sender.arrived(down_last)
    down_out[1 - core] = down_core[...].astype(F32)
    for _ in shared:
        pass
    sender.finish()


def back(masks, queries, kv, grad, near_wide, near_down, far_wide, far_down, shared):
    shape = jax.ShapeDtypeStruct
    rows, width = kv.shape[1:]
    wide, down = near_wide.shape[1:], near_down.shape[1:]
    space = lambda *dims: pltpu.VMEM(dims, BF16)
    return pl.pallas_call(
        back_kernel,
        in_specs=[VMEM] * 9,
        out_specs=[VMEM] * 5,
        out_shape=[
            shape(queries.shape, BF16),
            shape((rows, width), BF16),
            shape((2,) + wide[1:], F32),
            shape((2,) + down[1:], F32),
            shape(shared.shape[5:], F32),
        ],
        scratch_shapes=[
            space(4, rows, width),
            space(2, rows, width),
            space(rows, width),
            space(rows, width),
            *[space(*wide), space(*down)] * 4,
            *[space(*wide[1:]), space(*down[1:])] * 2,
            *[space(*(2,) * left, *shared.shape[5:]) for left in range(4, -1, -1)],
            *semaphores(19),
        ],
        compiler_params=pltpu.CompilerParams(
            collective_id=5, has_side_effects=True, vmem_limit_bytes=62 << 20
        ),
        name="back",
    )(masks, queries, kv, grad, near_wide, near_down, far_wide, far_down, shared)


def halving(sender, value, spaces, order, out, columns):
    left = list(AXES)
    for partner, landing in zip(order, spaces):
        place = left.index(partner)
        left.pop(place)
        rest = (slice(None),) * (len(left) - place + 1)
        at = lambda bit: (*(slice(None),) * place, bit, *rest, columns)
        into = (*(slice(None),) * (len(left) + 1), columns)
        own = bit_of(partner)
        number = sender.start(value.at[at(1 - own)], landing.at[into], partner)
        yield
        sender.arrived(number)
        if left:
            landing[into] = value[at(own)] + landing[into]
            value = landing
        else:
            out[into] = value[at(own)].astype(F32) + landing[into].astype(F32)


def reduce_kernel(*refs):
    values, parts, outs, part_out = refs[:3], refs[3:5], refs[5:8], refs[8]
    spaces, (core_recv, axis_recv, send, recv) = refs[9:-4], refs[-4:]

    def done(m, total):
        part_out[m] = total

    meet(AXES)
    sender = Sender(send, recv)
    orders = (
        (CORE, HALF, FAR, NEAR, SIDE),
        (CORE, SIDE, HALF, FAR, NEAR),
        (CORE, HALF, SIDE, FAR, NEAR),
    )
    steps = {}
    for i, (value, order) in enumerate(zip(values, orders)):
        cut, width = value.shape[-1] // 256 * 128, value.shape[-1]
        space = spaces[5 * i : 5 * i + 5]
        steps[i, 0] = halving(sender, value, space, order, outs[i], pl.ds(0, cut))
        steps[i, 1] = halving(sender, value, space, order, outs[i], pl.ds(cut, width - cut))
    collected = collecting(sender, parts, core_recv, axis_recv, done)
    in_turn([steps[1, 0], steps[1, 1], steps[0, 0], steps[2, 0], steps[0, 1], steps[2, 1], collected])
    sender.finish()


def reduce_dense(values, parts):
    blocks, scratch = [], []
    for value in values:
        rows = value.shape[0] // 32
        blocks.append(value.reshape((2,) * 5 + (rows, -1)).astype(BF16))
        scratch += [pltpu.VMEM((2,) * left + blocks[-1].shape[5:], BF16) for left in range(4, -1, -1)]
    return pl.pallas_call(
        reduce_kernel,
        in_specs=[VMEM] * 5,
        out_specs=[VMEM] * 4,
        out_shape=[
            *[jax.ShapeDtypeStruct(v.shape[5:], F32) for v in blocks],
            jax.ShapeDtypeStruct((2, *parts[0].shape[1:]), F32),
        ],
        scratch_shapes=[*scratch, *collecting_spaces(parts[0].shape[1:]), *semaphores(44)],
        compiler_params=pltpu.CompilerParams(
            collective_id=6, has_side_effects=True, vmem_limit_bytes=63 << 20
        ),
        name="reduce_dense",
    )(*blocks, *parts)


def attention_back(micro, masks, queries, kv, grad):
    row_count = grad.shape[0]
    wide = GROUP_HEADS * HEAD_DIM
    heads = lambda at: pl.BlockSpec((4, row_count, HEAD_DIM), lambda h: (0, micro, h + at))
    column = pl.BlockSpec((4, row_count, HEAD_DIM), lambda h: (0, 0, h))
    flat = jax.ShapeDtypeStruct((4, row_count, KV_HEADS * HEAD_DIM), BF16)
    return pl.pallas_call(
        functools.partial(attention_back_kernel, HEAD_DIM ** (-0.5)),
        grid=(KV_HEADS,),
        in_specs=[
            pl.BlockSpec((row_count, 4 * row_count), lambda h: (micro, 0)),
            pl.BlockSpec((row_count, wide), lambda h: (micro, h)),
            heads(0),
            heads(KV_HEADS),
            pl.BlockSpec((row_count, wide), lambda h: (0, h)),
        ],
        out_specs=[pl.BlockSpec((row_count, wide), lambda h: (0, h)), column, column],
        out_shape=[jax.ShapeDtypeStruct((row_count, HEADS * HEAD_DIM), BF16), flat, flat],
        compiler_params=pltpu.CompilerParams(vmem_limit_bytes=48 << 20),
        name="attention_back",
    )(masks, queries, kv, kv, grad)


def expert_kernel(
    slot_ref, scale_ref, column_ref, token_ref, cot_ref, *refs
):
    count = column_ref.shape[0]
    gate_refs, up_refs, down_refs = refs[:count], refs[count : 2 * count], refs[2 * count : 3 * count]
    rows_ref, cots_ref, hidden_ref, pre_ref, mixed_ref, graded_ref = refs[-10:-4]
    pick_ref, value_ref, extra_ref, back_ref = refs[-4:]
    width = down_refs[0].shape[0]
    blocks, row_count = token_ref.shape[0], token_ref.shape[2]
    room = rows_ref.shape[2] // blocks
    slot = lax.broadcasted_iota(jnp.int32, (room, row_count), 0)
    gates = []
    for b in range(blocks):
        for k in range(count):
            picked = slot == slot_ref[k, b]
            gates.append(jnp.sum(jnp.where(picked, scale_ref[k, b], 0.0), axis=1, keepdims=True))
            pick_ref[b, k * room : (k + 1) * room, :] = jnp.where(picked, 1.0, 0.0).astype(BF16)
        rows = dot(pick_ref[b], token_ref[b, 0], (1, 0)).astype(BF16)
        cots = dot(pick_ref[b], cot_ref[b, 0], (1, 0)).astype(BF16)
        for k in range(count):
            part = slice(b * room, (b + 1) * room)
            rows_ref[k, 0, part, :] = rows[k * room : (k + 1) * room]
            cots_ref[k, 0, part, :] = cots[k * room : (k + 1) * room]
    for k in range(count):
        gate = jnp.concatenate([gates[b * count + k] for b in range(blocks)])
        pre_gate = dot(rows_ref[k, 0], gate_refs[k][...], (1, 0))
        pre_up = dot(rows_ref[k, 0], up_refs[k][...], (1, 0))
        grad_hidden = dot(cots_ref[k, 0], down_refs[k][...], (1, 1))
        act, deriv = silu_parts(pre_gate)
        hidden = act * pre_up
        gate_grad = jnp.sum(hidden * grad_hidden, axis=1, keepdims=True)
        grad_hidden = grad_hidden * gate
        hidden_ref[k, 0] = (hidden * gate).astype(BF16)
        pre_ref[k, 0, :, :width] = (grad_hidden * pre_up * deriv).astype(BF16)
        pre_ref[k, 0, :, width:] = (grad_hidden * act).astype(BF16)
        value = dot(hidden_ref[k, 0], down_refs[k][...], (1, 0)).astype(BF16)
        back = dot(pre_ref[k, 0, :, :width], gate_refs[k][...], (1, 1))
        back = (back + dot(pre_ref[k, 0, :, width:], up_refs[k][...], (1, 1))).astype(BF16)
        extra = (gate_grad * column_ref[k]).astype(BF16)
        for b in range(blocks):
            to, part = slice(k * room, (k + 1) * room), slice(b * room, (b + 1) * room)
            value_ref[b, to, :] = value[part]
            back_ref[b, to, :] = back[part]
            extra_ref[b, to, :] = extra[part]
    model_width = token_ref.shape[3]
    for b in range(blocks):
        graded_ref[b] = dot(pick_ref[b], back_ref[b], (0, 0)).astype(BF16)
        mixed_ref[b, :, :model_width] = dot(pick_ref[b], value_ref[b], (0, 0)).astype(BF16)
        mixed_ref[b, :, model_width:] = dot(pick_ref[b], extra_ref[b], (0, 0)).astype(BF16)


def expert_pass(micro, slots, scales, columns, tokens, cots, gates, ups, downs, room, kept):
    count, (width, model_width) = len(downs), downs[0].shape
    blocks, micro_count, row_count = tokens.shape[:3]
    step = 2
    by_block = lambda *dims: pl.BlockSpec((step, *dims), lambda b: (b,) + (0,) * len(dims))
    by_slot = pl.BlockSpec((count, step, 1, row_count), lambda b: (0, b, 0, 0))
    whole = lambda *dims: pl.BlockSpec(dims, lambda b: (0,) * len(dims), pipeline_mode=pl.Buffered(1))
    saved = lambda cols: pl.BlockSpec((count, 1, step * room, cols), lambda b: (0, micro, b, 0))
    widths = (model_width, model_width, width, 2 * width)
    shapes = [jax.ShapeDtypeStruct((count, micro_count, blocks * room, w), BF16) for w in widths]
    args = [slots, scales, columns, tokens, cots, *gates, *ups, *downs]
    in_specs = [
        by_slot,
        by_slot,
        whole(count, 1, 128),
        pl.BlockSpec((step, 1, row_count, model_width), lambda b: (b, micro, 0, 0)),
        pl.BlockSpec((step, 1, row_count, model_width), lambda b: (b, micro, 0, 0)),
        *[whole(model_width, width)] * (2 * count),
        *[whole(width, model_width)] * count,
    ]
    aliases = {}
    if kept:
        aliases = {len(args) + i: i for i in range(len(kept))}
        in_specs += [pl.BlockSpec(memory_space=pl.ANY)] * len(kept)
        args += list(kept)
    out = pl.pallas_call(
        expert_kernel,
        grid=(blocks // step,),
        in_specs=in_specs,
        out_specs=[saved(w) for w in widths]
        + [by_block(row_count, model_width + 128), by_block(row_count, model_width)],
        out_shape=shapes
        + [
            jax.ShapeDtypeStruct((blocks, row_count, model_width + 128), BF16),
            jax.ShapeDtypeStruct((blocks, row_count, model_width), BF16),
        ],
        scratch_shapes=[
            pltpu.VMEM((step, count * room, row_count), BF16),
            pltpu.VMEM((step, count * room, model_width), BF16),
            pltpu.VMEM((step, count * room, 128), BF16),
            pltpu.VMEM((step, count * room, model_width), BF16),
        ],
        input_output_aliases=aliases,
        compiler_params=pltpu.CompilerParams(vmem_limit_bytes=60 << 20),
        name="experts",
    )(*args)
    return out[:4], out[4], out[5]


def attend_plain(queries, kv, masks, micro):
    row_count = masks.shape[1] // 4
    rows = slice(micro * row_count, (micro + 1) * row_count)
    allowed = masks[rows] > 0
    wide = KV_HEADS * HEAD_DIM
    heads = queries[rows].reshape(row_count, KV_HEADS, GROUP_HEADS, HEAD_DIM)
    keys = kv[:, rows, :wide].reshape(-1, KV_HEADS, HEAD_DIM)
    values = kv[:, rows, wide:].reshape(-1, KV_HEADS, HEAD_DIM)
    scores = mm("ikgd,jkd->kgij", heads, keys) * HEAD_DIM ** (-0.5)
    row_max = jnp.max(jnp.where(allowed, scores, NEGATIVE), axis=3, keepdims=True)
    expo = jnp.where(allowed, jnp.exp(jnp.where(allowed, scores, NEGATIVE) - row_max), 0.0)
    total = jnp.sum(expo, axis=3, keepdims=True)
    weights = (expo / jnp.where(total > 0.5, total, 1.0)).astype(BF16)
    return mm("kgij,jkd->ikgd", weights, values).reshape(row_count, HEADS * HEAD_DIM).astype(BF16)


def on_device(
    tokens,
    segment_ids,
    routes,
    route_gates,
    attn_gain,
    query_proj,
    key_proj,
    value_proj,
    output_proj,
    ffn_gain,
    shared_gate,
    shared_up,
    shared_down,
    expert_gate,
    expert_up,
    expert_down,
    output_cot,
):
    micro_count, row_count, model_width = tokens.shape
    exp_count = lax.axis_size("exp")
    local_experts, gate_rows, expert_width = expert_gate.shape
    down_rows = expert_down.shape[1]
    all_experts = local_experts * exp_count
    route_count = routes.shape[2]
    capacity = 4 * row_count * route_count // (3 * all_experts)
    query_width = HEADS * HEAD_DIM
    kv_width = KV_HEADS * HEAD_DIM
    far_steps = exp_count // 4
    assert lax.axis_size("seq") == 4 and local_experts == 2

    seq_index = lax.axis_index("seq")
    exp_index = lax.axis_index("exp")
    core = seq_index % 2
    half = seq_index // 2
    everywhere = ("seq", "exp")

    linked = exp_count == 8
    expert_range = jnp.arange(all_experts, dtype=jnp.int32)
    gate_table = jnp.sum(
        jnp.where(
            jnp.swapaxes(routes, 1, 2)[:, :, None, :] == expert_range[None, None, :, None],
            jnp.swapaxes(route_gates, 1, 2)[:, :, None, :],
            0.0,
        ),
        axis=1,
    )
    order = jnp.arange(row_count, dtype=jnp.int32)
    before = (order[:, None] < order[None, :]).astype(BF16)
    slots = jnp.arange(capacity, dtype=jnp.int32)
    expert_ids = [
        local_experts * ((exp_index - 4 * k + exp_count) % exp_count) + core
        for k in range(far_steps)
    ]
    kv_proj = jnp.concatenate([key_proj, value_proj], axis=1)
    shared_wide = jnp.concatenate([shared_gate, shared_up], axis=1)

    def gathered(value):
        return lax.all_gather(value, everywhere, axis=0, tiled=True)

    def mask_of(micro):
        segments = segment_ids[micro].reshape(4, row_count)
        key_ids = jnp.concatenate(
            [lax.dynamic_index_in_dim(segments, seq_index ^ j, 0, False) for j in range(4)]
        )
        key_pos = jnp.concatenate([(seq_index ^ j) * row_count + order for j in range(4)])
        query_ids, query_pos = key_ids[:row_count], key_pos[:row_count]
        allowed = (
            (key_ids[None, :] == query_ids[:, None])
            & (key_pos[None, :] <= query_pos[:, None])
            & (query_ids[:, None] >= 0)
        )
        return allowed.astype(jnp.int32)

    inputs = tokens.reshape(micro_count * row_count, model_width).astype(F32)
    inv_one = lax.rsqrt(jnp.mean(inputs * inputs, axis=1, keepdims=True) + EPSILON)
    masks = jnp.concatenate([mask_of(micro) for micro in range(micro_count)])
    if linked:
        gains = jnp.stack([attn_gain, ffn_gain]).astype(F32)
        share = gains.shape[1]
        gains = jnp.pad(gains, ((0, 6), (0, 128 - share)))
        lane = jnp.arange(128)[:, None]
        place = (lane == jnp.arange(model_width)[None, :] % share).astype(BF16)
        out = begin(
            tokens.reshape(micro_count * row_count, model_width), query_proj, kv_proj, gains, place, masks,
            (expert_gate, expert_up, expert_down), output_cot, gate_table,
        )
        query_full = out[0].reshape(model_width, query_width)
        kv_full = out[1].reshape(model_width, 2 * kv_width)
        gain_one, gain_two = out[2][0], out[2][1]
        normed_one, queries, kv, contexts = out[3:7]
        gate_all = [w.reshape(model_width, expert_width) for w in (out[7], out[10])]
        up_all = [w.reshape(model_width, expert_width) for w in (out[8], out[11])]
        down_all = [w.reshape(expert_width, model_width) for w in (out[9], out[12])]
        cot_blocks = out[13].reshape(8, micro_count, row_count, model_width)
        gate_blocks = out[14].reshape(8, micro_count, all_experts, row_count)
        out_proj = gathered(output_proj)
        shared_wide, shared_down = after((shared_wide, shared_down), contexts)
    else:
        query_full, kv_full = gathered(query_proj), gathered(kv_proj)
        gain_one, gain_two = gathered(attn_gain).astype(F32), gathered(ffn_gain).astype(F32)
        out_proj = gathered(output_proj)
        normed_one = (inputs * inv_one * gain_one).astype(BF16)
        queries = jnp.dot(normed_one, query_full, preferred_element_type=F32).astype(BF16)
        own = jnp.dot(normed_one, kv_full, preferred_element_type=F32).astype(BF16)
        across = exchange(own, "seq", 2)
        kv = jnp.stack([own, exchange(own, "seq", 1), across, exchange(across, "seq", 1)])
        contexts = jnp.concatenate([attend_plain(queries, kv, masks, m) for m in range(micro_count)])
        gate_blocks = jnp.concatenate(group_gather(gate_table))
        cot_blocks = jnp.concatenate(group_gather(output_cot))

        def parity(value):
            kept = lax.dynamic_index_in_dim(value, core, 0, False)
            sent = lax.dynamic_index_in_dim(value, 1 - core, 0, False)
            return in_order(core, kept, exchange(sent, "seq", 1), 0)

        wide_far = [parity(jnp.concatenate([expert_gate, expert_up], axis=2))]
        down_far = [parity(expert_down)]
        for _ in range(far_steps - 1):
            wide_far.append(rotate(wide_far[-1], "exp", 4))
            down_far.append(rotate(down_far[-1], "exp", 4))
        wide_full = [in_order(half, w, exchange(w, "seq", 2), 0) for w in wide_far]
        down_full = [in_order(half, w, exchange(w, "seq", 2), 0) for w in down_far]

    def sequence_sum(grad_keys, grad_values):
        grad = jnp.concatenate([grad_keys, grad_values], axis=2)
        part = grad[0::2].astype(F32) + exchange(grad[1::2], "seq", 1).astype(F32)
        return (part[0] + exchange(part[1].astype(BF16), "seq", 2).astype(F32)).astype(BF16)

    kept_rows = []

    def experts(micro, normed_blocks):
        gates = jnp.stack(
            [lax.dynamic_index_in_dim(gate_blocks[:, micro], e, 1, False) for e in expert_ids]
        )
        named = gates > 0.0
        rank = mm("kbs,st->kbt", named.astype(BF16), before).astype(jnp.int32)
        slot = jnp.where(named, rank, -1)
        if not linked:
            return experts_plain(gates, slot, normed_blocks[:, micro], cot_blocks[:, micro])
        columns = (
            lax.broadcasted_iota(jnp.int32, (far_steps, 1, 128), 2)
            == jnp.stack(expert_ids)[:, None, None]
        ).astype(F32)
        kept, mixed, graded = expert_pass(
            micro, slot[:, :, None], gates[:, :, None], columns,
            normed_blocks, cot_blocks, gate_all, up_all, down_all, capacity, kept_rows,
        )
        kept_rows[:] = kept
        return graded, mixed

    def experts_plain(gates, slot, normed_blocks, micro_cots):
        mixed, graded, kept = 0.0, 0.0, []
        for k in range(far_steps):
            picked = slot[k][:, None, :] == slots[None, :, None]
            pick = picked.astype(BF16)
            slot_gates = jnp.sum(jnp.where(picked, gates[k][:, None, :], 0.0), axis=2).reshape(-1, 1)
            rows = mm("bst,btd->bsd", pick, normed_blocks).astype(BF16).reshape(-1, model_width)
            cots = mm("bst,btd->bsd", pick, micro_cots).astype(BF16).reshape(-1, model_width)
            pre = jnp.dot(rows, wide_full[k], preferred_element_type=F32)
            pre_gate, pre_up = pre[:, :expert_width], pre[:, expert_width:]
            grad_hidden = mm("rd,fd->rf", cots, down_full[k])
            act, deriv = silu_parts(pre_gate)
            hidden = act * pre_up
            gate_grad = jnp.sum(hidden * grad_hidden, axis=1, keepdims=True)
            hidden = (hidden * slot_gates).astype(BF16)
            grad_hidden = grad_hidden * slot_gates
            grad_pre = jnp.concatenate(
                [(grad_hidden * pre_up * deriv).astype(BF16), (grad_hidden * act).astype(BF16)], axis=1
            )
            value = jnp.dot(hidden, down_full[k], preferred_element_type=F32).astype(BF16)
            column = (lax.broadcasted_iota(jnp.int32, (1, 128), 1) == expert_ids[k]).astype(F32)
            value = jnp.concatenate([value, (gate_grad * column).astype(BF16)], axis=1)
            grad_rows = mm("rf,df->rd", grad_pre, wide_full[k]).astype(BF16)
            blocks = pick.shape[0]
            mixed = mixed + mm("bst,bsd->btd", pick, value.reshape(blocks, capacity, -1))
            graded = graded + mm("bst,bsd->btd", pick, grad_rows.reshape(blocks, capacity, -1))
            kept.append((rows, cots, hidden, grad_pre))
        kept_rows.append(kept)
        return graded.astype(BF16), mixed.astype(BF16)

    up_proj, down_proj = gathered(shared_wide), gathered(shared_down)
    residual = inputs + jnp.dot(contexts, out_proj, preferred_element_type=F32)
    inv_two = lax.rsqrt(jnp.mean(residual * residual, axis=1, keepdims=True) + EPSILON)
    normed_two = (residual * inv_two * gain_two).astype(BF16)
    per_micro = normed_two.reshape(micro_count, row_count, model_width)
    token_blocks = spread(per_micro) if linked else jnp.concatenate(group_gather(per_micro))

    graded_parts, mixed_parts = [], []
    for micro in range(micro_count):
        graded, mixed = experts(micro, token_blocks)
        if not linked:
            graded = group_scatter(graded[:4], graded[4:])
            mixed = group_scatter(mixed[:4], mixed[4:])
            graded, mixed, token_blocks = lax.optimization_barrier((graded, mixed, token_blocks))
        graded_parts.append(graded)
        mixed_parts.append(mixed)

    upstream_low = output_cot.reshape(micro_count * row_count, model_width)
    shared_width = shared_gate.shape[1]
    if linked:
        grad_normed, shared_hidden, grad_shared_pre, shared_out = collect(
            *graded_parts, normed_two, upstream_low, up_proj, down_proj
        )
    else:
        shared_pre = jnp.dot(normed_two, up_proj, preferred_element_type=F32)
        shared_pre_gate, shared_pre_up = shared_pre[:, :shared_width], shared_pre[:, shared_width:]
        shared_act, shared_deriv = silu_parts(shared_pre_gate)
        shared_hidden = (shared_act * shared_pre_up).astype(BF16)
        shared_out = jnp.dot(shared_hidden, down_proj, preferred_element_type=F32)
        grad_shared_hidden = mm("rd,fd->rf", upstream_low, down_proj)
        grad_shared_pre = jnp.concatenate(
            [
                (grad_shared_hidden * shared_pre_up * shared_deriv).astype(BF16),
                (grad_shared_hidden * shared_act).astype(BF16),
            ],
            axis=1,
        )
        grad_from_shared = mm("rf,df->rd", grad_shared_pre, up_proj)
        grad_normed = jnp.concatenate(graded_parts) + grad_from_shared

    def summed(value):
        return lax.psum_scatter(
            value.astype(BF16), everywhere, scatter_dimension=0, tiled=True
        ).astype(F32)

    shared_up_sum = summed(mm("rd,rf->df", normed_two, grad_shared_pre))
    shared_down_sum = mm("rd,rf->df", shared_hidden, upstream_low)

    def flat(value):
        return value.reshape(micro_count * row_count, -1)

    grad_from_two, gain_two_sum = norm_back(grad_normed, residual, inv_two, gain_two)
    grad_residual = upstream_low.astype(F32) + grad_from_two
    grad_branch = grad_residual.astype(BF16)
    grad_context = mm("rd,id->ri", grad_branch, out_proj).astype(BF16)
    output_sum = mm("rd,rf->df", contexts, grad_branch)

    def expert_sum(left, right):
        own = None
        for k in reversed(range(far_steps)):
            lefts = jnp.concatenate([m[k][left] for m in kept_rows])
            rights = jnp.concatenate([m[k][right] for m in kept_rows])
            if own is not None:
                lefts, rights, own = lax.optimization_barrier((lefts, rights, own))
            total = mm("rd,rf->df", lefts, rights)
            rows = total.shape[0] // 2
            total = total.reshape(2, rows, -1)
            mine = lax.dynamic_index_in_dim(total, half, 0, False)
            sent = lax.dynamic_index_in_dim(total, 1 - half, 0, False).astype(BF16)
            total = mine + exchange(sent, "seq", 2).astype(F32)
            own = total if own is None else total + rotate(own.astype(BF16), "exp", -4).astype(F32)
        rows = own.shape[0] // 2
        own = own.reshape(2, rows, -1)
        kept = lax.dynamic_index_in_dim(own, core, 0, False)
        sent = lax.dynamic_index_in_dim(own, 1 - core, 0, False).astype(BF16)
        other = exchange(sent, "seq", 1).astype(F32)
        return in_order(core, kept[None], other[None], 0)

    if linked:
        products = []
        for k in range(far_steps):
            for left, right in ((0, 3), (2, 1)):
                total = mm("mrd,mrf->df", kept_rows[left][k], kept_rows[right][k]).astype(BF16)
                products.append(total.reshape(2, 2, total.shape[0] // 4, -1))
        blocks = shared_down_sum.astype(BF16).reshape((2,) * 5 + shared_down.shape)
        grad_query, grad_kv, wide_grad, down_grad, shared_down_sum = back(
            masks, queries, kv, grad_context, *products, blocks
        )
    else:
        shared_down_sum = summed(shared_down_sum)
        down_grad = expert_sum(2, 1)
        down_grad, kept_rows = lax.optimization_barrier((down_grad, kept_rows))
        wide_grad = expert_sum(0, 3)
        grad_queries, grad_kvs = [], []
        for micro in range(micro_count):
            rows = slice(micro * row_count, (micro + 1) * row_count)
            grad_query, grad_keys, grad_values = attention_back(
                micro, masks, queries, kv, grad_context[rows]
            )
            grad_queries.append(grad_query)
            grad_kvs.append(sequence_sum(grad_keys, grad_values))
        grad_query, grad_kv = jnp.concatenate(grad_queries), jnp.concatenate(grad_kvs)

    grad_normed_one = mm("ri,di->rd", grad_query, query_full) + mm("ri,di->rd", grad_kv, kv_full)
    grad_from_one, gain_one_sum = norm_back(grad_normed_one, inputs, inv_one, gain_one)
    token_grads = (grad_residual + grad_from_one).astype(BF16)
    column = lax.broadcasted_iota(jnp.int32, (1, 2 * kv_width + 128), 1)
    query_sum = mm("rd,rf->df", normed_one, grad_query)
    kv_sum = mm("rd,rf->df", normed_one, jnp.pad(grad_kv, ((0, 0), (0, 128))))
    kv_sum = jnp.where(column == 2 * kv_width, gain_one_sum[:, None], kv_sum)
    kv_sum = jnp.where(column == 2 * kv_width + 1, gain_two_sum[:, None], kv_sum)
    if linked:
        output_sum, query_sum, kv_sum, moe_outs = reduce_dense((output_sum, query_sum, kv_sum), mixed_parts)
        moe_outs = flat(moe_outs)
    else:
        output_sum, query_sum, kv_sum = summed(output_sum), summed(query_sum), summed(kv_sum)
        moe_outs = jnp.concatenate(mixed_parts)
    outputs = (residual + shared_out + moe_outs[:, :model_width]).astype(BF16)
    table = moe_outs[:, model_width : model_width + all_experts]
    gate_grads = jnp.sum(
        jnp.where(flat(routes)[:, :, None] == expert_range[None, None, :], table[:, None, :], 0.0),
        axis=2,
    )

    return (
        outputs.reshape(tokens.shape),
        token_grads.reshape(tokens.shape),
        gate_grads.reshape(routes.shape),
        kv_sum[:, 2 * kv_width],
        query_sum,
        kv_sum[:, :kv_width],
        kv_sum[:, kv_width : 2 * kv_width],
        output_sum,
        kv_sum[:, 2 * kv_width + 1],
        shared_up_sum[:, :shared_width],
        shared_up_sum[:, shared_width:],
        shared_down_sum,
        wide_grad[:, :, :expert_width],
        wide_grad[:, :, expert_width:],
        down_grad,
    )


def solution(mesh):
    rows = P(("seq", "exp"), None)
    wide = P("exp", "seq", None)
    flat = P(("seq", "exp"))
    return jax.shard_map(
        on_device,
        mesh=mesh,
        in_specs=(wide, P("exp", None), wide, wide, flat, rows, rows, rows, rows, flat, rows, rows, rows)
        + (wide,) * 4,
        out_specs=(wide, wide, wide, flat, rows, rows, rows, rows, flat, rows, rows, rows)
        + (wide,) * 3,
        check_vma=False,
    )
```

```python
import functools

import jax
import jax.numpy as jnp
from jax import lax
from jax.experimental import pallas as pl
from jax.experimental.pallas import tpu as pltpu
from jax.sharding import PartitionSpec as P

HEADS = 12
KV_HEADS = 4
HEAD_DIM = 128
GROUP_HEADS = HEADS // KV_HEADS
EPSILON = 1e-05
NEGATIVE = -1e30
F32 = jnp.float32
BF16 = jnp.bfloat16


def mm(spec, left, right):
    return jnp.einsum(spec, left, right, preferred_element_type=F32)


def exchange(value, axis, bit):
    size = lax.axis_size(axis)
    return lax.ppermute(value, axis, [(i, i ^ bit) for i in range(size)])


def rotate(value, axis, step):
    size = lax.axis_size(axis)
    return lax.ppermute(value, axis, [(i, (i + step) % size) for i in range(size)])


def after(value, *others):
    return lax.optimization_barrier((value, others))[0]


def in_order(flag, own, other, axis):
    return jnp.where(
        flag == 0,
        jnp.concatenate([own, other], axis),
        jnp.concatenate([other, own], axis),
    )


def silu_parts(pre_act):
    sigma_val = jax.nn.sigmoid(pre_act)
    return (pre_act * sigma_val, sigma_val * (1.0 + pre_act * (1.0 - sigma_val)))


def norm_back(grad_normed, values, inv_rms, gain):
    scaled = grad_normed * gain
    inner = jnp.mean(scaled * values, axis=1, keepdims=True)
    grad_values = inv_rms * scaled - values * (inv_rms * inv_rms * inv_rms) * inner
    return grad_values, jnp.sum(grad_normed * values * inv_rms, axis=0)


def group_gather(value):
    over_y = jnp.stack([value, exchange(value, "exp", 1)])
    over_z = jnp.concatenate([over_y, exchange(over_y, "exp", 2)])
    other = exchange(over_z, "seq", 1)
    return over_z, other


def group_scatter(own, other):
    part = own.astype(F32) + exchange(other, "seq", 1).astype(F32)
    part = part[:2] + exchange(part[2:].astype(BF16), "exp", 2).astype(F32)
    return part[0] + exchange(part[1].astype(BF16), "exp", 1).astype(F32)


def dot(left, right, over):
    return lax.dot_general(left, right, ((over[:1], over[1:]), ((), ())), preferred_element_type=F32)


def masked_softmax(query, keys, allowed, scale):
    scores = jnp.where(allowed, dot(query, keys, (1, 1)) * scale, NEGATIVE)
    expo = jnp.where(allowed, jnp.exp(scores - jnp.max(scores, axis=1, keepdims=True)), 0.0)
    total = jnp.sum(expo, axis=1, keepdims=True)
    return expo * (1.0 / jnp.where(total > 0.5, total, 1.0))


def attention_back_kernel(
    scale, mask_ref, query_ref, key_ref, value_ref, grad_ref, grad_query_ref, grad_key_ref, grad_value_ref
):
    keys = key_ref[...].reshape(-1, HEAD_DIM)
    values = value_ref[...].reshape(-1, HEAD_DIM)
    allowed = mask_ref[...] > 0
    grad_keys = grad_values = 0.0
    for g in range(GROUP_HEADS):
        lanes = slice(g * HEAD_DIM, (g + 1) * HEAD_DIM)
        query, grad = query_ref[:, lanes], grad_ref[:, lanes]
        weights = masked_softmax(query, keys, allowed, scale)
        grad_weights = dot(grad, values, (1, 1))
        delta = jnp.sum(weights * grad_weights, axis=1, keepdims=True)
        grad_scores = (weights * (grad_weights - delta)).astype(BF16)
        grad_query_ref[:, lanes] = (dot(grad_scores, keys, (1, 0)) * scale).astype(BF16)
        grad_keys = grad_keys + dot(query, grad_scores, (0, 0))
        grad_values = grad_values + dot(grad, weights.astype(BF16), (0, 0))
    grad_key_ref[...] = (grad_keys * scale).T.astype(BF16).reshape(grad_key_ref.shape)
    grad_value_ref[...] = grad_values.T.astype(BF16).reshape(grad_value_ref.shape)


MESH = pl.DeviceIdType.MESH
CORE, HALF = ("seq", 1), ("seq", 2)
SIDE, NEAR, FAR = ("exp", 1), ("exp", 2), ("exp", 4)


def bit_of(partner):
    axis, bit = partner
    return lax.axis_index(axis) // bit % 2


def device_of(partner):
    axis, bit = partner
    return {axis: lax.axis_index(axis) + bit - 2 * bit * bit_of(partner)}


def meet(partners):
    barrier = pltpu.get_barrier_semaphore()
    for partner in partners:
        pl.semaphore_signal(barrier, inc=1, device_id=device_of(partner), device_id_type=MESH)
    pl.semaphore_wait(barrier, len(partners))


class Sender:
    def __init__(self, send_sems, recv_sems):
        self.send_sems, self.recv_sems = send_sems, recv_sems
        self.copies, self.landed = [], set()

    def start(self, src, dst, partner):
        i = len(self.copies)
        copy = pltpu.make_async_remote_copy(
            src_ref=src,
            dst_ref=dst,
            send_sem=self.send_sems.at[i],
            recv_sem=self.recv_sems.at[i],
            device_id=device_of(partner),
            device_id_type=MESH,
        )
        copy.start()
        self.copies.append(copy)
        return i

    def arrived(self, *numbers):
        for i in numbers:
            if i not in self.landed:
                self.copies[i].wait_recv()
                self.landed.add(i)

    def finish(self):
        for i, copy in enumerate(self.copies):
            copy.wait_send()
            self.arrived(i)


def semaphores(count):
    return [pltpu.SemaphoreType.DMA((count,)), pltpu.SemaphoreType.DMA((count,))]


ANYWHERE = pl.BlockSpec(memory_space=pl.ANY)
VMEM = pl.BlockSpec(memory_space=pltpu.VMEM)
AXES = (HALF, CORE, FAR, NEAR, SIDE)


def doubling(sender, out, order, columns=None):
    held = []
    for partner in order:
        at = tuple(slice(None) if a in held else bit_of(a) for a in AXES)
        view = out.at[at] if columns is None else out.at[(*at, slice(None), columns)]
        number = sender.start(view, view, partner)
        yield
        sender.arrived(number)
        held.append(partner)


def in_turn(steps):
    steps = list(steps)
    while steps:
        steps = [s for s in steps if next(s, s) is not s]


def attention_heads(scale, rows, mask_ref, query_ref, kv_ref, context_ref):
    allowed = mask_ref[rows, :] > 0
    blocks = [kv_ref.at[j, rows, :] for j in range(4)]

    def head(h, _):
        at = pl.ds(pl.multiple_of(h * HEAD_DIM, HEAD_DIM), HEAD_DIM)
        value_at = pl.ds(pl.multiple_of((h + KV_HEADS) * HEAD_DIM, HEAD_DIM), HEAD_DIM)
        keys = jnp.concatenate([b[:, at] for b in blocks])
        values = jnp.concatenate([b[:, value_at] for b in blocks])
        for g in range(GROUP_HEADS):
            lanes = pl.ds(pl.multiple_of((h * GROUP_HEADS + g) * HEAD_DIM, HEAD_DIM), HEAD_DIM)
            weights = masked_softmax(query_ref[rows, lanes], keys, allowed, scale)
            context_ref[rows, lanes] = dot(weights.astype(BF16), values, (1, 0)).astype(BF16)
        return 0

    lax.fori_loop(0, KV_HEADS, head, 0)


def spreading(sender, value, out):
    count = value.shape[0] // 2
    part = [pl.ds(m * count, count) for m in range(2)]
    firsts = (
        (sender.start(value.at[part[0]], out.at[0, 0, 1, part[0]], SIDE), (0, 1), NEAR, part[0]),
        (sender.start(value.at[part[1]], out.at[0, 1, 0, part[1]], NEAR), (1, 0), SIDE, part[1]),
    )
    seconds = [
        (sender.start(value.at[part[0]], out.at[0, 1, 0, part[0]], NEAR), (1, 0), part[0]),
        (sender.start(value.at[part[1]], out.at[0, 0, 1, part[1]], SIDE), (0, 1), part[1]),
    ]
    sender.start(value, out.at[1, 0, 0], CORE)
    yield
    for number, at, partner, rows in firsts:
        sender.arrived(number)
        seconds.append((sender.start(out.at[(0, *at, rows)], out.at[0, 1, 1, rows], partner), (1, 1), rows))
        sender.start(out.at[(0, *at, rows)], out.at[(1, *at, rows)], CORE)
    yield
    for number, at, rows in seconds:
        sender.arrived(number)
        sender.start(out.at[(0, *at, rows)], out.at[(1, *at, rows)], CORE)


def begin_kernel(
    token_ref, query_shard, kv_shard, out_shard, gain_shard, place_ref, mask_ref,
    gate_ref, up_ref, down_ref, cot_ref, table_ref,
    query_full, kv_full, out_full, gain_ref, normed_ref, query_ref, kv_ref, context_ref, residual_ref, second_ref,
    gate_near, up_near, down_near, gate_far, up_far, down_far, cot_out, table_out, group_out,
    gain_land, gate_own, up_own, down_own, gate_half, up_half, down_half, send, recv, local,
):
    core, half = bit_of(CORE), bit_of(HALF)
    own = tuple(bit_of(a) for a in AXES)
    shards = ((query_shard, query_full), (kv_shard, kv_full), (out_shard, out_full), (gain_shard, gain_land))
    experts = ((gate_ref, gate_own), (up_ref, up_own), (down_ref, down_own))
    nears, fars = (gate_near, up_near, down_near), (gate_far, up_far, down_far)
    owns, halves = (gate_own, up_own, down_own), (gate_half, up_half, down_half)
    for shard, full in shards:
        full[own] = shard[...]
    for ref, mine in experts:
        mine[core] = ref[core]
    copies = [
        pltpu.make_async_copy(cot_ref, cot_out.at[0, 0, 0], local.at[6]),
        pltpu.make_async_copy(table_ref, table_out.at[0, 0, 0], local.at[7]),
    ]
    for copy in copies:
        copy.start()

    def keep(ref, out, i):
        copy = pltpu.make_async_copy(ref, out.at[half], local.at[i])
        copy.start()
        copies.append(copy)
        return sender.start(ref, out.at[half], HALF)

    meet(AXES)
    sender = Sender(send, recv)
    one, two = (NEAR, FAR, SIDE, HALF, CORE), (NEAR, FAR, HALF, SIDE, CORE)

    def pair(full):
        cut = full.shape[-1] // 2
        return [doubling(sender, full, one, pl.ds(0, cut)), doubling(sender, full, two, pl.ds(cut, cut))]

    def turn(*steps):
        for step in steps:
            next(step, None)

    kvs = [doubling(sender, gain_land, one), *pair(kv_full)]
    queries, outs = pair(query_full), pair(out_full)
    turn(*kvs)
    swaps = [sender.start(r.at[1 - core], o.at[core], CORE) for r, o in experts]
    turn(*queries)
    values = token_ref[...].astype(F32)
    inverse = lax.rsqrt(jnp.mean(values * values, axis=1, keepdims=True) + EPSILON)
    turn(*kvs)
    turn(*queries)
    sender.arrived(*swaps)
    keep(gate_own, gate_near, 0)
    turn(*kvs)
    turn(*kvs)
    turn(*queries)
    turn(*kvs)
    gate_sent = sender.start(gate_own, gate_half, FAR)
    turn(*kvs)
    turn(*queries)
    share = query_shard.shape[0]
    gains = gain_land[...].reshape(-1, 8, gain_land.shape[-1])
    owner = lax.broadcasted_iota(jnp.int32, (gains.shape[0], place_ref.shape[1]), 0)
    lane = lax.broadcasted_iota(jnp.int32, owner.shape, 1)
    mine = (lane >= owner * share) & (lane < (owner + 1) * share)
    for i in range(2):
        rows = dot(gains[:, i, :].astype(BF16), place_ref[...], (1, 0))
        gain_ref[i : i + 1, :] = jnp.sum(jnp.where(mine, rows, 0.0), axis=0, keepdims=True)
    normed_ref[...] = (values * inverse * gain_ref[0:1, :]).astype(BF16)
    width = normed_ref.shape[1]
    kv_ref[0] = dot(normed_ref[...], kv_full[...].reshape(width, -1), (1, 0)).astype(BF16)
    kv_half = sender.start(kv_ref.at[0], kv_ref.at[2], HALF)
    kv_core = sender.start(kv_ref.at[0], kv_ref.at[1], CORE)
    turn(*outs)
    turn(*queries)
    table_side = sender.start(table_ref, table_out.at[0, 0, 1], SIDE)
    cot_side = sender.start(cot_ref.at[0], cot_out.at[0, 0, 1, 0], SIDE)
    cot_near = sender.start(cot_ref.at[1], cot_out.at[0, 1, 0, 1], NEAR)
    turn(*queries)
    query_ref[...] = dot(normed_ref[...], query_full[...].reshape(width, -1), (1, 0)).astype(BF16)
    turn(*outs)
    sender.arrived(kv_half)
    kv_both = sender.start(kv_ref.at[2], kv_ref.at[3], CORE)
    keep(up_own, up_near, 1)
    sender.arrived(kv_core, kv_both)
    turn(*outs)
    scale = HEAD_DIM ** (-0.5)
    row_count = mask_ref.shape[1] // 4
    attention_heads(scale, pl.ds(0, row_count), mask_ref, query_ref, kv_ref, context_ref)
    turn(*outs)
    sender.arrived(gate_sent)
    up_sent = sender.start(up_own, up_half, FAR)
    keep(gate_half, gate_far, 3)
    sender.arrived(table_side, cot_side, cot_near)
    for copy in copies[:2]:
        copy.wait()
    table_near = sender.start(table_out.at[0, 0], table_out.at[0, 1], NEAR)
    cots = [
        sender.start(cot_out.at[0, 0, :, 0], cot_out.at[0, 1, :, 0], NEAR),
        sender.start(cot_out.at[0, :, 0, 1], cot_out.at[0, :, 1, 1], SIDE),
    ]
    attention_heads(scale, pl.ds(row_count, row_count), mask_ref, query_ref, kv_ref, context_ref)
    turn(*outs)
    sender.arrived(table_near)
    sender.start(table_out.at[0], table_out.at[1], CORE)
    turn(*outs)
    out_proj = out_full[...].reshape(-1, width)
    for m in range(2):
        rows = pl.ds(m * row_count, row_count)
        residual = token_ref[rows, :].astype(F32) + dot(context_ref[rows, :], out_proj, (1, 0))
        inverse = lax.rsqrt(jnp.mean(residual * residual, axis=1, keepdims=True) + EPSILON)
        residual_ref[rows, :] = residual
        second_ref[rows, :] = (residual * inverse * gain_ref[1:2, :]).astype(BF16)
    spread = spreading(sender, second_ref, group_out)
    next(spread)
    own_rows = pltpu.make_async_copy(second_ref, group_out.at[0, 0, 0], local.at[8])
    own_rows.start()
    keep(down_own, down_near, 2)
    sender.arrived(up_sent)
    down_sent = sender.start(down_own, down_half, FAR)
    keep(up_half, up_far, 4)
    sender.arrived(*cots)
    sender.start(cot_out.at[0], cot_out.at[1], CORE)
    next(spread)
    sender.arrived(down_sent)
    keep(down_half, down_far, 5)
    for _ in spread:
        pass
    for copy in copies[2:]:
        copy.wait()
    own_rows.wait()
    sender.finish()


def begin(tokens, query_proj, kv_proj, output_proj, gains, place, masks, experts, cot, table):
    shape = jax.ShapeDtypeStruct
    rows, width = tokens.shape
    shards = (query_proj, kv_proj, output_proj, gains)
    halves = [(2,) + w.shape[1:] for w in experts]
    full = lambda w: (2,) * 5 + w.shape
    return pl.pallas_call(
        begin_kernel,
        in_specs=[VMEM] * 12,
        out_specs=[VMEM] * 10 + [ANYWHERE] * 9,
        out_shape=[
            shape(full(query_proj), BF16),
            shape(full(kv_proj), BF16),
            shape(full(output_proj), BF16),
            shape((8, width), F32),
            shape((rows, width), BF16),
            shape((rows, query_proj.shape[1]), BF16),
            shape((4, rows, kv_proj.shape[1]), BF16),
            shape((rows, query_proj.shape[1]), BF16),
            shape((rows, width), F32),
            shape((rows, width), BF16),
            *[shape((2, *h), BF16) for h in halves] * 2,
            shape((2, 2, 2) + cot.shape, cot.dtype),
            shape((2, 2, 2) + table.shape, table.dtype),
            shape((2, 2, 2, rows, width), BF16),
        ],
        scratch_shapes=[
            pltpu.VMEM(full(gains), F32),
            *[pltpu.VMEM(h, BF16) for h in halves] * 2,
            *semaphores(76),
            pltpu.SemaphoreType.DMA((9,)),
        ],
        compiler_params=pltpu.CompilerParams(
            collective_id=0, has_side_effects=True, vmem_limit_bytes=60 << 20
        ),
        name="begin",
    )(tokens, *shards, place, masks, *experts, cot, table)


def collecting(sender, parts, core_recv, axis_recv, done):
    orders = ((parts[0], (NEAR, SIDE), (2, 3, 1, 0)), (parts[1], (SIDE, NEAR), (1, 3, 2, 0)))
    numbers, landing = {}, {}
    for place in range(4):
        for m, (ref, _, order) in enumerate(orders):
            b = order[place]
            numbers[m, b] = sender.start(ref.at[4 + b], core_recv.at[m, b], CORE)
    yield
    for place in range(2):
        for m, (ref, axes, order) in enumerate(orders):
            b = order[place]
            sender.arrived(numbers[m, b])
            core_recv[m, b] = ref[b] + core_recv[m, b]
            landing[m, place] = sender.start(core_recv.at[m, b], axis_recv.at[m, place], axes[0])
    yield
    for m, (ref, axes, order) in enumerate(orders):
        b = order[2]
        sender.arrived(numbers[m, b], landing[m, 1])
        total = ref[b].astype(F32) + core_recv[m, b].astype(F32) + axis_recv[m, 1].astype(F32)
        core_recv[m, b] = total.astype(BF16)
        landing[m, 2] = sender.start(core_recv.at[m, b], axis_recv.at[m, 2], axes[1])
    yield
    for m, (ref, _, order) in enumerate(orders):
        sender.arrived(numbers[m, 0], landing[m, 0], landing[m, 2])
        total = ref[0].astype(F32) + core_recv[m, 0].astype(F32)
        done(m, total + axis_recv[m, 0].astype(F32) + axis_recv[m, 2].astype(F32))


def collecting_spaces(block):
    return [pltpu.VMEM((2, 4, *block), BF16), pltpu.VMEM((2, 3, *block), BF16)]


def collect_kernel(
    first_ref, second_ref, normed_ref, cot_ref, wide_ref, down_ref,
    grad_ref, hidden_ref, pre_ref, out_ref, core_recv, axis_recv, send, recv,
):
    meet((CORE, SIDE, NEAR))
    sender = Sender(send, recv)
    width = down_ref.shape[0]
    row_count = first_ref.shape[1]

    def done(m, total):
        rows = pl.ds(m * row_count, row_count)
        grad_ref[rows, :] = grad_ref[rows, :] + total

    parts = collecting(sender, (first_ref, second_ref), core_recv, axis_recv, done)
    next(parts)
    pre_gate = dot(normed_ref[...], wide_ref[:, :width], (1, 0))
    pre_up = dot(normed_ref[...], wide_ref[:, width:], (1, 0))
    next(parts)
    act, deriv = silu_parts(pre_gate)
    hidden_ref[...] = (act * pre_up).astype(BF16)
    grad_hidden = dot(cot_ref[...], down_ref[...], (1, 1))
    pre_ref[:, :width] = (grad_hidden * pre_up * deriv).astype(BF16)
    pre_ref[:, width:] = (grad_hidden * act).astype(BF16)
    out_ref[...] = dot(hidden_ref[...], down_ref[...], (1, 0)).astype(out_ref.dtype)
    grad_ref[...] = dot(pre_ref[...], wide_ref[...], (1, 1))
    for _ in parts:
        pass
    sender.finish()


def collect(first, second, normed, cot, wide, down):
    block = first.shape[1:]
    rows, model_width = normed.shape
    shape = jax.ShapeDtypeStruct
    return pl.pallas_call(
        collect_kernel,
        in_specs=[VMEM] * 6,
        out_specs=[VMEM] * 4,
        out_shape=[
            shape((rows, model_width), F32),
            shape((rows, down.shape[0]), BF16),
            shape((rows, wide.shape[1]), BF16),
            shape((rows, model_width), F32),
        ],
        scratch_shapes=[*collecting_spaces(block), *semaphores(14)],
        compiler_params=pltpu.CompilerParams(
            collective_id=3, has_side_effects=True, vmem_limit_bytes=63 << 20
        ),
        name="collect",
    )(first, second, normed, cot, wide, down)


def back_kernel(
    mask_ref, query_ref, kv_ref, grad_ref, near_wide, near_down, far_wide, far_down, shared_ref,
    grad_query_ref, grad_kv_ref, wide_out, down_out, shared_out,
    part_ref, kv_core, kv_send, kv_half, far_wide_recv, far_down_recv, near_wide_recv, near_down_recv,
    wide_send, down_send, wide_recv, down_recv, wide_core, down_core, wide_own, down_own, *refs,
):
    spaces, (send, recv) = refs[:-2], refs[-2:]
    core, half = bit_of(CORE), bit_of(HALF)
    scale = HEAD_DIM ** (-0.5)
    row_count = mask_ref.shape[1] // 4

    def heads(micro):
        rows = pl.ds(micro * row_count, row_count)
        allowed = mask_ref[rows, :] > 0

        def head(h, _):
            at = pl.ds(pl.multiple_of(h * HEAD_DIM, HEAD_DIM), HEAD_DIM)
            value_at = pl.ds(pl.multiple_of((h + KV_HEADS) * HEAD_DIM, HEAD_DIM), HEAD_DIM)
            keys = jnp.concatenate([kv_ref[j, rows, at] for j in range(4)])
            values = jnp.concatenate([kv_ref[j, rows, value_at] for j in range(4)])
            grad_keys = grad_values = 0.0
            for g in range(GROUP_HEADS):
                lanes = pl.ds(pl.multiple_of((h * GROUP_HEADS + g) * HEAD_DIM, HEAD_DIM), HEAD_DIM)
                query, grad = query_ref[rows, lanes], grad_ref[rows, lanes]
                weights = masked_softmax(query, keys, allowed, scale)
                grad_weights = dot(grad, values, (1, 1))
                delta = jnp.sum(weights * grad_weights, axis=1, keepdims=True)
                grad_scores = (weights * (grad_weights - delta)).astype(BF16)
                grad_query_ref[rows, lanes] = (dot(grad_scores, keys, (1, 0)) * scale).astype(BF16)
                grad_keys = grad_keys + dot(query, grad_scores, (0, 0))
                grad_values = grad_values + dot(grad, weights.astype(BF16), (0, 0))
            grad_keys = (grad_keys * scale).T.astype(BF16)
            grad_values = grad_values.T.astype(BF16)
            for j in range(4):
                part_ref[j, rows, at] = grad_keys[j * row_count : (j + 1) * row_count]
                part_ref[j, rows, value_at] = grad_values[j * row_count : (j + 1) * row_count]
            return 0

        lax.fori_loop(0, KV_HEADS, head, 0)

    def add(*values):
        total = values[0][...].astype(F32)
        for value in values[1:]:
            total = total + value[...].astype(F32)
        return total

    meet(AXES)
    sender = Sender(send, recv)
    other = 1 - half
    across = [sender.start(far_wide.at[other, 0], far_wide_recv.at[0], HALF)]
    order = (CORE, SIDE, HALF, FAR, NEAR)
    shared = halving(sender, shared_ref, spaces, order, shared_out, slice(None))
    next(shared)
    heads(0)
    next(shared)
    across.append(sender.start(far_wide.at[other, 1], far_wide_recv.at[1], HALF))
    fars = []
    for q in range(2):
        if q:
            heads(1)
            next(shared)
            kv_sums = [sender.start(part_ref.at[2 * j + 1], kv_core.at[j], CORE) for j in range(2)]
        sender.arrived(across[q])
        wide_send[q] = add(far_wide[half, q], far_wide_recv[q]).astype(BF16)
        fars.append(sender.start(wide_send.at[q], wide_recv.at[q], FAR))
    far_last = sender.start(far_down.at[other], far_down_recv, HALF)
    sender.arrived(*kv_sums)
    kv_send[...] = add(part_ref[2], kv_core[1]).astype(BF16)
    kv_last = sender.start(kv_send, kv_half, HALF)
    near = [sender.start(near_wide.at[other], near_wide_recv, HALF)]
    sender.arrived(far_last)
    down_send[...] = add(far_down[half], far_down_recv).astype(BF16)
    fars.append(sender.start(down_send, down_recv, FAR))
    near.append(sender.start(near_down.at[other], near_down_recv, HALF))
    next(shared)
    sender.arrived(kv_last)
    grad_kv_ref[...] = add(part_ref[0], kv_core[0], kv_half[...]).astype(BF16)
    sender.arrived(*near, *fars[:2])
    next(shared)

    def finish(near_ref, near_recv, far_recv, own_ref, core_ref, out_ref):
        own_ref[...] = add(near_ref[half, 1 - core], near_recv[1 - core], far_recv[1 - core]).astype(BF16)
        number = sender.start(own_ref, core_ref, CORE)
        out_ref[core] = add(near_ref[half, core], near_recv[core], far_recv[core])
        return number

    wide_last = finish(near_wide, near_wide_recv, wide_recv, wide_own, wide_core, wide_out)
    sender.arrived(wide_last)
    wide_out[1 - core] = wide_core[...].astype(F32)
    sender.arrived(*fars)
    down_last = finish(near_down, near_down_recv, down_recv, down_own, down_core, down_out)
    sender.arrived(down_last)
    down_out[1 - core] = down_core[...].astype(F32)
    for _ in shared:
        pass
    sender.finish()


def back(masks, queries, kv, grad, near_wide, near_down, far_wide, far_down, shared):
    shape = jax.ShapeDtypeStruct
    rows, width = kv.shape[1:]
    wide, down = near_wide.shape[1:], near_down.shape[1:]
    space = lambda *dims: pltpu.VMEM(dims, BF16)
    return pl.pallas_call(
        back_kernel,
        in_specs=[VMEM] * 9,
        out_specs=[VMEM] * 5,
        out_shape=[
            shape(queries.shape, BF16),
            shape((rows, width), BF16),
            shape((2,) + wide[1:], F32),
            shape((2,) + down[1:], F32),
            shape(shared.shape[5:], F32),
        ],
        scratch_shapes=[
            space(4, rows, width),
            space(2, rows, width),
            space(rows, width),
            space(rows, width),
            *[space(*wide), space(*down)] * 4,
            *[space(*wide[1:]), space(*down[1:])] * 2,
            *[space(*(2,) * left, *shared.shape[5:]) for left in range(4, -1, -1)],
            *semaphores(19),
        ],
        compiler_params=pltpu.CompilerParams(
            collective_id=5, has_side_effects=True, vmem_limit_bytes=62 << 20
        ),
        name="back",
    )(masks, queries, kv, grad, near_wide, near_down, far_wide, far_down, shared)


def halving(sender, value, spaces, order, out, columns):
    left = list(AXES)
    for partner, landing in zip(order, spaces):
        place = left.index(partner)
        left.pop(place)
        rest = (slice(None),) * (len(left) - place + 1)
        at = lambda bit: (*(slice(None),) * place, bit, *rest, columns)
        into = (*(slice(None),) * (len(left) + 1), columns)
        own = bit_of(partner)
        number = sender.start(value.at[at(1 - own)], landing.at[into], partner)
        yield
        sender.arrived(number)
        if left:
            landing[into] = value[at(own)] + landing[into]
            value = landing
        else:
            out[into] = value[at(own)].astype(F32) + landing[into].astype(F32)


def reduce_kernel(*refs):
    values, parts, outs, part_out = refs[:3], refs[3:5], refs[5:8], refs[8]
    spaces, (core_recv, axis_recv, send, recv) = refs[9:-4], refs[-4:]

    def done(m, total):
        part_out[m] = total

    meet(AXES)
    sender = Sender(send, recv)
    orders = (
        (CORE, HALF, FAR, NEAR, SIDE),
        (CORE, SIDE, HALF, FAR, NEAR),
        (CORE, HALF, SIDE, FAR, NEAR),
    )
    steps = {}
    for i, (value, order) in enumerate(zip(values, orders)):
        cut, width = value.shape[-1] // 256 * 128, value.shape[-1]
        space = spaces[5 * i : 5 * i + 5]
        steps[i, 0] = halving(sender, value, space, order, outs[i], pl.ds(0, cut))
        steps[i, 1] = halving(sender, value, space, order, outs[i], pl.ds(cut, width - cut))
    collected = collecting(sender, parts, core_recv, axis_recv, done)
    in_turn([steps[1, 0], steps[1, 1], steps[0, 0], steps[2, 0], steps[0, 1], steps[2, 1], collected])
    sender.finish()


def reduce_dense(values, parts):
    blocks, scratch = [], []
    for value in values:
        rows = value.shape[0] // 32
        blocks.append(value.reshape((2,) * 5 + (rows, -1)).astype(BF16))
        scratch += [pltpu.VMEM((2,) * left + blocks[-1].shape[5:], BF16) for left in range(4, -1, -1)]
    return pl.pallas_call(
        reduce_kernel,
        in_specs=[VMEM] * 5,
        out_specs=[VMEM] * 4,
        out_shape=[
            *[jax.ShapeDtypeStruct(v.shape[5:], F32) for v in blocks],
            jax.ShapeDtypeStruct((2, *parts[0].shape[1:]), F32),
        ],
        scratch_shapes=[*scratch, *collecting_spaces(parts[0].shape[1:]), *semaphores(44)],
        compiler_params=pltpu.CompilerParams(
            collective_id=6, has_side_effects=True, vmem_limit_bytes=63 << 20
        ),
        name="reduce_dense",
    )(*blocks, *parts)


def attention_back(micro, masks, queries, kv, grad):
    row_count = grad.shape[0]
    wide = GROUP_HEADS * HEAD_DIM
    heads = lambda at: pl.BlockSpec((4, row_count, HEAD_DIM), lambda h: (0, micro, h + at))
    column = pl.BlockSpec((4, row_count, HEAD_DIM), lambda h: (0, 0, h))
    flat = jax.ShapeDtypeStruct((4, row_count, KV_HEADS * HEAD_DIM), BF16)
    return pl.pallas_call(
        functools.partial(attention_back_kernel, HEAD_DIM ** (-0.5)),
        grid=(KV_HEADS,),
        in_specs=[
            pl.BlockSpec((row_count, 4 * row_count), lambda h: (micro, 0)),
            pl.BlockSpec((row_count, wide), lambda h: (micro, h)),
            heads(0),
            heads(KV_HEADS),
            pl.BlockSpec((row_count, wide), lambda h: (0, h)),
        ],
        out_specs=[pl.BlockSpec((row_count, wide), lambda h: (0, h)), column, column],
        out_shape=[jax.ShapeDtypeStruct((row_count, HEADS * HEAD_DIM), BF16), flat, flat],
        compiler_params=pltpu.CompilerParams(vmem_limit_bytes=48 << 20),
        name="attention_back",
    )(masks, queries, kv, kv, grad)


def expert_kernel(
    slot_ref, scale_ref, column_ref, token_ref, cot_ref, *refs
):
    count = column_ref.shape[0]
    gate_refs, up_refs, down_refs = refs[:count], refs[count : 2 * count], refs[2 * count : 3 * count]
    rows_ref, cots_ref, hidden_ref, pre_ref, mixed_ref, graded_ref = refs[-10:-4]
    pick_ref, value_ref, extra_ref, back_ref = refs[-4:]
    width = down_refs[0].shape[0]
    blocks, row_count = token_ref.shape[0], token_ref.shape[2]
    room = rows_ref.shape[2] // blocks
    slot = lax.broadcasted_iota(jnp.int32, (room, row_count), 0)
    gates = []
    for b in range(blocks):
        for k in range(count):
            picked = slot == slot_ref[k, b]
            gates.append(jnp.sum(jnp.where(picked, scale_ref[k, b], 0.0), axis=1, keepdims=True))
            pick_ref[b, k * room : (k + 1) * room, :] = jnp.where(picked, 1.0, 0.0).astype(BF16)
        rows = dot(pick_ref[b], token_ref[b, 0], (1, 0)).astype(BF16)
        cots = dot(pick_ref[b], cot_ref[b, 0], (1, 0)).astype(BF16)
        for k in range(count):
            part = slice(b * room, (b + 1) * room)
            rows_ref[k, 0, part, :] = rows[k * room : (k + 1) * room]
            cots_ref[k, 0, part, :] = cots[k * room : (k + 1) * room]
    for k in range(count):
        gate = jnp.concatenate([gates[b * count + k] for b in range(blocks)])
        pre_gate = dot(rows_ref[k, 0], gate_refs[k][...], (1, 0))
        pre_up = dot(rows_ref[k, 0], up_refs[k][...], (1, 0))
        grad_hidden = dot(cots_ref[k, 0], down_refs[k][...], (1, 1))
        act, deriv = silu_parts(pre_gate)
        hidden = act * pre_up
        gate_grad = jnp.sum(hidden * grad_hidden, axis=1, keepdims=True)
        grad_hidden = grad_hidden * gate
        hidden_ref[k, 0] = (hidden * gate).astype(BF16)
        pre_ref[k, 0, :, :width] = (grad_hidden * pre_up * deriv).astype(BF16)
        pre_ref[k, 0, :, width:] = (grad_hidden * act).astype(BF16)
        value = dot(hidden_ref[k, 0], down_refs[k][...], (1, 0)).astype(BF16)
        back = dot(pre_ref[k, 0, :, :width], gate_refs[k][...], (1, 1))
        back = (back + dot(pre_ref[k, 0, :, width:], up_refs[k][...], (1, 1))).astype(BF16)
        extra = (gate_grad * column_ref[k]).astype(BF16)
        for b in range(blocks):
            to, part = slice(k * room, (k + 1) * room), slice(b * room, (b + 1) * room)
            value_ref[b, to, :] = value[part]
            back_ref[b, to, :] = back[part]
            extra_ref[b, to, :] = extra[part]
    model_width = token_ref.shape[3]
    for b in range(blocks):
        graded_ref[b] = dot(pick_ref[b], back_ref[b], (0, 0)).astype(BF16)
        mixed_ref[b, :, :model_width] = dot(pick_ref[b], value_ref[b], (0, 0)).astype(BF16)
        mixed_ref[b, :, model_width:] = dot(pick_ref[b], extra_ref[b], (0, 0)).astype(BF16)


def expert_pass(micro, slots, scales, columns, tokens, cots, gates, ups, downs, room, kept):
    count, (width, model_width) = len(downs), downs[0].shape
    blocks, micro_count, row_count = tokens.shape[:3]
    step = 2
    by_block = lambda *dims: pl.BlockSpec((step, *dims), lambda b: (b,) + (0,) * len(dims))
    by_slot = pl.BlockSpec((count, step, 1, row_count), lambda b: (0, b, 0, 0))
    whole = lambda *dims: pl.BlockSpec(dims, lambda b: (0,) * len(dims), pipeline_mode=pl.Buffered(1))
    saved = lambda cols: pl.BlockSpec((count, 1, step * room, cols), lambda b: (0, micro, b, 0))
    widths = (model_width, model_width, width, 2 * width)
    shapes = [jax.ShapeDtypeStruct((count, micro_count, blocks * room, w), BF16) for w in widths]
    args = [slots, scales, columns, tokens, cots, *gates, *ups, *downs]
    in_specs = [
        by_slot,
        by_slot,
        whole(count, 1, 128),
        pl.BlockSpec((step, 1, row_count, model_width), lambda b: (b, micro, 0, 0)),
        pl.BlockSpec((step, 1, row_count, model_width), lambda b: (b, micro, 0, 0)),
        *[whole(model_width, width)] * (2 * count),
        *[whole(width, model_width)] * count,
    ]
    aliases = {}
    if kept:
        aliases = {len(args) + i: i for i in range(len(kept))}
        in_specs += [pl.BlockSpec(memory_space=pl.ANY)] * len(kept)
        args += list(kept)
    out = pl.pallas_call(
        expert_kernel,
        grid=(blocks // step,),
        in_specs=in_specs,
        out_specs=[saved(w) for w in widths]
        + [by_block(row_count, model_width + 128), by_block(row_count, model_width)],
        out_shape=shapes
        + [
            jax.ShapeDtypeStruct((blocks, row_count, model_width + 128), BF16),
            jax.ShapeDtypeStruct((blocks, row_count, model_width), BF16),
        ],
        scratch_shapes=[
            pltpu.VMEM((step, count * room, row_count), BF16),
            pltpu.VMEM((step, count * room, model_width), BF16),
            pltpu.VMEM((step, count * room, 128), BF16),
            pltpu.VMEM((step, count * room, model_width), BF16),
        ],
        input_output_aliases=aliases,
        compiler_params=pltpu.CompilerParams(vmem_limit_bytes=60 << 20),
        name="experts",
    )(*args)
    return out[:4], out[4], out[5]


def attend_plain(queries, kv, masks, micro):
    row_count = masks.shape[1] // 4
    rows = slice(micro * row_count, (micro + 1) * row_count)
    allowed = masks[rows] > 0
    wide = KV_HEADS * HEAD_DIM
    heads = queries[rows].reshape(row_count, KV_HEADS, GROUP_HEADS, HEAD_DIM)
    keys = kv[:, rows, :wide].reshape(-1, KV_HEADS, HEAD_DIM)
    values = kv[:, rows, wide:].reshape(-1, KV_HEADS, HEAD_DIM)
    scores = mm("ikgd,jkd->kgij", heads, keys) * HEAD_DIM ** (-0.5)
    row_max = jnp.max(jnp.where(allowed, scores, NEGATIVE), axis=3, keepdims=True)
    expo = jnp.where(allowed, jnp.exp(jnp.where(allowed, scores, NEGATIVE) - row_max), 0.0)
    total = jnp.sum(expo, axis=3, keepdims=True)
    weights = (expo / jnp.where(total > 0.5, total, 1.0)).astype(BF16)
    return mm("kgij,jkd->ikgd", weights, values).reshape(row_count, HEADS * HEAD_DIM).astype(BF16)


def on_device(
    tokens,
    segment_ids,
    routes,
    route_gates,
    attn_gain,
    query_proj,
    key_proj,
    value_proj,
    output_proj,
    ffn_gain,
    shared_gate,
    shared_up,
    shared_down,
    expert_gate,
    expert_up,
    expert_down,
    output_cot,
):
    micro_count, row_count, model_width = tokens.shape
    exp_count = lax.axis_size("exp")
    local_experts, gate_rows, expert_width = expert_gate.shape
    down_rows = expert_down.shape[1]
    all_experts = local_experts * exp_count
    route_count = routes.shape[2]
    capacity = 4 * row_count * route_count // (3 * all_experts)
    query_width = HEADS * HEAD_DIM
    kv_width = KV_HEADS * HEAD_DIM
    far_steps = exp_count // 4
    assert lax.axis_size("seq") == 4 and local_experts == 2

    seq_index = lax.axis_index("seq")
    exp_index = lax.axis_index("exp")
    core = seq_index % 2
    half = seq_index // 2
    everywhere = ("seq", "exp")

    linked = exp_count == 8
    expert_range = jnp.arange(all_experts, dtype=jnp.int32)
    gate_table = jnp.sum(
        jnp.where(
            jnp.swapaxes(routes, 1, 2)[:, :, None, :] == expert_range[None, None, :, None],
            jnp.swapaxes(route_gates, 1, 2)[:, :, None, :],
            0.0,
        ),
        axis=1,
    )
    order = jnp.arange(row_count, dtype=jnp.int32)
    before = (order[:, None] < order[None, :]).astype(BF16)
    slots = jnp.arange(capacity, dtype=jnp.int32)
    expert_ids = [
        local_experts * ((exp_index - 4 * k + exp_count) % exp_count) + core
        for k in range(far_steps)
    ]
    kv_proj = jnp.concatenate([key_proj, value_proj], axis=1)
    shared_wide = jnp.concatenate([shared_gate, shared_up], axis=1)

    def gathered(value):
        return lax.all_gather(value, everywhere, axis=0, tiled=True)

    def mask_of(micro):
        segments = segment_ids[micro].reshape(4, row_count)
        key_ids = jnp.concatenate(
            [lax.dynamic_index_in_dim(segments, seq_index ^ j, 0, False) for j in range(4)]
        )
        key_pos = jnp.concatenate([(seq_index ^ j) * row_count + order for j in range(4)])
        query_ids, query_pos = key_ids[:row_count], key_pos[:row_count]
        allowed = (
            (key_ids[None, :] == query_ids[:, None])
            & (key_pos[None, :] <= query_pos[:, None])
            & (query_ids[:, None] >= 0)
        )
        return allowed.astype(jnp.int32)

    inputs = tokens.reshape(micro_count * row_count, model_width).astype(F32)
    inv_one = lax.rsqrt(jnp.mean(inputs * inputs, axis=1, keepdims=True) + EPSILON)
    masks = jnp.concatenate([mask_of(micro) for micro in range(micro_count)])
    if linked:
        gains = jnp.stack([attn_gain, ffn_gain]).astype(F32)
        share = gains.shape[1]
        gains = jnp.pad(gains, ((0, 6), (0, 128 - share)))
        lane = jnp.arange(128)[:, None]
        place = (lane == jnp.arange(model_width)[None, :] % share).astype(BF16)
        out = begin(
            tokens.reshape(micro_count * row_count, model_width), query_proj, kv_proj, output_proj, gains, place, masks,
            (expert_gate, expert_up, expert_down), output_cot, gate_table,
        )
        query_full = out[0].reshape(model_width, query_width)
        kv_full = out[1].reshape(model_width, 2 * kv_width)
        out_proj = out[2].reshape(query_width, model_width)
        gain_one, gain_two = out[3][0], out[3][1]
        normed_one, queries, kv, contexts, residual, normed_two = out[4:10]
        gate_all = [w.reshape(model_width, expert_width) for w in (out[10], out[13])]
        up_all = [w.reshape(model_width, expert_width) for w in (out[11], out[14])]
        down_all = [w.reshape(expert_width, model_width) for w in (out[12], out[15])]
        cot_blocks = out[16].reshape(8, micro_count, row_count, model_width)
        gate_blocks = out[17].reshape(8, micro_count, all_experts, row_count)
        token_blocks = out[18].reshape(8, micro_count, row_count, model_width)
        shared_wide, shared_down = after((shared_wide, shared_down), contexts)
    else:
        query_full, kv_full = gathered(query_proj), gathered(kv_proj)
        gain_one, gain_two = gathered(attn_gain).astype(F32), gathered(ffn_gain).astype(F32)
        out_proj = gathered(output_proj)
        normed_one = (inputs * inv_one * gain_one).astype(BF16)
        queries = jnp.dot(normed_one, query_full, preferred_element_type=F32).astype(BF16)
        own = jnp.dot(normed_one, kv_full, preferred_element_type=F32).astype(BF16)
        across = exchange(own, "seq", 2)
        kv = jnp.stack([own, exchange(own, "seq", 1), across, exchange(across, "seq", 1)])
        contexts = jnp.concatenate([attend_plain(queries, kv, masks, m) for m in range(micro_count)])
        gate_blocks = jnp.concatenate(group_gather(gate_table))
        cot_blocks = jnp.concatenate(group_gather(output_cot))

        def parity(value):
            kept = lax.dynamic_index_in_dim(value, core, 0, False)
            sent = lax.dynamic_index_in_dim(value, 1 - core, 0, False)
            return in_order(core, kept, exchange(sent, "seq", 1), 0)

        wide_far = [parity(jnp.concatenate([expert_gate, expert_up], axis=2))]
        down_far = [parity(expert_down)]
        for _ in range(far_steps - 1):
            wide_far.append(rotate(wide_far[-1], "exp", 4))
            down_far.append(rotate(down_far[-1], "exp", 4))
        wide_full = [in_order(half, w, exchange(w, "seq", 2), 0) for w in wide_far]
        down_full = [in_order(half, w, exchange(w, "seq", 2), 0) for w in down_far]

    def sequence_sum(grad_keys, grad_values):
        grad = jnp.concatenate([grad_keys, grad_values], axis=2)
        part = grad[0::2].astype(F32) + exchange(grad[1::2], "seq", 1).astype(F32)
        return (part[0] + exchange(part[1].astype(BF16), "seq", 2).astype(F32)).astype(BF16)

    kept_rows = []

    def experts(micro, normed_blocks):
        gates = jnp.stack(
            [lax.dynamic_index_in_dim(gate_blocks[:, micro], e, 1, False) for e in expert_ids]
        )
        named = gates > 0.0
        rank = mm("kbs,st->kbt", named.astype(BF16), before).astype(jnp.int32)
        slot = jnp.where(named, rank, -1)
        if not linked:
            return experts_plain(gates, slot, normed_blocks[:, micro], cot_blocks[:, micro])
        columns = (
            lax.broadcasted_iota(jnp.int32, (far_steps, 1, 128), 2)
            == jnp.stack(expert_ids)[:, None, None]
        ).astype(F32)
        kept, mixed, graded = expert_pass(
            micro, slot[:, :, None], gates[:, :, None], columns,
            normed_blocks, cot_blocks, gate_all, up_all, down_all, capacity, kept_rows,
        )
        kept_rows[:] = kept
        return graded, mixed

    def experts_plain(gates, slot, normed_blocks, micro_cots):
        mixed, graded, kept = 0.0, 0.0, []
        for k in range(far_steps):
            picked = slot[k][:, None, :] == slots[None, :, None]
            pick = picked.astype(BF16)
            slot_gates = jnp.sum(jnp.where(picked, gates[k][:, None, :], 0.0), axis=2).reshape(-1, 1)
            rows = mm("bst,btd->bsd", pick, normed_blocks).astype(BF16).reshape(-1, model_width)
            cots = mm("bst,btd->bsd", pick, micro_cots).astype(BF16).reshape(-1, model_width)
            pre = jnp.dot(rows, wide_full[k], preferred_element_type=F32)
            pre_gate, pre_up = pre[:, :expert_width], pre[:, expert_width:]
            grad_hidden = mm("rd,fd->rf", cots, down_full[k])
            act, deriv = silu_parts(pre_gate)
            hidden = act * pre_up
            gate_grad = jnp.sum(hidden * grad_hidden, axis=1, keepdims=True)
            hidden = (hidden * slot_gates).astype(BF16)
            grad_hidden = grad_hidden * slot_gates
            grad_pre = jnp.concatenate(
                [(grad_hidden * pre_up * deriv).astype(BF16), (grad_hidden * act).astype(BF16)], axis=1
            )
            value = jnp.dot(hidden, down_full[k], preferred_element_type=F32).astype(BF16)
            column = (lax.broadcasted_iota(jnp.int32, (1, 128), 1) == expert_ids[k]).astype(F32)
            value = jnp.concatenate([value, (gate_grad * column).astype(BF16)], axis=1)
            grad_rows = mm("rf,df->rd", grad_pre, wide_full[k]).astype(BF16)
            blocks = pick.shape[0]
            mixed = mixed + mm("bst,bsd->btd", pick, value.reshape(blocks, capacity, -1))
            graded = graded + mm("bst,bsd->btd", pick, grad_rows.reshape(blocks, capacity, -1))
            kept.append((rows, cots, hidden, grad_pre))
        kept_rows.append(kept)
        return graded.astype(BF16), mixed.astype(BF16)

    up_proj, down_proj = gathered(shared_wide), gathered(shared_down)
    if not linked:
        residual = inputs + jnp.dot(contexts, out_proj, preferred_element_type=F32)
    inv_two = lax.rsqrt(jnp.mean(residual * residual, axis=1, keepdims=True) + EPSILON)
    if not linked:
        normed_two = (residual * inv_two * gain_two).astype(BF16)
        token_blocks = jnp.concatenate(group_gather(normed_two.reshape(tokens.shape)))

    graded_parts, mixed_parts = [], []
    for micro in range(micro_count):
        graded, mixed = experts(micro, token_blocks)
        if not linked:
            graded = group_scatter(graded[:4], graded[4:])
            mixed = group_scatter(mixed[:4], mixed[4:])
            graded, mixed, token_blocks = lax.optimization_barrier((graded, mixed, token_blocks))
        graded_parts.append(graded)
        mixed_parts.append(mixed)

    upstream_low = output_cot.reshape(micro_count * row_count, model_width)
    shared_width = shared_gate.shape[1]
    if linked:
        grad_normed, shared_hidden, grad_shared_pre, shared_out = collect(
            *graded_parts, normed_two, upstream_low, up_proj, down_proj
        )
    else:
        shared_pre = jnp.dot(normed_two, up_proj, preferred_element_type=F32)
        shared_pre_gate, shared_pre_up = shared_pre[:, :shared_width], shared_pre[:, shared_width:]
        shared_act, shared_deriv = silu_parts(shared_pre_gate)
        shared_hidden = (shared_act * shared_pre_up).astype(BF16)
        shared_out = jnp.dot(shared_hidden, down_proj, preferred_element_type=F32)
        grad_shared_hidden = mm("rd,fd->rf", upstream_low, down_proj)
        grad_shared_pre = jnp.concatenate(
            [
                (grad_shared_hidden * shared_pre_up * shared_deriv).astype(BF16),
                (grad_shared_hidden * shared_act).astype(BF16),
            ],
            axis=1,
        )
        grad_from_shared = mm("rf,df->rd", grad_shared_pre, up_proj)
        grad_normed = jnp.concatenate(graded_parts) + grad_from_shared

    def summed(value):
        return lax.psum_scatter(
            value.astype(BF16), everywhere, scatter_dimension=0, tiled=True
        ).astype(F32)

    shared_up_sum = summed(mm("rd,rf->df", normed_two, grad_shared_pre))
    shared_down_sum = mm("rd,rf->df", shared_hidden, upstream_low)

    def flat(value):
        return value.reshape(micro_count * row_count, -1)

    grad_from_two, gain_two_sum = norm_back(grad_normed, residual, inv_two, gain_two)
    grad_residual = upstream_low.astype(F32) + grad_from_two
    grad_branch = grad_residual.astype(BF16)
    grad_context = mm("rd,id->ri", grad_branch, out_proj).astype(BF16)
    output_sum = mm("rd,rf->df", contexts, grad_branch)

    def expert_sum(left, right):
        own = None
        for k in reversed(range(far_steps)):
            lefts = jnp.concatenate([m[k][left] for m in kept_rows])
            rights = jnp.concatenate([m[k][right] for m in kept_rows])
            if own is not None:
                lefts, rights, own = lax.optimization_barrier((lefts, rights, own))
            total = mm("rd,rf->df", lefts, rights)
            rows = total.shape[0] // 2
            total = total.reshape(2, rows, -1)
            mine = lax.dynamic_index_in_dim(total, half, 0, False)
            sent = lax.dynamic_index_in_dim(total, 1 - half, 0, False).astype(BF16)
            total = mine + exchange(sent, "seq", 2).astype(F32)
            own = total if own is None else total + rotate(own.astype(BF16), "exp", -4).astype(F32)
        rows = own.shape[0] // 2
        own = own.reshape(2, rows, -1)
        kept = lax.dynamic_index_in_dim(own, core, 0, False)
        sent = lax.dynamic_index_in_dim(own, 1 - core, 0, False).astype(BF16)
        other = exchange(sent, "seq", 1).astype(F32)
        return in_order(core, kept[None], other[None], 0)

    if linked:
        products = []
        for k in range(far_steps):
            for left, right in ((0, 3), (2, 1)):
                total = mm("mrd,mrf->df", kept_rows[left][k], kept_rows[right][k]).astype(BF16)
                products.append(total.reshape(2, 2, total.shape[0] // 4, -1))
        blocks = shared_down_sum.astype(BF16).reshape((2,) * 5 + shared_down.shape)
        grad_query, grad_kv, wide_grad, down_grad, shared_down_sum = back(
            masks, queries, kv, grad_context, *products, blocks
        )
    else:
        shared_down_sum = summed(shared_down_sum)
        down_grad = expert_sum(2, 1)
        down_grad, kept_rows = lax.optimization_barrier((down_grad, kept_rows))
        wide_grad = expert_sum(0, 3)
        grad_queries, grad_kvs = [], []
        for micro in range(micro_count):
            rows = slice(micro * row_count, (micro + 1) * row_count)
            grad_query, grad_keys, grad_values = attention_back(
                micro, masks, queries, kv, grad_context[rows]
            )
            grad_queries.append(grad_query)
            grad_kvs.append(sequence_sum(grad_keys, grad_values))
        grad_query, grad_kv = jnp.concatenate(grad_queries), jnp.concatenate(grad_kvs)

    grad_normed_one = mm("ri,di->rd", grad_query, query_full) + mm("ri,di->rd", grad_kv, kv_full)
    grad_from_one, gain_one_sum = norm_back(grad_normed_one, inputs, inv_one, gain_one)
    token_grads = (grad_residual + grad_from_one).astype(BF16)
    column = lax.broadcasted_iota(jnp.int32, (1, 2 * kv_width + 128), 1)
    query_sum = mm("rd,rf->df", normed_one, grad_query)
    kv_sum = mm("rd,rf->df", normed_one, jnp.pad(grad_kv, ((0, 0), (0, 128))))
    kv_sum = jnp.where(column == 2 * kv_width, gain_one_sum[:, None], kv_sum)
    kv_sum = jnp.where(column == 2 * kv_width + 1, gain_two_sum[:, None], kv_sum)
    if linked:
        output_sum, query_sum, kv_sum, moe_outs = reduce_dense((output_sum, query_sum, kv_sum), mixed_parts)
        moe_outs = flat(moe_outs)
    else:
        output_sum, query_sum, kv_sum = summed(output_sum), summed(query_sum), summed(kv_sum)
        moe_outs = jnp.concatenate(mixed_parts)
    outputs = (residual + shared_out + moe_outs[:, :model_width]).astype(BF16)
    table = moe_outs[:, model_width : model_width + all_experts]
    gate_grads = jnp.sum(
        jnp.where(flat(routes)[:, :, None] == expert_range[None, None, :], table[:, None, :], 0.0),
        axis=2,
    )

    return (
        outputs.reshape(tokens.shape),
        token_grads.reshape(tokens.shape),
        gate_grads.reshape(routes.shape),
        kv_sum[:, 2 * kv_width],
        query_sum,
        kv_sum[:, :kv_width],
        kv_sum[:, kv_width : 2 * kv_width],
        output_sum,
        kv_sum[:, 2 * kv_width + 1],
        shared_up_sum[:, :shared_width],
        shared_up_sum[:, shared_width:],
        shared_down_sum,
        wide_grad[:, :, :expert_width],
        wide_grad[:, :, expert_width:],
        down_grad,
    )


def solution(mesh):
    rows = P(("seq", "exp"), None)
    wide = P("exp", "seq", None)
    flat = P(("seq", "exp"))
    return jax.shard_map(
        on_device,
        mesh=mesh,
        in_specs=(wide, P("exp", None), wide, wide, flat, rows, rows, rows, rows, flat, rows, rows, rows)
        + (wide,) * 4,
        out_specs=(wide, wide, wide, flat, rows, rows, rows, rows, flat, rows, rows, rows)
        + (wide,) * 3,
        check_vma=False,
    )
```

```python
import functools

import jax
import jax.numpy as jnp
from jax import lax
from jax.experimental import pallas as pl
from jax.experimental.pallas import tpu as pltpu
from jax.sharding import PartitionSpec as P

HEADS = 12
KV_HEADS = 4
HEAD_DIM = 128
GROUP_HEADS = HEADS // KV_HEADS
EPSILON = 1e-05
NEGATIVE = -1e30
F32 = jnp.float32
BF16 = jnp.bfloat16


def mm(spec, left, right):
    return jnp.einsum(spec, left, right, preferred_element_type=F32)


def exchange(value, axis, bit):
    size = lax.axis_size(axis)
    return lax.ppermute(value, axis, [(i, i ^ bit) for i in range(size)])


def rotate(value, axis, step):
    size = lax.axis_size(axis)
    return lax.ppermute(value, axis, [(i, (i + step) % size) for i in range(size)])


def after(value, *others):
    return lax.optimization_barrier((value, others))[0]


def in_order(flag, own, other, axis):
    return jnp.where(
        flag == 0,
        jnp.concatenate([own, other], axis),
        jnp.concatenate([other, own], axis),
    )


def silu_parts(pre_act):
    sigma_val = jax.nn.sigmoid(pre_act)
    return (pre_act * sigma_val, sigma_val * (1.0 + pre_act * (1.0 - sigma_val)))


def norm_back(grad_normed, values, inv_rms, gain):
    scaled = grad_normed * gain
    inner = jnp.mean(scaled * values, axis=1, keepdims=True)
    grad_values = inv_rms * scaled - values * (inv_rms * inv_rms * inv_rms) * inner
    return grad_values, jnp.sum(grad_normed * values * inv_rms, axis=0)


def group_gather(value):
    over_y = jnp.stack([value, exchange(value, "exp", 1)])
    over_z = jnp.concatenate([over_y, exchange(over_y, "exp", 2)])
    other = exchange(over_z, "seq", 1)
    return over_z, other


def group_scatter(own, other):
    part = own.astype(F32) + exchange(other, "seq", 1).astype(F32)
    part = part[:2] + exchange(part[2:].astype(BF16), "exp", 2).astype(F32)
    return part[0] + exchange(part[1].astype(BF16), "exp", 1).astype(F32)


def dot(left, right, over):
    return lax.dot_general(left, right, ((over[:1], over[1:]), ((), ())), preferred_element_type=F32)


def masked_softmax(query, keys, allowed, scale):
    scores = jnp.where(allowed, dot(query, keys, (1, 1)) * scale, NEGATIVE)
    expo = jnp.where(allowed, jnp.exp(scores - jnp.max(scores, axis=1, keepdims=True)), 0.0)
    total = jnp.sum(expo, axis=1, keepdims=True)
    return expo * (1.0 / jnp.where(total > 0.5, total, 1.0))


def attention_back_kernel(
    scale, mask_ref, query_ref, key_ref, value_ref, grad_ref, grad_query_ref, grad_key_ref, grad_value_ref
):
    keys = key_ref[...].reshape(-1, HEAD_DIM)
    values = value_ref[...].reshape(-1, HEAD_DIM)
    allowed = mask_ref[...] > 0
    grad_keys = grad_values = 0.0
    for g in range(GROUP_HEADS):
        lanes = slice(g * HEAD_DIM, (g + 1) * HEAD_DIM)
        query, grad = query_ref[:, lanes], grad_ref[:, lanes]
        weights = masked_softmax(query, keys, allowed, scale)
        grad_weights = dot(grad, values, (1, 1))
        delta = jnp.sum(weights * grad_weights, axis=1, keepdims=True)
        grad_scores = (weights * (grad_weights - delta)).astype(BF16)
        grad_query_ref[:, lanes] = (dot(grad_scores, keys, (1, 0)) * scale).astype(BF16)
        grad_keys = grad_keys + dot(query, grad_scores, (0, 0))
        grad_values = grad_values + dot(grad, weights.astype(BF16), (0, 0))
    grad_key_ref[...] = (grad_keys * scale).T.astype(BF16).reshape(grad_key_ref.shape)
    grad_value_ref[...] = grad_values.T.astype(BF16).reshape(grad_value_ref.shape)


MESH = pl.DeviceIdType.MESH
CORE, HALF = ("seq", 1), ("seq", 2)
SIDE, NEAR, FAR = ("exp", 1), ("exp", 2), ("exp", 4)


def bit_of(partner):
    axis, bit = partner
    return lax.axis_index(axis) // bit % 2


def device_of(partner):
    axis, bit = partner
    return {axis: lax.axis_index(axis) + bit - 2 * bit * bit_of(partner)}


def meet(partners):
    barrier = pltpu.get_barrier_semaphore()
    for partner in partners:
        pl.semaphore_signal(barrier, inc=1, device_id=device_of(partner), device_id_type=MESH)
    pl.semaphore_wait(barrier, len(partners))


class Sender:
    def __init__(self, send_sems, recv_sems):
        self.send_sems, self.recv_sems = send_sems, recv_sems
        self.copies, self.landed = [], set()

    def start(self, src, dst, partner):
        i = len(self.copies)
        copy = pltpu.make_async_remote_copy(
            src_ref=src,
            dst_ref=dst,
            send_sem=self.send_sems.at[i],
            recv_sem=self.recv_sems.at[i],
            device_id=device_of(partner),
            device_id_type=MESH,
        )
        copy.start()
        self.copies.append(copy)
        return i

    def arrived(self, *numbers):
        for i in numbers:
            if i not in self.landed:
                self.copies[i].wait_recv()
                self.landed.add(i)

    def finish(self):
        for i, copy in enumerate(self.copies):
            copy.wait_send()
            self.arrived(i)


def semaphores(count):
    return [pltpu.SemaphoreType.DMA((count,)), pltpu.SemaphoreType.DMA((count,))]


ANYWHERE = pl.BlockSpec(memory_space=pl.ANY)
VMEM = pl.BlockSpec(memory_space=pltpu.VMEM)
AXES = (HALF, CORE, FAR, NEAR, SIDE)


def doubling(sender, out, order, columns=None):
    held = []
    for partner in order:
        at = tuple(slice(None) if a in held else bit_of(a) for a in AXES)
        view = out.at[at] if columns is None else out.at[(*at, slice(None), columns)]
        number = sender.start(view, view, partner)
        yield
        sender.arrived(number)
        held.append(partner)


def in_turn(steps):
    steps = list(steps)
    while steps:
        steps = [s for s in steps if next(s, s) is not s]


def attention_heads(scale, rows, mask_ref, query_ref, kv_ref, context_ref):
    allowed = mask_ref[rows, :] > 0
    blocks = [kv_ref.at[j, rows, :] for j in range(4)]

    def head(h, _):
        at = pl.ds(pl.multiple_of(h * HEAD_DIM, HEAD_DIM), HEAD_DIM)
        value_at = pl.ds(pl.multiple_of((h + KV_HEADS) * HEAD_DIM, HEAD_DIM), HEAD_DIM)
        keys = jnp.concatenate([b[:, at] for b in blocks])
        values = jnp.concatenate([b[:, value_at] for b in blocks])
        for g in range(GROUP_HEADS):
            lanes = pl.ds(pl.multiple_of((h * GROUP_HEADS + g) * HEAD_DIM, HEAD_DIM), HEAD_DIM)
            weights = masked_softmax(query_ref[rows, lanes], keys, allowed, scale)
            context_ref[rows, lanes] = dot(weights.astype(BF16), values, (1, 0)).astype(BF16)
        return 0

    lax.fori_loop(0, KV_HEADS, head, 0)


def spreading(sender, value, out):
    count = value.shape[0] // 2
    part = [pl.ds(m * count, count) for m in range(2)]
    firsts = (
        (sender.start(value.at[part[0]], out.at[0, 0, 1, part[0]], SIDE), (0, 1), NEAR, part[0]),
        (sender.start(value.at[part[1]], out.at[0, 1, 0, part[1]], NEAR), (1, 0), SIDE, part[1]),
    )
    seconds = [
        (sender.start(value.at[part[0]], out.at[0, 1, 0, part[0]], NEAR), (1, 0), part[0]),
        (sender.start(value.at[part[1]], out.at[0, 0, 1, part[1]], SIDE), (0, 1), part[1]),
    ]
    sender.start(value, out.at[1, 0, 0], CORE)
    yield
    for number, at, partner, rows in firsts:
        sender.arrived(number)
        seconds.append((sender.start(out.at[(0, *at, rows)], out.at[0, 1, 1, rows], partner), (1, 1), rows))
        sender.start(out.at[(0, *at, rows)], out.at[(1, *at, rows)], CORE)
    yield
    for number, at, rows in seconds:
        sender.arrived(number)
        sender.start(out.at[(0, *at, rows)], out.at[(1, *at, rows)], CORE)


def begin_kernel(
    token_ref, query_shard, kv_shard, out_shard, gain_shard, place_ref, mask_ref,
    gate_ref, up_ref, down_ref, cot_ref, table_ref,
    query_full, kv_full, out_full, gain_ref, normed_ref, query_ref, kv_ref, context_ref, residual_ref, second_ref,
    gate_near, up_near, down_near, gate_far, up_far, down_far, cot_out, table_out, group_out,
    gain_land, gate_own, up_own, down_own, gate_half, up_half, down_half, send, recv, local,
):
    core, half = bit_of(CORE), bit_of(HALF)
    own = tuple(bit_of(a) for a in AXES)
    shards = ((query_shard, query_full), (kv_shard, kv_full), (out_shard, out_full), (gain_shard, gain_land))
    experts = ((gate_ref, gate_own), (up_ref, up_own), (down_ref, down_own))
    nears, fars = (gate_near, up_near, down_near), (gate_far, up_far, down_far)
    owns, halves = (gate_own, up_own, down_own), (gate_half, up_half, down_half)
    for shard, full in shards:
        full[own] = shard[...]
    for ref, mine in experts:
        mine[core] = ref[core]
    copies = [
        pltpu.make_async_copy(cot_ref, cot_out.at[0, 0, 0], local.at[6]),
        pltpu.make_async_copy(table_ref, table_out.at[0, 0, 0], local.at[7]),
    ]
    for copy in copies:
        copy.start()

    def keep(ref, out, i):
        copy = pltpu.make_async_copy(ref, out.at[half], local.at[i])
        copy.start()
        copies.append(copy)
        return sender.start(ref, out.at[half], HALF)

    meet(AXES)
    sender = Sender(send, recv)
    one, two = (NEAR, FAR, SIDE, HALF, CORE), (NEAR, FAR, HALF, SIDE, CORE)

    def pair(full):
        cut = full.shape[-1] // 2
        return [doubling(sender, full, one, pl.ds(0, cut)), doubling(sender, full, two, pl.ds(cut, cut))]

    def turn(*steps):
        for step in steps:
            next(step, None)

    kvs = [doubling(sender, gain_land, one), *pair(kv_full)]
    queries, outs = pair(query_full), pair(out_full)
    turn(*kvs)
    swaps = [sender.start(r.at[1 - core], o.at[core], CORE) for r, o in experts]
    table_side = sender.start(table_ref, table_out.at[0, 0, 1], SIDE)
    cot_side = sender.start(cot_ref.at[0], cot_out.at[0, 0, 1, 0], SIDE)
    turn(*queries)
    values = token_ref[...].astype(F32)
    inverse = lax.rsqrt(jnp.mean(values * values, axis=1, keepdims=True) + EPSILON)
    turn(*kvs)
    turn(*queries)
    cot_near = sender.start(cot_ref.at[1], cot_out.at[0, 1, 0, 1], NEAR)
    sender.arrived(*swaps)
    keep(gate_own, gate_near, 0)
    turn(*kvs)
    turn(*kvs)
    turn(*queries)
    turn(*kvs)
    gate_sent = sender.start(gate_own, gate_half, FAR)
    turn(*kvs)
    turn(*queries)
    share = query_shard.shape[0]
    gains = gain_land[...].reshape(-1, 8, gain_land.shape[-1])
    owner = lax.broadcasted_iota(jnp.int32, (gains.shape[0], place_ref.shape[1]), 0)
    lane = lax.broadcasted_iota(jnp.int32, owner.shape, 1)
    mine = (lane >= owner * share) & (lane < (owner + 1) * share)
    for i in range(2):
        rows = dot(gains[:, i, :].astype(BF16), place_ref[...], (1, 0))
        gain_ref[i : i + 1, :] = jnp.sum(jnp.where(mine, rows, 0.0), axis=0, keepdims=True)
    normed_ref[...] = (values * inverse * gain_ref[0:1, :]).astype(BF16)
    width = normed_ref.shape[1]
    kv_ref[0] = dot(normed_ref[...], kv_full[...].reshape(width, -1), (1, 0)).astype(BF16)
    kv_half = sender.start(kv_ref.at[0], kv_ref.at[2], HALF)
    kv_core = sender.start(kv_ref.at[0], kv_ref.at[1], CORE)
    turn(*outs)
    turn(*queries)
    turn(*queries)
    sender.arrived(table_side, cot_side, cot_near)
    for copy in copies[:2]:
        copy.wait()
    table_near = sender.start(table_out.at[0, 0], table_out.at[0, 1], NEAR)
    cots = [
        sender.start(cot_out.at[0, 0, :, 0], cot_out.at[0, 1, :, 0], NEAR),
        sender.start(cot_out.at[0, :, 0, 1], cot_out.at[0, :, 1, 1], SIDE),
    ]
    query_ref[...] = dot(normed_ref[...], query_full[...].reshape(width, -1), (1, 0)).astype(BF16)
    turn(*outs)
    sender.arrived(kv_half)
    kv_both = sender.start(kv_ref.at[2], kv_ref.at[3], CORE)
    keep(up_own, up_near, 1)
    sender.arrived(kv_core, kv_both)
    turn(*outs)
    scale = HEAD_DIM ** (-0.5)
    row_count = mask_ref.shape[1] // 4
    attention_heads(scale, pl.ds(0, row_count), mask_ref, query_ref, kv_ref, context_ref)
    turn(*outs)
    sender.arrived(gate_sent)
    up_sent = sender.start(up_own, up_half, FAR)
    attention_heads(scale, pl.ds(row_count, row_count), mask_ref, query_ref, kv_ref, context_ref)
    turn(*outs)
    keep(gate_half, gate_far, 3)
    keep(down_own, down_near, 2)
    sender.arrived(table_near)
    sender.start(table_out.at[0], table_out.at[1], CORE)
    turn(*outs)
    out_proj = out_full[...].reshape(-1, width)
    for m in range(2):
        rows = pl.ds(m * row_count, row_count)
        residual = token_ref[rows, :].astype(F32) + dot(context_ref[rows, :], out_proj, (1, 0))
        inverse = lax.rsqrt(jnp.mean(residual * residual, axis=1, keepdims=True) + EPSILON)
        residual_ref[rows, :] = residual
        second_ref[rows, :] = (residual * inverse * gain_ref[1:2, :]).astype(BF16)
    spread = spreading(sender, second_ref, group_out)
    next(spread)
    own_rows = pltpu.make_async_copy(second_ref, group_out.at[0, 0, 0], local.at[8])
    own_rows.start()
    sender.arrived(up_sent)
    down_sent = sender.start(down_own, down_half, FAR)
    keep(up_half, up_far, 4)
    sender.arrived(*cots)
    sender.start(cot_out.at[0], cot_out.at[1], CORE)
    next(spread)
    sender.arrived(down_sent)
    keep(down_half, down_far, 5)
    for _ in spread:
        pass
    for copy in copies[2:]:
        copy.wait()
    own_rows.wait()
    sender.finish()


def begin(tokens, query_proj, kv_proj, output_proj, gains, place, masks, experts, cot, table):
    shape = jax.ShapeDtypeStruct
    rows, width = tokens.shape
    shards = (query_proj, kv_proj, output_proj, gains)
    halves = [(2,) + w.shape[1:] for w in experts]
    full = lambda w: (2,) * 5 + w.shape
    return pl.pallas_call(
        begin_kernel,
        in_specs=[VMEM] * 12,
        out_specs=[VMEM] * 10 + [ANYWHERE] * 9,
        out_shape=[
            shape(full(query_proj), BF16),
            shape(full(kv_proj), BF16),
            shape(full(output_proj), BF16),
            shape((8, width), F32),
            shape((rows, width), BF16),
            shape((rows, query_proj.shape[1]), BF16),
            shape((4, rows, kv_proj.shape[1]), BF16),
            shape((rows, query_proj.shape[1]), BF16),
            shape((rows, width), F32),
            shape((rows, width), BF16),
            *[shape((2, *h), BF16) for h in halves] * 2,
            shape((2, 2, 2) + cot.shape, cot.dtype),
            shape((2, 2, 2) + table.shape, table.dtype),
            shape((2, 2, 2, rows, width), BF16),
        ],
        scratch_shapes=[
            pltpu.VMEM(full(gains), F32),
            *[pltpu.VMEM(h, BF16) for h in halves] * 2,
            *semaphores(76),
            pltpu.SemaphoreType.DMA((9,)),
        ],
        compiler_params=pltpu.CompilerParams(
            collective_id=0, has_side_effects=True, vmem_limit_bytes=60 << 20
        ),
        name="begin",
    )(tokens, *shards, place, masks, *experts, cot, table)


def collecting(sender, parts, core_recv, axis_recv, done):
    orders = ((parts[0], (NEAR, SIDE), (2, 3, 1, 0)), (parts[1], (SIDE, NEAR), (1, 3, 2, 0)))
    numbers, landing = {}, {}
    for place in range(4):
        for m, (ref, _, order) in enumerate(orders):
            b = order[place]
            numbers[m, b] = sender.start(ref.at[4 + b], core_recv.at[m, b], CORE)
    yield
    for place in range(2):
        for m, (ref, axes, order) in enumerate(orders):
            b = order[place]
            sender.arrived(numbers[m, b])
            core_recv[m, b] = ref[b] + core_recv[m, b]
            landing[m, place] = sender.start(core_recv.at[m, b], axis_recv.at[m, place], axes[0])
    yield
    for m, (ref, axes, order) in enumerate(orders):
        b = order[2]
        sender.arrived(numbers[m, b], landing[m, 1])
        total = ref[b].astype(F32) + core_recv[m, b].astype(F32) + axis_recv[m, 1].astype(F32)
        core_recv[m, b] = total.astype(BF16)
        landing[m, 2] = sender.start(core_recv.at[m, b], axis_recv.at[m, 2], axes[1])
    yield
    for m, (ref, _, order) in enumerate(orders):
        sender.arrived(numbers[m, 0], landing[m, 0], landing[m, 2])
        total = ref[0].astype(F32) + core_recv[m, 0].astype(F32)
        done(m, total + axis_recv[m, 0].astype(F32) + axis_recv[m, 2].astype(F32))


def collecting_spaces(block):
    return [pltpu.VMEM((2, 4, *block), BF16), pltpu.VMEM((2, 3, *block), BF16)]


def collect_kernel(
    first_ref, second_ref, normed_ref, cot_ref, wide_ref, down_ref,
    grad_ref, hidden_ref, pre_ref, out_ref, core_recv, axis_recv, send, recv,
):
    meet((CORE, SIDE, NEAR))
    sender = Sender(send, recv)
    width = down_ref.shape[0]
    row_count = first_ref.shape[1]

    def done(m, total):
        rows = pl.ds(m * row_count, row_count)
        grad_ref[rows, :] = grad_ref[rows, :] + total

    parts = collecting(sender, (first_ref, second_ref), core_recv, axis_recv, done)
    next(parts)
    pre_gate = dot(normed_ref[...], wide_ref[:, :width], (1, 0))
    pre_up = dot(normed_ref[...], wide_ref[:, width:], (1, 0))
    next(parts)
    act, deriv = silu_parts(pre_gate)
    hidden_ref[...] = (act * pre_up).astype(BF16)
    grad_hidden = dot(cot_ref[...], down_ref[...], (1, 1))
    pre_ref[:, :width] = (grad_hidden * pre_up * deriv).astype(BF16)
    pre_ref[:, width:] = (grad_hidden * act).astype(BF16)
    out_ref[...] = dot(hidden_ref[...], down_ref[...], (1, 0)).astype(out_ref.dtype)
    grad_ref[...] = dot(pre_ref[...], wide_ref[...], (1, 1))
    for _ in parts:
        pass
    sender.finish()


def collect(first, second, normed, cot, wide, down):
    block = first.shape[1:]
    rows, model_width = normed.shape
    shape = jax.ShapeDtypeStruct
    return pl.pallas_call(
        collect_kernel,
        in_specs=[VMEM] * 6,
        out_specs=[VMEM] * 4,
        out_shape=[
            shape((rows, model_width), F32),
            shape((rows, down.shape[0]), BF16),
            shape((rows, wide.shape[1]), BF16),
            shape((rows, model_width), F32),
        ],
        scratch_shapes=[*collecting_spaces(block), *semaphores(14)],
        compiler_params=pltpu.CompilerParams(
            collective_id=3, has_side_effects=True, vmem_limit_bytes=63 << 20
        ),
        name="collect",
    )(first, second, normed, cot, wide, down)


def back_kernel(
    mask_ref, query_ref, kv_ref, grad_ref, near_wide, near_down, far_wide, far_down, shared_ref,
    grad_query_ref, grad_kv_ref, wide_out, down_out, shared_out,
    part_ref, kv_core, kv_send, kv_half, far_wide_recv, far_down_recv, near_wide_recv, near_down_recv,
    wide_send, down_send, wide_recv, down_recv, wide_core, down_core, wide_own, down_own, *refs,
):
    spaces, (send, recv) = refs[:-2], refs[-2:]
    core, half = bit_of(CORE), bit_of(HALF)
    scale = HEAD_DIM ** (-0.5)
    row_count = mask_ref.shape[1] // 4

    def heads(micro):
        rows = pl.ds(micro * row_count, row_count)
        allowed = mask_ref[rows, :] > 0

        def head(h, _):
            at = pl.ds(pl.multiple_of(h * HEAD_DIM, HEAD_DIM), HEAD_DIM)
            value_at = pl.ds(pl.multiple_of((h + KV_HEADS) * HEAD_DIM, HEAD_DIM), HEAD_DIM)
            keys = jnp.concatenate([kv_ref[j, rows, at] for j in range(4)])
            values = jnp.concatenate([kv_ref[j, rows, value_at] for j in range(4)])
            grad_keys = grad_values = 0.0
            for g in range(GROUP_HEADS):
                lanes = pl.ds(pl.multiple_of((h * GROUP_HEADS + g) * HEAD_DIM, HEAD_DIM), HEAD_DIM)
                query, grad = query_ref[rows, lanes], grad_ref[rows, lanes]
                weights = masked_softmax(query, keys, allowed, scale)
                grad_weights = dot(grad, values, (1, 1))
                delta = jnp.sum(weights * grad_weights, axis=1, keepdims=True)
                grad_scores = (weights * (grad_weights - delta)).astype(BF16)
                grad_query_ref[rows, lanes] = (dot(grad_scores, keys, (1, 0)) * scale).astype(BF16)
                grad_keys = grad_keys + dot(query, grad_scores, (0, 0))
                grad_values = grad_values + dot(grad, weights.astype(BF16), (0, 0))
            grad_keys = (grad_keys * scale).T.astype(BF16)
            grad_values = grad_values.T.astype(BF16)
            for j in range(4):
                part_ref[j, rows, at] = grad_keys[j * row_count : (j + 1) * row_count]
                part_ref[j, rows, value_at] = grad_values[j * row_count : (j + 1) * row_count]
            return 0

        lax.fori_loop(0, KV_HEADS, head, 0)

    def add(*values):
        total = values[0][...].astype(F32)
        for value in values[1:]:
            total = total + value[...].astype(F32)
        return total

    meet(AXES)
    sender = Sender(send, recv)
    other = 1 - half
    across = [sender.start(far_wide.at[other, 0], far_wide_recv.at[0], HALF)]
    order = (CORE, SIDE, HALF, FAR, NEAR)
    shared = halving(sender, shared_ref, spaces, order, shared_out, slice(None))
    next(shared)
    heads(0)
    next(shared)
    across.append(sender.start(far_wide.at[other, 1], far_wide_recv.at[1], HALF))
    fars = []
    for q in range(2):
        if q:
            heads(1)
            next(shared)
            kv_sums = [sender.start(part_ref.at[2 * j + 1], kv_core.at[j], CORE) for j in range(2)]
        sender.arrived(across[q])
        wide_send[q] = add(far_wide[half, q], far_wide_recv[q]).astype(BF16)
        fars.append(sender.start(wide_send.at[q], wide_recv.at[q], FAR))
    far_last = sender.start(far_down.at[other], far_down_recv, HALF)
    sender.arrived(*kv_sums)
    kv_send[...] = add(part_ref[2], kv_core[1]).astype(BF16)
    kv_last = sender.start(kv_send, kv_half, HALF)
    near = [sender.start(near_wide.at[other], near_wide_recv, HALF)]
    sender.arrived(far_last)
    down_send[...] = add(far_down[half], far_down_recv).astype(BF16)
    fars.append(sender.start(down_send, down_recv, FAR))
    near.append(sender.start(near_down.at[other], near_down_recv, HALF))
    next(shared)
    sender.arrived(kv_last)
    grad_kv_ref[...] = add(part_ref[0], kv_core[0], kv_half[...]).astype(BF16)
    sender.arrived(*near, *fars[:2])
    next(shared)

    def finish(near_ref, near_recv, far_recv, own_ref, core_ref, out_ref):
        own_ref[...] = add(near_ref[half, 1 - core], near_recv[1 - core], far_recv[1 - core]).astype(BF16)
        number = sender.start(own_ref, core_ref, CORE)
        out_ref[core] = add(near_ref[half, core], near_recv[core], far_recv[core])
        return number

    wide_last = finish(near_wide, near_wide_recv, wide_recv, wide_own, wide_core, wide_out)
    sender.arrived(wide_last)
    wide_out[1 - core] = wide_core[...].astype(F32)
    sender.arrived(*fars)
    down_last = finish(near_down, near_down_recv, down_recv, down_own, down_core, down_out)
    sender.arrived(down_last)
    down_out[1 - core] = down_core[...].astype(F32)
    for _ in shared:
        pass
    sender.finish()


def back(masks, queries, kv, grad, near_wide, near_down, far_wide, far_down, shared):
    shape = jax.ShapeDtypeStruct
    rows, width = kv.shape[1:]
    wide, down = near_wide.shape[1:], near_down.shape[1:]
    space = lambda *dims: pltpu.VMEM(dims, BF16)
    return pl.pallas_call(
        back_kernel,
        in_specs=[VMEM] * 9,
        out_specs=[VMEM] * 5,
        out_shape=[
            shape(queries.shape, BF16),
            shape((rows, width), BF16),
            shape((2,) + wide[1:], F32),
            shape((2,) + down[1:], F32),
            shape(shared.shape[5:], F32),
        ],
        scratch_shapes=[
            space(4, rows, width),
            space(2, rows, width),
            space(rows, width),
            space(rows, width),
            *[space(*wide), space(*down)] * 4,
            *[space(*wide[1:]), space(*down[1:])] * 2,
            *[space(*(2,) * left, *shared.shape[5:]) for left in range(4, -1, -1)],
            *semaphores(19),
        ],
        compiler_params=pltpu.CompilerParams(
            collective_id=5, has_side_effects=True, vmem_limit_bytes=62 << 20
        ),
        name="back",
    )(masks, queries, kv, grad, near_wide, near_down, far_wide, far_down, shared)


def halving(sender, value, spaces, order, out, columns):
    left = list(AXES)
    for partner, landing in zip(order, spaces):
        place = left.index(partner)
        left.pop(place)
        rest = (slice(None),) * (len(left) - place + 1)
        at = lambda bit: (*(slice(None),) * place, bit, *rest, columns)
        into = (*(slice(None),) * (len(left) + 1), columns)
        own = bit_of(partner)
        number = sender.start(value.at[at(1 - own)], landing.at[into], partner)
        yield
        sender.arrived(number)
        if left:
            landing[into] = value[at(own)] + landing[into]
            value = landing
        else:
            out[into] = value[at(own)].astype(F32) + landing[into].astype(F32)


def reduce_kernel(*refs):
    values, parts, outs, part_out = refs[:3], refs[3:5], refs[5:8], refs[8]
    spaces, (core_recv, axis_recv, send, recv) = refs[9:-4], refs[-4:]

    def done(m, total):
        part_out[m] = total

    meet(AXES)
    sender = Sender(send, recv)
    orders = (
        (CORE, HALF, FAR, NEAR, SIDE),
        (CORE, SIDE, HALF, FAR, NEAR),
        (CORE, HALF, SIDE, FAR, NEAR),
    )
    steps = {}
    for i, (value, order) in enumerate(zip(values, orders)):
        cut, width = value.shape[-1] // 256 * 128, value.shape[-1]
        space = spaces[5 * i : 5 * i + 5]
        steps[i, 0] = halving(sender, value, space, order, outs[i], pl.ds(0, cut))
        steps[i, 1] = halving(sender, value, space, order, outs[i], pl.ds(cut, width - cut))
    collected = collecting(sender, parts, core_recv, axis_recv, done)
    in_turn([steps[1, 0], steps[1, 1], steps[0, 0], steps[2, 0], steps[0, 1], steps[2, 1], collected])
    sender.finish()


def reduce_dense(values, parts):
    blocks, scratch = [], []
    for value in values:
        rows = value.shape[0] // 32
        blocks.append(value.reshape((2,) * 5 + (rows, -1)).astype(BF16))
        scratch += [pltpu.VMEM((2,) * left + blocks[-1].shape[5:], BF16) for left in range(4, -1, -1)]
    return pl.pallas_call(
        reduce_kernel,
        in_specs=[VMEM] * 5,
        out_specs=[VMEM] * 4,
        out_shape=[
            *[jax.ShapeDtypeStruct(v.shape[5:], F32) for v in blocks],
            jax.ShapeDtypeStruct((2, *parts[0].shape[1:]), F32),
        ],
        scratch_shapes=[*scratch, *collecting_spaces(parts[0].shape[1:]), *semaphores(44)],
        compiler_params=pltpu.CompilerParams(
            collective_id=6, has_side_effects=True, vmem_limit_bytes=63 << 20
        ),
        name="reduce_dense",
    )(*blocks, *parts)


def attention_back(micro, masks, queries, kv, grad):
    row_count = grad.shape[0]
    wide = GROUP_HEADS * HEAD_DIM
    heads = lambda at: pl.BlockSpec((4, row_count, HEAD_DIM), lambda h: (0, micro, h + at))
    column = pl.BlockSpec((4, row_count, HEAD_DIM), lambda h: (0, 0, h))
    flat = jax.ShapeDtypeStruct((4, row_count, KV_HEADS * HEAD_DIM), BF16)
    return pl.pallas_call(
        functools.partial(attention_back_kernel, HEAD_DIM ** (-0.5)),
        grid=(KV_HEADS,),
        in_specs=[
            pl.BlockSpec((row_count, 4 * row_count), lambda h: (micro, 0)),
            pl.BlockSpec((row_count, wide), lambda h: (micro, h)),
            heads(0),
            heads(KV_HEADS),
            pl.BlockSpec((row_count, wide), lambda h: (0, h)),
        ],
        out_specs=[pl.BlockSpec((row_count, wide), lambda h: (0, h)), column, column],
        out_shape=[jax.ShapeDtypeStruct((row_count, HEADS * HEAD_DIM), BF16), flat, flat],
        compiler_params=pltpu.CompilerParams(vmem_limit_bytes=48 << 20),
        name="attention_back",
    )(masks, queries, kv, kv, grad)


def expert_kernel(
    slot_ref, scale_ref, column_ref, token_ref, cot_ref, *refs
):
    count = column_ref.shape[0]
    gate_refs, up_refs, down_refs = refs[:count], refs[count : 2 * count], refs[2 * count : 3 * count]
    rows_ref, cots_ref, hidden_ref, pre_ref, mixed_ref, graded_ref = refs[-10:-4]
    pick_ref, value_ref, extra_ref, back_ref = refs[-4:]
    width = down_refs[0].shape[0]
    blocks, row_count = token_ref.shape[0], token_ref.shape[2]
    room = rows_ref.shape[2] // blocks
    slot = lax.broadcasted_iota(jnp.int32, (room, row_count), 0)
    gates = []
    for b in range(blocks):
        for k in range(count):
            picked = slot == slot_ref[k, b]
            gates.append(jnp.sum(jnp.where(picked, scale_ref[k, b], 0.0), axis=1, keepdims=True))
            pick_ref[b, k * room : (k + 1) * room, :] = jnp.where(picked, 1.0, 0.0).astype(BF16)
        rows = dot(pick_ref[b], token_ref[b, 0], (1, 0)).astype(BF16)
        cots = dot(pick_ref[b], cot_ref[b, 0], (1, 0)).astype(BF16)
        for k in range(count):
            part = slice(b * room, (b + 1) * room)
            rows_ref[k, 0, part, :] = rows[k * room : (k + 1) * room]
            cots_ref[k, 0, part, :] = cots[k * room : (k + 1) * room]
    for k in range(count):
        gate = jnp.concatenate([gates[b * count + k] for b in range(blocks)])
        pre_gate = dot(rows_ref[k, 0], gate_refs[k][...], (1, 0))
        pre_up = dot(rows_ref[k, 0], up_refs[k][...], (1, 0))
        grad_hidden = dot(cots_ref[k, 0], down_refs[k][...], (1, 1))
        act, deriv = silu_parts(pre_gate)
        hidden = act * pre_up
        gate_grad = jnp.sum(hidden * grad_hidden, axis=1, keepdims=True)
        grad_hidden = grad_hidden * gate
        hidden_ref[k, 0] = (hidden * gate).astype(BF16)
        pre_ref[k, 0, :, :width] = (grad_hidden * pre_up * deriv).astype(BF16)
        pre_ref[k, 0, :, width:] = (grad_hidden * act).astype(BF16)
        value = dot(hidden_ref[k, 0], down_refs[k][...], (1, 0)).astype(BF16)
        back = dot(pre_ref[k, 0, :, :width], gate_refs[k][...], (1, 1))
        back = (back + dot(pre_ref[k, 0, :, width:], up_refs[k][...], (1, 1))).astype(BF16)
        extra = (gate_grad * column_ref[k]).astype(BF16)
        for b in range(blocks):
            to, part = slice(k * room, (k + 1) * room), slice(b * room, (b + 1) * room)
            value_ref[b, to, :] = value[part]
            back_ref[b, to, :] = back[part]
            extra_ref[b, to, :] = extra[part]
    model_width = token_ref.shape[3]
    for b in range(blocks):
        graded_ref[b] = dot(pick_ref[b], back_ref[b], (0, 0)).astype(BF16)
        mixed_ref[b, :, :model_width] = dot(pick_ref[b], value_ref[b], (0, 0)).astype(BF16)
        mixed_ref[b, :, model_width:] = dot(pick_ref[b], extra_ref[b], (0, 0)).astype(BF16)


def expert_pass(micro, slots, scales, columns, tokens, cots, gates, ups, downs, room, kept):
    count, (width, model_width) = len(downs), downs[0].shape
    blocks, micro_count, row_count = tokens.shape[:3]
    step = 2
    by_block = lambda *dims: pl.BlockSpec((step, *dims), lambda b: (b,) + (0,) * len(dims))
    by_slot = pl.BlockSpec((count, step, 1, row_count), lambda b: (0, b, 0, 0))
    whole = lambda *dims: pl.BlockSpec(dims, lambda b: (0,) * len(dims), pipeline_mode=pl.Buffered(1))
    saved = lambda cols: pl.BlockSpec((count, 1, step * room, cols), lambda b: (0, micro, b, 0))
    widths = (model_width, model_width, width, 2 * width)
    shapes = [jax.ShapeDtypeStruct((count, micro_count, blocks * room, w), BF16) for w in widths]
    args = [slots, scales, columns, tokens, cots, *gates, *ups, *downs]
    in_specs = [
        by_slot,
        by_slot,
        whole(count, 1, 128),
        pl.BlockSpec((step, 1, row_count, model_width), lambda b: (b, micro, 0, 0)),
        pl.BlockSpec((step, 1, row_count, model_width), lambda b: (b, micro, 0, 0)),
        *[whole(model_width, width)] * (2 * count),
        *[whole(width, model_width)] * count,
    ]
    aliases = {}
    if kept:
        aliases = {len(args) + i: i for i in range(len(kept))}
        in_specs += [pl.BlockSpec(memory_space=pl.ANY)] * len(kept)
        args += list(kept)
    out = pl.pallas_call(
        expert_kernel,
        grid=(blocks // step,),
        in_specs=in_specs,
        out_specs=[saved(w) for w in widths]
        + [by_block(row_count, model_width + 128), by_block(row_count, model_width)],
        out_shape=shapes
        + [
            jax.ShapeDtypeStruct((blocks, row_count, model_width + 128), BF16),
            jax.ShapeDtypeStruct((blocks, row_count, model_width), BF16),
        ],
        scratch_shapes=[
            pltpu.VMEM((step, count * room, row_count), BF16),
            pltpu.VMEM((step, count * room, model_width), BF16),
            pltpu.VMEM((step, count * room, 128), BF16),
            pltpu.VMEM((step, count * room, model_width), BF16),
        ],
        input_output_aliases=aliases,
        compiler_params=pltpu.CompilerParams(vmem_limit_bytes=60 << 20),
        name="experts",
    )(*args)
    return out[:4], out[4], out[5]


def attend_plain(queries, kv, masks, micro):
    row_count = masks.shape[1] // 4
    rows = slice(micro * row_count, (micro + 1) * row_count)
    allowed = masks[rows] > 0
    wide = KV_HEADS * HEAD_DIM
    heads = queries[rows].reshape(row_count, KV_HEADS, GROUP_HEADS, HEAD_DIM)
    keys = kv[:, rows, :wide].reshape(-1, KV_HEADS, HEAD_DIM)
    values = kv[:, rows, wide:].reshape(-1, KV_HEADS, HEAD_DIM)
    scores = mm("ikgd,jkd->kgij", heads, keys) * HEAD_DIM ** (-0.5)
    row_max = jnp.max(jnp.where(allowed, scores, NEGATIVE), axis=3, keepdims=True)
    expo = jnp.where(allowed, jnp.exp(jnp.where(allowed, scores, NEGATIVE) - row_max), 0.0)
    total = jnp.sum(expo, axis=3, keepdims=True)
    weights = (expo / jnp.where(total > 0.5, total, 1.0)).astype(BF16)
    return mm("kgij,jkd->ikgd", weights, values).reshape(row_count, HEADS * HEAD_DIM).astype(BF16)


def on_device(
    tokens,
    segment_ids,
    routes,
    route_gates,
    attn_gain,
    query_proj,
    key_proj,
    value_proj,
    output_proj,
    ffn_gain,
    shared_gate,
    shared_up,
    shared_down,
    expert_gate,
    expert_up,
    expert_down,
    output_cot,
):
    micro_count, row_count, model_width = tokens.shape
    exp_count = lax.axis_size("exp")
    local_experts, gate_rows, expert_width = expert_gate.shape
    down_rows = expert_down.shape[1]
    all_experts = local_experts * exp_count
    route_count = routes.shape[2]
    capacity = 4 * row_count * route_count // (3 * all_experts)
    query_width = HEADS * HEAD_DIM
    kv_width = KV_HEADS * HEAD_DIM
    far_steps = exp_count // 4
    assert lax.axis_size("seq") == 4 and local_experts == 2

    seq_index = lax.axis_index("seq")
    exp_index = lax.axis_index("exp")
    core = seq_index % 2
    half = seq_index // 2
    everywhere = ("seq", "exp")

    linked = exp_count == 8
    expert_range = jnp.arange(all_experts, dtype=jnp.int32)
    gate_table = jnp.sum(
        jnp.where(
            jnp.swapaxes(routes, 1, 2)[:, :, None, :] == expert_range[None, None, :, None],
            jnp.swapaxes(route_gates, 1, 2)[:, :, None, :],
            0.0,
        ),
        axis=1,
    )
    order = jnp.arange(row_count, dtype=jnp.int32)
    before = (order[:, None] < order[None, :]).astype(BF16)
    slots = jnp.arange(capacity, dtype=jnp.int32)
    expert_ids = [
        local_experts * ((exp_index - 4 * k + exp_count) % exp_count) + core
        for k in range(far_steps)
    ]
    kv_proj = jnp.concatenate([key_proj, value_proj], axis=1)
    shared_wide = jnp.concatenate([shared_gate, shared_up], axis=1)

    def gathered(value):
        return lax.all_gather(value, everywhere, axis=0, tiled=True)

    def mask_of(micro):
        segments = segment_ids[micro].reshape(4, row_count)
        key_ids = jnp.concatenate(
            [lax.dynamic_index_in_dim(segments, seq_index ^ j, 0, False) for j in range(4)]
        )
        key_pos = jnp.concatenate([(seq_index ^ j) * row_count + order for j in range(4)])
        query_ids, query_pos = key_ids[:row_count], key_pos[:row_count]
        allowed = (
            (key_ids[None, :] == query_ids[:, None])
            & (key_pos[None, :] <= query_pos[:, None])
            & (query_ids[:, None] >= 0)
        )
        return allowed.astype(jnp.int32)

    inputs = tokens.reshape(micro_count * row_count, model_width).astype(F32)
    inv_one = lax.rsqrt(jnp.mean(inputs * inputs, axis=1, keepdims=True) + EPSILON)
    masks = jnp.concatenate([mask_of(micro) for micro in range(micro_count)])
    if linked:
        gains = jnp.stack([attn_gain, ffn_gain]).astype(F32)
        share = gains.shape[1]
        gains = jnp.pad(gains, ((0, 6), (0, 128 - share)))
        lane = jnp.arange(128)[:, None]
        place = (lane == jnp.arange(model_width)[None, :] % share).astype(BF16)
        out = begin(
            tokens.reshape(micro_count * row_count, model_width), query_proj, kv_proj, output_proj, gains, place, masks,
            (expert_gate, expert_up, expert_down), output_cot, gate_table,
        )
        query_full = out[0].reshape(model_width, query_width)
        kv_full = out[1].reshape(model_width, 2 * kv_width)
        out_proj = out[2].reshape(query_width, model_width)
        gain_one, gain_two = out[3][0], out[3][1]
        normed_one, queries, kv, contexts, residual, normed_two = out[4:10]
        gate_all = [w.reshape(model_width, expert_width) for w in (out[10], out[13])]
        up_all = [w.reshape(model_width, expert_width) for w in (out[11], out[14])]
        down_all = [w.reshape(expert_width, model_width) for w in (out[12], out[15])]
        cot_blocks = out[16].reshape(8, micro_count, row_count, model_width)
        gate_blocks = out[17].reshape(8, micro_count, all_experts, row_count)
        token_blocks = out[18].reshape(8, micro_count, row_count, model_width)
        shared_wide = after(shared_wide, contexts)
    else:
        query_full, kv_full = gathered(query_proj), gathered(kv_proj)
        gain_one, gain_two = gathered(attn_gain).astype(F32), gathered(ffn_gain).astype(F32)
        out_proj = gathered(output_proj)
        normed_one = (inputs * inv_one * gain_one).astype(BF16)
        queries = jnp.dot(normed_one, query_full, preferred_element_type=F32).astype(BF16)
        own = jnp.dot(normed_one, kv_full, preferred_element_type=F32).astype(BF16)
        across = exchange(own, "seq", 2)
        kv = jnp.stack([own, exchange(own, "seq", 1), across, exchange(across, "seq", 1)])
        contexts = jnp.concatenate([attend_plain(queries, kv, masks, m) for m in range(micro_count)])
        gate_blocks = jnp.concatenate(group_gather(gate_table))
        cot_blocks = jnp.concatenate(group_gather(output_cot))

        def parity(value):
            kept = lax.dynamic_index_in_dim(value, core, 0, False)
            sent = lax.dynamic_index_in_dim(value, 1 - core, 0, False)
            return in_order(core, kept, exchange(sent, "seq", 1), 0)

        wide_far = [parity(jnp.concatenate([expert_gate, expert_up], axis=2))]
        down_far = [parity(expert_down)]
        for _ in range(far_steps - 1):
            wide_far.append(rotate(wide_far[-1], "exp", 4))
            down_far.append(rotate(down_far[-1], "exp", 4))
        wide_full = [in_order(half, w, exchange(w, "seq", 2), 0) for w in wide_far]
        down_full = [in_order(half, w, exchange(w, "seq", 2), 0) for w in down_far]

    def sequence_sum(grad_keys, grad_values):
        grad = jnp.concatenate([grad_keys, grad_values], axis=2)
        part = grad[0::2].astype(F32) + exchange(grad[1::2], "seq", 1).astype(F32)
        return (part[0] + exchange(part[1].astype(BF16), "seq", 2).astype(F32)).astype(BF16)

    kept_rows = []

    def experts(micro, normed_blocks):
        gates = jnp.stack(
            [lax.dynamic_index_in_dim(gate_blocks[:, micro], e, 1, False) for e in expert_ids]
        )
        named = gates > 0.0
        rank = mm("kbs,st->kbt", named.astype(BF16), before).astype(jnp.int32)
        slot = jnp.where(named, rank, -1)
        if not linked:
            return experts_plain(gates, slot, normed_blocks[:, micro], cot_blocks[:, micro])
        columns = (
            lax.broadcasted_iota(jnp.int32, (far_steps, 1, 128), 2)
            == jnp.stack(expert_ids)[:, None, None]
        ).astype(F32)
        kept, mixed, graded = expert_pass(
            micro, slot[:, :, None], gates[:, :, None], columns,
            normed_blocks, cot_blocks, gate_all, up_all, down_all, capacity, kept_rows,
        )
        kept_rows[:] = kept
        return graded, mixed

    def experts_plain(gates, slot, normed_blocks, micro_cots):
        mixed, graded, kept = 0.0, 0.0, []
        for k in range(far_steps):
            picked = slot[k][:, None, :] == slots[None, :, None]
            pick = picked.astype(BF16)
            slot_gates = jnp.sum(jnp.where(picked, gates[k][:, None, :], 0.0), axis=2).reshape(-1, 1)
            rows = mm("bst,btd->bsd", pick, normed_blocks).astype(BF16).reshape(-1, model_width)
            cots = mm("bst,btd->bsd", pick, micro_cots).astype(BF16).reshape(-1, model_width)
            pre = jnp.dot(rows, wide_full[k], preferred_element_type=F32)
            pre_gate, pre_up = pre[:, :expert_width], pre[:, expert_width:]
            grad_hidden = mm("rd,fd->rf", cots, down_full[k])
            act, deriv = silu_parts(pre_gate)
            hidden = act * pre_up
            gate_grad = jnp.sum(hidden * grad_hidden, axis=1, keepdims=True)
            hidden = (hidden * slot_gates).astype(BF16)
            grad_hidden = grad_hidden * slot_gates
            grad_pre = jnp.concatenate(
                [(grad_hidden * pre_up * deriv).astype(BF16), (grad_hidden * act).astype(BF16)], axis=1
            )
            value = jnp.dot(hidden, down_full[k], preferred_element_type=F32).astype(BF16)
            column = (lax.broadcasted_iota(jnp.int32, (1, 128), 1) == expert_ids[k]).astype(F32)
            value = jnp.concatenate([value, (gate_grad * column).astype(BF16)], axis=1)
            grad_rows = mm("rf,df->rd", grad_pre, wide_full[k]).astype(BF16)
            blocks = pick.shape[0]
            mixed = mixed + mm("bst,bsd->btd", pick, value.reshape(blocks, capacity, -1))
            graded = graded + mm("bst,bsd->btd", pick, grad_rows.reshape(blocks, capacity, -1))
            kept.append((rows, cots, hidden, grad_pre))
        kept_rows.append(kept)
        return graded.astype(BF16), mixed.astype(BF16)

    up_proj, down_proj = gathered(shared_wide), gathered(shared_down)
    if not linked:
        residual = inputs + jnp.dot(contexts, out_proj, preferred_element_type=F32)
    inv_two = lax.rsqrt(jnp.mean(residual * residual, axis=1, keepdims=True) + EPSILON)
    if not linked:
        normed_two = (residual * inv_two * gain_two).astype(BF16)
        token_blocks = jnp.concatenate(group_gather(normed_two.reshape(tokens.shape)))

    graded_parts, mixed_parts = [], []
    for micro in range(micro_count):
        graded, mixed = experts(micro, token_blocks)
        if not linked:
            graded = group_scatter(graded[:4], graded[4:])
            mixed = group_scatter(mixed[:4], mixed[4:])
            graded, mixed, token_blocks = lax.optimization_barrier((graded, mixed, token_blocks))
        graded_parts.append(graded)
        mixed_parts.append(mixed)

    upstream_low = output_cot.reshape(micro_count * row_count, model_width)
    shared_width = shared_gate.shape[1]
    if linked:
        grad_normed, shared_hidden, grad_shared_pre, shared_out = collect(
            *graded_parts, normed_two, upstream_low, up_proj, down_proj
        )
    else:
        shared_pre = jnp.dot(normed_two, up_proj, preferred_element_type=F32)
        shared_pre_gate, shared_pre_up = shared_pre[:, :shared_width], shared_pre[:, shared_width:]
        shared_act, shared_deriv = silu_parts(shared_pre_gate)
        shared_hidden = (shared_act * shared_pre_up).astype(BF16)
        shared_out = jnp.dot(shared_hidden, down_proj, preferred_element_type=F32)
        grad_shared_hidden = mm("rd,fd->rf", upstream_low, down_proj)
        grad_shared_pre = jnp.concatenate(
            [
                (grad_shared_hidden * shared_pre_up * shared_deriv).astype(BF16),
                (grad_shared_hidden * shared_act).astype(BF16),
            ],
            axis=1,
        )
        grad_from_shared = mm("rf,df->rd", grad_shared_pre, up_proj)
        grad_normed = jnp.concatenate(graded_parts) + grad_from_shared

    def summed(value):
        return lax.psum_scatter(
            value.astype(BF16), everywhere, scatter_dimension=0, tiled=True
        ).astype(F32)

    shared_up_sum = summed(mm("rd,rf->df", normed_two, grad_shared_pre))
    shared_down_sum = mm("rd,rf->df", shared_hidden, upstream_low)

    def flat(value):
        return value.reshape(micro_count * row_count, -1)

    grad_from_two, gain_two_sum = norm_back(grad_normed, residual, inv_two, gain_two)
    grad_residual = upstream_low.astype(F32) + grad_from_two
    grad_branch = grad_residual.astype(BF16)
    grad_context = mm("rd,id->ri", grad_branch, out_proj).astype(BF16)
    output_sum = mm("rd,rf->df", contexts, grad_branch)

    def expert_sum(left, right):
        own = None
        for k in reversed(range(far_steps)):
            lefts = jnp.concatenate([m[k][left] for m in kept_rows])
            rights = jnp.concatenate([m[k][right] for m in kept_rows])
            if own is not None:
                lefts, rights, own = lax.optimization_barrier((lefts, rights, own))
            total = mm("rd,rf->df", lefts, rights)
            rows = total.shape[0] // 2
            total = total.reshape(2, rows, -1)
            mine = lax.dynamic_index_in_dim(total, half, 0, False)
            sent = lax.dynamic_index_in_dim(total, 1 - half, 0, False).astype(BF16)
            total = mine + exchange(sent, "seq", 2).astype(F32)
            own = total if own is None else total + rotate(own.astype(BF16), "exp", -4).astype(F32)
        rows = own.shape[0] // 2
        own = own.reshape(2, rows, -1)
        kept = lax.dynamic_index_in_dim(own, core, 0, False)
        sent = lax.dynamic_index_in_dim(own, 1 - core, 0, False).astype(BF16)
        other = exchange(sent, "seq", 1).astype(F32)
        return in_order(core, kept[None], other[None], 0)

    if linked:
        products = []
        for k in range(far_steps):
            for left, right in ((0, 3), (2, 1)):
                total = mm("mrd,mrf->df", kept_rows[left][k], kept_rows[right][k]).astype(BF16)
                products.append(total.reshape(2, 2, total.shape[0] // 4, -1))
        blocks = shared_down_sum.astype(BF16).reshape((2,) * 5 + shared_down.shape)
        grad_query, grad_kv, wide_grad, down_grad, shared_down_sum = back(
            masks, queries, kv, grad_context, *products, blocks
        )
    else:
        shared_down_sum = summed(shared_down_sum)
        down_grad = expert_sum(2, 1)
        down_grad, kept_rows = lax.optimization_barrier((down_grad, kept_rows))
        wide_grad = expert_sum(0, 3)
        grad_queries, grad_kvs = [], []
        for micro in range(micro_count):
            rows = slice(micro * row_count, (micro + 1) * row_count)
            grad_query, grad_keys, grad_values = attention_back(
                micro, masks, queries, kv, grad_context[rows]
            )
            grad_queries.append(grad_query)
            grad_kvs.append(sequence_sum(grad_keys, grad_values))
        grad_query, grad_kv = jnp.concatenate(grad_queries), jnp.concatenate(grad_kvs)

    grad_normed_one = mm("ri,di->rd", grad_query, query_full) + mm("ri,di->rd", grad_kv, kv_full)
    grad_from_one, gain_one_sum = norm_back(grad_normed_one, inputs, inv_one, gain_one)
    token_grads = (grad_residual + grad_from_one).astype(BF16)
    column = lax.broadcasted_iota(jnp.int32, (1, 2 * kv_width + 128), 1)
    query_sum = mm("rd,rf->df", normed_one, grad_query)
    kv_sum = mm("rd,rf->df", normed_one, jnp.pad(grad_kv, ((0, 0), (0, 128))))
    kv_sum = jnp.where(column == 2 * kv_width, gain_one_sum[:, None], kv_sum)
    kv_sum = jnp.where(column == 2 * kv_width + 1, gain_two_sum[:, None], kv_sum)
    if linked:
        output_sum, query_sum, kv_sum, moe_outs = reduce_dense((output_sum, query_sum, kv_sum), mixed_parts)
        moe_outs = flat(moe_outs)
    else:
        output_sum, query_sum, kv_sum = summed(output_sum), summed(query_sum), summed(kv_sum)
        moe_outs = jnp.concatenate(mixed_parts)
    outputs = (residual + shared_out + moe_outs[:, :model_width]).astype(BF16)
    table = moe_outs[:, model_width : model_width + all_experts]
    gate_grads = jnp.sum(
        jnp.where(flat(routes)[:, :, None] == expert_range[None, None, :], table[:, None, :], 0.0),
        axis=2,
    )

    return (
        outputs.reshape(tokens.shape),
        token_grads.reshape(tokens.shape),
        gate_grads.reshape(routes.shape),
        kv_sum[:, 2 * kv_width],
        query_sum,
        kv_sum[:, :kv_width],
        kv_sum[:, kv_width : 2 * kv_width],
        output_sum,
        kv_sum[:, 2 * kv_width + 1],
        shared_up_sum[:, :shared_width],
        shared_up_sum[:, shared_width:],
        shared_down_sum,
        wide_grad[:, :, :expert_width],
        wide_grad[:, :, expert_width:],
        down_grad,
    )


def solution(mesh):
    rows = P(("seq", "exp"), None)
    wide = P("exp", "seq", None)
    flat = P(("seq", "exp"))
    return jax.shard_map(
        on_device,
        mesh=mesh,
        in_specs=(wide, P("exp", None), wide, wide, flat, rows, rows, rows, rows, flat, rows, rows, rows)
        + (wide,) * 4,
        out_specs=(wide, wide, wide, flat, rows, rows, rows, rows, flat, rows, rows, rows)
        + (wide,) * 3,
        check_vma=False,
    )
```
